32 devices in a mesh: uly: 4 (over x, core), blk: 8 (over z, y).
Axes of the slice: x: 2, y: 2, z: 4, core: 2. Of those that a mesh axis runs over, the one named last changes fastest.
Arguments:
- tokens: bfloat16 [4096, 2048], P(('blk', 'uly')), may hold values from -6 to 6
- lengths: int32 [4], replicated, may hold values from 1 to 1024, 2048 in all
- attn_gain: bfloat16 [2048], P(('uly', 'blk')), may hold values from 0.5 to 1.5
- w_qkv: bfloat16 [2048, 4096], P(('uly', 'blk')), may hold values from -0.125 to 0.125
- q_gain: bfloat16 [128], replicated, may hold values from 0.796875 to 1.796875
- k_gain: bfloat16 [128], replicated, may hold values from 0.796875 to 1.796875
- w_out: bfloat16 [2048, 2048], P(('uly', 'blk')), may hold values from -0.5 to 0.5
- mlp_gain: bfloat16 [2048], P(('uly', 'blk')), may hold values from 0.5 to 1.5
- w_gate_up: bfloat16 [2048, 12288], P(('uly', 'blk')), may hold values from -0.125 to 0.125
- w_down: bfloat16 [6144, 2048], P(('uly', 'blk')), may hold values from -0.078125 to 0.078125
- cotangent: float32 [4096, 2048], P(('blk', 'uly')), may hold values from -100 to 100
Outputs:
- output: bfloat16 [4096, 2048], P(('blk', 'uly'))
- d_tokens: float32 [4096, 2048], P(('blk', 'uly'))
- d_attn_gain: float32 [2048], P(('uly', 'blk'))
- d_w_qkv: float32 [2048, 4096], P(('uly', 'blk'))
- d_q_gain: float32 [128], replicated
- d_k_gain: float32 [128], replicated
- d_w_out: float32 [2048, 2048], P(('uly', 'blk'))
- d_mlp_gain: float32 [2048], P(('uly', 'blk'))
- d_w_gate_up: float32 [2048, 12288], P(('uly', 'blk'))
- d_w_down: float32 [6144, 2048], P(('uly', 'blk'))
The draws below stay inside these ranges and needn't reach their ends.
Inputs may be any that keep to these rules, and one draw needn't show every extreme that they name: The lengths sum to 2048; the longest is exactly 1024.
All inputs are finite; a program needn't handle non-finite values.
Results may differ from the reference program's by a relative error of at most 0.024.
Values may be sent and summed in bfloat16 or wider, within the bound.
A program may use at most 128 MiB of HBM per device.

```python
import math
import jax
import jax.numpy as jnp
import numpy as np
from jax import lax

D = 2048
HQ = 16
HK = 8
HD = 128
FF = 6144
PROMPT = 2048
CONT_LEN = 512
TOKENS = 4096
NCONT = 4
QKV = 4096


def draw_cotangent(key, part):
    key_rows, key_main = jax.random.split(key, 2)
    row_place = jnp.arange(TOKENS, dtype=jnp.float32)[:, None]
    rising = jnp.exp(jnp.log(3.0) * row_place / TOKENS)
    spread = jnp.exp(jax.random.uniform(key_rows, (TOKENS, 1), minval=-1.15, maxval=1.15))
    values = jnp.clip(jax.random.normal(key_main, (TOKENS, D)), -4.0, 4.0) * spread * rising
    return values.astype(jnp.float32)


def spiked(array, key, source, target, parts, factor):
    def block_of(dim):
        return (jnp.arange(array.shape[dim]) // (array.shape[dim] // parts)).reshape((-1,) + (1,) * (array.ndim - 1 - dim))

    near = jax.random.permutation(key, parts)[block_of(target)]
    far = (block_of(target) + parts // 2) % parts
    return jnp.where((block_of(source) == near) | (block_of(source) == far), factor * array, array)


def block_levels(rng, extent, cuts, smallest, largest):
    def one(dim, blocks):
        steps = jax.random.uniform(jax.random.fold_in(jax.random.fold_in(rng, 6), dim), (blocks,), jnp.float32, smallest / len(cuts), largest / len(cuts))
        return jnp.repeat(jnp.exp(steps), extent[dim] // blocks).reshape((-1,) + (1,) * (len(extent) - dim - 1))

    factor_of = one(*cuts[0])
    for cut in cuts[1:]:
        factor_of = factor_of * one(*cut)
    return factor_of


def profile(number_of, total, most, lean):
    weights = [(1 << 20) // math.isqrt(standing ** lean) + 1 for standing in range(2, number_of + 1)]
    spare, holding = total - most - (number_of - 1), [1] * (number_of - 1)
    while spare > 0:
        free = [i for i in range(number_of - 1) if holding[i] < most]
        mass, left = sum([weights[i] for i in free]), spare
        for i in free:
            extra = min(most - holding[i], max(1, left * weights[i] // mass), spare)
            holding[i] = holding[i] + extra
            spare = spare - extra
    return np.array([most] + holding)


def ragged(key, number_of, total, limit, slope):
    if number_of == 2:
        one = jax.random.randint(key, (), max(1, total - limit), min(limit, total - 1) + 1)
        return jnp.stack([one, total - one])
    sizes = jnp.asarray(profile(number_of, total, limit, slope), jnp.int32)
    twos = (number_of - 1) // 2
    giver, taker = sizes[1:1 + 2 * twos:2], sizes[2:2 + 2 * twos:2]
    room = jnp.minimum(giver - 1, limit - taker)
    shifted = jax.random.randint(jax.random.fold_in(key, 1), (twos,), 0, 1 << 20) % (room + 1)
    sizes = sizes.at[1:1 + 2 * twos:2].set(giver - shifted).at[2:2 + 2 * twos:2].set(taker + shifted)
    return sizes[jax.random.permutation(jax.random.fold_in(key, 2), number_of)]


def bell_draw(key, shape, scale, bound, shards=(), kind=jnp.bfloat16):
    level = block_levels(key, shape, shards, -0.22, 0.18) if shards else 1.0
    array = jax.random.normal(key, shape, jnp.float32) * scale * level
    return jnp.minimum(jnp.maximum(array, -bound), bound).astype(kind)


def heavy_noise(stream_key, extent, scale, most, pieces, heavy, kind=jnp.bfloat16):
    entries = scale * jax.random.normal(stream_key, extent, jnp.float32)
    if pieces:
        entries = entries * block_levels(stream_key, extent, pieces, -0.22, 0.18)
    return jnp.clip(spiked(entries, jax.random.fold_in(stream_key, 3), *heavy), -most, most).astype(kind)


def setup_inputs(seed: int = 0) -> dict:
    streams_of = jax.random.split(jax.random.key(seed), 12)
    tokens = heavy_noise(streams_of[0], (TOKENS, D), 1.0, 6.0, ((0, 32),), (0, 1, 32, 2.75))
    lengths = ragged(streams_of[1], NCONT, TOKENS - PROMPT, 2 * CONT_LEN, 2).astype(jnp.int32)
    attn_gain = jnp.clip(1.0 + 0.1 * jax.random.normal(streams_of[2], (D,), jnp.float32), 0.5, 1.5).astype(jnp.bfloat16)
    w_qkv = bell_draw(streams_of[3], (D, QKV), D ** -0.5, 0.125, ((0, 32),))
    q_gain = jnp.clip(jax.random.uniform(streams_of[4], (HD,), jnp.float32, 0.796875, 1.796875), 0.796875, 1.796875).astype(jnp.bfloat16)
    k_gain = jnp.clip(jax.random.uniform(streams_of[5], (HD,), jnp.float32, 0.796875, 1.796875), 0.796875, 1.796875).astype(jnp.bfloat16)
    w_out = bell_draw(streams_of[6], (HQ * HD, D), (4.0 / (HQ * HD) ** 0.5), 0.5, ((0, 32),))
    mlp_gain = jnp.clip(1.0 + 0.1 * jax.random.normal(streams_of[7], (D,), jnp.float32), 0.5, 1.5).astype(jnp.bfloat16)
    w_gate_up = bell_draw(streams_of[8], (D, 2 * FF), D ** -0.5, 0.125, ((0, 32),))
    w_down = bell_draw(streams_of[9], (FF, D), FF ** -0.5, 0.078125, ((0, 32),))
    cotangent = draw_cotangent(jax.random.fold_in(streams_of[11], 71), 0)
    return {"tokens": tokens, "lengths": lengths, "attn_gain": attn_gain, "w_qkv": w_qkv, "q_gain": q_gain, "k_gain": k_gain, "w_out": w_out, "mlp_gain": mlp_gain, "w_gate_up": w_gate_up, "w_down": w_down, "cotangent": cotangent}


EPSILON = 1e-06
ROPE_BASE = 1000000.0
NEGATIVE = -1e+30

@jax.custom_vjp
def low(v):
    return lax.optimization_barrier(v.astype(jnp.bfloat16)).astype(jnp.float32)

@jax.custom_vjp
def low_back(v):
    return v

def low_keep(v):
    return (low(v), None)

def low_pass(kept, grad):
    return (grad,)

def back_keep(v):
    return (v, None)

def back_low(kept, grad):
    return (low(grad),)
low.defvjp(low_keep, low_pass)
low_back.defvjp(back_keep, back_low)

def token_info(token_index, lengths):
    starts = (PROMPT + jnp.cumsum(lengths) - lengths).astype(jnp.int32)
    passed = token_index[:, None] >= starts[None, :]
    segment = lax.optimization_barrier(jnp.sum(passed.astype(jnp.int32), 1)).astype(jnp.int32)
    opening = jnp.maximum(lax.optimization_barrier(jnp.max(jnp.where(passed, starts[None, :], 0), 1)), PROMPT).astype(jnp.int32)
    return (segment, (token_index - opening + PROMPT).astype(jnp.int32))

def rotate(vectors, position):
    halfway = vectors.shape[-1] // 2
    inverse = ROPE_BASE ** (-2.0 * jnp.arange(halfway, dtype=jnp.float32) / vectors.shape[-1])
    angles = position.astype(jnp.float32)[:, None] * inverse[None, :]
    cosine = jnp.cos(angles)[:, None, :]
    sine_part = jnp.sin(angles)[:, None, :]
    former = vectors[..., :halfway]
    latter = vectors[..., halfway:]
    return jnp.concatenate([former * cosine - latter * sine_part, latter * cosine + former * sine_part], -1)

def head_norm(vectors, norm_gain):
    return vectors * lax.rsqrt(lax.optimization_barrier(jnp.mean(vectors * vectors, -1, keepdims=True)) + EPSILON) * norm_gain

def shape_heads(projected, position, q_gain, k_gain):
    row_total = projected.shape[0]
    queries = projected[:, :HQ * HD].reshape(row_total, HQ, HD)
    keys = projected[:, HQ * HD:(HQ + HK) * HD].reshape(row_total, HK, HD)
    return (rotate(head_norm(queries, q_gain), position), rotate(head_norm(keys, k_gain), position))

def attention(queries, keys, values, segment, position):
    row_total = queries.shape[0]
    block_size = min(512, row_total)
    block_total = row_total // block_size
    pairs = HQ // HK
    grouped = queries.reshape(block_total, block_size, HK, pairs, HD)
    factor_q = 1.0 / math.sqrt(HD)

    def one_block(inputs_here):
        rows_q, seg_rows, pos_rows = inputs_here
        scores = jnp.einsum('qgrd,kgd->grqk', rows_q, keys, precision=lax.Precision.HIGHEST) * factor_q
        scores = low_back(scores)
        allowed = (position[None, :] <= pos_rows[:, None]) & ((segment[None, :] == 0) | (segment[None, :] == seg_rows[:, None]))
        masked = jnp.where(allowed[None, None], scores, NEGATIVE)
        highest = lax.optimization_barrier(jnp.max(masked, -1, keepdims=True))
        weights = jnp.exp(masked - highest)
        probabilities = low(weights / lax.optimization_barrier(jnp.sum(weights, -1, keepdims=True)))
        return jnp.einsum('grqk,kgd->qgrd', probabilities, values, precision=lax.Precision.HIGHEST)
    mixed = lax.map(jax.checkpoint(one_block), (grouped, segment.reshape(block_total, block_size), position.reshape(block_total, block_size)))
    return mixed.reshape(row_total, HQ, HD)

def layer(inputs, attn_gain, w_qkv, q_gain, k_gain, w_out, mlp_gain, w_gate_up, w_down, segment, position):
    row_total = inputs.shape[0]
    highest = lax.Precision.HIGHEST
    inverse_one = lax.rsqrt(lax.optimization_barrier(jnp.mean(inputs * inputs, 1, keepdims=True)) + EPSILON)
    normed_one = low(inputs * inverse_one * attn_gain)
    projected = low_back(jnp.dot(normed_one, w_qkv, precision=highest))
    rotated_q, rotated_k = shape_heads(projected, position, q_gain, k_gain)
    values = projected[:, (HQ + HK) * HD:].reshape(row_total, HK, HD)
    queries = low(low_back(rotated_q))
    keys = low(low_back(rotated_k))
    values = low(low_back(values))
    mixed = attention(queries, keys, values, segment, position)
    mixed = low(low_back(mixed)).reshape(row_total, HQ * HD)
    hidden = inputs + low_back(jnp.dot(mixed, w_out, precision=highest))
    inverse_two = lax.rsqrt(lax.optimization_barrier(jnp.mean(hidden * hidden, 1, keepdims=True)) + EPSILON)
    normed_two = low(hidden * inverse_two * mlp_gain)
    both = low_back(jnp.dot(normed_two, w_gate_up, precision=highest))
    gate = both[:, :FF]
    up_part = both[:, FF:]
    activated = low(jax.nn.silu(gate) * up_part)
    return hidden + low_back(jnp.dot(activated, w_down, precision=highest))

def reference(tokens, lengths, attn_gain, w_qkv, q_gain, k_gain, w_out, mlp_gain, w_gate_up, w_down, cotangent):
    token_index = jnp.arange(tokens.shape[0], dtype=jnp.int32)
    segment, position = token_info(token_index, lengths)

    def forward(*params):
        return layer(*params, segment, position)
    params = tuple((argument.astype(jnp.float32) for argument in (tokens, attn_gain, w_qkv, q_gain, k_gain, w_out, mlp_gain, w_gate_up, w_down)))
    result, pullback = jax.vjp(forward, *params)
    gradients = pullback(cotangent.astype(jnp.float32))
    return (result.astype(jnp.bfloat16), gradients[0], gradients[1], gradients[2], gradients[3], gradients[4], gradients[5], gradients[6], gradients[7], gradients[8])
```

```python
import functools
import math

import jax
import jax.numpy as jnp
from jax import lax
from jax.experimental import pallas as pl
from jax.experimental.pallas import tpu as pltpu
from jax.sharding import PartitionSpec as P

D = 2048
HQ = 16
HK = 8
HD = 128
FF = 6144
PROMPT = 2048
LONGEST = 1024

SLOTS = 8
CHUNK = 128
QKV_SLOT = 512
GU_SLOT = 2 * FF // SLOTS
FF_SLOT = FF // SLOTS
EPSILON = 1e-06
ROPE_BASE = 1000000.0
SCALE = 1.0 / math.sqrt(HD)

F32 = jnp.float32
BF16 = jnp.bfloat16
MESH = pl.DeviceIdType.MESH
HBM = pl.BlockSpec(memory_space=pl.ANY)
VMEM = pl.BlockSpec(memory_space=pltpu.VMEM)
DMA = pltpu.SemaphoreType.DMA
THIRDS = (640, 640, 768)


def rem(a, n):
    return lax.rem(a, jnp.int32(n))


class Place:
    def __init__(self, groups):
        self.groups = groups
        self.u = lax.axis_index("uly")
        self.b = lax.axis_index("blk")
        self.x = self.u // 2
        self.c = rem(self.u, 2)
        self.g = self.b // 4
        self.bl = rem(self.b, 4)
        self.bits = (self.x, rem(self.bl, 2), self.bl // 2)

    def flip(self, *dims):
        x, y, z = (rem(v + 1, 2) if d in dims else v for d, v in enumerate(self.bits))
        return x, 2 * z + y

    def chunk(self, *dims):
        x, bl = self.flip(*dims)
        return 2 * bl + x

    def slot(self, *dims):
        x, bl = self.flip(*dims)
        return 4 * x + bl

    def cube(self, *dims):
        x, bl = self.flip(*dims)
        return (2 * x + self.c, 4 * self.g + bl)

    def sibling(self):
        return (2 * self.x + 1 - self.c, self.b)

    def ahead(self, i):
        return rem(self.g + i, self.groups)

    def behind(self, i):
        return rem(self.g + self.groups - i, self.groups)

    def mid(self, i):
        return (self.u, 4 * self.ahead(i) + self.bl)

    def mid_at(self, group):
        return (self.u, 4 * group + self.bl)


PEERS = ((0,), (1,), (2,), (0, 1), (0, 2), (1, 2), (0, 1, 2))


def meet(devices):
    barrier = pltpu.get_barrier_semaphore()
    for device in devices:
        pl.semaphore_signal(barrier, inc=1, device_id=device, device_id_type=MESH)
    pl.semaphore_wait(barrier, len(devices))


def remote(src, dst, send, recv, device):
    return pltpu.make_async_remote_copy(
        src_ref=src, dst_ref=dst, send_sem=send, recv_sem=recv, device_id=device, device_id_type=MESH
    )


def rows_at(start, count):
    return pl.ds(pl.multiple_of(start, 16), count)


def drive(*tasks):
    tasks = list(tasks)
    while tasks:
        tasks = [task for task in tasks if next(task, None) is not None]


def part_columns(widths):
    start = 0
    for p, width in enumerate(widths):
        yield p, (p, (p + 1) % 3, (p + 2) % 3), pl.ds(start, width)
        start += width


def gather_tokens(at, mine, block, local, send, recv, widths=THIRDS):
    own = pltpu.make_async_copy(mine, block.at[at.chunk()], local)
    own.start()
    sent = []

    def push(p, i, dims, along, cols):
        src = block.at[at.chunk(*dims), :, cols] if dims else mine.at[:, cols]
        copy = remote(src, block.at[at.chunk(*dims), :, cols], send.at[p, i], recv.at[p, i], at.cube(along))
        copy.start()
        sent.append(copy)

    def arrive(p, i, dims, cols):
        there = block.at[at.chunk(*dims), :, cols]
        remote(there, there, send.at[p, i], recv.at[p, i], at.cube(dims[0])).wait_recv()

    parts = list(part_columns(widths))
    for p, (a, b, c), cols in parts:
        push(p, 0, (), a, cols)
        push(p, 1, (), b, cols)
        push(p, 2, (), c, cols)
    yield True
    for p, (a, b, c), cols in parts:
        arrive(p, 0, (a,), cols)
        push(p, 3, (a,), b, cols)
        push(p, 4, (a,), c, cols)
    yield True
    for p, (a, b, c), cols in parts:
        arrive(p, 1, (b,), cols)
        push(p, 5, (b,), c, cols)
        arrive(p, 3, (a, b), cols)
        push(p, 6, (a, b), c, cols)
    yield True
    for p, (a, b, c), cols in parts:
        arrive(p, 2, (c,), cols)
        arrive(p, 4, (a, c), cols)
        arrive(p, 5, (b, c), cols)
        arrive(p, 6, (a, b, c), cols)
    for copy in sent:
        copy.wait_send()
    own.wait()


def add_rows(dst, terms, count, step=32):
    def body(i, carry):
        rows = pl.ds(pl.multiple_of(i * step, step), step)
        total = terms[0][rows, :].astype(F32)
        for term in terms[1:]:
            total = total + term[rows, :].astype(F32)
        dst[rows, :] = total.astype(dst.dtype)
        return carry

    lax.fori_loop(0, count // step, body, 0)


def scatter_tokens(at, part, land, out, send, recv, widths=THIRDS):
    sent = []

    def push(p, i, dims, along, cols):
        copy = remote(part.at[at.chunk(*dims), :, cols], land.at[i, :, cols], send.at[p, i], recv.at[p, i], at.cube(along))
        copy.start()
        sent.append(copy)

    def arrive(p, i, along, cols):
        remote(land.at[i, :, cols], land.at[i, :, cols], send.at[p, i], recv.at[p, i], at.cube(along)).wait_recv()

    def add(i, dims, cols):
        here = part.at[at.chunk(*dims), :, cols]
        add_rows(here, [here, land.at[i, :, cols]], CHUNK)

    parts = list(part_columns(widths))
    for p, (a, b, c), cols in parts:
        push(p, 3, (a, b, c), c, cols)
        push(p, 2, (b, c), c, cols)
    for p, (a, b, c), cols in parts:
        push(p, 1, (a, c), c, cols)
        push(p, 0, (c,), c, cols)
    yield True
    for p, (a, b, c), cols in parts:
        arrive(p, 3, c, cols)
        add(3, (a, b), cols)
        push(p, 5, (a, b), b, cols)
        arrive(p, 2, c, cols)
        add(2, (b,), cols)
        push(p, 4, (b,), b, cols)
    yield True
    for p, (a, b, c), cols in parts:
        arrive(p, 1, c, cols)
        add(1, (a,), cols)
        arrive(p, 5, b, cols)
        add(5, (a,), cols)
        push(p, 6, (a,), a, cols)
    yield True
    for p, (a, b, c), cols in parts:
        arrive(p, 0, c, cols)
        arrive(p, 4, b, cols)
        arrive(p, 6, a, cols)
        add_rows(
            out.at[:, cols],
            [part.at[at.chunk(), :, cols], land.at[0, :, cols], land.at[4, :, cols], land.at[6, :, cols]],
            CHUNK,
        )
    for copy in sent:
        copy.wait_send()


def gather_columns(at, mine, whole, local, send, recv, mid_send, mid_recv, sib_send, sib_recv):
    n, rows = at.groups, mine.shape[1]
    run = 4 * rows

    def row_of(u, b):
        return (u * (4 * n) + b) * rows

    own = rows_at(row_of(at.u, at.b), rows)
    here = pltpu.make_async_copy(mine.at[at.slot()], whole.at[own], local)
    here.start()
    sent = []
    for i, dims in enumerate(PEERS):
        copy = remote(mine.at[at.slot(*dims)], whole.at[own], send.at[i], recv.at[i], at.cube(*dims))
        copy.start()
        sent.append(copy)
    yield True
    for i, dims in enumerate(PEERS):
        u, b = at.cube(*dims)
        there = whole.at[rows_at(row_of(u, b), rows)]
        remote(there, there, send.at[i], recv.at[i], (u, b)).wait_recv()
    here.wait()

    def runs(core, group):
        return [whole.at[rows_at(row_of(2 * x + core, 4 * group), run)] for x in range(2)]

    def pass_on(i, group):
        for x, there in enumerate(runs(at.c, group)):
            copy = remote(there, there, sib_send.at[i, x], sib_recv.at[i, x], at.sibling())
            copy.start()
            sent.append(copy)

    for i in range(1, n):
        for x, there in enumerate(runs(at.c, at.g)):
            copy = remote(there, there, mid_send.at[i, x], mid_recv.at[i, x], at.mid(i))
            copy.start()
            sent.append(copy)
    pass_on(0, at.g)
    yield True
    for i in range(1, n):
        for x, there in enumerate(runs(at.c, at.behind(i))):
            remote(there, there, mid_send.at[i, x], mid_recv.at[i, x], at.mid(i)).wait_recv()
        pass_on(i, at.behind(i))
        yield True
    for i in range(n):
        for x, there in enumerate(runs(1 - at.c, at.behind(i))):
            remote(there, there, sib_send.at[i, x], sib_recv.at[i, x], at.sibling()).wait_recv()
    for copy in sent:
        copy.wait_send()


def gather_hidden(at, mine, whole, local, mid_send, mid_recv, sib_send, sib_recv):
    n, rows = at.groups, mine.shape[0]

    def place(core, group):
        return whole.at[rows_at((core * n + group) * rows, rows)]

    here = pltpu.make_async_copy(mine, place(at.c, at.g), local)
    here.start()
    sent = []
    for i in range(1, n):
        sent.append(remote(mine, place(at.c, at.g), mid_send.at[i], mid_recv.at[i], at.mid(i)))
    sent.append(remote(mine, place(at.c, at.g), sib_send.at[0], sib_recv.at[0], at.sibling()))
    for copy in sent:
        copy.start()
    yield True
    for i in range(1, n):
        there = place(at.c, at.behind(i))
        remote(there, there, mid_send.at[i], mid_recv.at[i], at.mid(i)).wait_recv()
        copy = remote(there, there, sib_send.at[i], sib_recv.at[i], at.sibling())
        copy.start()
        sent.append(copy)
        yield True
    for i in range(n):
        there = place(1 - at.c, at.behind(i))
        remote(there, there, sib_send.at[i], sib_recv.at[i], at.sibling()).wait_recv()
    for copy in sent:
        copy.wait_send()
    here.wait()


class OutRows:
    def __init__(self, at, rows):
        self.at, self.rows = at, rows
        self.per_half = max(at.groups // 2, 1)
        self.my_half = at.g // self.per_half
        self.to = 2 * at.c + self.my_half
        self.collects = at.bl == self.to
        self.slot_core = at.bl // 2 == at.c
        self.slot_half = rem(at.bl, 2)

    def group_rows(self, group, half):
        return rows_at((group - half * self.per_half) * (4 * self.rows), 4 * self.rows)

    def in_half(self, group, half):
        return group // self.per_half == half

    def device(self, bl):
        return (self.at.u, 4 * self.at.g + bl)


def gather_heads(at, mine, whole, local, send, recv, mid_send, mid_recv, sib_send, sib_recv):
    n, rows = at.groups, mine.shape[0]
    lay = OutRows(at, rows)
    base = (at.g - lay.my_half * lay.per_half) * (4 * rows)
    own = whole.at[rows_at(base + at.bl * rows, rows)]

    @pl.when(lay.collects)
    def _():
        pltpu.make_async_copy(mine, own, local).start()

    @pl.when(jnp.logical_not(lay.collects))
    def _():
        remote(mine, own, send.at[at.bl], recv.at[at.bl], lay.device(lay.to)).start()

    yield True

    @pl.when(lay.collects)
    def _():
        pltpu.make_async_copy(mine, own, local).wait()
        for bl in range(4):

            @pl.when(at.bl != bl)
            def _():
                there = whole.at[rows_at(base + bl * rows, rows)]
                remote(there, there, send.at[bl], recv.at[bl], lay.device(bl)).wait_recv()

        there = whole.at[lay.group_rows(at.g, lay.my_half)]
        for i in range(1, n):
            remote(there, there, mid_send.at[i], mid_recv.at[i], at.mid(i)).start()

    yield True

    @pl.when(lay.slot_core)
    def _():
        for i in range(1, n):
            group = at.behind(i)

            @pl.when(lay.in_half(group, lay.slot_half))
            def _():
                there = whole.at[lay.group_rows(group, lay.slot_half)]
                remote(there, there, mid_send.at[i], mid_recv.at[i], at.mid(i)).wait_recv()

        remote(whole, whole, sib_send, sib_recv, at.sibling()).start()

    yield True

    @pl.when(lay.slot_core)
    def _():
        remote(whole, whole, sib_send, sib_recv, at.sibling()).wait_send()

    @pl.when(jnp.logical_not(lay.slot_core))
    def _():
        remote(whole, whole, sib_send, sib_recv, at.sibling()).wait_recv()

    @pl.when(lay.collects)
    def _():
        there = whole.at[lay.group_rows(at.g, lay.my_half)]
        for i in range(1, n):
            remote(there, there, mid_send.at[i], mid_recv.at[i], at.mid(i)).wait_send()

    @pl.when(jnp.logical_not(lay.collects))
    def _():
        remote(mine, own, send.at[at.bl], recv.at[at.bl], lay.device(lay.to)).wait_send()


def scatter_columns(at, part, out, sib_land, mid_land, final, sems):
    n = at.groups
    send, recv, mid_send, mid_recv, sib_send, sib_recv, local = sems
    rows = out.shape[1]
    run, deep = 4 * rows, 4 * n * rows
    sent = []

    def of_core(x, core):
        return part.at[rows_at((2 * x + core) * deep, deep)]

    for x in range(2):
        copy = remote(of_core(x, 1 - at.c), sib_land.at[x], sib_send.at[x], sib_recv.at[x], at.sibling())
        copy.start()
        sent.append(copy)
    yield True
    for x in range(2):
        remote(sib_land.at[x], sib_land.at[x], sib_send.at[x], sib_recv.at[x], at.sibling()).wait_recv()
    for i in range(1, n):
        for x in range(2):
            offset = at.ahead(i) * run
            there = part.at[rows_at((2 * x + at.c) * deep + offset, run)]
            add_rows(there, [there, sib_land.at[x, rows_at(offset, run)]], run, 16)
            copy = remote(there, mid_land.at[i - 1, x], mid_send.at[i, x], mid_recv.at[i, x], at.mid(i))
            copy.start()
            sent.append(copy)
    yield True
    for i in range(1, n):
        for x in range(2):
            remote(mid_land.at[i - 1, x], mid_land.at[i - 1, x], mid_send.at[i, x], mid_recv.at[i, x], at.mid(i)).wait_recv()
    offset = at.g * run
    for x in range(2):
        add_rows(
            final.at[x],
            [part.at[rows_at((2 * x + at.c) * deep + offset, run)], sib_land.at[x, rows_at(offset, run)]]
            + [mid_land.at[i - 1, x] for i in range(1, n)],
            run,
            16,
        )
    for i, dims in enumerate(PEERS):
        x, bl = at.flip(*dims)
        copy = remote(
            final.at[x, rows_at(bl * rows, rows)], out.at[at.slot()], send.at[i], recv.at[i], at.cube(*dims)
        )
        copy.start()
        sent.append(copy)
    here = pltpu.make_async_copy(final.at[at.x, rows_at(at.bl * rows, rows)], out.at[at.slot()], local)
    here.start()
    yield True
    for i, dims in enumerate(PEERS):
        there = out.at[at.slot(*dims)]
        remote(there, there, send.at[i], recv.at[i], at.cube(*dims)).wait_recv()
    for copy in sent:
        copy.wait_send()
    here.wait()


def scatter_hidden(at, part, out, sib_land, mid_land, sems):
    n = at.groups
    mid_send, mid_recv, sib_send, sib_recv = sems
    rows = out.shape[0]
    there = part.at[rows_at((1 - at.c) * (n * rows), n * rows)]
    sent = [remote(there, sib_land, sib_send, sib_recv, at.sibling())]
    sent[0].start()
    yield True
    sent[0].wait_recv()
    for i in range(1, n):
        group = at.ahead(i)
        there = part.at[rows_at((at.c * n + group) * rows, rows)]
        add_rows(there, [there, sib_land.at[rows_at(group * rows, rows)]], rows, 16)
        copy = remote(there, mid_land.at[i - 1], mid_send.at[i], mid_recv.at[i], at.mid(i))
        copy.start()
        sent.append(copy)
    yield True
    for copy in sent[1:]:
        copy.wait_recv()
    add_rows(
        out,
        [part.at[rows_at((at.c * n + at.g) * rows, rows)], sib_land.at[rows_at(at.g * rows, rows)]]
        + [mid_land.at[i - 1] for i in range(1, n)],
        rows,
        16,
    )
    for copy in sent:
        copy.wait_send()


def scatter_heads(at, part, out, sib_land, mid_land, sems):
    n, rows = at.groups, out.shape[0]
    send, recv, mid_send, mid_recv, sib_send, sib_recv, local = sems
    lay = OutRows(at, rows)

    @pl.when(jnp.logical_not(lay.slot_core))
    def _():
        remote(part, sib_land, sib_send, sib_recv, at.sibling()).start()

    yield True

    @pl.when(lay.slot_core)
    def _():
        remote(part, sib_land, sib_send, sib_recv, at.sibling()).wait_recv()
        add_rows(part, [part, sib_land], 256, 16)
        for i in range(1, n):
            group = at.ahead(i)

            @pl.when(lay.in_half(group, lay.slot_half))
            def _():
                there = part.at[lay.group_rows(group, lay.slot_half)]
                remote(there, mid_land.at[i - 1], mid_send.at[i], mid_recv.at[i], at.mid(i)).start()

    yield True
    mine = part.at[lay.group_rows(at.g, lay.my_half)]
    base = (at.g - lay.my_half * lay.per_half) * (4 * rows)

    @pl.when(lay.collects)
    def _():
        for i in range(1, n):
            remote(mine, mid_land.at[i - 1], mid_send.at[i], mid_recv.at[i], at.mid(i)).wait_recv()
        add_rows(mine, [mine] + [mid_land.at[i - 1] for i in range(1, n)], 4 * rows, 16)
        for bl in range(4):
            there = part.at[rows_at(base + bl * rows, rows)]

            @pl.when(at.bl != bl)
            def _():
                remote(there, out, send.at[bl], recv, lay.device(bl)).start()

            @pl.when(at.bl == bl)
            def _():
                pltpu.make_async_copy(there, out, local).start()

    yield True

    @pl.when(jnp.logical_not(lay.collects))
    def _():
        remote(out, out, send.at[0], recv, lay.device(lay.to)).wait_recv()

    @pl.when(lay.collects)
    def _():
        for bl in range(4):
            there = part.at[rows_at(base + bl * rows, rows)]

            @pl.when(at.bl != bl)
            def _():
                remote(there, out, send.at[bl], recv, lay.device(bl)).wait_send()

            @pl.when(at.bl == bl)
            def _():
                pltpu.make_async_copy(there, out, local).wait()

    @pl.when(jnp.logical_not(lay.slot_core))
    def _():
        remote(part, sib_land, sib_send, sib_recv, at.sibling()).wait_send()

    @pl.when(lay.slot_core)
    def _():
        for i in range(1, n):
            group = at.ahead(i)

            @pl.when(lay.in_half(group, lay.slot_half))
            def _():
                there = part.at[lay.group_rows(group, lay.slot_half)]
                remote(there, mid_land.at[i - 1], mid_send.at[i], mid_recv.at[i], at.mid(i)).wait_send()


def sum_everywhere(at, mine, land, send, recv):
    for i, device in enumerate([at.sibling(), at.cube(0), at.cube(1), at.cube(2)]):
        copy = remote(mine, land.at[i], send.at[i], recv.at[i], device)
        copy.start()
        copy.wait()
        mine[...] = mine[...] + land[i]
        yield True
    sent = []
    for i in range(1, at.groups):
        copy = remote(mine, land.at[3 + i], send.at[3 + i], recv.at[3 + i], at.mid(i))
        copy.start()
        sent.append(copy)
    yield True
    for copy in sent:
        copy.wait()
    for i in range(1, at.groups):
        mine[...] = mine[...] + land[3 + i]


def everyone(at):
    return [at.cube(*dims) for dims in PEERS] + [at.sibling()] + [at.mid(i) for i in range(1, at.groups)]


def cube_only(at):
    return [at.cube(*dims) for dims in ((0,), (1,), (2,))]


def communicate(body, collective_id, ins, outs, scratch, in_specs, out_specs, limit=60):
    return pl.pallas_call(
        body,
        out_shape=outs,
        in_specs=in_specs,
        out_specs=out_specs,
        scratch_shapes=scratch,
        compiler_params=pltpu.CompilerParams(
            collective_id=collective_id, has_side_effects=True, vmem_limit_bytes=limit << 20
        ),
    )(*ins)


def like(shape, dtype=BF16):
    return jax.ShapeDtypeStruct(shape, dtype)


def gather_all(groups, xhat, dy, w_qkv, w_gu, w_down, w_out):
    def body(xhat, dy, w_qkv, w_gu, w_down, w_out, xhat_b, dy_b, qkv, gu, down, outw, local, tok_s, tok_r, col_s, col_r, mid2_s, mid2_r, sib2_s, sib2_r, mid1_s, mid1_r, sib1_s, sib1_r, head_s, head_r, hsib_s, hsib_r):
        at = Place(groups)
        meet(everyone(at))
        drive(
            gather_columns(at, w_qkv, qkv, local.at[0], col_s.at[0], col_r.at[0], mid2_s.at[0], mid2_r.at[0], sib2_s.at[0], sib2_r.at[0]),
            gather_tokens(at, xhat, xhat_b, local.at[1], tok_s.at[0], tok_r.at[0]),
            gather_heads(at, w_out, outw, local.at[2], head_s, head_r, mid1_s.at[0], mid1_r.at[0], hsib_s, hsib_r),
            gather_columns(at, w_gu, gu, local.at[3], col_s.at[1], col_r.at[1], mid2_s.at[1], mid2_r.at[1], sib2_s.at[1], sib2_r.at[1]),
            gather_tokens(at, dy, dy_b, local.at[4], tok_s.at[1], tok_r.at[1]),
            gather_hidden(at, w_down, down, local.at[5], mid1_s.at[1], mid1_r.at[1], sib1_s, sib1_r),
        )

    n = groups
    return communicate(
        body,
        0,
        (xhat, dy, w_qkv, w_gu, w_down, w_out),
        (
            like((SLOTS, CHUNK, D)),
            like((SLOTS, CHUNK, D)),
            like((D, QKV_SLOT)),
            like((D, GU_SLOT)),
            like((FF_SLOT, D)),
            like((D // SLOTS, D)),
        ),
        [DMA((6,)), DMA((2, 3, 7)), DMA((2, 3, 7)), DMA((2, 7)), DMA((2, 7)), DMA((2, n, 2)), DMA((2, n, 2)), DMA((2, n, 2)), DMA((2, n, 2)), DMA((2, n)), DMA((2, n)), DMA((n,)), DMA((n,)), DMA((4,)), DMA((4,)), DMA(()), DMA(())],
        [HBM] * 6,
        [HBM] * 6,
    )


def share_keys(groups, kv):
    def body(kv, own, prompt, before, local, send, recv, p_send, p_recv, b_send, b_recv):
        at = Place(groups)
        meet([at.sibling()] + [at.mid(i) for i in range(1, groups)])
        here = pltpu.make_async_copy(kv, own.at[:, at.c], local)
        here.start()
        sib = remote(kv, own.at[:, at.c], send.at[0], recv.at[0], at.sibling())
        sib.start()

        def to_group(i):
            return remote(kv, prompt.at[:, at.c], p_send.at[i], p_recv, at.mid_at(jnp.int32(i)))

        @pl.when(at.g == 0)
        def _():
            for i in range(1, groups):
                to_group(i).start()

        half = kv.at[pl.ds(4, 4)]

        def forward():
            return remote(half, before.at[:, at.c], b_send, b_recv, at.mid_at(at.g + 1))

        if groups > 2:

            @pl.when((at.g >= 1) & (at.g < groups - 1))
            def _():
                forward().start()

        relay = remote(prompt.at[:, at.c], prompt.at[:, at.c], send.at[1], recv.at[1], at.sibling())

        @pl.when(at.g > 0)
        def _():
            to_group(0).wait_recv()
            relay.start()

        if groups > 2:

            @pl.when(at.g > 1)
            def _():
                forward().wait_recv()
                again = remote(before.at[:, at.c], before.at[:, at.c], send.at[2], recv.at[2], at.sibling())
                again.start()
                again.wait()

        @pl.when(at.g > 0)
        def _():
            relay.wait()

        sib.wait()
        here.wait()

        @pl.when(at.g == 0)
        def _():
            for i in range(1, groups):
                to_group(i).wait_send()

        if groups > 2:

            @pl.when((at.g >= 1) & (at.g < groups - 1))
            def _():
                forward().wait_send()

    return communicate(
        body,
        1,
        (kv,),
        (like((8, 2, CHUNK, 2 * HD)), like((8, 2, CHUNK, 2 * HD)), like((4, 2, CHUNK, 2 * HD))),
        [DMA(()), DMA((3,)), DMA((3,)), DMA((groups,)), DMA(()), DMA(()), DMA(())],
        [HBM],
        [HBM] * 3,
    )


def return_keys(groups, own, prompt, before):
    def body(own, prompt, before, out, land, land_p, land_b, far_p, far_b, send, recv, p_send, p_recv, b_send, b_recv):
        at = Place(groups)
        meet([at.sibling()] + [at.mid(i) for i in range(1, groups)])

        def swap(array, place, i):
            return remote(array.at[:, 1 - at.c], place, send.at[i], recv.at[i], at.sibling())

        def merge(dst, terms, count):
            def one(i, carry):
                total = terms[0](i).astype(F32)
                for term in terms[1:]:
                    total = total + term(i).astype(F32)
                dst(i, total.astype(BF16))
                return carry

            lax.fori_loop(0, count, one, 0)

        first = swap(own, land, 0)
        second = swap(prompt, land_p, 1)
        third = swap(before, land_b, 2) if groups > 2 else None

        @pl.when(at.g > 0)
        def _():
            second.start()

        if groups > 2:

            @pl.when(at.g > 1)
            def _():
                third.start()

        first.start()

        def put(ref):
            def store(i, value):
                ref[i] = value

            return store

        def home(i):
            return remote(land_p, far_p.at[i - 1], p_send, p_recv.at[i - 1], at.mid_at(jnp.int32(0)))

        def back():
            return remote(land_b, far_b, b_send, b_recv, at.mid_at(at.g - 1))

        @pl.when(at.g > 0)
        def _():
            second.wait()
            merge(put(land_p), [lambda i: prompt[i, at.c], lambda i: land_p[i]], 8)
            for i in range(1, groups):

                @pl.when(at.g == i)
                def _():
                    home(i).start()

        if groups > 2:

            @pl.when(at.g > 1)
            def _():
                third.wait()
                merge(put(land_b), [lambda i: before[i, at.c], lambda i: land_b[i]], 4)
                back().start()

        first.wait()
        merge(put(land), [lambda i: own[i, at.c], lambda i: land[i]], 8)

        @pl.when(at.g == 0)
        def _():
            for i in range(1, groups):
                home(i).wait_recv()
                merge(put(land), [lambda j: land[j], lambda j, i=i: far_p[i - 1, j]], 8)

        if groups > 2:

            @pl.when((at.g >= 1) & (at.g < groups - 1))
            def _():
                back().wait_recv()
                merge(lambda i, v: land.__setitem__(i + 4, v), [lambda i: land[i + 4], lambda i: far_b[i]], 4)

            @pl.when(at.g > 1)
            def _():
                back().wait_send()

        @pl.when(at.g > 0)
        def _():
            home(1).wait_send()

        out[...] = land[...]

    near = pltpu.VMEM((8, CHUNK, 2 * HD), BF16)
    half = pltpu.VMEM((4, CHUNK, 2 * HD), BF16)
    return communicate(
        body,
        2,
        (own, prompt, before),
        like((8, CHUNK, 2 * HD)),
        [near, near, half, pltpu.VMEM((max(groups - 1, 1), 8, CHUNK, 2 * HD), BF16), half, DMA((3,)), DMA((3,)), DMA(()), DMA((groups,)), DMA(()), DMA(())],
        [VMEM] * 3,
        VMEM,
    )


def finish_branch(groups, part, tokens):
    def body(part, tokens, hidden, xhat_b, land, own, local, send_s, recv_s, send_g, recv_g):
        at = Place(groups)
        meet(cube_only(at))
        drive(scatter_tokens(at, part, land, hidden, send_s, recv_s))

        def norm(i, carry):
            rows = pl.ds(pl.multiple_of(i * 32, 32), 32)
            value = hidden[rows, :] + tokens[rows, :].astype(F32)
            hidden[rows, :] = value
            inverse = lax.rsqrt(jnp.mean(value * value, 1, keepdims=True) + EPSILON)
            own[rows, :] = (value * inverse).astype(BF16)
            return carry

        lax.fori_loop(0, CHUNK // 32, norm, 0)
        drive(gather_tokens(at, own, xhat_b, local, send_g, recv_g))

    return communicate(
        body,
        3,
        (part, tokens),
        (like((CHUNK, D), F32), like((SLOTS, CHUNK, D))),
        [pltpu.VMEM((7, CHUNK, D), BF16), pltpu.VMEM((CHUNK, D), BF16), DMA(()), DMA((3, 7)), DMA((3, 7)), DMA((3, 7)), DMA((3, 7))],
        [VMEM] * 2,
        [VMEM, HBM],
    )


def finish_mlp(groups, part_out, part_dx, hidden, cotangent, g_down, g_gu, hidden_rows, gu_rows):
    n = groups

    def body(part_out, part_dx, hidden, cotangent, g_down, g_gu, output, dhidden, dbranch_b, d_down, d_gu, land, own, dx, sib_gu, mid_gu, fin_gu, sib_d, mid_d, local, s1, r1, s2, r2, s3, r3, cs, cr, cms, cmr, css, csr, hms, hmr, hss, hsr):
        at = Place(groups)
        meet(everyone(at))

        def tokens_path():
            yield from scatter_tokens(at, part_dx, land, dx, s1, r1)

            def norm(i, carry):
                rows = pl.ds(pl.multiple_of(i * 32, 32), 32)
                value = hidden[rows, :]
                inverse = lax.rsqrt(jnp.mean(value * value, 1, keepdims=True) + EPSILON)
                unit = value * inverse
                grad = dx[rows, :]
                total = cotangent[rows, :] + inverse * (grad - unit * jnp.mean(grad * unit, 1, keepdims=True))
                dhidden[rows, :] = total
                own[rows, :] = total.astype(BF16)
                return carry

            lax.fori_loop(0, CHUNK // 32, norm, 0)
            yield from gather_tokens(at, own, dbranch_b, local.at[0], s2, r2)
            yield from scatter_tokens(at, part_out, land, dx, s3, r3)

            def add(i, carry):
                rows = pl.ds(pl.multiple_of(i * 32, 32), 32)
                output[rows, :] = (hidden[rows, :] + dx[rows, :]).astype(BF16)
                return carry

            lax.fori_loop(0, CHUNK // 32, add, 0)

        drive(
            tokens_path(),
            scatter_columns(at, g_gu, d_gu, sib_gu, mid_gu, fin_gu, (cs, cr, cms, cmr, css, csr, local.at[1])),
            scatter_hidden(at, g_down, d_down, sib_d, mid_d, (hms, hmr, hss, hsr)),
        )

    deep = 4 * n * gu_rows
    return communicate(
        body,
        4,
        (part_out, part_dx, hidden, cotangent, g_down, g_gu),
        (
            like((CHUNK, D)),
            like((CHUNK, D), F32),
            like((SLOTS, CHUNK, D)),
            like((hidden_rows, D), F32),
            like((SLOTS, gu_rows, GU_SLOT)),
        ),
        [
            pltpu.VMEM((7, CHUNK, D), BF16),
            pltpu.VMEM((CHUNK, D), BF16),
            pltpu.VMEM((CHUNK, D), F32),
            pltpu.VMEM((2, deep, GU_SLOT), BF16),
            pltpu.VMEM((max(n - 1, 1), 2, 4 * gu_rows, GU_SLOT), BF16),
            pltpu.VMEM((2, 4 * gu_rows, GU_SLOT), BF16),
            pltpu.VMEM((n * hidden_rows, D), BF16),
            pltpu.VMEM((max(n - 1, 1), hidden_rows, D), BF16),
            DMA((2,)),
            *[DMA((3, 7))] * 6,
            DMA((7,)),
            DMA((7,)),
            *[DMA((n, 2))] * 2,
            *[DMA((2,))] * 2,
            *[DMA((n,))] * 2,
            DMA(()),
            DMA(()),
        ],
        [VMEM] * 6,
        [VMEM, VMEM, HBM, VMEM, HBM],
    )


def finish_layer(groups, part_dx, tokens, dhidden, g_qkv, g_out, gains, rows):
    n = groups

    def body(part_dx, tokens, dhidden, g_qkv, g_out, gains, d_tokens, d_qkv, d_out, gain_sum, land, dx, sib_q, mid_q, fin_q, sib_o, mid_o, gain_land, local, s1, r1, cs, cr, cms, cmr, css, csr, os_, or_, oms, omr, oss, osr, gs, gr):
        at = Place(groups)
        meet(everyone(at))
        gain_sum[...] = gains[...]

        def tokens_path():
            yield from scatter_tokens(at, part_dx, land, dx, s1, r1)

            def norm(i, carry):
                rows = pl.ds(pl.multiple_of(i * 32, 32), 32)
                value = tokens[rows, :].astype(F32)
                inverse = lax.rsqrt(jnp.mean(value * value, 1, keepdims=True) + EPSILON)
                unit = value * inverse
                grad = dx[rows, :]
                d_tokens[rows, :] = dhidden[rows, :] + inverse * (grad - unit * jnp.mean(grad * unit, 1, keepdims=True))
                return carry

            lax.fori_loop(0, CHUNK // 32, norm, 0)

        drive(
            scatter_columns(at, g_qkv, d_qkv, sib_q, mid_q, fin_q, (cs, cr, cms, cmr, css, csr, local.at[0])),
            scatter_heads(at, g_out, d_out, sib_o, mid_o, (os_, or_, oms, omr, oss, osr, local.at[1])),
            tokens_path(),
            sum_everywhere(at, gain_sum, gain_land, gs, gr),
        )

    deep = 4 * n * rows
    return communicate(
        body,
        5,
        (part_dx, tokens, dhidden, g_qkv, g_out, gains),
        (
            like((CHUNK, D), F32),
            like((SLOTS, rows, QKV_SLOT)),
            like((rows, D)),
            like((8, HD), F32),
        ),
        [
            pltpu.VMEM((7, CHUNK, D), BF16),
            pltpu.VMEM((CHUNK, D), F32),
            pltpu.VMEM((2, deep, QKV_SLOT), BF16),
            pltpu.VMEM((max(n - 1, 1), 2, 4 * rows, QKV_SLOT), BF16),
            pltpu.VMEM((2, 4 * rows, QKV_SLOT), BF16),
            pltpu.VMEM((D // SLOTS, D), BF16),
            pltpu.VMEM((max(n - 1, 1), 4 * rows, D), BF16),
            pltpu.VMEM((4 + n, 8, HD), F32),
            DMA((2,)),
            DMA((3, 7)),
            DMA((3, 7)),
            DMA((7,)),
            DMA((7,)),
            *[DMA((n, 2))] * 2,
            *[DMA((2,))] * 2,
            DMA((4,)),
            DMA(()),
            *[DMA((n,))] * 2,
            DMA(()),
            DMA(()),
            DMA((4 + n,)),
            DMA((4 + n,)),
        ],
        [VMEM] * 6,
        [VMEM, HBM, VMEM, VMEM],
    )


NT = (((1,), (1,)), ((), ()))
TILE = 256


def visible(first_key, chunk_of_block, opening):
    key = first_key + lax.broadcasted_iota(jnp.int32, (TILE, 2 * CHUNK), 0)
    lane = lax.broadcasted_iota(jnp.int32, (TILE, 2 * CHUNK), 1)
    row = chunk_of_block * CHUNK + jnp.where(lane >= CHUNK, lane - CHUNK, lane)
    return (key <= row) & (key >= opening)


def key_range(group, chunk_of_block):
    stop = (chunk_of_block + 2) // 2
    start = jnp.where(group > 0, jnp.maximum(chunk_of_block * CHUNK - LONGEST, 0) // TILE, 0)
    return start, stop


def two_heads(block):
    return jnp.concatenate([block[:, :HD], block[:, HD:]], 0)


def two_columns(block):
    return jnp.concatenate([block[:CHUNK], block[CHUNK:]], 1)


def attend_body(groups, q_ref, own, prompt, before, open_ref, mixed, total, lse, own_vt, prompt_vt, before_vt):
    group = lax.axis_index("blk") // 4
    core = rem(lax.axis_index("uly"), 2)
    i = pl.program_id(0)
    chunk = 2 * i + core

    @pl.when(i == 0)
    def _():
        own_vt[...] = own[:, HD:].T
        prompt_vt[...] = prompt[:, HD:].T
        if groups > 2:
            before_vt[...] = before[:, HD:].T

    q = two_heads(q_ref[0])
    opening = open_ref[0]

    def step(keys, values_t, first, carry, masked, shift=0):
        norm, out = carry
        rows = pl.ds(pl.multiple_of(first, TILE), TILE)
        s = lax.dot_general(keys[rows, :HD], q, NT, preferred_element_type=F32)
        p = jnp.exp(s * SCALE)
        if masked:
            p = jnp.where(visible(first + shift, chunk, opening), p, 0.0)
        norm = norm + jnp.sum(p, 0, keepdims=True)
        out = out + jnp.dot(values_t[:, rows], p.astype(BF16), preferred_element_type=F32)
        return norm, out

    carry = (jnp.zeros((1, 2 * CHUNK), F32), jnp.zeros((HD, 2 * CHUNK), F32))
    carry = lax.fori_loop(
        0,
        jnp.where(group > 0, PROMPT // TILE, 0),
        lambda t, c: step(prompt, prompt_vt, t * TILE, c, False),
        carry,
    )
    if groups > 2:
        reach = before.shape[0]
        carry = lax.fori_loop(
            0,
            jnp.where((group > 1) & (chunk < reach // CHUNK), reach // TILE, 0),
            lambda t, c: step(before, before_vt, t * TILE, c, True, -reach),
            carry,
        )
    start, stop = key_range(group, chunk)
    norm, out = lax.fori_loop(start, stop, lambda t, c: step(own, own_vt, t * TILE, c, True), carry)
    out = out / norm
    total[0] = out
    lse[0] = jnp.log(norm)
    mixed[0] = two_columns(out.T.astype(BF16))


def attend(groups, q, own, prompt, before, opening):
    whole = lambda a: pl.BlockSpec(a.shape, lambda i: (0, 0))
    return pl.pallas_call(
        functools.partial(attend_body, groups),
        grid=(8,),
        out_shape=(like((8, CHUNK, 2 * HD)), like((8, HD, 2 * CHUNK), F32), like((8, 1, 2 * CHUNK), F32)),
        in_specs=[
            pl.BlockSpec((1, CHUNK, 2 * HD), lambda i: (i, 0, 0)),
            whole(own),
            whole(prompt),
            whole(before),
            pl.BlockSpec((1, 1, 2 * CHUNK), lambda i: (i, 0, 0)),
        ],
        out_specs=[
            pl.BlockSpec((1, CHUNK, 2 * HD), lambda i: (i, 0, 0)),
            pl.BlockSpec((1, HD, 2 * CHUNK), lambda i: (i, 0, 0)),
            pl.BlockSpec((1, 1, 2 * CHUNK), lambda i: (i, 0, 0)),
        ],
        scratch_shapes=[
            pltpu.VMEM((HD, own.shape[0]), BF16),
            pltpu.VMEM((HD, prompt.shape[0]), BF16),
            pltpu.VMEM((HD, before.shape[0]), BF16),
        ],
        compiler_params=pltpu.CompilerParams(vmem_limit_bytes=48 << 20),
    )(q, own, prompt, before, opening)


def attend_back_body(groups, q_ref, do_ref, own, prompt, before, open_ref, total, lse, dq_ref, d_own, d_prompt, d_before, own_kt, prompt_kt, before_kt, acc_own, acc_prompt, acc_before):
    group = lax.axis_index("blk") // 4
    core = rem(lax.axis_index("uly"), 2)
    i = pl.program_id(0)
    chunk = 2 * i + core

    @pl.when(i == 0)
    def _():
        own_kt[...] = own[:, :HD].T
        prompt_kt[...] = prompt[:, :HD].T
        acc_own[...] = jnp.zeros_like(acc_own)
        acc_prompt[...] = jnp.zeros_like(acc_prompt)
        if groups > 2:
            before_kt[...] = before[:, :HD].T
            acc_before[...] = jnp.zeros_like(acc_before)

    q = two_heads(q_ref[0])
    do = two_heads(do_ref[0])
    dot_rows = jnp.sum(do.astype(F32).T * total[0], 0, keepdims=True)
    logs = lse[0]
    opening = open_ref[0]

    def step(kv, keys_t, acc, first, dq, masked, shift=0):
        rows = pl.ds(pl.multiple_of(first, TILE), TILE)
        keys, values = kv[rows, :HD], kv[rows, HD:]
        s = lax.dot_general(keys, q, NT, preferred_element_type=F32)
        p = jnp.exp(s * SCALE - logs)
        if masked:
            p = jnp.where(visible(first + shift, chunk, opening), p, 0.0)
        dp = lax.dot_general(values, do, NT, preferred_element_type=F32)
        ds = (p * (dp - dot_rows)).astype(BF16)
        acc[rows, :HD] += jnp.dot(ds, q, preferred_element_type=F32)
        acc[rows, HD:] += jnp.dot(p.astype(BF16), do, preferred_element_type=F32)
        return dq + jnp.dot(keys_t[:, rows], ds, preferred_element_type=F32)

    dq = jnp.zeros((HD, 2 * CHUNK), F32)
    dq = lax.fori_loop(
        0,
        jnp.where(group > 0, PROMPT // TILE, 0),
        lambda t, c: step(prompt, prompt_kt, acc_prompt, t * TILE, c, False),
        dq,
    )
    if groups > 2:
        reach = before.shape[0]
        dq = lax.fori_loop(
            0,
            jnp.where((group > 1) & (chunk < reach // CHUNK), reach // TILE, 0),
            lambda t, c: step(before, before_kt, acc_before, t * TILE, c, True, -reach),
            dq,
        )
    start, stop = key_range(group, chunk)
    dq = lax.fori_loop(start, stop, lambda t, c: step(own, own_kt, acc_own, t * TILE, c, True), dq)
    dq_ref[0] = two_columns((dq.T * SCALE).astype(BF16))

    @pl.when(i == 7)
    def _():
        for acc, out in ((acc_own, d_own), (acc_prompt, d_prompt)) + (((acc_before, d_before),) if groups > 2 else ()):
            out[:, :HD] = (acc[:, :HD] * SCALE).astype(BF16)
            out[:, HD:] = acc[:, HD:].astype(BF16)


def attend_back(groups, q, do, own, prompt, before, opening, total, lse):
    whole = lambda a: pl.BlockSpec(a.shape, lambda i: (0, 0))
    chunk = pl.BlockSpec((1, CHUNK, 2 * HD), lambda i: (i, 0, 0))
    return pl.pallas_call(
        functools.partial(attend_back_body, groups),
        grid=(8,),
        out_shape=(like(q.shape), like(own.shape), like(prompt.shape), like(before.shape)),
        in_specs=[
            chunk,
            chunk,
            whole(own),
            whole(prompt),
            whole(before),
            pl.BlockSpec((1, 1, 2 * CHUNK), lambda i: (i, 0, 0)),
            pl.BlockSpec((1, HD, 2 * CHUNK), lambda i: (i, 0, 0)),
            pl.BlockSpec((1, 1, 2 * CHUNK), lambda i: (i, 0, 0)),
        ],
        out_specs=[chunk, whole(own), whole(prompt), whole(before)],
        scratch_shapes=[
            pltpu.VMEM((HD, own.shape[0]), BF16),
            pltpu.VMEM((HD, prompt.shape[0]), BF16),
            pltpu.VMEM((HD, before.shape[0]), BF16),
            pltpu.VMEM(own.shape, F32),
            pltpu.VMEM(prompt.shape, F32),
            pltpu.VMEM(before.shape, F32),
        ],
        compiler_params=pltpu.CompilerParams(vmem_limit_bytes=48 << 20),
    )(q, do, own, prompt, before, opening, total, lse)


def rotate(vectors, cosine, sine):
    former, latter = jnp.split(vectors, 2, -1)
    return jnp.concatenate([former * cosine - latter * sine, latter * cosine + former * sine], -1)


def dot(a, b, dims=((1,), (0,))):
    return lax.dot_general(a, b, (dims, ((), ())), preferred_element_type=F32)


def body(tokens, lengths, attn_gain, w_qkv, q_gain, k_gain, w_out, mlp_gain, w_gate_up, w_down, cotangent):
    blocks = lax.axis_size("blk")
    groups = blocks // 4
    rows = w_qkv.shape[0]
    hidden_rows = w_down.shape[0]
    group = lax.axis_index("blk") // 4
    core = lax.axis_index("uly") % 2
    gain_one = attn_gain.astype(F32)[:, None]
    gain_two = mlp_gain.astype(F32)[:, None]

    scaled = (w_qkv.astype(F32) * gain_one).astype(BF16)
    by_slot = jnp.concatenate(
        [
            scaled[:, : HQ * HD].reshape(rows, SLOTS, 2 * HD),
            scaled[:, HQ * HD : (HQ + HK) * HD].reshape(rows, SLOTS, HD),
            scaled[:, (HQ + HK) * HD :].reshape(rows, SLOTS, HD),
        ],
        2,
    ).transpose(1, 0, 2)
    scaled_gu = (w_gate_up.astype(F32) * gain_two).astype(BF16)
    gu_by_slot = (
        scaled_gu.reshape(rows, 2, 2, 2, groups, 4, hidden_rows)
        .transpose(2, 5, 0, 1, 3, 4, 6)
        .reshape(SLOTS, rows, GU_SLOT)
    )
    inputs = tokens.astype(F32)
    xhat = (inputs * lax.rsqrt(jnp.mean(inputs * inputs, 1, keepdims=True) + EPSILON)).astype(BF16)
    dy = cotangent.astype(BF16)
    xhat_b, dy_b, qkv_w, gu_w, down_w, out_w = gather_all(groups, xhat, dy, by_slot, gu_by_slot, w_down, w_out)
    xhat_b = xhat_b.reshape(SLOTS * CHUNK, D)
    dy_b = dy_b.reshape(SLOTS * CHUNK, D)

    starts = PROMPT + jnp.sum(
        jnp.where(jnp.arange(lengths.shape[0])[:, None] > jnp.arange(lengths.shape[0])[None, :], lengths[None, :], 0), 1
    )
    index = (
        group * (2 * SLOTS * CHUNK)
        + (2 * jnp.arange(SLOTS, dtype=jnp.int32)[:, None] + core) * CHUNK
        + jnp.arange(CHUNK, dtype=jnp.int32)[None, :]
    )
    opening = jnp.max(jnp.where(index[..., None] >= starts, starts, 0), -1)
    position = jnp.where(index < PROMPT, index, index - opening + PROMPT).reshape(-1)
    opening = opening - group * (2 * SLOTS * CHUNK)
    opening = jnp.concatenate([opening, opening], 1)[:, None, :]
    inverse = ROPE_BASE ** (-2.0 * jnp.arange(HD // 2, dtype=F32) / HD)
    angles = position.astype(F32)[:, None] * inverse[None, :]
    cosine, sine = jnp.cos(angles)[:, None, :], jnp.sin(angles)[:, None, :]

    raw = dot(xhat_b, qkv_w).reshape(SLOTS * CHUNK, 4, HD)
    head_gain = jnp.stack([q_gain, q_gain, k_gain]).astype(F32)[None]

    def shape_heads(heads, gain):
        normed = heads * lax.rsqrt(jnp.mean(heads * heads, -1, keepdims=True) + EPSILON) * gain
        return rotate(normed, cosine, sine)

    turned, pullback = jax.vjp(shape_heads, raw[:, :3], jnp.broadcast_to(head_gain, (1, 3, HD)))
    turned = turned.astype(BF16)
    queries = turned[:, :2].reshape(SLOTS, CHUNK, 2 * HD)
    keys_values = jnp.stack([turned[:, 2], raw[:, 3].astype(BF16)], 1).reshape(SLOTS, CHUNK, 2 * HD)
    own, prompt, before = share_keys(groups, keys_values)
    own, prompt, before = (a.reshape(-1, 2 * HD) for a in (own, prompt, before))
    mixed, total, lse = attend(groups, queries, own, prompt, before, opening)
    mixed = mixed.reshape(SLOTS * CHUNK, 2 * HD)
    hidden, xhat2_b = finish_branch(groups, dot(mixed, out_w).astype(BF16).reshape(SLOTS, CHUNK, D), tokens)
    xhat2_b = xhat2_b.reshape(SLOTS * CHUNK, D)

    both = dot(xhat2_b, gu_w)
    gate, up = both[:, :FF_SLOT], both[:, FF_SLOT:]
    sigmoid = jax.nn.sigmoid(gate)
    act = (gate * sigmoid * up).astype(BF16)
    part_out = dot(act, down_w).astype(BF16)
    g_down = dot(act, dy_b, ((0,), (0,))).astype(BF16)
    dact = dot(dy_b, down_w, ((1,), (1,)))
    dboth = jnp.concatenate(
        [dact * up * sigmoid * (1.0 + gate * (1.0 - sigmoid)), dact * gate * sigmoid], 1
    ).astype(BF16)
    g_gu = dot(xhat2_b, dboth, ((0,), (0,))).astype(BF16)
    part_dx2 = dot(dboth, gu_w, ((1,), (1,))).astype(BF16)
    output, dhidden, dbranch_b, d_w_down, gu_back = finish_mlp(
        groups,
        part_out.reshape(SLOTS, CHUNK, D),
        part_dx2.reshape(SLOTS, CHUNK, D),
        hidden,
        cotangent,
        g_down,
        g_gu,
        hidden_rows,
        rows,
    )
    dbranch_b = dbranch_b.reshape(SLOTS * CHUNK, D)
    g_out = dot(mixed, dbranch_b, ((0,), (0,))).astype(BF16)
    dmixed = dot(dbranch_b, out_w, ((1,), (1,))).astype(BF16).reshape(SLOTS, CHUNK, 2 * HD)
    dq, d_own, d_prompt, d_before = attend_back(groups, queries, dmixed, own, prompt, before, opening, total, lse)
    dkv = return_keys(
        groups,
        d_own.reshape(8, 2, CHUNK, 2 * HD),
        d_prompt.reshape(8, 2, CHUNK, 2 * HD),
        d_before.reshape(4, 2, CHUNK, 2 * HD),
    ).reshape(SLOTS * CHUNK, 2, HD)
    d_turned = jnp.concatenate([dq.reshape(SLOTS * CHUNK, 2, HD), dkv[:, :1]], 1).astype(F32)
    dqk, d_gain = pullback(d_turned)
    draw = jnp.concatenate([dqk.astype(BF16), dkv[:, 1:]], 1).reshape(SLOTS * CHUNK, QKV_SLOT)
    g_qkv = dot(xhat_b, draw, ((0,), (0,))).astype(BF16)
    part_dx = dot(draw, qkv_w, ((1,), (1,))).astype(BF16)
    gains = jnp.concatenate([(d_gain[0, 0] + d_gain[0, 1])[None], d_gain[0, 2][None], jnp.zeros((6, HD), F32)], 0)
    d_tokens, qkv_back, d_w_out, gain_sum = finish_layer(
        groups, part_dx.reshape(SLOTS, CHUNK, D), tokens, dhidden, g_qkv, g_out, gains, rows
    )

    qkv_back = qkv_back.astype(F32).transpose(1, 0, 2)
    raw_qkv = jnp.concatenate(
        [
            qkv_back[:, :, : 2 * HD].reshape(rows, HQ * HD),
            qkv_back[:, :, 2 * HD : 3 * HD].reshape(rows, HK * HD),
            qkv_back[:, :, 3 * HD :].reshape(rows, HK * HD),
        ],
        1,
    )
    raw_gu = (
        gu_back.astype(F32)
        .reshape(2, 4, rows, 2, 2, groups, hidden_rows)
        .transpose(2, 3, 0, 4, 5, 1, 6)
        .reshape(rows, 2 * FF)
    )
    return (
        output,
        d_tokens,
        jnp.sum(raw_qkv * w_qkv.astype(F32), 1),
        raw_qkv * gain_one,
        gain_sum[0],
        gain_sum[1],
        d_w_out.astype(F32),
        jnp.sum(raw_gu * w_gate_up.astype(F32), 1),
        raw_gu * gain_two,
        d_w_down,
    )


def solution(mesh):
    tokens = P(("blk", "uly"), None)
    weight = P(("uly", "blk"), None)
    gain = P(("uly", "blk"))
    return jax.shard_map(
        body,
        mesh=mesh,
        in_specs=(tokens, P(), gain, weight, P(), P(), weight, gain, weight, weight, tokens),
        out_specs=(tokens, tokens, gain, weight, P(), P(), weight, gain, weight, weight),
        check_vma=False,
    )
```

```python
import functools
import math

import jax
import jax.numpy as jnp
from jax import lax
from jax.experimental import pallas as pl
from jax.experimental.pallas import tpu as pltpu
from jax.sharding import PartitionSpec as P

D = 2048
HQ = 16
HK = 8
HD = 128
FF = 6144
PROMPT = 2048
LONGEST = 1024

SLOTS = 8
CHUNK = 128
QKV_SLOT = 512
GU_SLOT = 2 * FF // SLOTS
FF_SLOT = FF // SLOTS
EPSILON = 1e-06
ROPE_BASE = 1000000.0
SCALE = 1.0 / math.sqrt(HD)

F32 = jnp.float32
BF16 = jnp.bfloat16
MESH = pl.DeviceIdType.MESH
HBM = pl.BlockSpec(memory_space=pl.ANY)
VMEM = pl.BlockSpec(memory_space=pltpu.VMEM)
DMA = pltpu.SemaphoreType.DMA
PARTS = ((0, 1, 2), 256), ((1, 2, 0), 768), ((2, 0, 1), 1024)


def rem(a, n):
    return lax.rem(a, jnp.int32(n))


class Place:
    def __init__(self, groups):
        self.groups = groups
        self.u = lax.axis_index("uly")
        self.b = lax.axis_index("blk")
        self.x = self.u // 2
        self.c = rem(self.u, 2)
        self.g = self.b // 4
        self.bl = rem(self.b, 4)
        self.bits = (self.x, rem(self.bl, 2), self.bl // 2)

    def flip(self, *dims):
        x, y, z = (rem(v + 1, 2) if d in dims else v for d, v in enumerate(self.bits))
        return x, 2 * z + y

    def chunk(self, *dims):
        x, bl = self.flip(*dims)
        return 2 * bl + x

    def slot(self, *dims):
        x, bl = self.flip(*dims)
        return 4 * x + bl

    def cube(self, *dims):
        x, bl = self.flip(*dims)
        return (2 * x + self.c, 4 * self.g + bl)

    def sibling(self):
        return (2 * self.x + 1 - self.c, self.b)

    def ahead(self, i):
        return rem(self.g + i, self.groups)

    def behind(self, i):
        return rem(self.g + self.groups - i, self.groups)

    def mid(self, i):
        return (self.u, 4 * self.ahead(i) + self.bl)

    def mid_at(self, group):
        return (self.u, 4 * group + self.bl)


PEERS = ((0,), (1,), (2,), (0, 1), (0, 2), (1, 2), (0, 1, 2))


def meet(devices):
    barrier = pltpu.get_barrier_semaphore()
    for device in devices:
        pl.semaphore_signal(barrier, inc=1, device_id=device, device_id_type=MESH)
    pl.semaphore_wait(barrier, len(devices))


def remote(src, dst, send, recv, device):
    return pltpu.make_async_remote_copy(
        src_ref=src, dst_ref=dst, send_sem=send, recv_sem=recv, device_id=device, device_id_type=MESH
    )


def rows_at(start, count):
    return pl.ds(pl.multiple_of(start, 16), count)


def drive(*tasks):
    tasks = list(tasks)
    while tasks:
        tasks = [task for task in tasks if next(task, None) is not None]


def beside(main, *bulk):
    for _ in main:
        for task in bulk:
            next(task, None)


def part_columns():
    start = 0
    for p, (order, width) in enumerate(PARTS):
        yield p, order, pl.ds(start, width)
        start += width


def gather_tokens(at, mine, block, local, send, recv):
    own = pltpu.make_async_copy(mine, block.at[at.chunk()], local)
    own.start()
    sent = []

    def push(p, i, dims, along, cols):
        src = block.at[at.chunk(*dims), :, cols] if dims else mine.at[:, cols]
        copy = remote(src, block.at[at.chunk(*dims), :, cols], send.at[p, i], recv.at[p, i], at.cube(along))
        copy.start()
        sent.append(copy)

    def arrive(p, i, dims, cols):
        there = block.at[at.chunk(*dims), :, cols]
        remote(there, there, send.at[p, i], recv.at[p, i], at.cube(dims[0])).wait_recv()

    parts = list(part_columns())
    for p, (a, b, c), cols in parts:
        push(p, 0, (), a, cols)
        push(p, 1, (), b, cols)
        push(p, 2, (), c, cols)
    yield True
    for p, (a, b, c), cols in parts:
        arrive(p, 0, (a,), cols)
        push(p, 3, (a,), b, cols)
        push(p, 4, (a,), c, cols)
    yield True
    for p, (a, b, c), cols in parts:
        arrive(p, 1, (b,), cols)
        push(p, 5, (b,), c, cols)
        arrive(p, 3, (a, b), cols)
        push(p, 6, (a, b), c, cols)
    yield True
    for p, (a, b, c), cols in parts:
        arrive(p, 2, (c,), cols)
        arrive(p, 4, (a, c), cols)
        arrive(p, 5, (b, c), cols)
        arrive(p, 6, (a, b, c), cols)
    for copy in sent:
        copy.wait_send()
    own.wait()


def add_rows(dst, terms, count, step=32):
    def body(i, carry):
        rows = pl.ds(pl.multiple_of(i * step, step), step)
        total = terms[0][rows, :].astype(F32)
        for term in terms[1:]:
            total = total + term[rows, :].astype(F32)
        dst[rows, :] = total.astype(dst.dtype)
        return carry

    lax.fori_loop(0, count // step, body, 0)


def scatter_tokens(at, part, land, out, send, recv):
    sent = []

    def push(p, i, dims, along, cols):
        copy = remote(part.at[at.chunk(*dims), :, cols], land.at[i, :, cols], send.at[p, i], recv.at[p, i], at.cube(along))
        copy.start()
        sent.append(copy)

    def arrive(p, i, along, cols):
        remote(land.at[i, :, cols], land.at[i, :, cols], send.at[p, i], recv.at[p, i], at.cube(along)).wait_recv()

    def add(i, dims, cols):
        here = part.at[at.chunk(*dims), :, cols]
        add_rows(here, [here, land.at[i, :, cols]], CHUNK)

    parts = list(part_columns())
    for p, (a, b, c), cols in parts:
        push(p, 3, (a, b, c), c, cols)
        push(p, 2, (b, c), c, cols)
    for p, (a, b, c), cols in parts:
        push(p, 1, (a, c), c, cols)
        push(p, 0, (c,), c, cols)
    yield True
    for p, (a, b, c), cols in parts:
        arrive(p, 3, c, cols)
        add(3, (a, b), cols)
        push(p, 5, (a, b), b, cols)
        arrive(p, 2, c, cols)
        add(2, (b,), cols)
        push(p, 4, (b,), b, cols)
    yield True
    for p, (a, b, c), cols in parts:
        arrive(p, 1, c, cols)
        add(1, (a,), cols)
        arrive(p, 5, b, cols)
        add(5, (a,), cols)
        push(p, 6, (a,), a, cols)
    yield True
    for p, (a, b, c), cols in parts:
        arrive(p, 0, c, cols)
        arrive(p, 4, b, cols)
        arrive(p, 6, a, cols)
        add_rows(
            out.at[:, cols],
            [part.at[at.chunk(), :, cols], land.at[0, :, cols], land.at[4, :, cols], land.at[6, :, cols]],
            CHUNK,
        )
    for copy in sent:
        copy.wait_send()


def column_row(at, rows, u, b):
    return (u * (4 * at.groups) + b) * rows


def columns_in_cube(at, mine, whole, local, send, recv):
    rows = mine.shape[1]
    own = rows_at(column_row(at, rows, at.u, at.b), rows)
    here = pltpu.make_async_copy(mine.at[at.slot()], whole.at[own], local)
    here.start()
    sent = []
    for i, dims in enumerate(PEERS):
        copy = remote(mine.at[at.slot(*dims)], whole.at[own], send.at[i], recv.at[i], at.cube(*dims))
        copy.start()
        sent.append(copy)
    yield True
    for i, dims in enumerate(PEERS):
        u, b = at.cube(*dims)
        there = whole.at[rows_at(column_row(at, rows, u, b), rows)]
        remote(there, there, send.at[i], recv.at[i], (u, b)).wait_recv()
    for copy in sent:
        copy.wait_send()
    here.wait()


def columns_across(at, whole, rows, mid_send, mid_recv, sib_send, sib_recv):
    n, pieces = at.groups, mid_send.shape[2]
    step = 4 * rows // pieces
    sent = []

    def piece(core, group, x, k):
        return whole.at[rows_at(column_row(at, rows, 2 * x + core, 4 * group) + k * step, step)]

    def pass_on(i, x, k):
        there = piece(at.c, at.behind(i), x, k)
        copy = remote(there, there, sib_send.at[i, x, k], sib_recv.at[i, x, k], at.sibling())
        copy.start()
        sent.append(copy)

    order = [(x, k) for x in range(2) for k in range(pieces)]
    for i in range(1, n):
        for x, k in order:
            there = piece(at.c, at.g, x, k)
            copy = remote(there, there, mid_send.at[i, x, k], mid_recv.at[i, x, k], at.mid(i))
            copy.start()
            sent.append(copy)
            if i == 1:
                pass_on(0, x, k)
            yield True
    for i in range(1, n):
        for x, k in order:
            there = piece(at.c, at.behind(i), x, k)
            remote(there, there, mid_send.at[i, x, k], mid_recv.at[i, x, k], at.mid(i)).wait_recv()
            pass_on(i, x, k)
    for i in range(n):
        for x, k in order:
            there = piece(1 - at.c, at.behind(i), x, k)
            remote(there, there, sib_send.at[i, x, k], sib_recv.at[i, x, k], at.sibling()).wait_recv()
    for copy in sent:
        copy.wait_send()


class OutRows:
    def __init__(self, at, rows):
        self.at, self.rows = at, rows
        self.per_half = max(at.groups // 2, 1)
        self.my_half = at.g // self.per_half
        self.to = 2 * at.c + self.my_half
        self.collects = at.bl == self.to
        self.slot_core = at.bl // 2 == at.c
        self.slot_half = rem(at.bl, 2)

    def group_rows(self, group, half):
        return rows_at((group - half * self.per_half) * (4 * self.rows), 4 * self.rows)

    def in_half(self, group, half):
        return group // self.per_half == half

    def device(self, bl):
        return (self.at.u, 4 * self.at.g + bl)


def gather_heads(at, mine, whole, local, send, recv, sib_send, sib_recv):
    n, rows = mine.shape[0], mine.shape[1]
    lay = OutRows(at, rows)

    def place(group, bl):
        half = group // lay.per_half
        return whole.at[rows_at(((group - half * lay.per_half) * 4 + bl) * rows, rows)]

    def push(i):
        group = at.behind(i)
        to = 2 * at.c + group // lay.per_half
        here = pltpu.make_async_copy(mine.at[i], place(group, at.bl), local.at[i])
        there = remote(mine.at[i], place(group, at.bl), send.at[i], recv.at[i, at.bl], lay.device(to))
        return at.bl == to, here, there

    for i in range(n):
        stays, here, there = push(i)

        @pl.when(stays)
        def _():
            here.start()

        @pl.when(jnp.logical_not(stays))
        def _():
            there.start()

    yield True

    @pl.when(lay.slot_core)
    def _():
        for i in range(n):
            group = at.behind(i)

            @pl.when(lay.in_half(group, lay.slot_half))
            def _():
                pltpu.make_async_copy(mine.at[i], place(group, at.bl), local.at[i]).wait()
                for bl in range(4):

                    @pl.when(at.bl != bl)
                    def _():
                        there = place(group, bl)
                        remote(there, there, send.at[i], recv.at[i, bl], lay.device(bl)).wait_recv()

        remote(whole, whole, sib_send, sib_recv, at.sibling()).start()

    yield True

    @pl.when(lay.slot_core)
    def _():
        remote(whole, whole, sib_send, sib_recv, at.sibling()).wait_send()

    @pl.when(jnp.logical_not(lay.slot_core))
    def _():
        remote(whole, whole, sib_send, sib_recv, at.sibling()).wait_recv()

    for i in range(n):
        stays, here, there = push(i)

        @pl.when(jnp.logical_not(stays))
        def _():
            there.wait_send()


def columns_home(at, final, out, send, recv, local):
    sent = []
    for i, dims in enumerate(PEERS):
        x, bl = at.flip(*dims)
        copy = remote(final.at[x, bl], out.at[at.slot()], send.at[i], recv.at[i], at.cube(*dims))
        copy.start()
        sent.append(copy)
    here = pltpu.make_async_copy(final.at[at.x, at.bl], out.at[at.slot()], local)
    here.start()
    yield True
    for i, dims in enumerate(PEERS):
        there = out.at[at.slot(*dims)]
        remote(there, there, send.at[i], recv.at[i], at.cube(*dims)).wait_recv()
    for copy in sent:
        copy.wait_send()
    here.wait()


def columns_sum(at, part, sib_land, mid_land, final, sems):
    n, rows = at.groups, final.shape[2]
    mid_send, mid_recv, sib_send, sib_recv = sems
    run, deep = 4 * rows, 4 * n * rows
    sent = []

    def of_core(x, core):
        return part.at[rows_at((2 * x + core) * deep, deep)]

    for x in range(2):
        copy = remote(of_core(x, 1 - at.c), sib_land.at[x], sib_send.at[x], sib_recv.at[x], at.sibling())
        copy.start()
        sent.append(copy)
    yield True
    for x in range(2):
        remote(sib_land.at[x], sib_land.at[x], sib_send.at[x], sib_recv.at[x], at.sibling()).wait_recv()
        for i in range(1, n):
            for k in range(4):
                offset = at.ahead(i) * run + k * rows
                there = part.at[rows_at((2 * x + at.c) * deep + offset, rows)]
                add_rows(there, [there, sib_land.at[x, rows_at(offset, rows)]], rows, 16)
                copy = remote(there, mid_land.at[i - 1, x, k], mid_send.at[i, x, k], mid_recv.at[i, x, k], at.mid(i))
                copy.start()
                sent.append(copy)
                yield True
    for x in range(2):
        for k in range(4):
            for i in range(1, n):
                there = mid_land.at[i - 1, x, k]
                remote(there, there, mid_send.at[i, x, k], mid_recv.at[i, x, k], at.mid(i)).wait_recv()
            offset = at.g * run + k * rows
            add_rows(
                final.at[x, k],
                [part.at[rows_at((2 * x + at.c) * deep + offset, rows)], sib_land.at[x, rows_at(offset, rows)]]
                + [mid_land.at[i - 1, x, k] for i in range(1, n)],
                rows,
                16,
            )
    for copy in sent:
        copy.wait_send()


def scatter_heads(at, part, out, sib_land, mid_land, sems):
    n, rows = at.groups, out.shape[0]
    send, recv, mid_send, mid_recv, sib_send, sib_recv, local = sems
    lay = OutRows(at, rows)

    @pl.when(jnp.logical_not(lay.slot_core))
    def _():
        remote(part, sib_land, sib_send, sib_recv, at.sibling()).start()

    yield True

    @pl.when(lay.slot_core)
    def _():
        remote(part, sib_land, sib_send, sib_recv, at.sibling()).wait_recv()
        add_rows(part, [part, sib_land], 256, 16)
        for i in range(1, n):
            group = at.ahead(i)

            @pl.when(lay.in_half(group, lay.slot_half))
            def _():
                there = part.at[lay.group_rows(group, lay.slot_half)]
                remote(there, mid_land.at[i - 1], mid_send.at[i], mid_recv.at[i], at.mid(i)).start()

    yield True
    mine = part.at[lay.group_rows(at.g, lay.my_half)]
    base = (at.g - lay.my_half * lay.per_half) * (4 * rows)

    @pl.when(lay.collects)
    def _():
        for i in range(1, n):
            remote(mine, mid_land.at[i - 1], mid_send.at[i], mid_recv.at[i], at.mid(i)).wait_recv()
        add_rows(mine, [mine] + [mid_land.at[i - 1] for i in range(1, n)], 4 * rows, 16)
        for bl in range(4):
            there = part.at[rows_at(base + bl * rows, rows)]

            @pl.when(at.bl != bl)
            def _():
                remote(there, out, send.at[bl], recv, lay.device(bl)).start()

            @pl.when(at.bl == bl)
            def _():
                pltpu.make_async_copy(there, out, local).start()

    yield True

    @pl.when(jnp.logical_not(lay.collects))
    def _():
        remote(out, out, send.at[0], recv, lay.device(lay.to)).wait_recv()

    @pl.when(lay.collects)
    def _():
        for bl in range(4):
            there = part.at[rows_at(base + bl * rows, rows)]

            @pl.when(at.bl != bl)
            def _():
                remote(there, out, send.at[bl], recv, lay.device(bl)).wait_send()

            @pl.when(at.bl == bl)
            def _():
                pltpu.make_async_copy(there, out, local).wait()

    @pl.when(jnp.logical_not(lay.slot_core))
    def _():
        remote(part, sib_land, sib_send, sib_recv, at.sibling()).wait_send()

    @pl.when(lay.slot_core)
    def _():
        for i in range(1, n):
            group = at.ahead(i)

            @pl.when(lay.in_half(group, lay.slot_half))
            def _():
                there = part.at[lay.group_rows(group, lay.slot_half)]
                remote(there, mid_land.at[i - 1], mid_send.at[i], mid_recv.at[i], at.mid(i)).wait_send()


def sum_everywhere(at, mine, land, send, recv):
    for i, device in enumerate([at.sibling(), at.cube(0), at.cube(1), at.cube(2)]):
        copy = remote(mine, land.at[i], send.at[i], recv.at[i], device)
        copy.start()
        copy.wait()
        mine[...] = mine[...] + land[i]
        yield True
    sent = []
    for i in range(1, at.groups):
        copy = remote(mine, land.at[3 + i], send.at[3 + i], recv.at[3 + i], at.mid(i))
        copy.start()
        sent.append(copy)
    yield True
    for copy in sent:
        copy.wait()
    for i in range(1, at.groups):
        mine[...] = mine[...] + land[3 + i]


def everyone(at):
    return [at.cube(*dims) for dims in PEERS] + [at.sibling()] + [at.mid(i) for i in range(1, at.groups)]


def cube_only(at):
    return [at.cube(*dims) for dims in ((0,), (1,), (2,))]


def communicate(body, collective_id, ins, outs, scratch, in_specs, out_specs, limit=60):
    return pl.pallas_call(
        body,
        out_shape=outs,
        in_specs=in_specs,
        out_specs=out_specs,
        scratch_shapes=scratch,
        compiler_params=pltpu.CompilerParams(
            collective_id=collective_id, has_side_effects=True, vmem_limit_bytes=limit << 20
        ),
    )(*ins)


def like(shape, dtype=BF16):
    return jax.ShapeDtypeStruct(shape, dtype)


def gather_first(groups, xhat, w_qkv):
    n = groups
    rows = w_qkv.shape[1]

    def body(xhat, w_qkv, xhat_b, qkv, local, tok_s, tok_r, col_s, col_r, mid_s, mid_r, sib_s, sib_r):
        at = Place(groups)
        meet(everyone(at))

        def columns():
            yield from columns_in_cube(at, w_qkv, qkv, local.at[0], col_s, col_r)
            yield from columns_across(at, qkv, rows, mid_s, mid_r, sib_s, sib_r)

        drive(columns(), gather_tokens(at, xhat, xhat_b, local.at[1], tok_s, tok_r))

    return communicate(
        body,
        0,
        (xhat, w_qkv),
        (like((SLOTS, CHUNK, D)), like((D, QKV_SLOT))),
        [DMA((2,)), *[DMA((len(PARTS), 7))] * 2, *[DMA((7,))] * 2, *[DMA((n, 2, 1))] * 4],
        [HBM] * 2,
        [HBM] * 2,
    )


def return_keys(groups, own, prompt, before):
    def body(own, prompt, before, out, land, land_p, land_b, far_p, far_b, send, recv, p_send, p_recv, b_send, b_recv):
        at = Place(groups)
        meet([at.sibling()] + [at.mid(i) for i in range(1, groups)])

        def swap(array, place, i):
            return remote(array.at[:, 1 - at.c], place, send.at[i], recv.at[i], at.sibling())

        def merge(dst, terms, count):
            def one(i, carry):
                total = terms[0](i).astype(F32)
                for term in terms[1:]:
                    total = total + term(i).astype(F32)
                dst(i, total.astype(BF16))
                return carry

            lax.fori_loop(0, count, one, 0)

        first = swap(own, land, 0)
        second = swap(prompt, land_p, 1)
        third = swap(before, land_b, 2) if groups > 2 else None

        @pl.when(at.g > 0)
        def _():
            second.start()

        if groups > 2:

            @pl.when(at.g > 1)
            def _():
                third.start()

        first.start()

        def put(ref):
            def store(i, value):
                ref[i] = value

            return store

        def home(i):
            return remote(land_p, far_p.at[i - 1], p_send, p_recv.at[i - 1], at.mid_at(jnp.int32(0)))

        def back():
            return remote(land_b, far_b, b_send, b_recv, at.mid_at(at.g - 1))

        @pl.when(at.g > 0)
        def _():
            second.wait()
            merge(put(land_p), [lambda i: prompt[i, at.c], lambda i: land_p[i]], 8)
            for i in range(1, groups):

                @pl.when(at.g == i)
                def _():
                    home(i).start()

        if groups > 2:

            @pl.when(at.g > 1)
            def _():
                third.wait()
                merge(put(land_b), [lambda i: before[i, at.c], lambda i: land_b[i]], 4)
                back().start()

        first.wait()
        merge(put(land), [lambda i: own[i, at.c], lambda i: land[i]], 8)

        @pl.when(at.g == 0)
        def _():
            for i in range(1, groups):
                home(i).wait_recv()
                merge(put(land), [lambda j: land[j], lambda j, i=i: far_p[i - 1, j]], 8)

        if groups > 2:

            @pl.when((at.g >= 1) & (at.g < groups - 1))
            def _():
                back().wait_recv()
                merge(lambda i, v: land.__setitem__(i + 4, v), [lambda i: land[i + 4], lambda i: far_b[i]], 4)

            @pl.when(at.g > 1)
            def _():
                back().wait_send()

        @pl.when(at.g > 0)
        def _():
            home(1).wait_send()

        out[...] = land[...]

    near = pltpu.VMEM((8, CHUNK, 2 * HD), BF16)
    half = pltpu.VMEM((4, CHUNK, 2 * HD), BF16)
    return communicate(
        body,
        2,
        (own, prompt, before),
        like((8, CHUNK, 2 * HD)),
        [near, near, half, pltpu.VMEM((max(groups - 1, 1), 8, CHUNK, 2 * HD), BF16), half, DMA((3,)), DMA((3,)), DMA(()), DMA((groups,)), DMA(()), DMA(())],
        [VMEM] * 3,
        VMEM,
    )


def finish_mlp(groups, part_dx, hidden, cotangent, g_gu, rows):
    n = groups

    def body(part_dx, hidden, cotangent, g_gu, dhidden, dbranch_b, gu_sum, land, own, dx, sib_gu, mid_gu, local, s1, r1, s2, r2, cms, cmr, css, csr):
        at = Place(groups)
        meet(everyone(at))
        columns = columns_sum(at, g_gu, sib_gu, mid_gu, gu_sum, (cms, cmr, css, csr))
        next(columns)
        beside(scatter_tokens(at, part_dx, land, dx, s1, r1), columns)

        def norm(i, carry):
            rows = pl.ds(pl.multiple_of(i * 32, 32), 32)
            value = hidden[rows, :]
            inverse = lax.rsqrt(jnp.mean(value * value, 1, keepdims=True) + EPSILON)
            unit = value * inverse
            grad = dx[rows, :]
            total = cotangent[rows, :] + inverse * (grad - unit * jnp.mean(grad * unit, 1, keepdims=True))
            dhidden[rows, :] = total
            own[rows, :] = total.astype(BF16)
            return carry

        lax.fori_loop(0, CHUNK // 32, norm, 0)
        beside(gather_tokens(at, own, dbranch_b, local, s2, r2), columns)
        drive(columns)

    return communicate(
        body,
        4,
        (part_dx, hidden, cotangent, g_gu),
        (like((CHUNK, D), F32), like((SLOTS, CHUNK, D)), like((2, 4, rows, GU_SLOT))),
        [
            pltpu.VMEM((7, CHUNK, D), BF16),
            pltpu.VMEM((CHUNK, D), BF16),
            pltpu.VMEM((CHUNK, D), F32),
            pltpu.VMEM((2, 4 * n * rows, GU_SLOT), BF16),
            pltpu.VMEM((max(n - 1, 1), 2, 4, rows, GU_SLOT), BF16),
            DMA(()),
            *[DMA((len(PARTS), 7))] * 4,
            *[DMA((n, 2, 4))] * 2,
            *[DMA((2,))] * 2,
        ],
        [VMEM] * 4,
        [VMEM, HBM, VMEM],
    )


def finish_layer(groups, part_dx, part_out, tokens, hidden, dhidden, g_qkv, g_gu, g_out, gains, rows):
    n = groups

    def body(part_dx, part_out, tokens, hidden, dhidden, g_qkv, g_gu, g_out, gains, d_tokens, output, d_qkv, d_gu, d_out, gain_sum, land, land2, dx, sib_q, mid_q, fin_q, sib_o, mid_o, gain_land, local, s1, r1, s2, r2, cs, cr, cms, cmr, css, csr, ds_, dr_, os_, or_, oms, omr, oss, osr, gs, gr):
        at = Place(groups)
        meet(everyone(at))
        gain_sum[...] = gains[...]

        def in_path():
            yield from scatter_tokens(at, part_dx, land, dx, s1, r1)

            def norm(i, carry):
                rows = pl.ds(pl.multiple_of(i * 32, 32), 32)
                value = tokens[rows, :].astype(F32)
                inverse = lax.rsqrt(jnp.mean(value * value, 1, keepdims=True) + EPSILON)
                unit = value * inverse
                grad = dx[rows, :]
                d_tokens[rows, :] = dhidden[rows, :] + inverse * (grad - unit * jnp.mean(grad * unit, 1, keepdims=True))
                return carry

            lax.fori_loop(0, CHUNK // 32, norm, 0)
            yield from scatter_tokens(at, part_out, land2, dx, s2, r2)

            def add(i, carry):
                rows = pl.ds(pl.multiple_of(i * 32, 32), 32)
                output[rows, :] = (hidden[rows, :] + dx[rows, :]).astype(BF16)
                return carry

            lax.fori_loop(0, CHUNK // 32, add, 0)

        def columns():
            yield from columns_sum(at, g_qkv, sib_q, mid_q, fin_q, (cms, cmr, css, csr))
            yield from columns_home(at, fin_q, d_qkv, cs, cr, local.at[0])

        drive(
            columns(),
            scatter_heads(at, g_out, d_out, sib_o, mid_o, (os_, or_, oms, omr, oss, osr, local.at[1])),
            columns_home(at, g_gu, d_gu, ds_, dr_, local.at[2]),
            in_path(),
            sum_everywhere(at, gain_sum, gain_land, gs, gr),
        )

    deep = 4 * n * rows
    tok = DMA((len(PARTS), 7))
    return communicate(
        body,
        5,
        (part_dx, part_out, tokens, hidden, dhidden, g_qkv, g_gu, g_out, gains),
        (
            like((CHUNK, D), F32),
            like((CHUNK, D)),
            like((SLOTS, rows, QKV_SLOT)),
            like((SLOTS, rows, GU_SLOT)),
            like((rows, D)),
            like((8, HD), F32),
        ),
        [
            pltpu.VMEM((7, CHUNK, D), BF16),
            pltpu.VMEM((7, CHUNK, D), BF16),
            pltpu.VMEM((CHUNK, D), F32),
            pltpu.VMEM((2, deep, QKV_SLOT), BF16),
            pltpu.VMEM((max(n - 1, 1), 2, 4, rows, QKV_SLOT), BF16),
            pltpu.VMEM((2, 4, rows, QKV_SLOT), BF16),
            pltpu.VMEM((D // SLOTS, D), BF16),
            pltpu.VMEM((max(n - 1, 1), 4 * rows, D), BF16),
            pltpu.VMEM((4 + n, 8, HD), F32),
            DMA((3,)),
            tok,
            tok,
            tok,
            tok,
            DMA((7,)),
            DMA((7,)),
            *[DMA((n, 2, 4))] * 2,
            *[DMA((2,))] * 2,
            DMA((7,)),
            DMA((7,)),
            DMA((4,)),
            DMA(()),
            *[DMA((n,))] * 2,
            DMA(()),
            DMA(()),
            DMA((4 + n,)),
            DMA((4 + n,)),
        ],
        [VMEM] * 6 + [HBM] + [VMEM] * 2,
        [VMEM, VMEM, HBM, HBM, VMEM, VMEM],
    )


NT = (((1,), (1,)), ((), ()))
WIDE = 512
SCALE_2 = SCALE / math.log(2.0)


def visible(first_key, chunk_of_block, opening, tile):
    key = first_key + lax.broadcasted_iota(jnp.int32, (tile, 2 * CHUNK), 0)
    lane = lax.broadcasted_iota(jnp.int32, (1, 2 * CHUNK), 1)
    row = chunk_of_block * CHUNK + jnp.where(lane >= CHUNK, lane - CHUNK, lane)
    return (key <= row) & (key >= opening)


def key_range(group, chunk_of_block, tile):
    stop = (chunk_of_block * CHUNK + CHUNK + tile - 1) // tile
    start = jnp.where(group > 0, jnp.maximum(chunk_of_block * CHUNK - LONGEST, 0) // tile, 0)
    return start, stop


def two_heads(block):
    return jnp.concatenate([block[:, :HD], block[:, HD:]], 0)


def two_columns(block):
    return jnp.concatenate([block[:CHUNK], block[CHUNK:]], 1)


def turn_values(kv, turned):
    for t in range(kv.shape[0]):
        turned[:, pl.ds(2 * CHUNK * t, 2 * CHUNK)] = kv[t].reshape(2 * CHUNK, 2 * HD)[:, HD:].T


def attention_block(groups, q, kv, opening, w_out, tokens, gu_mine, dy):
    n = groups
    gu_rows = gu_mine.shape[1]
    reach = 4

    def body(q_ref, kv, open_ref, out_mine, tokens, gu_mine, dy, mixed, total, lse, own, prompt, before, w_out, hidden, xhat_b, gu, dy_b, own_vt, prompt_vt, before_vt, part, land, mine, local, ks, kr, ps, pr, bs, br, s1, r1, s2, r2, s3, r3, cs, cr, cms, cmr, css, csr, hl, hs, hr, hss, hsr):
        at = Place(groups)
        group, core = at.g, at.c
        meet(everyone(at))

        here = pltpu.make_async_copy(kv, own.at[:, core], local.at[0])
        here.start()
        sib = remote(kv, own.at[:, core], ks.at[0], kr.at[0], at.sibling())
        sib.start()

        def to_group(i):
            return remote(kv, prompt.at[:, core], ps.at[i], pr, at.mid_at(jnp.int32(i)))

        def forward():
            return remote(kv.at[pl.ds(reach, reach)], before.at[:, core], bs, br, at.mid_at(group + 1))

        def across(ref, i):
            return remote(ref.at[:, core], ref.at[:, core], ks.at[i], kr.at[i], at.sibling())

        @pl.when(group == 0)
        def _():
            for i in range(1, n):
                to_group(i).start()

        if n > 2:

            @pl.when((group >= 1) & (group < n - 1))
            def _():
                forward().start()

        heads = gather_heads(at, out_mine, w_out, hl, hs, hr, hss, hsr)
        next(heads)
        columns = columns_in_cube(at, gu_mine, gu, local.at[1], cs, cr)
        next(columns)
        here.wait()
        sib.wait()
        turn_values(own, own_vt)

        def step(kv, values_t, tile, chunk, q, opening, carry, masked, shift=0):
            norm, out = carry
            first = tile * WIDE
            parts = []
            for k in range(WIDE // CHUNK):
                keys = kv[tile * (WIDE // (2 * CHUNK)) + k // 2, k % 2][:, :HD]
                p = jnp.exp2(lax.dot_general(keys, q, NT, preferred_element_type=F32) * SCALE_2)
                if masked:
                    p = jnp.where(visible(first + shift + k * CHUNK, chunk, opening, CHUNK), p, 0.0)
                norm = norm + jnp.sum(p, 0, keepdims=True)
                parts.append(p.astype(BF16))
            first = first if isinstance(first, int) else pl.multiple_of(first, WIDE)
            out = out + jnp.dot(
                values_t[:, pl.ds(first, WIDE)], jnp.concatenate(parts, 0), preferred_element_type=F32
            )
            return norm, out

        def own_part(i, carry):
            chunk = 2 * i + core
            query, opening = two_heads(q_ref[i]), open_ref[i]
            start, stop = key_range(group, chunk, WIDE)
            zero = (jnp.zeros((1, 2 * CHUNK), F32), jnp.zeros((HD, 2 * CHUNK), F32))
            norm, out = lax.fori_loop(
                start, stop, lambda t, c: step(own, own_vt, t, chunk, query, opening, c, True), zero
            )
            lse[i] = norm
            total[i] = out
            return carry

        lax.fori_loop(0, SLOTS, own_part, 0)

        @pl.when(group > 0)
        def _():
            to_group(0).wait_recv()
            across(prompt, 1).start()

        if n > 2:

            @pl.when(group > 1)
            def _():
                forward().wait_recv()
                across(before, 2).start()

        drive(columns)
        columns = columns_across(at, gu, gu_rows, cms, cmr, css, csr)
        next(columns)
        next(heads)
        tokens_dy = gather_tokens(at, dy, dy_b, local.at[3], s3, r3)
        next(tokens_dy)

        @pl.when(group > 0)
        def _():
            across(prompt, 1).wait()
            turn_values(prompt, prompt_vt)

            def prompt_part(i, carry):
                query = two_heads(q_ref[i])
                state = (lse[i], total[i])
                for t in range(PROMPT // WIDE):
                    state = step(prompt, prompt_vt, t, 0, query, None, state, False)
                lse[i], total[i] = state
                return carry

            lax.fori_loop(0, SLOTS, prompt_part, 0)

        if n > 2:

            @pl.when(group > 1)
            def _():
                across(before, 2).wait()
                turn_values(before, before_vt)

                def before_part(i, carry):
                    query, opening = two_heads(q_ref[i]), open_ref[i]
                    state = (lse[i], total[i])
                    for t in range(LONGEST // WIDE):
                        state = step(before, before_vt, t, 2 * i + core, query, opening, state, True, -LONGEST)
                    lse[i], total[i] = state
                    return carry

                lax.fori_loop(0, reach, before_part, 0)

        next(tokens_dy)
        drive(heads)

        def project(i, carry):
            norm = lse[i]
            out = total[i] / norm
            total[i] = out
            lse[i] = jnp.log(norm)
            rows = two_columns(out.T.astype(BF16))
            mixed[i] = rows
            part[i] = jnp.dot(rows, w_out[...], preferred_element_type=F32).astype(BF16)
            return carry

        lax.fori_loop(0, SLOTS, project, 0)
        beside(scatter_tokens(at, part, land, hidden, s1, r1), columns, tokens_dy)

        def norm_rows(i, carry):
            rows = pl.ds(pl.multiple_of(i * 32, 32), 32)
            value = hidden[rows, :] + tokens[rows, :].astype(F32)
            hidden[rows, :] = value
            inverse = lax.rsqrt(jnp.mean(value * value, 1, keepdims=True) + EPSILON)
            mine[rows, :] = (value * inverse).astype(BF16)
            return carry

        lax.fori_loop(0, CHUNK // 32, norm_rows, 0)
        beside(gather_tokens(at, mine, xhat_b, local.at[4], s2, r2), columns)
        drive(tokens_dy, columns)

        @pl.when(group == 0)
        def _():
            for i in range(1, n):
                to_group(i).wait_send()

        if n > 2:

            @pl.when((group >= 1) & (group < n - 1))
            def _():
                forward().wait_send()

    block = (SLOTS, 2, CHUNK, 2 * HD)
    end = (reach, 2, CHUNK, 2 * HD)
    return communicate(
        body,
        1,
        (q, kv, opening, w_out, tokens, gu_mine, dy),
        (
            like((SLOTS, CHUNK, 2 * HD)),
            like((SLOTS, HD, 2 * CHUNK), F32),
            like((SLOTS, 1, 2 * CHUNK), F32),
            like(block),
            like(block),
            like(end),
            like((D // SLOTS, D)),
            like((CHUNK, D), F32),
            like((SLOTS, CHUNK, D)),
            like((D, GU_SLOT)),
            like((SLOTS, CHUNK, D)),
        ),
        [
            pltpu.VMEM((HD, 2 * SLOTS * CHUNK), BF16),
            pltpu.VMEM((HD, PROMPT), BF16),
            pltpu.VMEM((HD, LONGEST), BF16),
            pltpu.VMEM((SLOTS, CHUNK, D), BF16),
            pltpu.VMEM((7, CHUNK, D), BF16),
            pltpu.VMEM((CHUNK, D), BF16),
            DMA((5,)),
            *[DMA((3,))] * 2,
            DMA((n,)),
            *[DMA(())] * 3,
            *[DMA((len(PARTS), 7))] * 6,
            *[DMA((7,))] * 2,
            *[DMA((n, 2, 4))] * 4,
            *[DMA((n,))] * 2,
            DMA((n, 4)),
            *[DMA(())] * 2,
        ],
        [VMEM] * 5 + [HBM] * 2,
        [VMEM] * 8 + [HBM] * 3,
    )


def attend_back_body(groups, q_ref, do_ref, own, prompt, before, open_ref, total, lse, dq_ref, d_own, d_prompt, d_before, own_kt, prompt_kt, before_kt, acc_own, acc_prompt, acc_before, dq_sum):
    group = lax.axis_index("blk") // 4
    core = rem(lax.axis_index("uly"), 2)
    i = pl.program_id(0)
    chunk = 2 * i + core

    @pl.when(i == 0)
    def _():
        own_kt[...] = own[:, :HD].T
        prompt_kt[...] = prompt[:, :HD].T
        acc_own[...] = jnp.zeros_like(acc_own)
        acc_prompt[...] = jnp.zeros_like(acc_prompt)
        if groups > 2:
            before_kt[...] = before[:, :HD].T
            acc_before[...] = jnp.zeros_like(acc_before)

    q = two_heads(q_ref[0])
    do = two_heads(do_ref[0])
    dot_rows = jnp.sum(do.astype(F32).T * total[0], 0, keepdims=True)
    logs = lse[0] * (1.0 / math.log(2.0))
    opening = open_ref[0]

    def step(kv, keys_t, acc, first, dq, masked, shift=0):
        rows = pl.ds(first if isinstance(first, int) else pl.multiple_of(first, WIDE), WIDE)
        keys, values = kv[rows, :HD], kv[rows, HD:]
        s = lax.dot_general(keys, q, NT, preferred_element_type=F32)
        p = jnp.exp2(s * SCALE_2 - logs)
        if masked:
            p = jnp.where(visible(first + shift, chunk, opening, WIDE), p, 0.0)
        dp = lax.dot_general(values, do, NT, preferred_element_type=F32)
        ds = (p * (dp - dot_rows)).astype(BF16)
        acc[rows, :HD] += jnp.dot(ds, q, preferred_element_type=F32)
        acc[rows, HD:] += jnp.dot(p.astype(BF16), do, preferred_element_type=F32)
        return dq + jnp.dot(keys_t[:, rows], ds, preferred_element_type=F32)

    start, stop = key_range(group, chunk, WIDE)
    dq_sum[...] = lax.fori_loop(
        start,
        stop,
        lambda t, c: step(own, own_kt, acc_own, t * WIDE, c, True),
        jnp.zeros((HD, 2 * CHUNK), F32),
    )

    @pl.when(group > 0)
    def _():
        dq = dq_sum[...]
        for t in range(PROMPT // WIDE):
            dq = step(prompt, prompt_kt, acc_prompt, t * WIDE, dq, False)
        dq_sum[...] = dq

    if groups > 2:

        @pl.when((group > 1) & (chunk < before.shape[0] // CHUNK))
        def _():
            dq = dq_sum[...]
            for t in range(before.shape[0] // WIDE):
                dq = step(before, before_kt, acc_before, t * WIDE, dq, True, -before.shape[0])
            dq_sum[...] = dq

    dq = dq_sum[...]
    dq_ref[0] = two_columns((dq.T * SCALE).astype(BF16))

    @pl.when(i == 7)
    def _():
        for acc, out in ((acc_own, d_own), (acc_prompt, d_prompt)) + (((acc_before, d_before),) if groups > 2 else ()):
            out[:, :HD] = (acc[:, :HD] * SCALE).astype(BF16)
            out[:, HD:] = acc[:, HD:].astype(BF16)


def attend_back(groups, q, do, own, prompt, before, opening, total, lse):
    whole = lambda a: pl.BlockSpec(a.shape, lambda i: (0, 0))
    chunk = pl.BlockSpec((1, CHUNK, 2 * HD), lambda i: (i, 0, 0))
    return pl.pallas_call(
        functools.partial(attend_back_body, groups),
        grid=(8,),
        out_shape=(like(q.shape), like(own.shape), like(prompt.shape), like(before.shape)),
        in_specs=[
            chunk,
            chunk,
            whole(own),
            whole(prompt),
            whole(before),
            pl.BlockSpec((1, 1, 2 * CHUNK), lambda i: (i, 0, 0)),
            pl.BlockSpec((1, HD, 2 * CHUNK), lambda i: (i, 0, 0)),
            pl.BlockSpec((1, 1, 2 * CHUNK), lambda i: (i, 0, 0)),
        ],
        out_specs=[chunk, whole(own), whole(prompt), whole(before)],
        scratch_shapes=[
            pltpu.VMEM((HD, own.shape[0]), BF16),
            pltpu.VMEM((HD, prompt.shape[0]), BF16),
            pltpu.VMEM((HD, before.shape[0]), BF16),
            pltpu.VMEM(own.shape, F32),
            pltpu.VMEM(prompt.shape, F32),
            pltpu.VMEM(before.shape, F32),
            pltpu.VMEM((HD, 2 * CHUNK), F32),
        ],
        compiler_params=pltpu.CompilerParams(vmem_limit_bytes=48 << 20),
    )(q, do, own, prompt, before, opening, total, lse)


def rotate(vectors, cosine, sine):
    former, latter = jnp.split(vectors, 2, -1)
    return jnp.concatenate([former * cosine - latter * sine, latter * cosine + former * sine], -1)


def dot(a, b, dims=((1,), (0,))):
    return lax.dot_general(a, b, (dims, ((), ())), preferred_element_type=F32)


def across(x, i):
    blocks = lax.axis_size("blk")
    return lax.ppermute(x, "blk", [(b, (b + 4 * i) % blocks) for b in range(blocks)])


def by_group(parts, group):
    n = len(parts)
    if n == 2:
        return jnp.where(group == 0, jnp.stack(parts), jnp.stack(parts[::-1]))
    every = jnp.stack(parts)
    return jnp.stack([lax.dynamic_index_in_dim(every, (group + n - i) % n, 0, keepdims=False) for i in range(n)])


def other_core(x):
    return lax.ppermute(x, "uly", [(u, u + 1 - 2 * (u % 2)) for u in range(4)])


def swap_core_y(x):
    blocks = lax.axis_size("blk")
    pairs = []
    for u in range(4):
        for b in range(blocks):
            core, y = u % 2, b % 2
            pairs.append((u * blocks + b, (u - core + y) * blocks + b - y + core))
    return lax.ppermute(x, ("uly", "blk"), pairs)


def sum_cores(part, axis, core):
    mine = lax.dynamic_index_in_dim(part, core, axis, keepdims=False)
    theirs = lax.dynamic_index_in_dim(part, 1 - core, axis, keepdims=False)
    return (mine.astype(F32) + other_core(theirs).astype(F32)).astype(BF16)


def sum_across(part, axis, group):
    n = part.shape[axis]
    total = lax.dynamic_index_in_dim(part, group, axis, keepdims=False).astype(F32)
    for i in range(1, n):
        total = total + across(lax.dynamic_index_in_dim(part, (group + i) % n, axis, keepdims=False), i).astype(F32)
    return total.astype(BF16)


def body(tokens, lengths, attn_gain, w_qkv, q_gain, k_gain, w_out, mlp_gain, w_gate_up, w_down, cotangent):
    blocks = lax.axis_size("blk")
    groups = blocks // 4
    rows = w_qkv.shape[0]
    hidden_rows = w_down.shape[0]
    group = lax.axis_index("blk") // 4
    core = lax.axis_index("uly") % 2
    gain_one = attn_gain.astype(F32)[:, None]
    gain_two = mlp_gain.astype(F32)[:, None]

    scaled = (w_qkv.astype(F32) * gain_one).astype(BF16)
    by_slot = jnp.concatenate(
        [
            scaled[:, : HQ * HD].reshape(rows, SLOTS, 2 * HD),
            scaled[:, HQ * HD : (HQ + HK) * HD].reshape(rows, SLOTS, HD),
            scaled[:, (HQ + HK) * HD :].reshape(rows, SLOTS, HD),
        ],
        2,
    ).transpose(1, 0, 2)
    scaled_gu = (w_gate_up.astype(F32) * gain_two).astype(BF16)
    gu_by_slot = (
        scaled_gu.reshape(rows, 2, 2, 2, groups, 2, 2 * hidden_rows)
        .transpose(2, 5, 3, 0, 1, 4, 6)
        .reshape(SLOTS, rows, GU_SLOT)
    )
    inputs = tokens.astype(F32)
    xhat = (inputs * lax.rsqrt(jnp.mean(inputs * inputs, 1, keepdims=True) + EPSILON)).astype(BF16)
    dy = cotangent.astype(BF16)
    out_mine = jnp.stack([w_out] + [across(w_out, i) for i in range(1, groups)])
    xhat_b, qkv_w = gather_first(groups, xhat, by_slot)
    down_mine, qkv_w = lax.optimization_barrier((swap_core_y(w_down), qkv_w))
    down_half = by_group([down_mine] + [across(down_mine, i) for i in range(1, groups)], group)
    down_other = other_core(down_half)
    down_w = jnp.where(core == 0, jnp.stack([down_half, down_other], 1), jnp.stack([down_other, down_half], 1)).reshape(FF_SLOT, D)
    xhat_b = xhat_b.reshape(SLOTS * CHUNK, D)

    starts = PROMPT + jnp.sum(
        jnp.where(jnp.arange(lengths.shape[0])[:, None] > jnp.arange(lengths.shape[0])[None, :], lengths[None, :], 0), 1
    )
    index = (
        group * (2 * SLOTS * CHUNK)
        + (2 * jnp.arange(SLOTS, dtype=jnp.int32)[:, None] + core) * CHUNK
        + jnp.arange(CHUNK, dtype=jnp.int32)[None, :]
    )
    opening = jnp.max(jnp.where(index[..., None] >= starts, starts, 0), -1)
    position = jnp.where(index < PROMPT, index, index - opening + PROMPT).reshape(-1)
    opening = opening - group * (2 * SLOTS * CHUNK)
    opening = jnp.concatenate([opening, opening], 1)[:, None, :]
    inverse = ROPE_BASE ** (-2.0 * jnp.arange(HD // 2, dtype=F32) / HD)
    angles = position.astype(F32)[:, None] * inverse[None, :]
    cosine, sine = jnp.cos(angles)[:, None, :], jnp.sin(angles)[:, None, :]

    raw = dot(xhat_b, qkv_w).reshape(SLOTS * CHUNK, 4, HD)
    head_gain = jnp.stack([q_gain, q_gain, k_gain]).astype(F32)[None]

    def shape_heads(heads, gain):
        normed = heads * lax.rsqrt(jnp.mean(heads * heads, -1, keepdims=True) + EPSILON) * gain
        return rotate(normed, cosine, sine)

    turned, pullback = jax.vjp(shape_heads, raw[:, :3], jnp.broadcast_to(head_gain, (1, 3, HD)))
    turned = turned.astype(BF16)
    queries = turned[:, :2].reshape(SLOTS, CHUNK, 2 * HD)
    keys_values = jnp.stack([turned[:, 2], raw[:, 3].astype(BF16)], 1).reshape(SLOTS, CHUNK, 2 * HD)
    mixed, total, lse, own, prompt, before, out_w, hidden, xhat2_b, gu_w, dy_b = attention_block(
        groups, queries, keys_values, opening, out_mine, tokens, gu_by_slot, dy
    )
    own, prompt, before = (a.reshape(-1, 2 * HD) for a in (own, prompt, before))
    mixed = mixed.reshape(SLOTS * CHUNK, 2 * HD)
    dy_b = dy_b.reshape(SLOTS * CHUNK, D)
    xhat2_b = xhat2_b.reshape(SLOTS * CHUNK, D)

    both = dot(xhat2_b, gu_w)
    gate, up = both[:, :FF_SLOT], both[:, FF_SLOT:]
    sigmoid = jax.nn.sigmoid(gate)
    act = (gate * sigmoid * up).astype(BF16)
    part_out = dot(act, down_w).astype(BF16)
    g_down = dot(act, dy_b, ((0,), (0,))).astype(BF16)
    dact = dot(dy_b, down_w, ((1,), (1,)))
    dboth = jnp.concatenate(
        [dact * up * sigmoid * (1.0 + gate * (1.0 - sigmoid)), dact * gate * sigmoid], 1
    ).astype(BF16)
    g_gu = dot(xhat2_b, dboth, ((0,), (0,))).astype(BF16)
    part_dx2 = dot(dboth, gu_w, ((1,), (1,))).astype(BF16)
    dhidden, dbranch_b, gu_sum = finish_mlp(groups, part_dx2.reshape(SLOTS, CHUNK, D), hidden, cotangent, g_gu, rows)
    down_sum = sum_across(sum_cores(g_down.reshape(groups, 2, hidden_rows, D), 1, core), 0, group)
    d_w_down = swap_core_y(down_sum)
    dbranch_b = dbranch_b.reshape(SLOTS * CHUNK, D)
    g_out = dot(mixed, dbranch_b, ((0,), (0,))).astype(BF16)
    dmixed = dot(dbranch_b, out_w, ((1,), (1,))).astype(BF16).reshape(SLOTS, CHUNK, 2 * HD)
    dq, d_own, d_prompt, d_before = attend_back(groups, queries, dmixed, own, prompt, before, opening, total, lse)
    dkv = return_keys(
        groups,
        d_own.reshape(8, 2, CHUNK, 2 * HD),
        d_prompt.reshape(8, 2, CHUNK, 2 * HD),
        d_before.reshape(4, 2, CHUNK, 2 * HD),
    ).reshape(SLOTS * CHUNK, 2, HD)
    d_turned = jnp.concatenate([dq.reshape(SLOTS * CHUNK, 2, HD), dkv[:, :1]], 1).astype(F32)
    dqk, d_gain = pullback(d_turned)
    draw = jnp.concatenate([dqk.astype(BF16), dkv[:, 1:]], 1).reshape(SLOTS * CHUNK, QKV_SLOT)
    g_qkv = dot(xhat_b, draw, ((0,), (0,))).astype(BF16)
    part_dx = dot(draw, qkv_w, ((1,), (1,))).astype(BF16)
    gains = jnp.concatenate([(d_gain[0, 0] + d_gain[0, 1])[None], d_gain[0, 2][None], jnp.zeros((6, HD), F32)], 0)
    d_tokens, output, qkv_back, gu_back, d_w_out, gain_sum = finish_layer(
        groups,
        part_dx.reshape(SLOTS, CHUNK, D),
        part_out.reshape(SLOTS, CHUNK, D),
        tokens,
        hidden,
        dhidden,
        g_qkv,
        gu_sum,
        g_out,
        gains,
        rows,
    )

    qkv_back = qkv_back.astype(F32).transpose(1, 0, 2)
    raw_qkv = jnp.concatenate(
        [
            qkv_back[:, :, : 2 * HD].reshape(rows, HQ * HD),
            qkv_back[:, :, 2 * HD : 3 * HD].reshape(rows, HK * HD),
            qkv_back[:, :, 3 * HD :].reshape(rows, HK * HD),
        ],
        1,
    )
    raw_gu = (
        gu_back.astype(F32)
        .reshape(2, 2, 2, rows, 2, groups, 2 * hidden_rows)
        .transpose(3, 4, 0, 2, 5, 1, 6)
        .reshape(rows, 2 * FF)
    )
    return (
        output,
        d_tokens,
        jnp.sum(raw_qkv * w_qkv.astype(F32), 1),
        raw_qkv * gain_one,
        gain_sum[0],
        gain_sum[1],
        d_w_out.astype(F32),
        jnp.sum(raw_gu * w_gate_up.astype(F32), 1),
        raw_gu * gain_two,
        d_w_down.astype(F32),
    )


def solution(mesh):
    tokens = P(("blk", "uly"), None)
    weight = P(("uly", "blk"), None)
    gain = P(("uly", "blk"))
    return jax.shard_map(
        body,
        mesh=mesh,
        in_specs=(tokens, P(), gain, weight, P(), P(), weight, gain, weight, weight, tokens),
        out_specs=(tokens, tokens, gain, weight, P(), P(), weight, gain, weight, weight),
        check_vma=False,
    )
```

```python
import math
import types

import jax
import jax.numpy as jnp
from jax import lax
from jax.experimental import pallas as pl
from jax.experimental.pallas import tpu as pltpu
from jax.sharding import PartitionSpec as P

D = 2048
HQ = 16
HK = 8
HD = 128
FF = 6144
PROMPT = 2048
LONGEST = 1024

SLOTS = 8
CHUNK = 128
QKV_SLOT = 512
GU_SLOT = 2 * FF // SLOTS
FF_SLOT = FF // SLOTS
EPSILON = 1e-06
ROPE_BASE = 1000000.0
SCALE = 1.0 / math.sqrt(HD)

F32 = jnp.float32
BF16 = jnp.bfloat16
MESH = pl.DeviceIdType.MESH
HBM = pl.BlockSpec(memory_space=pl.ANY)
VMEM = pl.BlockSpec(memory_space=pltpu.VMEM)
DMA = pltpu.SemaphoreType.DMA
PARTS = ((0, 1, 2), 256), ((1, 2, 0), 768), ((2, 0, 1), 1024)


def rem(a, n):
    return lax.rem(a, jnp.int32(n))


class Place:
    def __init__(self, groups):
        self.groups = groups
        self.u = lax.axis_index("uly")
        self.b = lax.axis_index("blk")
        self.x = self.u // 2
        self.c = rem(self.u, 2)
        self.g = self.b // 4
        self.bl = rem(self.b, 4)
        self.bits = (self.x, rem(self.bl, 2), self.bl // 2)

    def flip(self, *dims):
        x, y, z = (rem(v + 1, 2) if d in dims else v for d, v in enumerate(self.bits))
        return x, 2 * z + y

    def chunk(self, *dims):
        x, bl = self.flip(*dims)
        return 2 * bl + x

    def slot(self, *dims):
        x, bl = self.flip(*dims)
        return 4 * x + bl

    def cube(self, *dims):
        x, bl = self.flip(*dims)
        return (2 * x + self.c, 4 * self.g + bl)

    def sibling(self):
        return (2 * self.x + 1 - self.c, self.b)

    def ahead(self, i):
        return rem(self.g + i, self.groups)

    def behind(self, i):
        return rem(self.g + self.groups - i, self.groups)

    def mid(self, i):
        return (self.u, 4 * self.ahead(i) + self.bl)

    def diagonal(self):
        x, y, z = self.bits
        return (2 * x + 1 - self.c, 4 * self.g + 2 * z + 1 - y)

    def mid_at(self, group):
        return (self.u, 4 * group + self.bl)


PEERS = ((0,), (1,), (2,), (0, 1), (0, 2), (1, 2), (0, 1, 2))


def meet(devices):
    barrier = pltpu.get_barrier_semaphore()
    for device in devices:
        pl.semaphore_signal(barrier, inc=1, device_id=device, device_id_type=MESH)
    pl.semaphore_wait(barrier, len(devices))


def remote(src, dst, send, recv, device):
    return pltpu.make_async_remote_copy(
        src_ref=src, dst_ref=dst, send_sem=send, recv_sem=recv, device_id=device, device_id_type=MESH
    )


def rows_at(start, count):
    return pl.ds(pl.multiple_of(start, 16), count)


def drive(*tasks):
    tasks = list(tasks)
    while tasks:
        tasks = [task for task in tasks if next(task, None) is not None]


def steps(task, count):
    for _ in range(count):
        next(task, None)


def beside(main, *bulk):
    for _ in main:
        for task in bulk:
            next(task, None)


def in_turn(*tasks):
    for task, count in tasks:
        for _ in range(count):
            next(task, None)
            yield True


def part_columns():
    start = 0
    for p, (order, width) in enumerate(PARTS):
        yield p, order, pl.ds(start, width)
        start += width


def gather_tokens(at, mine, block, local, send, recv):
    own = pltpu.make_async_copy(mine, block.at[at.chunk()], local)
    own.start()
    sent = []

    def push(p, i, dims, along, cols):
        src = block.at[at.chunk(*dims), :, cols] if dims else mine.at[:, cols]
        copy = remote(src, block.at[at.chunk(*dims), :, cols], send.at[p, i], recv.at[p, i], at.cube(along))
        copy.start()
        sent.append(copy)

    def arrive(p, i, dims, cols):
        there = block.at[at.chunk(*dims), :, cols]
        remote(there, there, send.at[p, i], recv.at[p, i], at.cube(dims[0])).wait_recv()

    parts = list(part_columns())
    for p, (a, b, c), cols in parts:
        push(p, 0, (), a, cols)
        push(p, 1, (), b, cols)
        push(p, 2, (), c, cols)
    yield True
    for p, (a, b, c), cols in parts:
        arrive(p, 0, (a,), cols)
        push(p, 3, (a,), b, cols)
        push(p, 4, (a,), c, cols)
        yield True
    for p, (a, b, c), cols in parts:
        arrive(p, 1, (b,), cols)
        push(p, 5, (b,), c, cols)
        arrive(p, 3, (a, b), cols)
        push(p, 6, (a, b), c, cols)
        yield True
    for p, (a, b, c), cols in parts:
        arrive(p, 2, (c,), cols)
        arrive(p, 4, (a, c), cols)
        arrive(p, 5, (b, c), cols)
        arrive(p, 6, (a, b, c), cols)
    for copy in sent:
        copy.wait_send()
    own.wait()


def add_rows(dst, terms, count, step=32):
    def body(i, carry):
        rows = pl.ds(pl.multiple_of(i * step, step), step)
        total = terms[0][rows, :].astype(F32)
        for term in terms[1:]:
            total = total + term[rows, :].astype(F32)
        dst[rows, :] = total.astype(dst.dtype)
        return carry

    lax.fori_loop(0, count // step, body, 0)


def scatter_tokens(at, part, land, out, send, recv):
    sent = []

    def push(p, i, dims, along, cols):
        copy = remote(part.at[at.chunk(*dims), :, cols], land.at[i, :, cols], send.at[p, i], recv.at[p, i], at.cube(along))
        copy.start()
        sent.append(copy)

    def arrive(p, i, along, cols):
        remote(land.at[i, :, cols], land.at[i, :, cols], send.at[p, i], recv.at[p, i], at.cube(along)).wait_recv()

    def add(i, dims, cols):
        here = part.at[at.chunk(*dims), :, cols]
        add_rows(here, [here, land.at[i, :, cols]], CHUNK)

    parts = list(part_columns())
    for p, (a, b, c), cols in parts:
        push(p, 3, (a, b, c), c, cols)
        push(p, 2, (b, c), c, cols)
    for p, (a, b, c), cols in parts:
        push(p, 1, (a, c), c, cols)
        push(p, 0, (c,), c, cols)
    yield True
    for p, (a, b, c), cols in parts:
        arrive(p, 3, c, cols)
        add(3, (a, b), cols)
        push(p, 5, (a, b), b, cols)
        arrive(p, 2, c, cols)
        add(2, (b,), cols)
        push(p, 4, (b,), b, cols)
        yield True
    for p, (a, b, c), cols in parts:
        arrive(p, 1, c, cols)
        add(1, (a,), cols)
        arrive(p, 5, b, cols)
        add(5, (a,), cols)
        push(p, 6, (a,), a, cols)
        yield True
    for p, (a, b, c), cols in parts:
        arrive(p, 0, c, cols)
        arrive(p, 4, b, cols)
        arrive(p, 6, a, cols)
        add_rows(
            out.at[:, cols],
            [part.at[at.chunk(), :, cols], land.at[0, :, cols], land.at[4, :, cols], land.at[6, :, cols]],
            CHUNK,
        )
    for copy in sent:
        copy.wait_send()


def column_row(at, rows, u, b):
    return (u * (4 * at.groups) + b) * rows


def columns_in_cube(at, mine, whole, local, send, recv):
    rows = mine.shape[1]
    own = rows_at(column_row(at, rows, at.u, at.b), rows)
    here = pltpu.make_async_copy(mine.at[at.slot()], whole.at[own], local)
    here.start()
    sent = []
    for i, dims in enumerate(PEERS):
        copy = remote(mine.at[at.slot(*dims)], whole.at[own], send.at[i], recv.at[i], at.cube(*dims))
        copy.start()
        sent.append(copy)
    yield True
    for i, dims in enumerate(PEERS):
        u, b = at.cube(*dims)
        there = whole.at[rows_at(column_row(at, rows, u, b), rows)]
        remote(there, there, send.at[i], recv.at[i], (u, b)).wait_recv()
    for copy in sent:
        copy.wait_send()
    here.wait()


def columns_across(at, whole, rows, mid_send, mid_recv, sib_send, sib_recv):
    n, pieces = at.groups, mid_send.shape[2]
    step = 4 * rows // pieces
    sent = []

    def piece(core, group, x, k):
        return whole.at[rows_at(column_row(at, rows, 2 * x + core, 4 * group) + k * step, step)]

    def pass_on(i, x, k):
        there = piece(at.c, at.behind(i), x, k)
        copy = remote(there, there, sib_send.at[i, x, k], sib_recv.at[i, x, k], at.sibling())
        copy.start()
        sent.append(copy)

    order = [(x, k) for x in range(2) for k in range(pieces)]
    for i in range(1, n):
        for x, k in order:
            there = piece(at.c, at.g, x, k)
            copy = remote(there, there, mid_send.at[i, x, k], mid_recv.at[i, x, k], at.mid(i))
            copy.start()
            sent.append(copy)
            if i == 1:
                pass_on(0, x, k)
            yield True
    for i in range(1, n):
        for x, k in order:
            there = piece(at.c, at.behind(i), x, k)
            remote(there, there, mid_send.at[i, x, k], mid_recv.at[i, x, k], at.mid(i)).wait_recv()
            pass_on(i, x, k)
    for i in range(n):
        for x, k in order:
            there = piece(1 - at.c, at.behind(i), x, k)
            remote(there, there, sib_send.at[i, x, k], sib_recv.at[i, x, k], at.sibling()).wait_recv()
    for copy in sent:
        copy.wait_send()


def gather_hidden(at, mine, whole, local, turn_send, turn_recv, mid_send, mid_recv, sib_send, sib_recv):
    n, rows, pieces = at.groups, mine.shape[0], mid_send.shape[1]
    step = rows // pieces
    own = whole.at[at.g, at.c]
    stays = at.bits[1] == at.c
    here = pltpu.make_async_copy(mine, own, local)
    there = remote(mine, whole.at[at.g, 1 - at.c], turn_send, turn_recv, at.diagonal())

    @pl.when(stays)
    def _():
        here.start()

    @pl.when(jnp.logical_not(stays))
    def _():
        there.start()

    yield True

    @pl.when(stays)
    def _():
        here.wait()

    @pl.when(jnp.logical_not(stays))
    def _():
        there.wait()

    sent = []
    for i in range(1, n):
        for k in range(pieces):
            piece = own.at[pl.ds(k * step, step)]
            copy = remote(piece, piece, mid_send.at[i, k], mid_recv.at[i, k], at.mid(i))
            copy.start()
            sent.append(copy)
            yield True

    def pass_on(i):
        group = whole.at[at.behind(i), at.c]
        copy = remote(group, group, sib_send.at[i], sib_recv.at[i], at.sibling())
        copy.start()
        sent.append(copy)

    pass_on(0)
    for i in range(1, n):
        for k in range(pieces):
            piece = whole.at[at.behind(i), at.c, pl.ds(k * step, step)]
            remote(piece, piece, mid_send.at[i, k], mid_recv.at[i, k], at.mid(i)).wait_recv()
        pass_on(i)
    for i in range(n):
        group = whole.at[at.behind(i), 1 - at.c]
        remote(group, group, sib_send.at[i], sib_recv.at[i], at.sibling()).wait_recv()
    for copy in sent:
        copy.wait_send()


class OutRows:
    def __init__(self, at, rows):
        self.at, self.rows = at, rows
        self.per_half = max(at.groups // 2, 1)
        self.my_half = at.g // self.per_half
        self.to = 2 * self.my_half + at.c
        self.collects = at.bl == self.to
        self.slot_core = rem(at.bl, 2) == at.c
        self.slot_half = at.bl // 2

    def group_rows(self, group, half):
        return rows_at((group - half * self.per_half) * (4 * self.rows), 4 * self.rows)

    def in_half(self, group, half):
        return group // self.per_half == half

    def device(self, bl):
        return (self.at.u, 4 * self.at.g + bl)


def gather_heads(at, mine, whole, local, send, recv, sib_send, sib_recv):
    n, rows = mine.shape[0], mine.shape[1]
    lay = OutRows(at, rows)

    def place(group, bl):
        half = group // lay.per_half
        return whole.at[rows_at(((group - half * lay.per_half) * 4 + bl) * rows, rows)]

    def push(i):
        group = at.behind(i)
        to = 2 * (group // lay.per_half) + at.c
        here = pltpu.make_async_copy(mine.at[i], place(group, at.bl), local.at[i])
        there = remote(mine.at[i], place(group, at.bl), send.at[i], recv.at[i, at.bl], lay.device(to))
        return at.bl == to, here, there

    for i in range(n):
        stays, here, there = push(i)

        @pl.when(stays)
        def _():
            here.start()

        @pl.when(jnp.logical_not(stays))
        def _():
            there.start()

    yield True

    @pl.when(lay.slot_core)
    def _():
        for i in range(n):
            group = at.behind(i)

            @pl.when(lay.in_half(group, lay.slot_half))
            def _():
                pltpu.make_async_copy(mine.at[i], place(group, at.bl), local.at[i]).wait()
                for bl in range(4):

                    @pl.when(at.bl != bl)
                    def _():
                        there = place(group, bl)
                        remote(there, there, send.at[i], recv.at[i, bl], lay.device(bl)).wait_recv()

        remote(whole, whole, sib_send, sib_recv, at.sibling()).start()

    yield True

    @pl.when(lay.slot_core)
    def _():
        remote(whole, whole, sib_send, sib_recv, at.sibling()).wait_send()

    @pl.when(jnp.logical_not(lay.slot_core))
    def _():
        remote(whole, whole, sib_send, sib_recv, at.sibling()).wait_recv()

    for i in range(n):
        stays, here, there = push(i)

        @pl.when(jnp.logical_not(stays))
        def _():
            there.wait_send()


def columns_home(at, final, out, send, recv, local):
    sent = []
    for i, dims in enumerate(PEERS):
        x, bl = at.flip(*dims)
        copy = remote(final.at[x, bl], out.at[at.slot()], send.at[i], recv.at[i], at.cube(*dims))
        copy.start()
        sent.append(copy)
    here = pltpu.make_async_copy(final.at[at.x, at.bl], out.at[at.slot()], local)
    here.start()
    yield True
    for i, dims in enumerate(PEERS):
        there = out.at[at.slot(*dims)]
        remote(there, there, send.at[i], recv.at[i], at.cube(*dims)).wait_recv()
    for copy in sent:
        copy.wait_send()
    here.wait()


def columns_sum(at, part, sib_land, mid_land, final, sems):
    n, rows = at.groups, final.shape[2]
    mid_send, mid_recv, sib_send, sib_recv = sems
    run, deep = 4 * rows, 4 * n * rows
    sent = []

    def of_core(x, core):
        return part.at[rows_at((2 * x + core) * deep, deep)]

    for x in range(2):
        copy = remote(of_core(x, 1 - at.c), sib_land.at[x], sib_send.at[x], sib_recv.at[x], at.sibling())
        copy.start()
        sent.append(copy)
    yield True
    for x in range(2):
        remote(sib_land.at[x], sib_land.at[x], sib_send.at[x], sib_recv.at[x], at.sibling()).wait_recv()
        for i in range(1, n):
            for k in range(4):
                offset = at.ahead(i) * run + k * rows
                there = part.at[rows_at((2 * x + at.c) * deep + offset, rows)]
                add_rows(there, [there, sib_land.at[x, rows_at(offset, rows)]], rows, 16)
                copy = remote(there, mid_land.at[i - 1, x, k], mid_send.at[i, x, k], mid_recv.at[i, x, k], at.mid(i))
                copy.start()
                sent.append(copy)
                yield True
    for x in range(2):
        for k in range(4):
            for i in range(1, n):
                there = mid_land.at[i - 1, x, k]
                remote(there, there, mid_send.at[i, x, k], mid_recv.at[i, x, k], at.mid(i)).wait_recv()
            offset = at.g * run + k * rows
            add_rows(
                final.at[x, k],
                [part.at[rows_at((2 * x + at.c) * deep + offset, rows)], sib_land.at[x, rows_at(offset, rows)]]
                + [mid_land.at[i - 1, x, k] for i in range(1, n)],
                rows,
                16,
            )
    for copy in sent:
        copy.wait_send()


def hidden_sum(at, part, out, sib_land, mid_land, final, sems):
    n, rows = at.groups, out.shape[0]
    pieces, step = mid_land.shape[1], mid_land.shape[2]
    mid_send, mid_recv, sib_send, sib_recv, turn_send, turn_recv, local = sems
    across = remote(part.at[:, 1 - at.c], sib_land, sib_send, sib_recv, at.sibling())
    across.start()
    yield True
    across.wait()
    sent = []
    for i in range(1, n):
        group = at.ahead(i)
        for k in range(pieces):
            at_k = pl.ds(k * step, step)
            there = part.at[group, at.c, at_k]
            add_rows(there, [there, sib_land.at[group, at_k]], step, 16)
            copy = remote(there, mid_land.at[i - 1, k], mid_send.at[i, k], mid_recv.at[i, k], at.mid(i))
            copy.start()
            sent.append(copy)
            yield True
    for copy in sent:
        copy.wait()
    for k in range(pieces):
        at_k = pl.ds(k * step, step)
        add_rows(
            final.at[at_k],
            [part.at[at.g, at.c, at_k], sib_land.at[at.g, at_k]] + [mid_land.at[i - 1, k] for i in range(1, n)],
            step,
            16,
        )
    stays = at.bits[1] == at.c
    here = pltpu.make_async_copy(final, out, local)
    there = remote(final, out, turn_send, turn_recv, at.diagonal())

    @pl.when(stays)
    def _():
        here.start()
        here.wait()

    @pl.when(jnp.logical_not(stays))
    def _():
        there.start()
        there.wait()


def scatter_heads(at, part, out, sib_land, mid_land, sems):
    n, rows = at.groups, out.shape[0]
    send, recv, mid_send, mid_recv, sib_send, sib_recv, local = sems
    lay = OutRows(at, rows)

    @pl.when(jnp.logical_not(lay.slot_core))
    def _():
        remote(part, sib_land, sib_send, sib_recv, at.sibling()).start()

    yield True

    @pl.when(lay.slot_core)
    def _():
        remote(part, sib_land, sib_send, sib_recv, at.sibling()).wait_recv()
        add_rows(part, [part, sib_land], 256, 16)
        for i in range(1, n):
            group = at.ahead(i)

            @pl.when(lay.in_half(group, lay.slot_half))
            def _():
                there = part.at[lay.group_rows(group, lay.slot_half)]
                remote(there, mid_land.at[i - 1], mid_send.at[i], mid_recv.at[i], at.mid(i)).start()

    yield True
    mine = part.at[lay.group_rows(at.g, lay.my_half)]
    base = (at.g - lay.my_half * lay.per_half) * (4 * rows)

    @pl.when(lay.collects)
    def _():
        for i in range(1, n):
            remote(mine, mid_land.at[i - 1], mid_send.at[i], mid_recv.at[i], at.mid(i)).wait_recv()
        add_rows(mine, [mine] + [mid_land.at[i - 1] for i in range(1, n)], 4 * rows, 16)
        for bl in range(4):
            there = part.at[rows_at(base + bl * rows, rows)]

            @pl.when(at.bl != bl)
            def _():
                remote(there, out, send.at[bl], recv, lay.device(bl)).start()

            @pl.when(at.bl == bl)
            def _():
                pltpu.make_async_copy(there, out, local).start()

    yield True

    @pl.when(jnp.logical_not(lay.collects))
    def _():
        remote(out, out, send.at[0], recv, lay.device(lay.to)).wait_recv()

    @pl.when(lay.collects)
    def _():
        for bl in range(4):
            there = part.at[rows_at(base + bl * rows, rows)]

            @pl.when(at.bl != bl)
            def _():
                remote(there, out, send.at[bl], recv, lay.device(bl)).wait_send()

            @pl.when(at.bl == bl)
            def _():
                pltpu.make_async_copy(there, out, local).wait()

    @pl.when(jnp.logical_not(lay.slot_core))
    def _():
        remote(part, sib_land, sib_send, sib_recv, at.sibling()).wait_send()

    @pl.when(lay.slot_core)
    def _():
        for i in range(1, n):
            group = at.ahead(i)

            @pl.when(lay.in_half(group, lay.slot_half))
            def _():
                there = part.at[lay.group_rows(group, lay.slot_half)]
                remote(there, mid_land.at[i - 1], mid_send.at[i], mid_recv.at[i], at.mid(i)).wait_send()


def sum_everywhere(at, mine, land, send, recv):
    for i, device in enumerate([at.sibling(), at.cube(0), at.cube(1), at.cube(2)]):
        copy = remote(mine, land.at[i], send.at[i], recv.at[i], device)
        copy.start()
        copy.wait()
        mine[...] = mine[...] + land[i]
        yield True
    sent = []
    for i in range(1, at.groups):
        copy = remote(mine, land.at[3 + i], send.at[3 + i], recv.at[3 + i], at.mid(i))
        copy.start()
        sent.append(copy)
    yield True
    for copy in sent:
        copy.wait()
    for i in range(1, at.groups):
        mine[...] = mine[...] + land[3 + i]


def everyone(at):
    return [at.cube(*dims) for dims in PEERS] + [at.sibling()] + [at.mid(i) for i in range(1, at.groups)]


def cube_only(at):
    return [at.cube(*dims) for dims in ((0,), (1,), (2,))]


def communicate(body, collective_id, ins, outs, scratch, in_specs, out_specs, limit=60):
    return pl.pallas_call(
        body,
        out_shape=outs,
        in_specs=in_specs,
        out_specs=out_specs,
        scratch_shapes=scratch,
        compiler_params=pltpu.CompilerParams(
            collective_id=collective_id, has_side_effects=True, vmem_limit_bytes=limit << 20
        ),
    )(*ins)


def like(shape, dtype=BF16):
    return jax.ShapeDtypeStruct(shape, dtype)


def finish_layer(groups, part_dx, tokens, dhidden, g_qkv, g_out, gains, rows):
    n = groups

    def body(part_dx, tokens, dhidden, g_qkv, g_out, gains, d_tokens, d_qkv, d_out, gain_sum, land, dx, sib_q, mid_q, fin_q, sib_o, mid_o, gain_land, local, s1, r1, cs, cr, cms, cmr, css, csr, os_, or_, oms, omr, oss, osr, gs, gr):
        at = Place(groups)
        meet(everyone(at))
        gain_sum[...] = gains[...]

        def in_path():
            yield from scatter_tokens(at, part_dx, land, dx, s1, r1)

            def norm(i, carry):
                rows = pl.ds(pl.multiple_of(i * 32, 32), 32)
                value = tokens[rows, :].astype(F32)
                inverse = lax.rsqrt(jnp.mean(value * value, 1, keepdims=True) + EPSILON)
                unit = value * inverse
                grad = dx[rows, :]
                d_tokens[rows, :] = dhidden[rows, :] + inverse * (grad - unit * jnp.mean(grad * unit, 1, keepdims=True))
                return carry

            lax.fori_loop(0, CHUNK // 32, norm, 0)

        def columns():
            yield from columns_sum(at, g_qkv, sib_q, mid_q, fin_q, (cms, cmr, css, csr))
            yield from columns_home(at, fin_q, d_qkv, cs, cr, local.at[0])

        wide = columns()
        heads = scatter_heads(at, g_out, d_out, sib_o, mid_o, (os_, or_, oms, omr, oss, osr, local.at[1]))
        sums = sum_everywhere(at, gain_sum, gain_land, gs, gr)
        next(wide)
        next(heads)
        bulk = in_turn((wide, 4), (heads, 1), (wide, 4))
        beside(in_path(), bulk)
        drive(heads, wide, sums)

    deep = 4 * n * rows
    tok = DMA((len(PARTS), 7))
    return communicate(
        body,
        5,
        (part_dx, tokens, dhidden, g_qkv, g_out, gains),
        (
            like((CHUNK, D), F32),
            like((SLOTS, rows, QKV_SLOT)),
            like((rows, D)),
            like((8, HD), F32),
        ),
        [
            pltpu.VMEM((7, CHUNK, D), BF16),
            pltpu.VMEM((CHUNK, D), F32),
            pltpu.VMEM((2, deep, QKV_SLOT), BF16),
            pltpu.VMEM((max(n - 1, 1), 2, 4, rows, QKV_SLOT), BF16),
            pltpu.VMEM((2, 4, rows, QKV_SLOT), BF16),
            pltpu.VMEM((D // SLOTS, D), BF16),
            pltpu.VMEM((max(n - 1, 1), 4 * rows, D), BF16),
            pltpu.VMEM((4 + n, 8, HD), F32),
            DMA((2,)),
            tok,
            tok,
            DMA((7,)),
            DMA((7,)),
            *[DMA((n, 2, 4))] * 2,
            *[DMA((2,))] * 2,
            DMA((4,)),
            DMA(()),
            *[DMA((n,))] * 2,
            DMA(()),
            DMA(()),
            DMA((4 + n,)),
            DMA((4 + n,)),
        ],
        [VMEM] * 6,
        [VMEM, HBM, VMEM, VMEM],
    )


NT = (((1,), (1,)), ((), ()))
WIDE = 512
SCALE_2 = SCALE / math.log(2.0)


def visible(first_key, chunk_of_block, opening, tile):
    key = first_key + lax.broadcasted_iota(jnp.int32, (tile, 2 * CHUNK), 0)
    lane = lax.broadcasted_iota(jnp.int32, (1, 2 * CHUNK), 1)
    row = chunk_of_block * CHUNK + jnp.where(lane >= CHUNK, lane - CHUNK, lane)
    return (key <= row) & (key >= opening)


def key_range(group, chunk_of_block, tile):
    stop = (chunk_of_block * CHUNK + CHUNK + tile - 1) // tile
    start = jnp.where(group > 0, jnp.maximum(chunk_of_block * CHUNK - LONGEST, 0) // tile, 0)
    return start, stop


def two_heads(block):
    return jnp.concatenate([block[:, :HD], block[:, HD:]], 0)


def two_columns(block):
    return jnp.concatenate([block[:CHUNK], block[CHUNK:]], 1)


def turn_values(kv, turned):
    for t in range(kv.shape[0]):
        turned[:, pl.ds(2 * CHUNK * t, 2 * CHUNK)] = kv[t].reshape(2 * CHUNK, 2 * HD)[:, HD:].T


def front_block(groups, rows, hidden_rows, ins):
    n = groups

    def body(r):
        at = Place(n)
        group, core = at.g, at.c
        meet(everyone(at) + [at.diagonal()])
        wide = columns_in_cube(at, r.qkv_mine, r.qkv, r.local.at[0], r.qs, r.qr)
        next(wide)
        tokens = gather_tokens(at, r.xhat, r.xhat_b, r.local.at[1], r.s1, r.r1)
        next(tokens)
        lower = gather_hidden(at, r.down_mine, r.down, r.local.at[2], r.hts, r.htr, r.hms, r.hmr, r.hss, r.hsr)
        next(lower)
        out_here = pltpu.make_async_copy(r.out_mine, r.out_all.at[0], r.local.at[3])
        out_here.start()
        steps(tokens, 3)
        drive(wide)
        wide = columns_across(at, r.qkv, rows, r.qms, r.qmr, r.qss, r.qsr)
        steps(wide, 2 * (n - 1))
        steps(tokens, 3)
        columns = columns_in_cube(at, r.gu_mine, r.gu, r.local.at[4], r.cs, r.cr)
        next(columns)
        far = [remote(r.out_mine, r.out_all.at[i], r.fs.at[i], r.fr.at[i], at.mid(i)) for i in range(1, n)]
        for copy in far:
            copy.start()
        drive(tokens)
        drive(wide)

        def project_in(i, carry):
            four = pl.ds(pl.multiple_of(4 * i, 4), 4)
            raw = jnp.dot(r.xhat_b[four].reshape(4 * CHUNK, D), r.qkv[...], preferred_element_type=F32)
            cosine, sine = r.cosine[four].reshape(4 * CHUNK, HD), r.sine[four].reshape(4 * CHUNK, HD)
            heads = []
            for h in range(3):
                head = raw[:, h * HD : (h + 1) * HD]
                gain = r.head_gain[h : h + 1, :]
                normed = head * lax.rsqrt(jnp.mean(head * head, 1, keepdims=True) + EPSILON) * gain
                heads.append((normed * cosine + pltpu.roll(normed, HD // 2, 1) * sine).astype(BF16))
            r.raw[four] = raw[:, : 3 * HD].reshape(4, CHUNK, 3 * HD)
            r.q[four] = jnp.concatenate(heads[:2], 1).reshape(4, CHUNK, 2 * HD)
            r.kv[four] = jnp.concatenate([heads[2], raw[:, 3 * HD :].astype(BF16)], 1).reshape(4, CHUNK, 2 * HD)
            return carry

        lax.fori_loop(0, 2, project_in, 0)

        here = pltpu.make_async_copy(r.kv, r.own.at[:, core], r.local.at[1])
        here.start()
        sib = remote(r.kv, r.own.at[:, core], r.ks.at[0], r.kr.at[0], at.sibling())
        sib.start()

        def to_group(i):
            return remote(r.kv, r.prompt.at[:, core], r.ps.at[i], r.pr, at.mid_at(jnp.int32(i)))

        def forward():
            half = r.kv.at[pl.ds(SLOTS // 2, SLOTS // 2)]
            return remote(half, r.before.at[:, core], r.bs, r.br, at.mid_at(group + 1))

        def across(ref, i):
            return remote(ref.at[:, core], ref.at[:, core], r.ks.at[i], r.kr.at[i], at.sibling())

        @pl.when(group == 0)
        def _():
            for i in range(1, n):
                to_group(i).start()

        if n > 2:

            @pl.when((group >= 1) & (group < n - 1))
            def _():
                forward().start()

        steps(lower, 1)
        out_here.wait()
        for copy in far:
            copy.wait()
        heads = gather_heads(at, r.out_all, r.w_out, r.hl, r.hs, r.hr, r.os, r.orr)
        next(heads)
        here.wait()
        sib.wait()
        turn_values(r.own, r.own_vt)
        drive(columns)
        columns = columns_across(at, r.gu, rows, r.cms, r.cmr, r.css, r.csr)
        bulk = in_turn((lower, r.hms.shape[1] * (n - 1) - 1), (columns, 8 * (n - 1)))
        steps(bulk, 1)
        dy = gather_tokens(at, r.dy, r.dy_b, r.local.at[0], r.s3, r.r3)
        next(dy)

        def step(kv, values_t, tile, chunk, q, opening, carry, masked, shift=0):
            norm, out = carry
            first = tile * WIDE
            parts = []
            for k in range(WIDE // CHUNK):
                keys = kv[tile * (WIDE // (2 * CHUNK)) + k // 2, k % 2][:, :HD]
                p = jnp.exp2(lax.dot_general(keys, q, NT, preferred_element_type=F32) * SCALE_2)
                if masked:
                    p = jnp.where(visible(first + shift + k * CHUNK, chunk, opening, CHUNK), p, 0.0)
                norm = norm + jnp.sum(p, 0, keepdims=True)
                parts.append(p.astype(BF16))
            first = first if isinstance(first, int) else pl.multiple_of(first, WIDE)
            out = out + jnp.dot(
                values_t[:, pl.ds(first, WIDE)], jnp.concatenate(parts, 0), preferred_element_type=F32
            )
            return norm, out

        def own_part(i, carry):
            chunk = 2 * i + core
            query, opening = two_heads(r.q[i]), r.opening[i]
            start, stop = key_range(group, chunk, WIDE)
            zero = (jnp.zeros((1, 2 * CHUNK), F32), jnp.zeros((HD, 2 * CHUNK), F32))
            norm, out = lax.fori_loop(
                start, stop, lambda t, c: step(r.own, r.own_vt, t, chunk, query, opening, c, True), zero
            )
            r.lse[i] = norm
            r.total[i] = out
            return carry

        lax.fori_loop(0, SLOTS, own_part, 0)
        next(heads)
        steps(bulk, 1)

        @pl.when(group > 0)
        def _():
            to_group(0).wait_recv()
            across(r.prompt, 1).start()

        if n > 2:

            @pl.when(group > 1)
            def _():
                forward().wait_recv()
                across(r.before, 2).start()

        steps(dy, 3)
        steps(bulk, 1)

        @pl.when(group > 0)
        def _():
            across(r.prompt, 1).wait()
            turn_values(r.prompt, r.prompt_vt)

            def prompt_part(i, carry):
                query = two_heads(r.q[i])
                state = (r.lse[i], r.total[i])
                for t in range(PROMPT // WIDE):
                    state = step(r.prompt, r.prompt_vt, t, 0, query, None, state, False)
                r.lse[i], r.total[i] = state
                return carry

            lax.fori_loop(0, SLOTS, prompt_part, 0)

        if n > 2:

            @pl.when(group > 1)
            def _():
                across(r.before, 2).wait()
                turn_values(r.before, r.before_vt)

                def before_part(i, carry):
                    query, opening = two_heads(r.q[i]), r.opening[i]
                    state = (r.lse[i], r.total[i])
                    for t in range(LONGEST // WIDE):
                        state = step(r.before, r.before_vt, t, 2 * i + core, query, opening, state, True, -LONGEST)
                    r.lse[i], r.total[i] = state
                    return carry

                lax.fori_loop(0, SLOTS // 2, before_part, 0)

        steps(dy, 3)
        steps(bulk, 1)
        drive(heads)

        def project_out(i, carry):
            norm = r.lse[i]
            out = r.total[i] / norm
            r.total[i] = out
            r.lse[i] = jnp.log(norm)
            row = two_columns(out.T.astype(BF16))
            r.mixed[i] = row
            r.part[i] = jnp.dot(row, r.w_out[...], preferred_element_type=F32).astype(BF16)
            return carry

        lax.fori_loop(0, SLOTS, project_out, 0)
        beside(scatter_tokens(at, r.part, r.land, r.hidden, r.s4, r.r4), bulk)

        def norm_rows(i, carry):
            rows = pl.ds(pl.multiple_of(i * 32, 32), 32)
            value = r.hidden[rows, :] + r.tokens[rows, :].astype(F32)
            r.hidden[rows, :] = value
            inverse = lax.rsqrt(jnp.mean(value * value, 1, keepdims=True) + EPSILON)
            r.mine[rows, :] = (value * inverse).astype(BF16)
            return carry

        lax.fori_loop(0, CHUNK // 32, norm_rows, 0)
        beside(gather_tokens(at, r.mine, r.xhat2_b, r.local.at[5], r.s2, r.r2), bulk)
        drive(dy, bulk)
        drive(lower, columns)

        @pl.when(group == 0)
        def _():
            for i in range(1, n):
                to_group(i).wait_send()

        if n > 2:

            @pl.when((group >= 1) & (group < n - 1))
            def _():
                forward().wait_send()

    chunks = (SLOTS, CHUNK, 2 * HD)
    block, end = (SLOTS, 2, CHUNK, 2 * HD), (SLOTS // 2, 2, CHUNK, 2 * HD)
    tok = DMA((len(PARTS), 7))
    pieces = max(hidden_rows // 48, 1)
    return kernel(
        1,
        body,
        {name: (a, HBM if name.endswith("_mine") or name == "dy" else VMEM) for name, a in ins.items()},
        {
            "xhat_b": (like((SLOTS, CHUNK, D)), VMEM),
            "qkv": (like((D, QKV_SLOT)), VMEM),
            "raw": (like((SLOTS, CHUNK, 3 * HD), F32), VMEM),
            "q": (like(chunks), VMEM),
            "mixed": (like(chunks), VMEM),
            "total": (like((SLOTS, HD, 2 * CHUNK), F32), VMEM),
            "lse": (like((SLOTS, 1, 2 * CHUNK), F32), VMEM),
            "own": (like(block), VMEM),
            "prompt": (like(block), VMEM),
            "before": (like(end), VMEM),
            "w_out": (like((D // SLOTS, D)), VMEM),
            "hidden": (like((CHUNK, D), F32), VMEM),
            "xhat2_b": (like((SLOTS, CHUNK, D)), HBM),
            "gu": (like((D, GU_SLOT)), HBM),
            "down": (like((n, 2, hidden_rows, D)), HBM),
            "dy_b": (like((SLOTS, CHUNK, D)), HBM),
        },
        {
            "kv": pltpu.VMEM(chunks, BF16),
            "own_vt": pltpu.VMEM((HD, 2 * SLOTS * CHUNK), BF16),
            "prompt_vt": pltpu.VMEM((HD, PROMPT), BF16),
            "before_vt": pltpu.VMEM((HD, LONGEST), BF16),
            "part": pltpu.VMEM((SLOTS, CHUNK, D), BF16),
            "land": pltpu.VMEM((7, CHUNK, D), BF16),
            "mine": pltpu.VMEM((CHUNK, D), BF16),
            "out_all": pltpu.VMEM((n, rows, D), BF16),
            "local": DMA((6,)),
            **{name: tok for name in ("s1", "r1", "s2", "r2", "s3", "r3", "s4", "r4")},
            **{name: DMA((7,)) for name in ("qs", "qr", "cs", "cr")},
            **{name: DMA((n, 2, 1)) for name in ("qms", "qmr", "qss", "qsr")},
            **{name: DMA((n, 2, 4)) for name in ("cms", "cmr", "css", "csr")},
            **{name: DMA((n, pieces)) for name in ("hms", "hmr")},
            **{name: DMA((n,)) for name in ("hss", "hsr", "fs", "fr", "hl", "hs", "ps")},
            **{name: DMA(()) for name in ("hts", "htr", "os", "orr", "pr", "bs", "br")},
            "hr": DMA((n, 4)),
            **{name: DMA((3,)) for name in ("ks", "kr")},
        },
    )


def attention_back(at, r, part):
    kv, keys_t, acc = getattr(r, part), getattr(r, part + "_kt"), getattr(r, "acc_" + part)
    keys_t[...] = kv[:, :HD].T
    acc[...] = jnp.zeros_like(acc)
    shift = -LONGEST if part == "before" else 0

    def step(t, dq, q, do, dot_rows, logs, chunk, opening):
        first = t * WIDE
        rows = pl.ds(first if isinstance(first, int) else pl.multiple_of(first, WIDE), WIDE)
        keys, values = kv[rows, :HD], kv[rows, HD:]
        p = jnp.exp2(lax.dot_general(keys, q, NT, preferred_element_type=F32) * SCALE_2 - logs)
        if part != "prompt":
            p = jnp.where(visible(first + shift, chunk, opening, WIDE), p, 0.0)
        dp = lax.dot_general(values, do, NT, preferred_element_type=F32)
        ds = (p * (dp - dot_rows)).astype(BF16)
        acc[rows, :HD] += jnp.dot(ds, q, preferred_element_type=F32)
        acc[rows, HD:] += jnp.dot(p.astype(BF16), do, preferred_element_type=F32)
        return dq + jnp.dot(keys_t[:, rows], ds, preferred_element_type=F32)

    def one(i, carry):
        chunk = 2 * i + at.c
        q, do = two_heads(r.q[i]), two_heads(r.do[i])
        args = (q, do, r.dots[i], r.lse[i] * (1.0 / math.log(2.0)), chunk, r.opening[i])
        if part == "own":
            start, stop = key_range(at.g, chunk, WIDE)
            r.dq_sum[i] = lax.fori_loop(start, stop, lambda t, dq: step(t, dq, *args), r.dq_sum[i])
        else:
            dq = r.dq_sum[i]
            for t in range(kv.shape[0] // WIDE):
                dq = step(t, dq, *args)
            r.dq_sum[i] = dq
        return carry

    lax.fori_loop(0, SLOTS if part != "before" else SLOTS // 2, one, 0)
    out = getattr(r, "d_" + part)
    for t in range(out.shape[0] * 2):
        out[t // 2, t % 2, :, :HD] = (acc[t * CHUNK : (t + 1) * CHUNK, :HD] * SCALE).astype(BF16)
        out[t // 2, t % 2, :, HD:] = acc[t * CHUNK : (t + 1) * CHUNK, HD:].astype(BF16)


def add_chunks(dst, first, other, skip=0):
    def one(i, carry):
        dst[i + skip] = (first(i).astype(F32) + other[i].astype(F32)).astype(BF16)
        return carry

    lax.fori_loop(0, other.shape[0], one, 0)


def kernel(collective_id, body, ins, outs, scratch):
    names = [*ins, *outs, *scratch]
    return dict(
        zip(
            outs,
            communicate(
                lambda *refs: body(types.SimpleNamespace(**dict(zip(names, refs)))),
                collective_id,
                tuple(a for a, _ in ins.values()),
                tuple(a for a, _ in outs.values()),
                list(scratch.values()),
                [spec for _, spec in ins.values()],
                [spec for _, spec in outs.values()],
            ),
        )
    )


def back_block(groups, rows, hidden_rows, ins):
    n = groups

    def body(r):
        at = Place(n)
        group = at.g
        bring_dx = pltpu.make_async_copy(r.part_dx, r.part, r.local.at[3])
        bring_dx.start()
        meet(everyone(at) + [at.diagonal()])
        columns = columns_sum(at, r.g_gu, r.sib_gu, r.mid_gu, r.gu_sum, (r.cms, r.cmr, r.css, r.csr))
        lower = hidden_sum(at, r.g_down, r.d_down, r.sib_d, r.mid_d, r.fin_d, (r.hms, r.hmr, r.hss, r.hsr, r.hts, r.htr, r.local.at[1]))
        next(columns)
        next(lower)
        bring_dx.wait()
        bulk = in_turn((columns, 8 * (n - 1)), (lower, r.mid_d.shape[1] * (n - 1)))
        beside(scatter_tokens(at, r.part, r.land, r.dx, r.s1, r.r1), bulk)
        bring_out = pltpu.make_async_copy(r.part_out, r.part, r.local.at[3])
        bring_out.start()

        def norm(i, carry):
            rows = pl.ds(pl.multiple_of(i * 32, 32), 32)
            value = r.hidden[rows, :]
            inverse = lax.rsqrt(jnp.mean(value * value, 1, keepdims=True) + EPSILON)
            unit = value * inverse
            grad = r.dx[rows, :]
            total = r.cotangent[rows, :] + inverse * (grad - unit * jnp.mean(grad * unit, 1, keepdims=True))
            r.dhidden[rows, :] = total
            r.mine[rows, :] = total.astype(BF16)
            return carry

        lax.fori_loop(0, CHUNK // 32, norm, 0)
        beside(gather_tokens(at, r.mine, r.dbranch, r.local.at[0], r.s2, r.r2), bulk)
        drive(bulk)
        bring_out.wait()
        result = scatter_tokens(at, r.part, r.land2, r.dx, r.s3, r.r3)
        next(result)

        def heads(i, carry):
            do = lax.dot_general(r.dbranch[i], r.w_out[...], NT, preferred_element_type=F32).astype(BF16)
            r.do[i] = do
            r.dots[i] = jnp.sum(two_heads(do).astype(F32).T * r.total[i], 0, keepdims=True)
            r.dq_sum[i] = jnp.zeros((HD, 2 * CHUNK), F32)
            return carry

        lax.fori_loop(0, SLOTS, heads, 0)

        def swap(array, place, i):
            return remote(array.at[:, 1 - at.c], place, r.ks.at[i], r.kr.at[i], at.sibling())

        def home(i):
            return remote(r.land_p, r.far_p.at[i - 1], r.ps, r.pr.at[i - 1], at.mid_at(jnp.int32(0)))

        def back():
            return remote(r.land_b, r.far_b, r.bs, r.br, at.mid_at(group - 1))

        @pl.when(group > 0)
        def _():
            attention_back(at, r, "prompt")
            swap(r.d_prompt, r.land_p, 1).start()

        if n > 2:

            @pl.when(group > 1)
            def _():
                attention_back(at, r, "before")
                swap(r.d_before, r.land_b, 2).start()

        @pl.when(group > 0)
        def _():
            swap(r.d_prompt, r.land_p, 1).wait()
            add_chunks(r.land_p, lambda i: r.d_prompt[i, at.c], r.land_p)
            for i in range(1, n):

                @pl.when(group == i)
                def _():
                    home(i).start()

        if n > 2:

            @pl.when(group > 1)
            def _():
                swap(r.d_before, r.land_b, 2).wait()
                add_chunks(r.land_b, lambda i: r.d_before[i, at.c], r.land_b)
                back().start()

        steps(result, 3)
        attention_back(at, r, "own")
        first = swap(r.d_own, r.land_k, 0)
        first.start()
        steps(result, 3)

        def queries(i, carry):
            r.dq[i] = two_columns((r.dq_sum[i].T * SCALE).astype(BF16))
            return carry

        lax.fori_loop(0, SLOTS, queries, 0)
        drive(columns)
        bring = columns_home(at, r.gu_sum, r.d_gu, r.ds, r.dr, r.local.at[2])
        next(bring)
        first.wait()
        add_chunks(r.dkv, lambda i: r.d_own[i, at.c], r.land_k)
        drive(result)

        def add(i, carry):
            rows = pl.ds(pl.multiple_of(i * 32, 32), 32)
            r.output[rows, :] = (r.hidden[rows, :] + r.dx[rows, :]).astype(BF16)
            return carry

        lax.fori_loop(0, CHUNK // 32, add, 0)

        @pl.when(group == 0)
        def _():
            for i in range(1, n):
                home(i).wait_recv()
                add_chunks(r.dkv, lambda j: r.dkv[j], r.far_p.at[i - 1])

        if n > 2:

            @pl.when((group >= 1) & (group < n - 1))
            def _():
                back().wait_recv()
                add_chunks(r.dkv, lambda j: r.dkv[j + SLOTS // 2], r.far_b, SLOTS // 2)

            @pl.when(group > 1)
            def _():
                back().wait_send()

        @pl.when(group > 0)
        def _():
            home(1).wait_send()

        drive(bring, lower)

    chunks = (SLOTS, CHUNK, 2 * HD)
    block, end = (SLOTS, 2, CHUNK, 2 * HD), (SLOTS // 2, 2, CHUNK, 2 * HD)
    tok = DMA((len(PARTS), 7))
    near, half = pltpu.VMEM(chunks, BF16), pltpu.VMEM((SLOTS // 2, CHUNK, 2 * HD), BF16)
    own, prompt, before = 2 * SLOTS * CHUNK, PROMPT, LONGEST
    far = max(n - 1, 1)
    pieces = max(hidden_rows // 48, 1)
    return kernel(
        2,
        body,
        {name: (a, HBM if name in ("part_dx", "part_out") else VMEM) for name, a in ins.items()},
        {
            "dhidden": (like((CHUNK, D), F32), VMEM),
            "output": (like((CHUNK, D)), VMEM),
            "dbranch": (like((SLOTS, CHUNK, D)), VMEM),
            "dq": (like(chunks), VMEM),
            "dkv": (like(chunks), VMEM),
            "d_gu": (like((SLOTS, rows, GU_SLOT)), HBM),
            "d_down": (like((hidden_rows, D)), HBM),
        },
        {
            "part": pltpu.VMEM((SLOTS, CHUNK, D), BF16),
            "land": pltpu.VMEM((7, CHUNK, D), BF16),
            "land2": pltpu.VMEM((7, CHUNK, D), BF16),
            "mine": pltpu.VMEM((CHUNK, D), BF16),
            "dx": pltpu.VMEM((CHUNK, D), F32),
            "sib_gu": pltpu.VMEM((2, 4 * n * rows, GU_SLOT), BF16),
            "mid_gu": pltpu.VMEM((far, 2, 4, rows, GU_SLOT), BF16),
            "gu_sum": pltpu.VMEM((2, 4, rows, GU_SLOT), BF16),
            "sib_d": pltpu.VMEM((n, hidden_rows, D), BF16),
            "mid_d": pltpu.VMEM((far, pieces, 48, D), BF16),
            "fin_d": pltpu.VMEM((hidden_rows, D), BF16),
            "do": near,
            "dots": pltpu.VMEM((SLOTS, 1, 2 * CHUNK), F32),
            "dq_sum": pltpu.VMEM((SLOTS, HD, 2 * CHUNK), F32),
            "own_kt": pltpu.VMEM((HD, own), BF16),
            "prompt_kt": pltpu.VMEM((HD, prompt), BF16),
            "before_kt": pltpu.VMEM((HD, before), BF16),
            "acc_own": pltpu.VMEM((own, 2 * HD), F32),
            "acc_prompt": pltpu.VMEM((prompt, 2 * HD), F32),
            "acc_before": pltpu.VMEM((before, 2 * HD), F32),
            "d_own": pltpu.VMEM(block, BF16),
            "d_prompt": pltpu.VMEM(block, BF16),
            "d_before": pltpu.VMEM(end, BF16),
            "land_k": near,
            "land_p": near,
            "land_b": half,
            "far_p": pltpu.VMEM((far, *chunks), BF16),
            "far_b": half,
            "local": DMA((4,)),
            **{name: tok for name in ("s1", "r1", "s2", "r2", "s3", "r3")},
            **{name: DMA((n, 2, 4)) for name in ("cms", "cmr")},
            **{name: DMA((2,)) for name in ("css", "csr")},
            **{name: DMA((n, pieces)) for name in ("hms", "hmr")},
            **{name: DMA(()) for name in ("hss", "hsr", "hts", "htr")},
            **{name: DMA((7,)) for name in ("ds", "dr")},
            **{name: DMA((3,)) for name in ("ks", "kr")},
            "ps": DMA(()),
            "pr": DMA((n,)),
            "bs": DMA(()),
            "br": DMA(()),
        },
    )


def rotate(vectors, cosine, sine):
    former, latter = jnp.split(vectors, 2, -1)
    return jnp.concatenate([former * cosine - latter * sine, latter * cosine + former * sine], -1)


def dot(a, b, dims=((1,), (0,))):
    return lax.dot_general(a, b, (dims, ((), ())), preferred_element_type=F32)


def body(tokens, lengths, attn_gain, w_qkv, q_gain, k_gain, w_out, mlp_gain, w_gate_up, w_down, cotangent):
    blocks = lax.axis_size("blk")
    groups = blocks // 4
    rows = w_qkv.shape[0]
    hidden_rows = w_down.shape[0]
    group = lax.axis_index("blk") // 4
    core = lax.axis_index("uly") % 2
    gain_one = attn_gain.astype(F32)[:, None]
    gain_two = mlp_gain.astype(F32)[:, None]

    def by_pair(cols):
        return cols.reshape(rows, 2, 2, 2, -1).transpose(1, 3, 2, 0, 4).reshape(SLOTS, rows, -1)

    scaled = (w_qkv.astype(F32) * gain_one).astype(BF16)
    qkv_mine = jnp.concatenate(
        [
            by_pair(scaled[:, : HQ * HD]),
            by_pair(scaled[:, HQ * HD : (HQ + HK) * HD]),
            by_pair(scaled[:, (HQ + HK) * HD :]),
        ],
        2,
    )
    scaled_gu = (w_gate_up.astype(F32) * gain_two).astype(BF16)
    gu_mine = (
        scaled_gu.reshape(rows, 2, 2, 2, groups, 2, 2 * hidden_rows)
        .transpose(2, 5, 3, 0, 1, 4, 6)
        .reshape(SLOTS, rows, GU_SLOT)
    )
    inputs = tokens.astype(F32)
    xhat = (inputs * lax.rsqrt(jnp.mean(inputs * inputs, 1, keepdims=True) + EPSILON)).astype(BF16)

    starts = PROMPT + jnp.sum(
        jnp.where(jnp.arange(lengths.shape[0])[:, None] > jnp.arange(lengths.shape[0])[None, :], lengths[None, :], 0), 1
    )
    index = (
        group * (2 * SLOTS * CHUNK)
        + (2 * jnp.arange(SLOTS, dtype=jnp.int32)[:, None] + core) * CHUNK
        + jnp.arange(CHUNK, dtype=jnp.int32)[None, :]
    )
    opening = jnp.max(jnp.where(index[..., None] >= starts, starts, 0), -1)
    position = jnp.where(index < PROMPT, index, index - opening + PROMPT)
    opening = opening - group * (2 * SLOTS * CHUNK)
    opening = jnp.concatenate([opening, opening], 1)[:, None, :]
    inverse = ROPE_BASE ** (-2.0 * jnp.arange(HD // 2, dtype=F32) / HD)
    angles = position.astype(F32)[:, :, None] * inverse
    cosine, sine = jnp.cos(angles), jnp.sin(angles)
    head_gain = jnp.stack([q_gain, q_gain, k_gain]).astype(F32)

    front = front_block(
        groups,
        rows,
        hidden_rows,
        {
            "xhat": xhat,
            "tokens": tokens,
            "opening": opening,
            "cosine": jnp.concatenate([cosine, cosine], 2),
            "sine": jnp.concatenate([-sine, sine], 2),
            "head_gain": head_gain,
            "qkv_mine": qkv_mine,
            "gu_mine": gu_mine,
            "down_mine": w_down,
            "out_mine": w_out,
            "dy": cotangent.astype(BF16),
        },
    )
    xhat_b, xhat2_b, dy_b = (front[name].reshape(SLOTS * CHUNK, D) for name in ("xhat_b", "xhat2_b", "dy_b"))
    own, prompt, before = (front[name].reshape(-1, 2 * HD) for name in ("own", "prompt", "before"))
    mixed = front["mixed"].reshape(SLOTS * CHUNK, 2 * HD)
    hidden, out_w, qkv_w, gu_w = front["hidden"], front["w_out"], front["qkv"], front["gu"]
    down_w = front["down"].reshape(FF_SLOT, D)

    both = dot(xhat2_b, gu_w)
    gate, up = both[:, :FF_SLOT], both[:, FF_SLOT:]
    sigmoid = jax.nn.sigmoid(gate)
    act = (gate * sigmoid * up).astype(BF16)
    part_out = dot(act, down_w).astype(BF16)
    g_down = dot(act, dy_b, ((0,), (0,))).astype(BF16)
    dact = dot(dy_b, down_w, ((1,), (1,)))
    dboth = jnp.concatenate(
        [dact * up * sigmoid * (1.0 + gate * (1.0 - sigmoid)), dact * gate * sigmoid], 1
    ).astype(BF16)
    g_gu = dot(xhat2_b, dboth, ((0,), (0,))).astype(BF16)
    part_dx2 = dot(dboth, gu_w, ((1,), (1,))).astype(BF16)
    back = back_block(
        groups,
        rows,
        hidden_rows,
        {
            "part_dx": part_dx2.reshape(SLOTS, CHUNK, D),
            "part_out": part_out.reshape(SLOTS, CHUNK, D),
            "hidden": hidden,
            "cotangent": cotangent,
            "g_gu": g_gu,
            "g_down": g_down.reshape(groups, 2, hidden_rows, D),
            "w_out": out_w,
            "q": front["q"],
            "own": own,
            "prompt": prompt,
            "before": before,
            "opening": opening,
            "total": front["total"],
            "lse": front["lse"],
        },
    )
    output, dhidden = back["output"], back["dhidden"]
    g_out = dot(mixed, back["dbranch"].reshape(SLOTS * CHUNK, D), ((0,), (0,))).astype(BF16)
    dq, dkv = back["dq"], back["dkv"].reshape(SLOTS * CHUNK, 2, HD)
    cosine, sine = cosine.reshape(-1, 1, HD // 2), sine.reshape(-1, 1, HD // 2)

    def shape_heads(heads, gain):
        normed = heads * lax.rsqrt(jnp.mean(heads * heads, -1, keepdims=True) + EPSILON) * gain
        return rotate(normed, cosine, sine)

    _, pullback = jax.vjp(shape_heads, front["raw"].reshape(SLOTS * CHUNK, 3, HD), head_gain[None])
    d_turned = jnp.concatenate([dq.reshape(SLOTS * CHUNK, 2, HD), dkv[:, :1]], 1).astype(F32)
    dqk, d_gain = pullback(d_turned)
    draw = jnp.concatenate([dqk.astype(BF16), dkv[:, 1:]], 1).reshape(SLOTS * CHUNK, QKV_SLOT)
    g_qkv = dot(xhat_b, draw, ((0,), (0,))).astype(BF16)
    part_dx = dot(draw, qkv_w, ((1,), (1,))).astype(BF16)
    gains = jnp.concatenate([(d_gain[0, 0] + d_gain[0, 1])[None], d_gain[0, 2][None], jnp.zeros((6, HD), F32)], 0)
    d_tokens, qkv_back, d_w_out, gain_sum = finish_layer(
        groups, part_dx.reshape(SLOTS, CHUNK, D), tokens, dhidden, g_qkv, g_out, gains, rows
    )

    def from_pair(cols):
        return cols.reshape(2, 2, 2, rows, -1).transpose(3, 0, 2, 1, 4).reshape(rows, -1)

    raw_qkv = lax.optimization_barrier(
        jnp.concatenate(
            [
                from_pair(qkv_back[:, :, : 2 * HD]),
                from_pair(qkv_back[:, :, 2 * HD : 3 * HD]),
                from_pair(qkv_back[:, :, 3 * HD :]),
            ],
            1,
        )
    ).astype(F32)
    raw_gu = lax.optimization_barrier(
        back["d_gu"]
        .reshape(2, 2, 2, rows, 2, groups, 2 * hidden_rows)
        .transpose(3, 4, 0, 2, 5, 1, 6)
        .reshape(rows, 2 * FF)
    ).astype(F32)
    return (
        output,
        d_tokens,
        jnp.sum(raw_qkv * w_qkv.astype(F32), 1),
        raw_qkv * gain_one,
        gain_sum[0],
        gain_sum[1],
        d_w_out.astype(F32),
        jnp.sum(raw_gu * w_gate_up.astype(F32), 1),
        raw_gu * gain_two,
        back["d_down"].astype(F32),
    )


def solution(mesh):
    tokens = P(("blk", "uly"), None)
    weight = P(("uly", "blk"), None)
    gain = P(("uly", "blk"))
    return jax.shard_map(
        body,
        mesh=mesh,
        in_specs=(tokens, P(), gain, weight, P(), P(), weight, gain, weight, weight, tokens),
        out_specs=(tokens, tokens, gain, weight, P(), P(), weight, gain, weight, weight),
        check_vma=False,
    )
```

```python
import math
import types

import jax
import jax.numpy as jnp
import numpy as np
from jax import lax
from jax.experimental import pallas as pl
from jax.experimental.pallas import tpu as pltpu
from jax.sharding import PartitionSpec as P

D = 2048
HQ = 16
HK = 8
HD = 128
FF = 6144
PROMPT = 2048
LONGEST = 1024

SLOTS = 8
CHUNK = 128
QKV_SLOT = 512
GU_SLOT = 2 * FF // SLOTS
FF_SLOT = FF // SLOTS
EPSILON = 1e-06
ROPE_BASE = 1000000.0
SCALE = 1.0 / math.sqrt(HD)

F32 = jnp.float32
BF16 = jnp.bfloat16
MESH = pl.DeviceIdType.MESH
HBM = pl.BlockSpec(memory_space=pl.ANY)
VMEM = pl.BlockSpec(memory_space=pltpu.VMEM)
DMA = pltpu.SemaphoreType.DMA
PARTS = ((0, 1, 2), 256), ((1, 2, 0), 768), ((2, 0, 1), 1024)


def rem(a, n):
    return lax.rem(a, jnp.int32(n))


class Place:
    def __init__(self, groups):
        self.groups = groups
        self.u = lax.axis_index("uly")
        self.b = lax.axis_index("blk")
        self.x = self.u // 2
        self.c = rem(self.u, 2)
        self.g = self.b // 4
        self.bl = rem(self.b, 4)
        self.bits = (self.x, rem(self.bl, 2), self.bl // 2)

    def flip(self, *dims):
        x, y, z = (rem(v + 1, 2) if d in dims else v for d, v in enumerate(self.bits))
        return x, 2 * z + y

    def coords(self, *dims):
        return [rem(v + 1, 2) if d in dims else v for d, v in enumerate(self.bits)]

    def chunk(self, *dims):
        x, bl = self.flip(*dims)
        return 2 * bl + x

    def slot(self, *dims):
        x, bl = self.flip(*dims)
        return 4 * x + bl

    def cube(self, *dims):
        x, bl = self.flip(*dims)
        return (2 * x + self.c, 4 * self.g + bl)

    def sibling(self):
        return (2 * self.x + 1 - self.c, self.b)

    def ahead(self, i):
        return rem(self.g + i, self.groups)

    def behind(self, i):
        return rem(self.g + self.groups - i, self.groups)

    def mid(self, i):
        return (self.u, 4 * self.ahead(i) + self.bl)

    def diagonal(self):
        x, y, z = self.bits
        return (2 * x + 1 - self.c, 4 * self.g + 2 * z + 1 - y)

    def mid_at(self, group):
        return (self.u, 4 * group + self.bl)


PEERS = ((0,), (1,), (2,), (0, 1), (0, 2), (1, 2), (0, 1, 2))


def meet(devices):
    barrier = pltpu.get_barrier_semaphore()
    for device in devices:
        pl.semaphore_signal(barrier, inc=1, device_id=device, device_id_type=MESH)
    pl.semaphore_wait(barrier, len(devices))


def remote(src, dst, send, recv, device):
    return pltpu.make_async_remote_copy(
        src_ref=src, dst_ref=dst, send_sem=send, recv_sem=recv, device_id=device, device_id_type=MESH
    )


def rows_at(start, count):
    return pl.ds(pl.multiple_of(start, 16), count)


def drive(*tasks):
    tasks = list(tasks)
    while tasks:
        tasks = [task for task in tasks if next(task, None) is not None]


def steps(task, count):
    for _ in range(count):
        next(task, None)


def paced(loop, count, between, when=None):
    def one(i, carry):
        loop(i)
        return carry

    for k in range(4):
        run = (k * count // 4, (k + 1) * count // 4)
        if when is None:
            lax.fori_loop(*run, one, 0)
        else:

            @pl.when(when)
            def _():
                lax.fori_loop(*run, one, 0)

        between()


def piece_rows(rows):
    return 32 if rows % 32 == 0 else 16


def beside(main, *bulk):
    for _ in main:
        for task in bulk:
            next(task, None)


def in_turn(*tasks):
    for task, count in tasks:
        for _ in range(count):
            next(task, None)
            yield True


def part_columns():
    start = 0
    for p, (order, width) in enumerate(PARTS):
        yield p, order, pl.ds(start, width)
        start += width


def gather_tokens(at, mine, block, local, send, recv):
    own = pltpu.make_async_copy(mine, block.at[at.chunk()], local)
    own.start()
    sent = []

    def push(p, i, dims, along, cols):
        src = block.at[at.chunk(*dims), :, cols] if dims else mine.at[:, cols]
        copy = remote(src, block.at[at.chunk(*dims), :, cols], send.at[p, i], recv.at[p, i], at.cube(along))
        copy.start()
        sent.append(copy)

    def arrive(p, i, dims, cols):
        there = block.at[at.chunk(*dims), :, cols]
        remote(there, there, send.at[p, i], recv.at[p, i], at.cube(dims[0])).wait_recv()

    parts = list(part_columns())
    over = [sorted(parts, key=lambda part: part[1][k] == 2) for k in range(3)]
    for p, (a, b, c), cols in parts:
        push(p, 0, (), a, cols)
        push(p, 1, (), b, cols)
        push(p, 2, (), c, cols)
    yield True
    for p, (a, b, c), cols in over[0]:
        arrive(p, 0, (a,), cols)
        push(p, 3, (a,), b, cols)
        push(p, 4, (a,), c, cols)
        yield True
    for p, (a, b, c), cols in over[1]:
        arrive(p, 1, (b,), cols)
        push(p, 5, (b,), c, cols)
        arrive(p, 3, (a, b), cols)
        push(p, 6, (a, b), c, cols)
        yield True
    for p, (a, b, c), cols in parts:
        arrive(p, 2, (c,), cols)
        arrive(p, 4, (a, c), cols)
        arrive(p, 5, (b, c), cols)
        arrive(p, 6, (a, b, c), cols)
    for copy in sent:
        copy.wait_send()
    own.wait()


def add_rows(dst, terms, count, step=32):
    def body(i, carry):
        rows = pl.ds(pl.multiple_of(i * step, step), step)
        total = terms[0][rows, :].astype(F32)
        for term in terms[1:]:
            total = total + term[rows, :].astype(F32)
        dst[rows, :] = total.astype(dst.dtype)
        return carry

    lax.fori_loop(0, count // step, body, 0)


def scatter_tokens(at, part, land, out, send, recv):
    sent = []

    def push(p, i, dims, along, cols):
        copy = remote(part.at[at.chunk(*dims), :, cols], land.at[i, :, cols], send.at[p, i], recv.at[p, i], at.cube(along))
        copy.start()
        sent.append(copy)

    def arrive(p, i, along, cols):
        remote(land.at[i, :, cols], land.at[i, :, cols], send.at[p, i], recv.at[p, i], at.cube(along)).wait_recv()

    def add(i, dims, cols):
        here = part.at[at.chunk(*dims), :, cols]
        add_rows(here, [here, land.at[i, :, cols]], CHUNK)

    parts = list(part_columns())
    over = [sorted(parts, key=lambda part: part[1][k] == 2) for k in range(3)]
    for p, (a, b, c), cols in parts:
        push(p, 3, (a, b, c), c, cols)
        push(p, 2, (b, c), c, cols)
    for p, (a, b, c), cols in parts:
        push(p, 1, (a, c), c, cols)
        push(p, 0, (c,), c, cols)
    yield True
    for p, (a, b, c), cols in over[2]:
        arrive(p, 3, c, cols)
        add(3, (a, b), cols)
        push(p, 5, (a, b), b, cols)
        arrive(p, 2, c, cols)
        add(2, (b,), cols)
        push(p, 4, (b,), b, cols)
        yield True
    for p, (a, b, c), cols in over[1]:
        arrive(p, 1, c, cols)
        add(1, (a,), cols)
        arrive(p, 5, b, cols)
        add(5, (a,), cols)
        push(p, 6, (a,), a, cols)
        yield True
    for p, (a, b, c), cols in over[0]:
        arrive(p, 0, c, cols)
        arrive(p, 4, b, cols)
        arrive(p, 6, a, cols)
        add_rows(
            out.at[:, cols],
            [part.at[at.chunk(), :, cols], land.at[0, :, cols], land.at[4, :, cols], land.at[6, :, cols]],
            CHUNK,
        )
    for copy in sent:
        copy.wait_send()


def column_row(at, rows, u, b):
    return (u * (4 * at.groups) + b) * rows


class Columns:
    def qkv(x, y, z):
        pair = 4 * x + 2 * y + z
        return [(pair * (2 * HD), 2 * HD), (HQ * HD + pair * HD, HD), ((HQ + HK) * HD + pair * HD, HD)]

    def gate_up(groups, hidden_rows):
        wide = 2 * hidden_rows
        if wide % 128:
            return lambda x, y, z: [((4 * x + 2 * z + y) * GU_SLOT, GU_SLOT)]

        def runs(x, y, z):
            return [
                (half * FF + (((2 * x + y) * groups + group) * 2 + z) * wide, wide)
                for half in range(2)
                for group in range(groups)
            ]

        return runs


def column_runs(ref, whole, runs):
    at = 0
    for first, width in runs:
        yield ref.at[:, pl.ds(pl.multiple_of(first, 128), width)], whole.at[:, pl.ds(at, width)]
        at += width


def columns_in_cube(at, mine, whole, runs, local, send, recv, rows):
    own = rows_at(column_row(at, rows, at.u, at.b), rows)
    here = []
    for k, (src, dst) in enumerate(column_runs(mine, whole.at[own], runs(*at.coords()))):
        here.append(pltpu.make_async_copy(src, dst, local.at[k]))
        here[-1].start()
    sent = []
    for i, dims in enumerate(PEERS):
        for k, (src, dst) in enumerate(column_runs(mine, whole.at[own], runs(*at.coords(*dims)))):
            copy = remote(src, dst, send.at[i, k], recv.at[i, k], at.cube(*dims))
            copy.start()
            sent.append(copy)
    yield True
    for i, dims in enumerate(PEERS):
        u, b = at.cube(*dims)
        there = whole.at[rows_at(column_row(at, rows, u, b), rows)]
        for k, (_, dst) in enumerate(column_runs(mine, there, runs(*at.coords()))):
            remote(dst, dst, send.at[i, k], recv.at[i, k], (u, b)).wait_recv()
    for copy in sent:
        copy.wait_send()
    for copy in here:
        copy.wait()


def columns_across(at, whole, rows, mid_send, mid_recv, sib_send, sib_recv):
    n, pieces = at.groups, mid_send.shape[2]
    step = 4 * rows // pieces
    sent = []

    def piece(core, group, x, k):
        return whole.at[rows_at(column_row(at, rows, 2 * x + core, 4 * group) + k * step, step)]

    def pass_on(i, x, k):
        there = piece(at.c, at.behind(i), x, k)
        copy = remote(there, there, sib_send.at[i, x, k], sib_recv.at[i, x, k], at.sibling())
        copy.start()
        sent.append(copy)

    order = [(x, k) for x in range(2) for k in range(pieces)]
    for i in range(1, n):
        for x, k in order:
            there = piece(at.c, at.g, x, k)
            copy = remote(there, there, mid_send.at[i, x, k], mid_recv.at[i, x, k], at.mid(i))
            copy.start()
            sent.append(copy)
            if i == 1:
                pass_on(0, x, k)
            yield True
    for i in range(1, n):
        for x, k in order:
            there = piece(at.c, at.behind(i), x, k)
            remote(there, there, mid_send.at[i, x, k], mid_recv.at[i, x, k], at.mid(i)).wait_recv()
            pass_on(i, x, k)
    for i in range(n):
        for x, k in order:
            there = piece(1 - at.c, at.behind(i), x, k)
            remote(there, there, sib_send.at[i, x, k], sib_recv.at[i, x, k], at.sibling()).wait_recv()
    for copy in sent:
        copy.wait_send()


def gather_hidden(at, mine, whole, local, turn_send, turn_recv, mid_send, mid_recv, sib_send, sib_recv):
    n, rows, pieces = at.groups, mine.shape[0], mid_send.shape[1]
    step = rows // pieces
    own = whole.at[at.g, at.c]
    stays = at.bits[1] == at.c
    here = pltpu.make_async_copy(mine, own, local)
    there = remote(mine, whole.at[at.g, 1 - at.c], turn_send, turn_recv, at.diagonal())

    @pl.when(stays)
    def _():
        here.start()

    @pl.when(jnp.logical_not(stays))
    def _():
        there.start()

    yield True

    @pl.when(stays)
    def _():
        here.wait()

    @pl.when(jnp.logical_not(stays))
    def _():
        there.wait()

    sent = []
    for i in range(1, n):
        for k in range(pieces):
            piece = own.at[pl.ds(k * step, step)]
            copy = remote(piece, piece, mid_send.at[i, k], mid_recv.at[i, k], at.mid(i))
            copy.start()
            sent.append(copy)
            yield True

    def pass_on(i):
        group = whole.at[at.behind(i), at.c]
        copy = remote(group, group, sib_send.at[i], sib_recv.at[i], at.sibling())
        copy.start()
        sent.append(copy)

    pass_on(0)
    for i in range(1, n):
        for k in range(pieces):
            piece = whole.at[at.behind(i), at.c, pl.ds(k * step, step)]
            remote(piece, piece, mid_send.at[i, k], mid_recv.at[i, k], at.mid(i)).wait_recv()
        pass_on(i)
    for i in range(n):
        group = whole.at[at.behind(i), 1 - at.c]
        remote(group, group, sib_send.at[i], sib_recv.at[i], at.sibling()).wait_recv()
    for copy in sent:
        copy.wait_send()


class OutRows:
    def __init__(self, at, rows):
        self.at, self.rows = at, rows
        self.per_half = max(at.groups // 2, 1)
        self.my_half = at.g // self.per_half
        self.to = 2 * self.my_half + at.c
        self.collects = at.bl == self.to
        self.slot_core = rem(at.bl, 2) == at.c
        self.slot_half = at.bl // 2

    def group_rows(self, group, half):
        return rows_at((group - half * self.per_half) * (4 * self.rows), 4 * self.rows)

    def in_half(self, group, half):
        return group // self.per_half == half

    def device(self, bl):
        return (self.at.u, 4 * self.at.g + bl)


def gather_heads(at, mine, whole, local, send, recv, sib_send, sib_recv):
    n, rows = mine.shape[0], mine.shape[1]
    lay = OutRows(at, rows)

    def place(group, bl):
        half = group // lay.per_half
        return whole.at[rows_at(((group - half * lay.per_half) * 4 + bl) * rows, rows)]

    def push(i):
        group = at.behind(i)
        to = 2 * (group // lay.per_half) + at.c
        here = pltpu.make_async_copy(mine.at[i], place(group, at.bl), local.at[i])
        there = remote(mine.at[i], place(group, at.bl), send.at[i], recv.at[i, at.bl], lay.device(to))
        return at.bl == to, here, there

    for i in range(n):
        stays, here, there = push(i)

        @pl.when(stays)
        def _():
            here.start()

        @pl.when(jnp.logical_not(stays))
        def _():
            there.start()

    yield True

    @pl.when(lay.slot_core)
    def _():
        for i in range(n):
            group = at.behind(i)

            @pl.when(lay.in_half(group, lay.slot_half))
            def _():
                pltpu.make_async_copy(mine.at[i], place(group, at.bl), local.at[i]).wait()
                for bl in range(4):

                    @pl.when(at.bl != bl)
                    def _():
                        there = place(group, bl)
                        remote(there, there, send.at[i], recv.at[i, bl], lay.device(bl)).wait_recv()

        remote(whole, whole, sib_send, sib_recv, at.sibling()).start()

    yield True

    @pl.when(lay.slot_core)
    def _():
        remote(whole, whole, sib_send, sib_recv, at.sibling()).wait_send()

    @pl.when(jnp.logical_not(lay.slot_core))
    def _():
        remote(whole, whole, sib_send, sib_recv, at.sibling()).wait_recv()

    for i in range(n):
        stays, here, there = push(i)

        @pl.when(jnp.logical_not(stays))
        def _():
            there.wait_send()


def columns_home(at, final, out, runs, send, recv, local):
    sent = []
    for i, dims in enumerate(PEERS):
        x, bl = at.flip(*dims)
        for k, (dst, src) in enumerate(column_runs(out, final.at[x, bl], runs(*at.coords()))):
            copy = remote(src, dst, send.at[i, k], recv.at[i, k], at.cube(*dims))
            copy.start()
            sent.append(copy)
    here = []
    for k, (dst, src) in enumerate(column_runs(out, final.at[at.x, at.bl], runs(*at.coords()))):
        here.append(pltpu.make_async_copy(src, dst, local.at[k]))
        here[-1].start()
    yield True
    for i, dims in enumerate(PEERS):
        for k, (there, _) in enumerate(column_runs(out, final.at[at.x, at.bl], runs(*at.coords(*dims)))):
            remote(there, there, send.at[i, k], recv.at[i, k], at.cube(*dims)).wait_recv()
    for copy in sent:
        copy.wait_send()
    for copy in here:
        copy.wait()


def columns_sum(at, part, sib_land, mid_land, final, sems, at_once=1):
    n, rows = at.groups, final.shape[2]
    mid_send, mid_recv, sib_send, sib_recv = sems
    run, deep = 4 * rows, 4 * n * rows
    step = piece_rows(rows)
    pieces = [(k, j) for k in range(4) for j in range(rows // step)]
    sent = []

    def of_core(x, core):
        return part.at[rows_at((2 * x + core) * deep, deep)]

    for x in range(2):
        copy = remote(of_core(x, 1 - at.c), sib_land.at[x], sib_send.at[x], sib_recv.at[x], at.sibling())
        copy.start()
        sent.append(copy)
    yield True
    for x in range(2):
        remote(sib_land.at[x], sib_land.at[x], sib_send.at[x], sib_recv.at[x], at.sibling()).wait_recv()
        for i in range(1, n):
            for m, (k, j) in enumerate(pieces):
                offset = at.ahead(i) * run + k * rows + j * step
                there = part.at[rows_at((2 * x + at.c) * deep + offset, step)]
                add_rows(there, [there, sib_land.at[x, rows_at(offset, step)]], step, 16)
                land = mid_land.at[i - 1, x, k, pl.ds(j * step, step)]
                copy = remote(there, land, mid_send.at[i, x, m], mid_recv.at[i, x, m], at.mid(i))
                copy.start()
                sent.append(copy)
                if m % at_once == at_once - 1:
                    yield True
    for x in range(2):
        for m, (k, j) in enumerate(pieces):
            for i in range(1, n):
                there = mid_land.at[i - 1, x, k, pl.ds(j * step, step)]
                remote(there, there, mid_send.at[i, x, m], mid_recv.at[i, x, m], at.mid(i)).wait_recv()
            offset = at.g * run + k * rows + j * step
            rows_here = pl.ds(j * step, step)
            add_rows(
                final.at[x, k, rows_here],
                [part.at[rows_at((2 * x + at.c) * deep + offset, step)], sib_land.at[x, rows_at(offset, step)]]
                + [mid_land.at[i - 1, x, k, rows_here] for i in range(1, n)],
                step,
                16,
            )
    for copy in sent:
        copy.wait_send()


def hidden_sum(at, part, out, sib_land, mid_land, final, sems):
    n, rows = at.groups, out.shape[0]
    pieces, step = mid_land.shape[1], mid_land.shape[2]
    mid_send, mid_recv, sib_send, sib_recv, turn_send, turn_recv, local = sems
    across = remote(part.at[:, 1 - at.c], sib_land, sib_send, sib_recv, at.sibling())
    across.start()
    yield True
    across.wait()
    sent = []
    for i in range(1, n):
        group = at.ahead(i)
        for k in range(pieces):
            at_k = pl.ds(k * step, step)
            there = part.at[group, at.c, at_k]
            add_rows(there, [there, sib_land.at[group, at_k]], step, 16)
            copy = remote(there, mid_land.at[i - 1, k], mid_send.at[i, k], mid_recv.at[i, k], at.mid(i))
            copy.start()
            sent.append(copy)
            yield True
    for copy in sent:
        copy.wait()
    for k in range(pieces):
        at_k = pl.ds(k * step, step)
        add_rows(
            final.at[at_k],
            [part.at[at.g, at.c, at_k], sib_land.at[at.g, at_k]] + [mid_land.at[i - 1, k] for i in range(1, n)],
            step,
            16,
        )
    stays = at.bits[1] == at.c
    here = pltpu.make_async_copy(final, out, local)
    there = remote(final, out, turn_send, turn_recv, at.diagonal())

    @pl.when(stays)
    def _():
        here.start()

    @pl.when(jnp.logical_not(stays))
    def _():
        there.start()

    yield True

    @pl.when(stays)
    def _():
        here.wait()

    @pl.when(jnp.logical_not(stays))
    def _():
        there.wait()


def scatter_heads(at, part, out, sib_land, mid_land, sems):
    n, rows = at.groups, out.shape[0]
    send, recv, mid_send, mid_recv, sib_send, sib_recv, local = sems
    lay = OutRows(at, rows)

    @pl.when(jnp.logical_not(lay.slot_core))
    def _():
        remote(part, sib_land, sib_send, sib_recv, at.sibling()).start()

    yield True

    @pl.when(lay.slot_core)
    def _():
        remote(part, sib_land, sib_send, sib_recv, at.sibling()).wait_recv()
        add_rows(part, [part, sib_land], 256, 16)
        for i in range(1, n):
            group = at.ahead(i)

            @pl.when(lay.in_half(group, lay.slot_half))
            def _():
                there = part.at[lay.group_rows(group, lay.slot_half)]
                remote(there, mid_land.at[i - 1], mid_send.at[i], mid_recv.at[i], at.mid(i)).start()

    yield True
    mine = part.at[lay.group_rows(at.g, lay.my_half)]
    base = (at.g - lay.my_half * lay.per_half) * (4 * rows)

    @pl.when(lay.collects)
    def _():
        for i in range(1, n):
            remote(mine, mid_land.at[i - 1], mid_send.at[i], mid_recv.at[i], at.mid(i)).wait_recv()
        add_rows(mine, [mine] + [mid_land.at[i - 1] for i in range(1, n)], 4 * rows, 16)
        for bl in range(4):
            there = part.at[rows_at(base + bl * rows, rows)]

            @pl.when(at.bl != bl)
            def _():
                remote(there, out, send.at[bl], recv, lay.device(bl)).start()

            @pl.when(at.bl == bl)
            def _():
                pltpu.make_async_copy(there, out, local).start()

    yield True

    @pl.when(jnp.logical_not(lay.collects))
    def _():
        remote(out, out, send.at[0], recv, lay.device(lay.to)).wait_recv()

    @pl.when(lay.collects)
    def _():
        for bl in range(4):
            there = part.at[rows_at(base + bl * rows, rows)]

            @pl.when(at.bl != bl)
            def _():
                remote(there, out, send.at[bl], recv, lay.device(bl)).wait_send()

            @pl.when(at.bl == bl)
            def _():
                pltpu.make_async_copy(there, out, local).wait()

    @pl.when(jnp.logical_not(lay.slot_core))
    def _():
        remote(part, sib_land, sib_send, sib_recv, at.sibling()).wait_send()

    @pl.when(lay.slot_core)
    def _():
        for i in range(1, n):
            group = at.ahead(i)

            @pl.when(lay.in_half(group, lay.slot_half))
            def _():
                there = part.at[lay.group_rows(group, lay.slot_half)]
                remote(there, mid_land.at[i - 1], mid_send.at[i], mid_recv.at[i], at.mid(i)).wait_send()


def sum_everywhere(at, mine, land, send, recv):
    for i, device in enumerate([at.sibling(), at.cube(0), at.cube(1), at.cube(2)]):
        copy = remote(mine, land.at[i], send.at[i], recv.at[i], device)
        copy.start()
        yield True
        copy.wait()
        mine[...] = mine[...] + land[i]
    sent = []
    for i in range(1, at.groups):
        copy = remote(mine, land.at[3 + i], send.at[3 + i], recv.at[3 + i], at.mid(i))
        copy.start()
        sent.append(copy)
    yield True
    for copy in sent:
        copy.wait()
    for i in range(1, at.groups):
        mine[...] = mine[...] + land[3 + i]


def everyone(at):
    return [at.cube(*dims) for dims in PEERS] + [at.sibling()] + [at.mid(i) for i in range(1, at.groups)]


def cube_only(at):
    return [at.cube(*dims) for dims in ((0,), (1,), (2,))]


def communicate(body, collective_id, ins, outs, scratch, in_specs, out_specs, limit=60):
    return pl.pallas_call(
        body,
        out_shape=outs,
        in_specs=in_specs,
        out_specs=out_specs,
        scratch_shapes=scratch,
        compiler_params=pltpu.CompilerParams(
            collective_id=collective_id, has_side_effects=True, vmem_limit_bytes=limit << 20
        ),
    )(*ins)


def like(shape, dtype=BF16):
    return jax.ShapeDtypeStruct(shape, dtype)


NT = (((1,), (1,)), ((), ()))
WIDE = 512
SCALE_2 = SCALE / math.log(2.0)


def visible(first_key, chunk_of_block, opening, tile):
    key = first_key + lax.broadcasted_iota(jnp.int32, (tile, 2 * CHUNK), 0)
    lane = lax.broadcasted_iota(jnp.int32, (1, 2 * CHUNK), 1)
    row = chunk_of_block * CHUNK + jnp.where(lane >= CHUNK, lane - CHUNK, lane)
    return (key <= row) & (key >= opening)


def key_range(group, chunk_of_block, tile):
    stop = (chunk_of_block * CHUNK + CHUNK + tile - 1) // tile
    start = jnp.where(group > 0, jnp.maximum(chunk_of_block * CHUNK - LONGEST, 0) // tile, 0)
    return start, stop


def two_heads(block):
    return jnp.concatenate([block[:, :HD], block[:, HD:]], 0)


def two_columns(block):
    return jnp.concatenate([block[:CHUNK], block[CHUNK:]], 1)


def turn_values(kv, turned):
    for t in range(kv.shape[0]):
        turned[:, pl.ds(2 * CHUNK * t, 2 * CHUNK)] = kv[t].reshape(2 * CHUNK, 2 * HD)[:, HD:].T


def front_block(groups, rows, hidden_rows, ins):
    n = groups
    gate_up = Columns.gate_up(groups, hidden_rows)
    count = len(gate_up(0, 0, 0))
    pieces = hidden_rows // piece_rows(hidden_rows)
    gu_pieces = 4 * rows // piece_rows(4 * rows)

    def body(r):
        at = Place(n)
        group, core = at.g, at.c

        def first_norm(i, carry):
            rows_i = pl.ds(pl.multiple_of(i * 32, 32), 32)
            value = r.tokens[rows_i, :].astype(F32)
            r.xhat[rows_i, :] = (value * lax.rsqrt(jnp.mean(value * value, 1, keepdims=True) + EPSILON)).astype(BF16)
            return carry

        lax.fori_loop(0, CHUNK // 32, first_norm, 0)
        r.qkv_mine[...] = (r.w_qkv[...].astype(F32) * r.gain_one[...]).astype(BF16)
        meet(everyone(at) + [at.diagonal()])
        wide = columns_in_cube(at, r.qkv_mine, r.qkv, Columns.qkv, r.qkv_local, r.qs, r.qr, rows)
        next(wide)
        tokens = gather_tokens(at, r.xhat, r.xhat_b, r.local.at[1], r.s1, r.r1)
        next(tokens)
        lower = gather_hidden(at, r.down_mine, r.down, r.local.at[2], r.hts, r.htr, r.hms, r.hmr, r.hss, r.hsr)
        next(lower)
        out_here = pltpu.make_async_copy(r.out_mine, r.out_all.at[0], r.local.at[3])
        out_here.start()

        def scale(i, carry):
            cols = pl.ds(pl.multiple_of(i * 1024, 1024), 1024)
            r.gu_mine[:, cols] = (r.w_gu[:, cols].astype(F32) * r.gain_two[...]).astype(BF16)
            return carry

        lax.fori_loop(0, 2 * FF // 1024, scale, 0)

        def round_dy(i, carry):
            rows_i = pl.ds(pl.multiple_of(i * 32, 32), 32)
            r.dy[rows_i, :] = r.cotangent[rows_i, :].astype(BF16)
            return carry

        lax.fori_loop(0, CHUNK // 32, round_dy, 0)
        steps(tokens, 3)
        drive(wide)
        wide = columns_across(at, r.qkv, rows, r.qms, r.qmr, r.qss, r.qsr)
        steps(wide, 2 * (n - 1))
        steps(tokens, 3)
        columns = columns_in_cube(at, r.gu_mine, r.gu, gate_up, r.gu_local, r.cs, r.cr, rows)
        next(columns)
        far = [remote(r.out_mine, r.out_all.at[i], r.fs.at[i], r.fr.at[i], at.mid(i)) for i in range(1, n)]
        for copy in far:
            copy.start()
        steps(lower, 1)
        drive(tokens)
        drive(wide)

        def project_in(i):
            four = pl.ds(pl.multiple_of(4 * i, 4), 4)
            raw = jnp.dot(r.xhat_b[four].reshape(4 * CHUNK, D), r.qkv[...], preferred_element_type=F32)
            cosine, sine = r.cosine[four].reshape(4 * CHUNK, HD), r.sine[four].reshape(4 * CHUNK, HD)
            heads = []
            for h in range(3):
                head = raw[:, h * HD : (h + 1) * HD]
                gain = r.head_gain[h : h + 1, :]
                normed = head * lax.rsqrt(jnp.mean(head * head, 1, keepdims=True) + EPSILON) * gain
                heads.append((normed * cosine + pltpu.roll(normed, HD // 2, 1) * sine).astype(BF16))
            r.raw[four] = raw[:, : 3 * HD].reshape(4, CHUNK, 3 * HD)
            r.q[four] = jnp.concatenate(heads[:2], 1).reshape(4, CHUNK, 2 * HD)
            r.kv[four] = jnp.concatenate([heads[2], raw[:, 3 * HD :].astype(BF16)], 1).reshape(4, CHUNK, 2 * HD)

        for i in range(2):
            lax.fori_loop(i, i + 1, lambda i, carry: (project_in(i), carry)[1], 0)

        here = pltpu.make_async_copy(r.kv, r.own.at[:, core], r.local.at[1])
        here.start()
        sib = remote(r.kv, r.own.at[:, core], r.ks.at[0], r.kr.at[0], at.sibling())
        sib.start()

        def to_group(i):
            return remote(r.kv, r.prompt.at[:, core], r.ps.at[i], r.pr, at.mid_at(jnp.int32(i)))

        def forward():
            half = r.kv.at[pl.ds(SLOTS // 2, SLOTS // 2)]
            return remote(half, r.before.at[:, core], r.bs, r.br, at.mid_at(group + 1))

        def across(ref, i):
            return remote(ref.at[:, core], ref.at[:, core], r.ks.at[i], r.kr.at[i], at.sibling())

        @pl.when(group == 0)
        def _():
            for i in range(1, n):
                to_group(i).start()

        if n > 2:

            @pl.when((group >= 1) & (group < n - 1))
            def _():
                forward().start()

        out_here.wait()
        for copy in far:
            copy.wait()
        heads = gather_heads(at, r.out_all, r.w_out, r.hl, r.hs, r.hr, r.os, r.orr)
        next(heads)
        here.wait()
        sib.wait()
        turn_values(r.own, r.own_vt)
        drive(columns)
        columns = columns_across(at, r.gu, rows, r.cms, r.cmr, r.css, r.csr)
        bulk = in_turn((lower, pieces * (n - 1) - 1), (columns, 2 * gu_pieces * (n - 1)))
        steps(bulk, 1)
        dy = gather_tokens(at, r.dy, r.dy_b, r.local.at[0], r.s3, r.r3)
        next(dy)

        def step(kv, values_t, tile, chunk, q, opening, carry, masked, shift=0):
            norm, out = carry
            first = tile * WIDE
            parts = []
            for k in range(WIDE // CHUNK):
                keys = kv[tile * (WIDE // (2 * CHUNK)) + k // 2, k % 2][:, :HD]
                p = jnp.exp2(lax.dot_general(keys, q, NT, preferred_element_type=F32) * SCALE_2)
                if masked:
                    p = jnp.where(visible(first + shift + k * CHUNK, chunk, opening, CHUNK), p, 0.0)
                norm = norm + jnp.sum(p, 0, keepdims=True)
                parts.append(p.astype(BF16))
            first = first if isinstance(first, int) else pl.multiple_of(first, WIDE)
            out = out + jnp.dot(
                values_t[:, pl.ds(first, WIDE)], jnp.concatenate(parts, 0), preferred_element_type=F32
            )
            return norm, out

        def own_part(i):
            chunk = 2 * i + core
            query, opening = two_heads(r.q[i]), r.opening[i]
            start, stop = key_range(group, chunk, WIDE)
            zero = (jnp.zeros((1, 2 * CHUNK), F32), jnp.zeros((HD, 2 * CHUNK), F32))
            norm, out = lax.fori_loop(
                start, stop, lambda t, c: step(r.own, r.own_vt, t, chunk, query, opening, c, True), zero
            )
            r.lse[i] = norm
            r.total[i] = out

        paced(own_part, SLOTS, lambda: steps(bulk, 1))
        next(heads)

        @pl.when(group > 0)
        def _():
            to_group(0).wait_recv()
            across(r.prompt, 1).start()

        if n > 2:

            @pl.when(group > 1)
            def _():
                forward().wait_recv()
                across(r.before, 2).start()

        steps(dy, 3)
        steps(bulk, 1)

        @pl.when(group > 0)
        def _():
            across(r.prompt, 1).wait()
            turn_values(r.prompt, r.prompt_vt)

        def prompt_part(i):
            query = two_heads(r.q[i])
            state = (r.lse[i], r.total[i])
            for t in range(PROMPT // WIDE):
                state = step(r.prompt, r.prompt_vt, t, 0, query, None, state, False)
            r.lse[i], r.total[i] = state

        paced(prompt_part, SLOTS, lambda: steps(bulk, 1), group > 0)

        if n > 2:

            @pl.when(group > 1)
            def _():
                across(r.before, 2).wait()
                turn_values(r.before, r.before_vt)

                def before_part(i, carry):
                    query, opening = two_heads(r.q[i]), r.opening[i]
                    state = (r.lse[i], r.total[i])
                    for t in range(LONGEST // WIDE):
                        state = step(r.before, r.before_vt, t, 2 * i + core, query, opening, state, True, -LONGEST)
                    r.lse[i], r.total[i] = state
                    return carry

                lax.fori_loop(0, SLOTS // 2, before_part, 0)

        steps(dy, 3)
        steps(bulk, 1)
        drive(heads)

        def project_out(i, carry):
            norm = r.lse[i]
            out = r.total[i] / norm
            r.total[i] = out
            r.lse[i] = jnp.log(norm)
            row = two_columns(out.T.astype(BF16))
            r.mixed[i] = row
            r.part[i] = jnp.dot(row, r.w_out[...], preferred_element_type=F32).astype(BF16)
            return carry

        lax.fori_loop(0, SLOTS, project_out, 0)
        beside(scatter_tokens(at, r.part, r.land, r.hidden, r.s4, r.r4), bulk)

        def norm_rows(i, carry):
            rows = pl.ds(pl.multiple_of(i * 32, 32), 32)
            value = r.hidden[rows, :] + r.tokens[rows, :].astype(F32)
            r.hidden[rows, :] = value
            inverse = lax.rsqrt(jnp.mean(value * value, 1, keepdims=True) + EPSILON)
            r.mine[rows, :] = (value * inverse).astype(BF16)
            return carry

        lax.fori_loop(0, CHUNK // 32, norm_rows, 0)
        beside(gather_tokens(at, r.mine, r.xhat2_b, r.local.at[5], r.s2, r.r2), bulk)
        drive(dy, bulk)
        drive(lower, columns)

        @pl.when(group == 0)
        def _():
            for i in range(1, n):
                to_group(i).wait_send()

        if n > 2:

            @pl.when((group >= 1) & (group < n - 1))
            def _():
                forward().wait_send()

    chunks = (SLOTS, CHUNK, 2 * HD)
    block, end = (SLOTS, 2, CHUNK, 2 * HD), (SLOTS // 2, 2, CHUNK, 2 * HD)
    tok = DMA((len(PARTS), 7))
    return kernel(
        1,
        body,
        {name: (a, HBM if name in ("down_mine", "out_mine") else VMEM) for name, a in ins.items()},
        {
            "xhat_b": (like((SLOTS, CHUNK, D)), VMEM),
            "qkv": (like((D, QKV_SLOT)), VMEM),
            "raw": (like((SLOTS, CHUNK, 3 * HD), F32), VMEM),
            "q": (like(chunks), VMEM),
            "mixed": (like(chunks), VMEM),
            "total": (like((SLOTS, HD, 2 * CHUNK), F32), VMEM),
            "lse": (like((SLOTS, 1, 2 * CHUNK), F32), VMEM),
            "own": (like(block), VMEM),
            "prompt": (like(block), VMEM),
            "before": (like(end), VMEM),
            "w_out": (like((D // SLOTS, D)), VMEM),
            "hidden": (like((CHUNK, D), F32), VMEM),
            "xhat2_b": (like((SLOTS, CHUNK, D)), HBM),
            "gu": (like((D, GU_SLOT)), HBM),
            "down": (like((n, 2, hidden_rows, D)), HBM),
            "dy_b": (like((SLOTS, CHUNK, D)), HBM),
        },
        {
            "kv": pltpu.VMEM(chunks, BF16),
            "xhat": pltpu.VMEM((CHUNK, D), BF16),
            "dy": pltpu.VMEM((CHUNK, D), BF16),
            "qkv_mine": pltpu.VMEM((rows, (HQ + 2 * HK) * HD), BF16),
            "gu_mine": pltpu.VMEM((rows, 2 * FF), BF16),
            "own_vt": pltpu.VMEM((HD, 2 * SLOTS * CHUNK), BF16),
            "prompt_vt": pltpu.VMEM((HD, PROMPT), BF16),
            "before_vt": pltpu.VMEM((HD, LONGEST), BF16),
            "part": pltpu.VMEM((SLOTS, CHUNK, D), BF16),
            "land": pltpu.VMEM((7, CHUNK, D), BF16),
            "mine": pltpu.VMEM((CHUNK, D), BF16),
            "out_all": pltpu.VMEM((n, rows, D), BF16),
            "local": DMA((6,)),
            **{name: tok for name in ("s1", "r1", "s2", "r2", "s3", "r3", "s4", "r4")},
            **{name: DMA((7, 3)) for name in ("qs", "qr")},
            **{name: DMA((7, count)) for name in ("cs", "cr")},
            "qkv_local": DMA((3,)),
            "gu_local": DMA((count,)),
            **{name: DMA((n, 2, 1)) for name in ("qms", "qmr", "qss", "qsr")},
            **{name: DMA((n, 2, gu_pieces)) for name in ("cms", "cmr", "css", "csr")},
            **{name: DMA((n, pieces)) for name in ("hms", "hmr")},
            **{name: DMA((n,)) for name in ("hss", "hsr", "fs", "fr", "hl", "hs", "ps")},
            **{name: DMA(()) for name in ("hts", "htr", "os", "orr", "pr", "bs", "br")},
            "hr": DMA((n, 4)),
            **{name: DMA((3,)) for name in ("ks", "kr")},
        },
    )


def attention_back(at, r, part, between, when=None):
    kv, keys_t, acc = getattr(r, part), getattr(r, part + "_kt"), getattr(r, "acc_" + part)

    def begin():
        keys_t[...] = kv[:, :HD].T
        acc[...] = jnp.zeros_like(acc)

    shift = -LONGEST if part == "before" else 0

    def step(t, dq, q, do, dot_rows, logs, chunk, opening):
        first = t * WIDE
        rows = pl.ds(first if isinstance(first, int) else pl.multiple_of(first, WIDE), WIDE)
        keys, values = kv[rows, :HD], kv[rows, HD:]
        p = jnp.exp2(lax.dot_general(keys, q, NT, preferred_element_type=F32) * SCALE_2 - logs)
        if part != "prompt":
            p = jnp.where(visible(first + shift, chunk, opening, WIDE), p, 0.0)
        dp = lax.dot_general(values, do, NT, preferred_element_type=F32)
        ds = (p * (dp - dot_rows)).astype(BF16)
        acc[rows, :HD] += jnp.dot(ds, q, preferred_element_type=F32)
        acc[rows, HD:] += jnp.dot(p.astype(BF16), do, preferred_element_type=F32)
        return dq + jnp.dot(keys_t[:, rows], ds, preferred_element_type=F32)

    def one(i):
        chunk = 2 * i + at.c
        q, do = two_heads(r.q[i]), two_heads(r.do[i])
        args = (q, do, r.dots[i], r.lse[i] * (1.0 / math.log(2.0)), chunk, r.opening[i])
        if part == "own":
            start, stop = key_range(at.g, chunk, WIDE)
            r.dq_sum[i] = lax.fori_loop(start, stop, lambda t, dq: step(t, dq, *args), r.dq_sum[i])
        else:
            dq = r.dq_sum[i]
            for t in range(kv.shape[0] // WIDE):
                dq = step(t, dq, *args)
            r.dq_sum[i] = dq

    def end():
        out = getattr(r, "d_" + part)
        for t in range(out.shape[0] * 2):
            out[t // 2, t % 2, :, :HD] = (acc[t * CHUNK : (t + 1) * CHUNK, :HD] * SCALE).astype(BF16)
            out[t // 2, t % 2, :, HD:] = acc[t * CHUNK : (t + 1) * CHUNK, HD:].astype(BF16)

    count = SLOTS if part != "before" else SLOTS // 2
    if when is None:
        begin()
        paced(one, count, between)
        end()
    else:
        pl.when(when)(begin)
        paced(one, count, between, when)
        pl.when(when)(end)


def add_chunks(dst, first, other, skip=0):
    def one(i, carry):
        dst[i + skip] = (first(i).astype(F32) + other[i].astype(F32)).astype(BF16)
        return carry

    lax.fori_loop(0, other.shape[0], one, 0)


def kernel(collective_id, body, ins, outs, scratch):
    names = [*ins, *outs, *scratch]
    return dict(
        zip(
            outs,
            communicate(
                lambda *refs: body(types.SimpleNamespace(**dict(zip(names, refs)))),
                collective_id,
                tuple(a for a, _ in ins.values()),
                tuple(a for a, _ in outs.values()),
                list(scratch.values()),
                [spec for _, spec in ins.values()],
                [spec for _, spec in outs.values()],
            ),
        )
    )


def back_block(groups, rows, ins):
    n = groups

    def body(r):
        at = Place(n)
        group = at.g
        bring_dx = pltpu.make_async_copy(r.part_dx, r.part, r.local.at[3])
        bring_dx.start()
        meet(everyone(at) + [at.diagonal()])
        columns = columns_sum(at, r.g_gu, r.sib_gu, r.mid_gu, r.gu_sum, (r.cms, r.cmr, r.css, r.csr))
        next(columns)
        bring_dx.wait()
        bulk = in_turn((columns, r.cms.shape[1] * r.cms.shape[2] * (n - 1)))
        beside(scatter_tokens(at, r.part, r.land, r.dx, r.s1, r.r1), bulk)
        bring_out = pltpu.make_async_copy(r.part_out, r.part, r.local.at[3])
        bring_out.start()

        def norm(i, carry):
            rows = pl.ds(pl.multiple_of(i * 32, 32), 32)
            value = r.hidden[rows, :]
            inverse = lax.rsqrt(jnp.mean(value * value, 1, keepdims=True) + EPSILON)
            unit = value * inverse
            grad = r.dx[rows, :]
            total = r.cotangent[rows, :] + inverse * (grad - unit * jnp.mean(grad * unit, 1, keepdims=True))
            r.dhidden[rows, :] = total
            r.mine[rows, :] = total.astype(BF16)
            return carry

        lax.fori_loop(0, CHUNK // 32, norm, 0)
        beside(gather_tokens(at, r.mine, r.dbranch, r.local.at[0], r.s2, r.r2), bulk)
        bring_out.wait()
        result = scatter_tokens(at, r.part, r.land2, r.dx, r.s3, r.r3)
        next(result)

        def heads(i, carry):
            do = lax.dot_general(r.dbranch[i], r.w_out[...], NT, preferred_element_type=F32).astype(BF16)
            r.do[i] = do
            r.dots[i] = jnp.sum(two_heads(do).astype(F32).T * r.total[i], 0, keepdims=True)
            r.dq_sum[i] = jnp.zeros((HD, 2 * CHUNK), F32)
            return carry

        lax.fori_loop(0, SLOTS, heads, 0)

        def swap(array, place, i):
            return remote(array.at[:, 1 - at.c], place, r.ks.at[i], r.kr.at[i], at.sibling())

        def home(i):
            return remote(r.land_p, r.far_p.at[i - 1], r.ps, r.pr.at[i - 1], at.mid_at(jnp.int32(0)))

        def back():
            return remote(r.land_b, r.far_b, r.bs, r.br, at.mid_at(group - 1))

        def between():
            steps(bulk, 1)
            steps(result, 1)

        attention_back(at, r, "prompt", between, group > 0)

        @pl.when(group > 0)
        def _():
            swap(r.d_prompt, r.land_p, 1).start()

        if n > 2:
            attention_back(at, r, "before", between, group > 1)

            @pl.when(group > 1)
            def _():
                swap(r.d_before, r.land_b, 2).start()

        @pl.when(group > 0)
        def _():
            swap(r.d_prompt, r.land_p, 1).wait()
            add_chunks(r.land_p, lambda i: r.d_prompt[i, at.c], r.land_p)
            for i in range(1, n):

                @pl.when(group == i)
                def _():
                    home(i).start()

        if n > 2:

            @pl.when(group > 1)
            def _():
                swap(r.d_before, r.land_b, 2).wait()
                add_chunks(r.land_b, lambda i: r.d_before[i, at.c], r.land_b)
                back().start()

        attention_back(at, r, "own", between)
        first = swap(r.d_own, r.land_k, 0)
        first.start()
        drive(bulk)

        def queries(i, carry):
            r.dq[i] = two_columns((r.dq_sum[i].T * SCALE).astype(BF16))
            return carry

        lax.fori_loop(0, SLOTS, queries, 0)
        first.wait()
        add_chunks(r.dkv, lambda i: r.d_own[i, at.c], r.land_k)
        drive(result)

        def add(i, carry):
            rows = pl.ds(pl.multiple_of(i * 32, 32), 32)
            r.output[rows, :] = (r.hidden[rows, :] + r.dx[rows, :]).astype(BF16)
            return carry

        lax.fori_loop(0, CHUNK // 32, add, 0)

        @pl.when(group == 0)
        def _():
            for i in range(1, n):
                home(i).wait_recv()
                add_chunks(r.dkv, lambda j: r.dkv[j], r.far_p.at[i - 1])

        if n > 2:

            @pl.when((group >= 1) & (group < n - 1))
            def _():
                back().wait_recv()
                add_chunks(r.dkv, lambda j: r.dkv[j + SLOTS // 2], r.far_b, SLOTS // 2)

            @pl.when(group > 1)
            def _():
                back().wait_send()

        @pl.when(group > 0)
        def _():
            home(1).wait_send()

        drive(columns)

    chunks = (SLOTS, CHUNK, 2 * HD)
    block, end = (SLOTS, 2, CHUNK, 2 * HD), (SLOTS // 2, 2, CHUNK, 2 * HD)
    tok = DMA((len(PARTS), 7))
    near, half = pltpu.VMEM(chunks, BF16), pltpu.VMEM((SLOTS // 2, CHUNK, 2 * HD), BF16)
    own, prompt, before = 2 * SLOTS * CHUNK, PROMPT, LONGEST
    far = max(n - 1, 1)
    gu_pieces = 4 * (rows // piece_rows(rows))
    return kernel(
        2,
        body,
        {name: (a, HBM if name in ("part_dx", "part_out") else VMEM) for name, a in ins.items()},
        {
            "dhidden": (like((CHUNK, D), F32), VMEM),
            "output": (like((CHUNK, D)), VMEM),
            "dbranch": (like((SLOTS, CHUNK, D)), VMEM),
            "dq": (like(chunks), VMEM),
            "dkv": (like(chunks), VMEM),
            "gu_sum": (like((2, 4, rows, GU_SLOT)), VMEM),
        },
        {
            "part": pltpu.VMEM((SLOTS, CHUNK, D), BF16),
            "land": pltpu.VMEM((7, CHUNK, D), BF16),
            "land2": pltpu.VMEM((7, CHUNK, D), BF16),
            "mine": pltpu.VMEM((CHUNK, D), BF16),
            "dx": pltpu.VMEM((CHUNK, D), F32),
            "sib_gu": pltpu.VMEM((2, 4 * n * rows, GU_SLOT), BF16),
            "mid_gu": pltpu.VMEM((far, 2, 4, rows, GU_SLOT), BF16),
            "do": near,
            "dots": pltpu.VMEM((SLOTS, 1, 2 * CHUNK), F32),
            "dq_sum": pltpu.VMEM((SLOTS, HD, 2 * CHUNK), F32),
            "own_kt": pltpu.VMEM((HD, own), BF16),
            "prompt_kt": pltpu.VMEM((HD, prompt), BF16),
            "before_kt": pltpu.VMEM((HD, before), BF16),
            "acc_own": pltpu.VMEM((own, 2 * HD), F32),
            "acc_prompt": pltpu.VMEM((prompt, 2 * HD), F32),
            "acc_before": pltpu.VMEM((before, 2 * HD), F32),
            "d_own": pltpu.VMEM(block, BF16),
            "d_prompt": pltpu.VMEM(block, BF16),
            "d_before": pltpu.VMEM(end, BF16),
            "land_k": near,
            "land_p": near,
            "land_b": half,
            "far_p": pltpu.VMEM((far, *chunks), BF16),
            "far_b": half,
            "local": DMA((4,)),
            **{name: tok for name in ("s1", "r1", "s2", "r2", "s3", "r3")},
            **{name: DMA((n, 2, gu_pieces)) for name in ("cms", "cmr")},
            **{name: DMA((2,)) for name in ("css", "csr")},
            **{name: DMA((3,)) for name in ("ks", "kr")},
            "ps": DMA(()),
            "pr": DMA((n,)),
            "bs": DMA(()),
            "br": DMA(()),
        },
    )


def last_block(groups, rows, hidden_rows, ins):
    n = groups
    gate_up = Columns.gate_up(groups, hidden_rows)
    count = len(gate_up(0, 0, 0))
    pieces = hidden_rows // piece_rows(hidden_rows)

    def unscale(dst, grad, weight, gain, d_gain):
        total = jnp.zeros((rows, 1), F32)
        for k in range(dst.shape[1] // 2048):
            cols = pl.ds(2048 * k, 2048)
            value = grad[:, cols].astype(F32)
            dst[:, cols] = value * gain[...]
            total = total + jnp.sum(value * weight[:, cols].astype(F32), 1, keepdims=True)
        d_gain[...] = total

    def body(r):
        at = Place(n)
        meet(everyone(at) + [at.diagonal()])
        lower = hidden_sum(at, r.g_down, r.down, r.sib_d, r.mid_d, r.fin_d, (r.hms, r.hmr, r.hss, r.hsr, r.hts, r.htr, r.local.at[0]))
        next(lower)
        bring = columns_home(at, r.gu_sum, r.gu, gate_up, r.ds, r.dr, r.gu_local)
        next(bring)
        steps(lower, 2)
        turned = r.mixed[...].reshape(SLOTS * CHUNK, 2 * HD).T

        for k in range(D // 512):
            cols = pl.ds(512 * k, 512)
            r.g_out[:, cols] = jnp.dot(
                turned, r.dbranch[:, :, cols].reshape(SLOTS * CHUNK, 512), preferred_element_type=F32
            ).astype(BF16)
        heads = scatter_heads(at, r.g_out, r.out, r.sib_o, r.mid_o, (r.os, r.orr, r.oms, r.omr, r.oss, r.osr, r.local.at[1]))
        next(heads)
        steps(lower, 1)
        r.gain_sum[...] = jnp.zeros_like(r.gain_sum)

        def through_heads(i, carry):
            two = pl.ds(pl.multiple_of(2 * i, 2), 2)
            cosine, sine = r.cosine[two].reshape(2 * CHUNK, HD), r.sine[two].reshape(2 * CHUNK, HD)
            raw = r.raw[two].reshape(2 * CHUNK, 3 * HD)
            dq, dkv = r.dq[two].reshape(2 * CHUNK, 2 * HD), r.dkv[two].reshape(2 * CHUNK, 2 * HD)
            parts = []
            for h in range(3):
                grad = (dq[:, h * HD : (h + 1) * HD] if h < 2 else dkv[:, :HD]).astype(F32)
                head = raw[:, h * HD : (h + 1) * HD]
                inverse = lax.rsqrt(jnp.mean(head * head, 1, keepdims=True) + EPSILON)
                unit = head * inverse
                back = grad * cosine + pltpu.roll(grad * sine, HD // 2, 1)
                at_row = 0 if h < 2 else 1
                r.gain_sum[at_row : at_row + 1, :] += jnp.sum(back * unit, 0, keepdims=True)
                back = back * r.head_gain[h : h + 1, :]
                parts.append((inverse * (back - unit * jnp.mean(back * unit, 1, keepdims=True))).astype(BF16))
            draw = jnp.concatenate(parts + [dkv[:, HD:]], 1)
            r.draw[two] = draw.reshape(2, CHUNK, QKV_SLOT)
            return carry

        lax.fori_loop(0, SLOTS // 2, through_heads, 0)
        next(heads)
        sums = sum_everywhere(at, r.gain_sum, r.gain_land, r.gs, r.gr)
        for h in range(QKV_SLOT // HD):
            steps(sums, 1)
            if h < 3 and n == 2:
                steps(lower, 1)
            cols = pl.ds(h * HD, HD)
            turned = r.draw[:, :, cols].reshape(SLOTS * CHUNK, HD).T
            grad = jnp.dot(turned, r.xhat_b[...].reshape(SLOTS * CHUNK, D), preferred_element_type=F32)
            r.g_qkv[:, cols] = grad.astype(BF16).T
        wide = columns_sum(at, r.g_qkv, r.sib_q, r.mid_q, r.fin_q, (r.cms, r.cmr, r.css, r.csr), 4)
        next(wide)

        def part_dx(i, carry):
            two = pl.ds(pl.multiple_of(2 * i, 2), 2)
            grad = lax.dot_general(
                r.draw[two].reshape(2 * CHUNK, QKV_SLOT), r.qkv[...], NT, preferred_element_type=F32
            )
            r.part[two] = grad.astype(BF16).reshape(2, CHUNK, D)
            return carry

        lax.fori_loop(0, SLOTS // 2, part_dx, 0)
        steps(wide, 1)
        bulk = in_turn((wide, 2 * (rows // piece_rows(rows)) * (n - 1) - 1))
        beside(scatter_tokens(at, r.part, r.land, r.dx, r.s1, r.r1), bulk)

        def norm(i, carry):
            rows = pl.ds(pl.multiple_of(i * 32, 32), 32)
            value = r.tokens[rows, :].astype(F32)
            inverse = lax.rsqrt(jnp.mean(value * value, 1, keepdims=True) + EPSILON)
            unit = value * inverse
            grad = r.dx[rows, :]
            r.d_tokens[rows, :] = r.dhidden[rows, :] + inverse * (grad - unit * jnp.mean(grad * unit, 1, keepdims=True))
            return carry

        lax.fori_loop(0, CHUNK // 32, norm, 0)
        for _ in range(pieces * (n - 1) + 1 - (6 if n == 2 else 3)):
            next(lower)
        next(heads)
        drive(bring)
        unscale(r.d_gu, r.gu, r.w_gu, r.gain_two, r.d_gain_two)
        drive(wide)
        home = columns_home(at, r.fin_q, r.qkv_rows, Columns.qkv, r.cs, r.cr, r.qkv_local)
        next(home)
        drive(lower)

        def lower_out(i, carry):
            rows_i = pl.ds(pl.multiple_of(i * 16, 16), 16)
            r.d_down[rows_i, :] = r.down[rows_i, :].astype(F32)
            return carry

        lax.fori_loop(0, hidden_rows // 16, lower_out, 0)
        drive(bulk, sums, heads)
        r.d_out[...] = r.out[...].astype(F32)
        drive(home)
        unscale(r.d_qkv, r.qkv_rows, r.w_qkv, r.gain_one, r.d_gain_one)

    deep = 4 * n * rows
    far = max(n - 1, 1)
    return kernel(
        3,
        body,
        {name: (a, HBM if name == "gu_sum" else VMEM) for name, a in ins.items()},
        {
            "d_gu": (like((rows, 2 * FF), F32), VMEM),
            "d_tokens": (like((CHUNK, D), F32), VMEM),
            "d_qkv": (like((rows, (HQ + 2 * HK) * HD), F32), VMEM),
            "d_out": (like((rows, D), F32), VMEM),
            "d_down": (like((hidden_rows, D), F32), VMEM),
            "d_gain_one": (like((rows, 1), F32), VMEM),
            "d_gain_two": (like((rows, 1), F32), VMEM),
            "gain_sum": (like((8, HD), F32), VMEM),
        },
        {
            "gu": pltpu.VMEM((rows, 2 * FF), BF16),
            "qkv_rows": pltpu.VMEM((rows, (HQ + 2 * HK) * HD), BF16),
            "out": pltpu.VMEM((rows, D), BF16),
            "down": pltpu.VMEM((hidden_rows, D), BF16),
            "sib_d": pltpu.VMEM((n, hidden_rows, D), BF16),
            "mid_d": pltpu.VMEM((far, pieces, piece_rows(hidden_rows), D), BF16),
            "fin_d": pltpu.VMEM((hidden_rows, D), BF16),
            **{name: DMA((n, pieces)) for name in ("hms", "hmr")},
            **{name: DMA(()) for name in ("hss", "hsr", "hts", "htr")},
            "part": pltpu.VMEM((SLOTS, CHUNK, D), BF16),
            "land": pltpu.VMEM((7, CHUNK, D), BF16),
            "dx": pltpu.VMEM((CHUNK, D), F32),
            "draw": pltpu.VMEM((SLOTS, CHUNK, QKV_SLOT), BF16),
            "g_qkv": pltpu.VMEM((D, QKV_SLOT), BF16),
            "sib_q": pltpu.VMEM((2, deep, QKV_SLOT), BF16),
            "mid_q": pltpu.VMEM((far, 2, 4, rows, QKV_SLOT), BF16),
            "fin_q": pltpu.VMEM((2, 4, rows, QKV_SLOT), BF16),
            "g_out": pltpu.VMEM((D // SLOTS, D), BF16),
            "sib_o": pltpu.VMEM((D // SLOTS, D), BF16),
            "mid_o": pltpu.VMEM((far, 4 * rows, D), BF16),
            "gain_land": pltpu.VMEM((4 + n, 8, HD), F32),
            "local": DMA((2,)),
            **{name: DMA((len(PARTS), 7)) for name in ("s1", "r1")},
            **{name: DMA((7, 3)) for name in ("cs", "cr")},
            "qkv_local": DMA((3,)),
            **{name: DMA((7, count)) for name in ("ds", "dr")},
            "gu_local": DMA((count,)),
            **{name: DMA((n, 2, 4 * (rows // piece_rows(rows)))) for name in ("cms", "cmr")},
            **{name: DMA((2,)) for name in ("css", "csr")},
            "os": DMA((4,)),
            **{name: DMA(()) for name in ("orr", "oss", "osr")},
            **{name: DMA((n,)) for name in ("oms", "omr")},
            **{name: DMA((4 + n,)) for name in ("gs", "gr")},
        },
    )


def dot(a, b, dims=((1,), (0,))):
    return lax.dot_general(a, b, (dims, ((), ())), preferred_element_type=F32)


def body(tokens, lengths, attn_gain, w_qkv, q_gain, k_gain, w_out, mlp_gain, w_gate_up, w_down, cotangent):
    blocks = lax.axis_size("blk")
    groups = blocks // 4
    rows = w_qkv.shape[0]
    hidden_rows = w_down.shape[0]
    group = lax.axis_index("blk") // 4
    core = lax.axis_index("uly") % 2
    gain_one = attn_gain.astype(F32)[:, None]
    gain_two = mlp_gain.astype(F32)[:, None]

    direct = (2 * hidden_rows) % 128 == 0
    w_gu = w_gate_up
    if not direct:
        w_gu = (
            w_gate_up.reshape(rows, 2, 2, 2, groups, 2, 2 * hidden_rows)
            .transpose(0, 2, 5, 3, 1, 4, 6)
            .reshape(rows, 2 * FF)
        )

    starts = PROMPT + jnp.sum(
        jnp.where(jnp.arange(lengths.shape[0])[:, None] > jnp.arange(lengths.shape[0])[None, :], lengths[None, :], 0), 1
    )
    index = (
        group * (2 * SLOTS * CHUNK)
        + (2 * jnp.arange(SLOTS, dtype=jnp.int32)[:, None] + core) * CHUNK
        + jnp.arange(CHUNK, dtype=jnp.int32)[None, :]
    )
    opening = jnp.max(jnp.where(index[..., None] >= starts, starts, 0), -1)
    position = jnp.where(index < PROMPT, index, index - opening + PROMPT)
    opening = opening - group * (2 * SLOTS * CHUNK)
    opening = jnp.concatenate([opening, opening], 1)[:, None, :]
    lane = np.arange(HD)
    angles = position.astype(F32)[:, :, None] * (ROPE_BASE ** (-2.0 * jnp.asarray(lane % (HD // 2), F32) / HD))
    cosine, sine = jnp.cos(angles), jnp.sin(angles) * np.where(lane < HD // 2, -1.0, 1.0).astype(np.float32)
    head_gain = jnp.stack([q_gain, q_gain, k_gain]).astype(F32)

    front = front_block(
        groups,
        rows,
        hidden_rows,
        {
            "tokens": tokens,
            "cotangent": cotangent,
            "w_qkv": w_qkv,
            "w_gu": w_gu,
            "gain_one": gain_one,
            "gain_two": gain_two,
            "opening": opening,
            "cosine": cosine,
            "sine": sine,
            "head_gain": head_gain,
            "down_mine": w_down,
            "out_mine": w_out,
        },
    )
    xhat2_b, dy_b = (front[name].reshape(SLOTS * CHUNK, D) for name in ("xhat2_b", "dy_b"))
    own, prompt, before = (front[name].reshape(-1, 2 * HD) for name in ("own", "prompt", "before"))
    gu_w, down_w = front["gu"], front["down"].reshape(FF_SLOT, D)

    both = dot(xhat2_b, gu_w)
    gate, up = both[:, :FF_SLOT], both[:, FF_SLOT:]
    sigmoid = jax.nn.sigmoid(gate)
    act = (gate * sigmoid * up).astype(BF16)
    part_out = dot(act, down_w).astype(BF16)
    g_down = dot(act, dy_b, ((0,), (0,))).astype(BF16)
    dact = dot(dy_b, down_w, ((1,), (1,)))
    dboth = jnp.concatenate(
        [dact * up * sigmoid * (1.0 + gate * (1.0 - sigmoid)), dact * gate * sigmoid], 1
    ).astype(BF16)
    g_gu = dot(xhat2_b, dboth, ((0,), (0,))).astype(BF16)
    part_dx2 = dot(dboth, gu_w, ((1,), (1,))).astype(BF16)
    back = back_block(
        groups,
        rows,
        {
            "part_dx": part_dx2.reshape(SLOTS, CHUNK, D),
            "part_out": part_out.reshape(SLOTS, CHUNK, D),
            "hidden": front["hidden"],
            "cotangent": cotangent,
            "g_gu": g_gu,
            "w_out": front["w_out"],
            "q": front["q"],
            "own": own,
            "prompt": prompt,
            "before": before,
            "opening": opening,
            "total": front["total"],
            "lse": front["lse"],
        },
    )
    last = last_block(
        groups,
        rows,
        hidden_rows,
        {
            "gu_sum": back["gu_sum"],
            "g_down": g_down.reshape(groups, 2, hidden_rows, D),
            "w_qkv": w_qkv,
            "w_gu": w_gu,
            "gain_one": gain_one,
            "gain_two": gain_two,
            "dq": back["dq"],
            "dkv": back["dkv"],
            "raw": front["raw"],
            "cosine": cosine,
            "sine": sine,
            "head_gain": head_gain,
            "xhat_b": front["xhat_b"],
            "qkv": front["qkv"],
            "mixed": front["mixed"],
            "dbranch": back["dbranch"],
            "tokens": tokens,
            "dhidden": back["dhidden"],
        },
    )
    d_gu = last["d_gu"]
    if not direct:
        d_gu = (
            d_gu.reshape(rows, 2, 2, 2, 2, groups, 2 * hidden_rows)
            .transpose(0, 4, 1, 3, 5, 2, 6)
            .reshape(rows, 2 * FF)
        )
    return (
        back["output"],
        last["d_tokens"],
        last["d_gain_one"][:, 0],
        last["d_qkv"],
        last["gain_sum"][0],
        last["gain_sum"][1],
        last["d_out"],
        last["d_gain_two"][:, 0],
        d_gu,
        last["d_down"],
    )


def solution(mesh):
    tokens = P(("blk", "uly"), None)
    weight = P(("uly", "blk"), None)
    gain = P(("uly", "blk"))
    return jax.shard_map(
        body,
        mesh=mesh,
        in_specs=(tokens, P(), gain, weight, P(), P(), weight, gain, weight, weight, tokens),
        out_specs=(tokens, tokens, gain, weight, P(), P(), weight, gain, weight, weight),
        check_vma=False,
    )
```

```python
import math
import types

import jax
import jax.numpy as jnp
import numpy as np
from jax import lax
from jax.experimental import pallas as pl
from jax.experimental.pallas import tpu as pltpu
from jax.sharding import PartitionSpec as P

D = 2048
HQ = 16
HK = 8
HD = 128
FF = 6144
PROMPT = 2048
LONGEST = 1024

SLOTS = 8
CHUNK = 128
QKV_SLOT = 512
GU_SLOT = 2 * FF // SLOTS
FF_SLOT = FF // SLOTS
EPSILON = 1e-06
ROPE_BASE = 1000000.0
SCALE = 1.0 / math.sqrt(HD)
WINDOW = 10

F32 = jnp.float32
BF16 = jnp.bfloat16
MESH = pl.DeviceIdType.MESH
HBM = pl.BlockSpec(memory_space=pl.ANY)
VMEM = pl.BlockSpec(memory_space=pltpu.VMEM)
DMA = pltpu.SemaphoreType.DMA
PARTS = ((0, 1, 2), 256), ((1, 2, 0), 768), ((2, 0, 1), 1024)


def rem(a, n):
    return lax.rem(a, jnp.int32(n))


class Place:
    def __init__(self, groups):
        self.groups = groups
        self.u = lax.axis_index("uly")
        self.b = lax.axis_index("blk")
        self.x = self.u // 2
        self.c = rem(self.u, 2)
        self.g = self.b // 4
        self.bl = rem(self.b, 4)
        self.bits = (self.x, rem(self.bl, 2), self.bl // 2)

    def flip(self, *dims):
        x, y, z = (rem(v + 1, 2) if d in dims else v for d, v in enumerate(self.bits))
        return x, 2 * z + y

    def coords(self, *dims):
        return [rem(v + 1, 2) if d in dims else v for d, v in enumerate(self.bits)]

    def chunk(self, *dims):
        x, bl = self.flip(*dims)
        return 2 * bl + x

    def slot(self, *dims):
        x, bl = self.flip(*dims)
        return 4 * x + bl

    def cube(self, *dims):
        x, bl = self.flip(*dims)
        return (2 * x + self.c, 4 * self.g + bl)

    def sibling(self):
        return (2 * self.x + 1 - self.c, self.b)

    def ahead(self, i):
        return rem(self.g + i, self.groups)

    def behind(self, i):
        return rem(self.g + self.groups - i, self.groups)

    def mid(self, i):
        return (self.u, 4 * self.ahead(i) + self.bl)

    def diagonal(self):
        x, y, z = self.bits
        return (2 * x + 1 - self.c, 4 * self.g + 2 * z + 1 - y)

    def mid_at(self, group):
        return (self.u, 4 * group + self.bl)


PEERS = ((0,), (1,), (2,), (0, 1), (0, 2), (1, 2), (0, 1, 2))


def meet(devices):
    barrier = pltpu.get_barrier_semaphore()
    for device in devices:
        pl.semaphore_signal(barrier, inc=1, device_id=device, device_id_type=MESH)
    pl.semaphore_wait(barrier, len(devices))


def remote(src, dst, send, recv, device):
    return pltpu.make_async_remote_copy(
        src_ref=src, dst_ref=dst, send_sem=send, recv_sem=recv, device_id=device, device_id_type=MESH
    )


def rows_at(start, count):
    return pl.ds(pl.multiple_of(start, 16), count)


def drive(*tasks):
    tasks = list(tasks)
    while tasks:
        tasks = [task for task in tasks if next(task, None) is not None]


def steps(task, count):
    for _ in range(count):
        next(task, None)


def paced(loop, count, between, when=None):
    def one(i, carry):
        loop(i)
        return carry

    for k in range(4):
        run = (k * count // 4, (k + 1) * count // 4)
        if when is None:
            lax.fori_loop(*run, one, 0)
        else:

            @pl.when(when)
            def _():
                lax.fori_loop(*run, one, 0)

        between()


def piece_rows(rows):
    return 32 if rows % 32 == 0 else 16


def beside(main, *bulk):
    for _ in main:
        for task in bulk:
            next(task, None)


def in_turn(*tasks):
    for task, count in tasks:
        for _ in range(count):
            next(task, None)
            yield True


def part_columns():
    start = 0
    for p, (order, width) in enumerate(PARTS):
        yield p, order, pl.ds(start, width)
        start += width


def gather_tokens(at, mine, block, local, send, recv):
    own = pltpu.make_async_copy(mine, block.at[at.chunk()], local)
    own.start()
    sent = []

    def push(p, i, dims, along, cols):
        src = block.at[at.chunk(*dims), :, cols] if dims else mine.at[:, cols]
        copy = remote(src, block.at[at.chunk(*dims), :, cols], send.at[p, i], recv.at[p, i], at.cube(along))
        copy.start()
        sent.append(copy)

    def arrive(p, i, dims, cols):
        there = block.at[at.chunk(*dims), :, cols]
        remote(there, there, send.at[p, i], recv.at[p, i], at.cube(dims[0])).wait_recv()

    parts = list(part_columns())
    over = [sorted(parts, key=lambda part: part[1][k] == 2) for k in range(3)]
    for p, (a, b, c), cols in parts:
        push(p, 0, (), a, cols)
        push(p, 1, (), b, cols)
        push(p, 2, (), c, cols)
    yield True
    for p, (a, b, c), cols in over[0]:
        arrive(p, 0, (a,), cols)
        push(p, 3, (a,), b, cols)
        push(p, 4, (a,), c, cols)
        yield True
    for p, (a, b, c), cols in over[1]:
        arrive(p, 1, (b,), cols)
        push(p, 5, (b,), c, cols)
        arrive(p, 3, (a, b), cols)
        push(p, 6, (a, b), c, cols)
        yield True
    for p, (a, b, c), cols in parts:
        arrive(p, 2, (c,), cols)
        arrive(p, 4, (a, c), cols)
        arrive(p, 5, (b, c), cols)
        arrive(p, 6, (a, b, c), cols)
    for copy in sent:
        copy.wait_send()
    own.wait()


def add_rows(dst, terms, count, step=32):
    def body(i, carry):
        rows = pl.ds(pl.multiple_of(i * step, step), step)
        total = terms[0][rows, :].astype(F32)
        for term in terms[1:]:
            total = total + term[rows, :].astype(F32)
        dst[rows, :] = total.astype(dst.dtype)
        return carry

    lax.fori_loop(0, count // step, body, 0)


def scatter_tokens(at, part, land, out, send, recv):
    sent = []

    def push(p, i, dims, along, cols):
        copy = remote(part.at[at.chunk(*dims), :, cols], land.at[i, :, cols], send.at[p, i], recv.at[p, i], at.cube(along))
        copy.start()
        sent.append(copy)

    def arrive(p, i, along, cols):
        remote(land.at[i, :, cols], land.at[i, :, cols], send.at[p, i], recv.at[p, i], at.cube(along)).wait_recv()

    def add(i, dims, cols):
        here = part.at[at.chunk(*dims), :, cols]
        add_rows(here, [here, land.at[i, :, cols]], CHUNK)

    parts = list(part_columns())
    over = [sorted(parts, key=lambda part: part[1][k] == 2) for k in range(3)]
    for p, (a, b, c), cols in parts:
        push(p, 3, (a, b, c), c, cols)
        push(p, 2, (b, c), c, cols)
    for p, (a, b, c), cols in parts:
        push(p, 1, (a, c), c, cols)
        push(p, 0, (c,), c, cols)
    yield True
    for p, (a, b, c), cols in over[2]:
        arrive(p, 3, c, cols)
        add(3, (a, b), cols)
        push(p, 5, (a, b), b, cols)
        arrive(p, 2, c, cols)
        add(2, (b,), cols)
        push(p, 4, (b,), b, cols)
        yield True
    for p, (a, b, c), cols in over[1]:
        arrive(p, 1, c, cols)
        add(1, (a,), cols)
        arrive(p, 5, b, cols)
        add(5, (a,), cols)
        push(p, 6, (a,), a, cols)
        yield True
    for p, (a, b, c), cols in over[0]:
        arrive(p, 0, c, cols)
        arrive(p, 4, b, cols)
        arrive(p, 6, a, cols)
        add_rows(
            out.at[:, cols],
            [part.at[at.chunk(), :, cols], land.at[0, :, cols], land.at[4, :, cols], land.at[6, :, cols]],
            CHUNK,
        )
    for copy in sent:
        copy.wait_send()


def column_row(at, rows, u, b):
    return (u * (4 * at.groups) + b) * rows


class Columns:
    def qkv(x, y, z):
        pair = 4 * x + 2 * y + z
        return [(pair * (2 * HD), 2 * HD), (HQ * HD + pair * HD, HD), ((HQ + HK) * HD + pair * HD, HD)]

    def gate_up(groups, hidden_rows):
        wide = 2 * hidden_rows
        if wide % 128:
            return lambda x, y, z: [((4 * x + 2 * z + y) * GU_SLOT, GU_SLOT)]

        def runs(x, y, z):
            return [
                (half * FF + (((2 * x + y) * groups + group) * 2 + z) * wide, wide)
                for half in range(2)
                for group in range(groups)
            ]

        return runs


def column_runs(ref, whole, runs):
    at = 0
    for first, width in runs:
        yield ref.at[:, pl.ds(pl.multiple_of(first, 128), width)], whole.at[:, pl.ds(at, width)]
        at += width


def columns_in_cube(at, mine, whole, runs, local, send, recv, rows):
    own = rows_at(column_row(at, rows, at.u, at.b), rows)
    here = []
    for k, (src, dst) in enumerate(column_runs(mine, whole.at[own], runs(*at.coords()))):
        here.append(pltpu.make_async_copy(src, dst, local.at[k]))
        here[-1].start()
    sent = []
    for i, dims in enumerate(PEERS):
        for k, (src, dst) in enumerate(column_runs(mine, whole.at[own], runs(*at.coords(*dims)))):
            copy = remote(src, dst, send.at[i, k], recv.at[i, k], at.cube(*dims))
            copy.start()
            sent.append(copy)
    yield True
    for i, dims in enumerate(PEERS):
        u, b = at.cube(*dims)
        there = whole.at[rows_at(column_row(at, rows, u, b), rows)]
        for k, (_, dst) in enumerate(column_runs(mine, there, runs(*at.coords()))):
            remote(dst, dst, send.at[i, k], recv.at[i, k], (u, b)).wait_recv()
    for copy in sent:
        copy.wait_send()
    for copy in here:
        copy.wait()


def columns_across(at, whole, rows, mid_send, mid_recv, sib_send, sib_recv):
    n, pieces = at.groups, mid_send.shape[2]
    step = 4 * rows // pieces
    sent = []

    def piece(core, group, x, k):
        return whole.at[rows_at(column_row(at, rows, 2 * x + core, 4 * group) + k * step, step)]

    def pass_on(i, x, k):
        there = piece(at.c, at.behind(i), x, k)
        copy = remote(there, there, sib_send.at[i, x, k], sib_recv.at[i, x, k], at.sibling())
        copy.start()
        sent.append(copy)

    order = [(x, k) for x in range(2) for k in range(pieces)]
    every = [(i, x, k) for i in range(1, n) for x, k in order]

    def arrived(i, x, k):
        there = piece(at.c, at.behind(i), x, k)
        remote(there, there, mid_send.at[i, x, k], mid_recv.at[i, x, k], at.mid(i)).wait_recv()
        pass_on(i, x, k)

    for m, (i, x, k) in enumerate(every):
        there = piece(at.c, at.g, x, k)
        copy = remote(there, there, mid_send.at[i, x, k], mid_recv.at[i, x, k], at.mid(i))
        copy.start()
        sent.append(copy)
        if i == 1:
            pass_on(0, x, k)
        if m >= WINDOW:
            arrived(*every[m - WINDOW])
        yield True
    for one in every[max(len(every) - WINDOW, 0) :]:
        arrived(*one)
    for i in range(n):
        for x, k in order:
            there = piece(1 - at.c, at.behind(i), x, k)
            remote(there, there, sib_send.at[i, x, k], sib_recv.at[i, x, k], at.sibling()).wait_recv()
    for copy in sent:
        copy.wait_send()


def gather_hidden(at, mine, whole, local, turn_send, turn_recv, mid_send, mid_recv, sib_send, sib_recv):
    n, rows, pieces = at.groups, mine.shape[0], mid_send.shape[1]
    step = rows // pieces
    own = whole.at[at.g, at.c]
    stays = at.bits[1] == at.c
    here = pltpu.make_async_copy(mine, own, local)
    there = remote(mine, whole.at[at.g, 1 - at.c], turn_send, turn_recv, at.diagonal())

    @pl.when(stays)
    def _():
        here.start()

    @pl.when(jnp.logical_not(stays))
    def _():
        there.start()

    yield True

    @pl.when(stays)
    def _():
        here.wait()

    @pl.when(jnp.logical_not(stays))
    def _():
        there.wait()

    sent = []
    for i in range(1, n):
        for k in range(pieces):
            piece = own.at[pl.ds(k * step, step)]
            copy = remote(piece, piece, mid_send.at[i, k], mid_recv.at[i, k], at.mid(i))
            copy.start()
            sent.append(copy)
            yield True

    def pass_on(i):
        group = whole.at[at.behind(i), at.c]
        copy = remote(group, group, sib_send.at[i], sib_recv.at[i], at.sibling())
        copy.start()
        sent.append(copy)

    pass_on(0)
    for i in range(1, n):
        for k in range(pieces):
            piece = whole.at[at.behind(i), at.c, pl.ds(k * step, step)]
            remote(piece, piece, mid_send.at[i, k], mid_recv.at[i, k], at.mid(i)).wait_recv()
        pass_on(i)
    for i in range(n):
        group = whole.at[at.behind(i), 1 - at.c]
        remote(group, group, sib_send.at[i], sib_recv.at[i], at.sibling()).wait_recv()
    for copy in sent:
        copy.wait_send()


class OutRows:
    def __init__(self, at, rows):
        self.at, self.rows = at, rows
        self.per_half = max(at.groups // 2, 1)
        self.my_half = at.g // self.per_half
        self.to = 2 * self.my_half + at.c
        self.collects = at.bl == self.to
        self.slot_core = rem(at.bl, 2) == at.c
        self.slot_half = at.bl // 2

    def group_rows(self, group, half):
        return rows_at((group - half * self.per_half) * (4 * self.rows), 4 * self.rows)

    def in_half(self, group, half):
        return group // self.per_half == half

    def device(self, bl):
        return (self.at.u, 4 * self.at.g + bl)


def gather_heads(at, mine, whole, local, send, recv, sib_send, sib_recv):
    n, rows = mine.shape[0], mine.shape[1]
    lay = OutRows(at, rows)

    def place(group, bl):
        half = group // lay.per_half
        return whole.at[rows_at(((group - half * lay.per_half) * 4 + bl) * rows, rows)]

    def push(i):
        group = at.behind(i)
        to = 2 * (group // lay.per_half) + at.c
        here = pltpu.make_async_copy(mine.at[i], place(group, at.bl), local.at[i])
        there = remote(mine.at[i], place(group, at.bl), send.at[i], recv.at[i, at.bl], lay.device(to))
        return at.bl == to, here, there

    for i in range(n):
        stays, here, there = push(i)

        @pl.when(stays)
        def _():
            here.start()

        @pl.when(jnp.logical_not(stays))
        def _():
            there.start()

    yield True

    @pl.when(lay.slot_core)
    def _():
        for i in range(n):
            group = at.behind(i)

            @pl.when(lay.in_half(group, lay.slot_half))
            def _():
                pltpu.make_async_copy(mine.at[i], place(group, at.bl), local.at[i]).wait()
                for bl in range(4):

                    @pl.when(at.bl != bl)
                    def _():
                        there = place(group, bl)
                        remote(there, there, send.at[i], recv.at[i, bl], lay.device(bl)).wait_recv()

        remote(whole, whole, sib_send, sib_recv, at.sibling()).start()

    yield True

    @pl.when(lay.slot_core)
    def _():
        remote(whole, whole, sib_send, sib_recv, at.sibling()).wait_send()

    @pl.when(jnp.logical_not(lay.slot_core))
    def _():
        remote(whole, whole, sib_send, sib_recv, at.sibling()).wait_recv()

    for i in range(n):
        stays, here, there = push(i)

        @pl.when(jnp.logical_not(stays))
        def _():
            there.wait_send()


def columns_home(at, final, out, runs, send, recv, local):
    sent = []
    for i, dims in enumerate(PEERS):
        x, bl = at.flip(*dims)
        for k, (dst, src) in enumerate(column_runs(out, final.at[x, bl], runs(*at.coords()))):
            copy = remote(src, dst, send.at[i, k], recv.at[i, k], at.cube(*dims))
            copy.start()
            sent.append(copy)
    here = []
    for k, (dst, src) in enumerate(column_runs(out, final.at[at.x, at.bl], runs(*at.coords()))):
        here.append(pltpu.make_async_copy(src, dst, local.at[k]))
        here[-1].start()
    yield True
    for i, dims in enumerate(PEERS):
        for k, (there, _) in enumerate(column_runs(out, final.at[at.x, at.bl], runs(*at.coords(*dims)))):
            remote(there, there, send.at[i, k], recv.at[i, k], at.cube(*dims)).wait_recv()
    for copy in sent:
        copy.wait_send()
    for copy in here:
        copy.wait()


def columns_sum(at, part, sib_land, mid_land, final, sems, at_once=1):
    n, rows = at.groups, final.shape[2]
    mid_send, mid_recv, sib_send, sib_recv = sems
    run, deep = 4 * rows, 4 * n * rows
    step = piece_rows(rows)
    pieces = [(k, j) for k in range(4) for j in range(rows // step)]
    sent = []

    def of_core(x, core):
        return part.at[rows_at((2 * x + core) * deep, deep)]

    for x in range(2):
        copy = remote(of_core(x, 1 - at.c), sib_land.at[x], sib_send.at[x], sib_recv.at[x], at.sibling())
        copy.start()
        sent.append(copy)
    yield True
    for x in range(2):
        remote(sib_land.at[x], sib_land.at[x], sib_send.at[x], sib_recv.at[x], at.sibling()).wait_recv()
        for i in range(1, n):
            for m, (k, j) in enumerate(pieces):
                offset = at.ahead(i) * run + k * rows + j * step
                there = part.at[rows_at((2 * x + at.c) * deep + offset, step)]
                add_rows(there, [there, sib_land.at[x, rows_at(offset, step)]], step, 16)
                land = mid_land.at[i - 1, x, k, pl.ds(j * step, step)]
                copy = remote(there, land, mid_send.at[i, x, m], mid_recv.at[i, x, m], at.mid(i))
                copy.start()
                sent.append(copy)
                if m % at_once == at_once - 1:
                    yield True
    for x in range(2):
        for m, (k, j) in enumerate(pieces):
            for i in range(1, n):
                there = mid_land.at[i - 1, x, k, pl.ds(j * step, step)]
                remote(there, there, mid_send.at[i, x, m], mid_recv.at[i, x, m], at.mid(i)).wait_recv()
            offset = at.g * run + k * rows + j * step
            rows_here = pl.ds(j * step, step)
            add_rows(
                final.at[x, k, rows_here],
                [part.at[rows_at((2 * x + at.c) * deep + offset, step)], sib_land.at[x, rows_at(offset, step)]]
                + [mid_land.at[i - 1, x, k, rows_here] for i in range(1, n)],
                step,
                16,
            )
    for copy in sent:
        copy.wait_send()


def turn_hidden(at, final, out, turn_send, turn_recv, local):
    stays = at.bits[1] == at.c
    here = pltpu.make_async_copy(final, out, local)
    there = remote(final, out, turn_send, turn_recv, at.diagonal())

    @pl.when(stays)
    def _():
        here.start()

    @pl.when(jnp.logical_not(stays))
    def _():
        there.start()

    yield True

    @pl.when(stays)
    def _():
        here.wait()

    @pl.when(jnp.logical_not(stays))
    def _():
        there.wait()


def scatter_heads(at, part, out, sib_land, mid_land, sems):
    n, rows = at.groups, out.shape[0]
    send, recv, mid_send, mid_recv, sib_send, sib_recv, local = sems
    lay = OutRows(at, rows)

    @pl.when(jnp.logical_not(lay.slot_core))
    def _():
        remote(part, sib_land, sib_send, sib_recv, at.sibling()).start()

    yield True

    @pl.when(lay.slot_core)
    def _():
        remote(part, sib_land, sib_send, sib_recv, at.sibling()).wait_recv()
        add_rows(part, [part, sib_land], 256, 16)
        for i in range(1, n):
            group = at.ahead(i)

            @pl.when(lay.in_half(group, lay.slot_half))
            def _():
                there = part.at[lay.group_rows(group, lay.slot_half)]
                remote(there, mid_land.at[i - 1], mid_send.at[i], mid_recv.at[i], at.mid(i)).start()

    yield True
    mine = part.at[lay.group_rows(at.g, lay.my_half)]
    base = (at.g - lay.my_half * lay.per_half) * (4 * rows)

    @pl.when(lay.collects)
    def _():
        for i in range(1, n):
            remote(mine, mid_land.at[i - 1], mid_send.at[i], mid_recv.at[i], at.mid(i)).wait_recv()
        add_rows(mine, [mine] + [mid_land.at[i - 1] for i in range(1, n)], 4 * rows, 16)
        for bl in range(4):
            there = part.at[rows_at(base + bl * rows, rows)]

            @pl.when(at.bl != bl)
            def _():
                remote(there, out, send.at[bl], recv, lay.device(bl)).start()

            @pl.when(at.bl == bl)
            def _():
                pltpu.make_async_copy(there, out, local).start()

    yield True

    @pl.when(jnp.logical_not(lay.collects))
    def _():
        remote(out, out, send.at[0], recv, lay.device(lay.to)).wait_recv()

    @pl.when(lay.collects)
    def _():
        for bl in range(4):
            there = part.at[rows_at(base + bl * rows, rows)]

            @pl.when(at.bl != bl)
            def _():
                remote(there, out, send.at[bl], recv, lay.device(bl)).wait_send()

            @pl.when(at.bl == bl)
            def _():
                pltpu.make_async_copy(there, out, local).wait()

    @pl.when(jnp.logical_not(lay.slot_core))
    def _():
        remote(part, sib_land, sib_send, sib_recv, at.sibling()).wait_send()

    @pl.when(lay.slot_core)
    def _():
        for i in range(1, n):
            group = at.ahead(i)

            @pl.when(lay.in_half(group, lay.slot_half))
            def _():
                there = part.at[lay.group_rows(group, lay.slot_half)]
                remote(there, mid_land.at[i - 1], mid_send.at[i], mid_recv.at[i], at.mid(i)).wait_send()


def sum_everywhere(at, mine, land, send, recv):
    for i, device in enumerate([at.sibling(), at.cube(0), at.cube(1), at.cube(2)]):
        copy = remote(mine, land.at[i], send.at[i], recv.at[i], device)
        copy.start()
        yield True
        copy.wait()
        mine[...] = mine[...] + land[i]
    sent = []
    for i in range(1, at.groups):
        copy = remote(mine, land.at[3 + i], send.at[3 + i], recv.at[3 + i], at.mid(i))
        copy.start()
        sent.append(copy)
    yield True
    for copy in sent:
        copy.wait()
    for i in range(1, at.groups):
        mine[...] = mine[...] + land[3 + i]


def everyone(at):
    return [at.cube(*dims) for dims in PEERS] + [at.sibling()] + [at.mid(i) for i in range(1, at.groups)]


def cube_only(at):
    return [at.cube(*dims) for dims in ((0,), (1,), (2,))]


def communicate(body, collective_id, ins, outs, scratch, in_specs, out_specs, limit=60):
    return pl.pallas_call(
        body,
        out_shape=outs,
        in_specs=in_specs,
        out_specs=out_specs,
        scratch_shapes=scratch,
        compiler_params=pltpu.CompilerParams(
            collective_id=collective_id, has_side_effects=True, vmem_limit_bytes=limit << 20
        ),
    )(*ins)


def like(shape, dtype=BF16):
    return jax.ShapeDtypeStruct(shape, dtype)


NT = (((1,), (1,)), ((), ()))
WIDE = 512
SCALE_2 = SCALE / math.log(2.0)


def visible(first_key, chunk_of_block, opening, tile):
    key = first_key + lax.broadcasted_iota(jnp.int32, (tile, 2 * CHUNK), 0)
    lane = lax.broadcasted_iota(jnp.int32, (1, 2 * CHUNK), 1)
    row = chunk_of_block * CHUNK + jnp.where(lane >= CHUNK, lane - CHUNK, lane)
    return (key <= row) & (key >= opening)


def key_range(group, chunk_of_block, tile):
    stop = (chunk_of_block * CHUNK + CHUNK + tile - 1) // tile
    start = jnp.where(group > 0, jnp.maximum(chunk_of_block * CHUNK - LONGEST, 0) // tile, 0)
    return start, stop


def two_heads(block):
    return jnp.concatenate([block[:, :HD], block[:, HD:]], 0)


def two_columns(block):
    return jnp.concatenate([block[:CHUNK], block[CHUNK:]], 1)


def turn_values(kv, turned):
    for t in range(kv.shape[0]):
        turned[:, pl.ds(2 * CHUNK * t, 2 * CHUNK)] = kv[t].reshape(2 * CHUNK, 2 * HD)[:, HD:].T


def front_block(groups, rows, hidden_rows, ins):
    n = groups
    gate_up = Columns.gate_up(groups, hidden_rows)
    count = len(gate_up(0, 0, 0))
    pieces = hidden_rows // piece_rows(hidden_rows)
    gu_pieces = 4 * rows // piece_rows(4 * rows)

    def body(r):
        at = Place(n)
        group, core = at.g, at.c

        def first_norm(i, carry):
            rows_i = pl.ds(pl.multiple_of(i * 32, 32), 32)
            value = r.tokens[rows_i, :].astype(F32)
            r.xhat[rows_i, :] = (value * lax.rsqrt(jnp.mean(value * value, 1, keepdims=True) + EPSILON)).astype(BF16)
            return carry

        lax.fori_loop(0, CHUNK // 32, first_norm, 0)
        r.qkv_mine[...] = (r.w_qkv[...].astype(F32) * r.gain_one[...]).astype(BF16)
        meet(everyone(at) + [at.diagonal()])
        far = [remote(r.out_mine, r.out_all.at[i], r.fs.at[i], r.fr.at[i], at.mid(i)) for i in range(1, n)]
        for copy in far:
            copy.start()
        wide = columns_in_cube(at, r.qkv_mine, r.qkv, Columns.qkv, r.qkv_local, r.qs, r.qr, rows)
        next(wide)
        tokens = gather_tokens(at, r.xhat, r.xhat_b, r.local.at[1], r.s1, r.r1)
        next(tokens)
        lower = gather_hidden(at, r.down_mine, r.down, r.local.at[2], r.hts, r.htr, r.hms, r.hmr, r.hss, r.hsr)
        next(lower)
        out_here = pltpu.make_async_copy(r.out_mine, r.out_all.at[0], r.local.at[3])
        out_here.start()

        def scale(i, carry):
            cols = pl.ds(pl.multiple_of(i * 1024, 1024), 1024)
            r.gu_mine[:, cols] = (r.w_gu[:, cols].astype(F32) * r.gain_two[...]).astype(BF16)
            return carry

        lax.fori_loop(0, 2 * FF // 1024, scale, 0)

        def round_dy(i, carry):
            rows_i = pl.ds(pl.multiple_of(i * 32, 32), 32)
            r.dy[rows_i, :] = r.cotangent[rows_i, :].astype(BF16)
            return carry

        lax.fori_loop(0, CHUNK // 32, round_dy, 0)
        steps(tokens, 3)
        drive(wide)
        wide = columns_across(at, r.qkv, rows, r.qms, r.qmr, r.qss, r.qsr)
        steps(wide, 2 * (n - 1))
        steps(tokens, 3)
        columns = columns_in_cube(at, r.gu_mine, r.gu, gate_up, r.gu_local, r.cs, r.cr, rows)
        next(columns)
        out_here.wait()
        for copy in far:
            copy.wait()
        heads = gather_heads(at, r.out_all, r.w_out, r.hl, r.hs, r.hr, r.os, r.orr)
        next(heads)
        steps(lower, 1)
        drive(tokens)
        drive(wide)

        def project_in(i):
            four = pl.ds(pl.multiple_of(4 * i, 4), 4)
            raw = jnp.dot(r.xhat_b[four].reshape(4 * CHUNK, D), r.qkv[...], preferred_element_type=F32)
            cosine, sine = r.cosine[four].reshape(4 * CHUNK, HD), r.sine[four].reshape(4 * CHUNK, HD)
            heads = []
            for h in range(3):
                head = raw[:, h * HD : (h + 1) * HD]
                gain = r.head_gain[h : h + 1, :]
                normed = head * lax.rsqrt(jnp.mean(head * head, 1, keepdims=True) + EPSILON) * gain
                heads.append((normed * cosine + pltpu.roll(normed, HD // 2, 1) * sine).astype(BF16))
            r.raw[four] = raw[:, : 3 * HD].reshape(4, CHUNK, 3 * HD)
            r.q[four] = jnp.concatenate(heads[:2], 1).reshape(4, CHUNK, 2 * HD)
            r.kv[four] = jnp.concatenate([heads[2], raw[:, 3 * HD :].astype(BF16)], 1).reshape(4, CHUNK, 2 * HD)

        for i in range(2):
            lax.fori_loop(i, i + 1, lambda i, carry: (project_in(i), carry)[1], 0)

        here = pltpu.make_async_copy(r.kv, r.own.at[:, core], r.local.at[1])
        here.start()
        sib = remote(r.kv, r.own.at[:, core], r.ks.at[0], r.kr.at[0], at.sibling())
        sib.start()

        def to_group(i):
            return remote(r.kv, r.prompt.at[:, core], r.ps.at[i], r.pr, at.mid_at(jnp.int32(i)))

        def forward():
            half = r.kv.at[pl.ds(SLOTS // 2, SLOTS // 2)]
            return remote(half, r.before.at[:, core], r.bs, r.br, at.mid_at(group + 1))

        def across(ref, i):
            return remote(ref.at[:, core], ref.at[:, core], r.ks.at[i], r.kr.at[i], at.sibling())

        @pl.when(group == 0)
        def _():
            for i in range(1, n):
                to_group(i).start()

        if n > 2:

            @pl.when((group >= 1) & (group < n - 1))
            def _():
                forward().start()

        here.wait()
        sib.wait()
        turn_values(r.own, r.own_vt)
        drive(columns)
        columns = columns_across(at, r.gu, rows, r.cms, r.cmr, r.css, r.csr)
        bulk = in_turn((lower, pieces * (n - 1) - 1), (columns, 2 * gu_pieces * (n - 1)))
        steps(bulk, 1)
        dy = gather_tokens(at, r.dy, r.dy_b, r.local.at[4], r.s3, r.r3)
        next(dy)

        def step(kv, values_t, tile, chunk, q, opening, carry, masked, shift=0):
            norm, out = carry
            first = tile * WIDE
            parts = []
            for k in range(WIDE // CHUNK):
                keys = kv[tile * (WIDE // (2 * CHUNK)) + k // 2, k % 2][:, :HD]
                p = jnp.exp2(lax.dot_general(keys, q, NT, preferred_element_type=F32) * SCALE_2)
                if masked:
                    p = jnp.where(visible(first + shift + k * CHUNK, chunk, opening, CHUNK), p, 0.0)
                norm = norm + jnp.sum(p, 0, keepdims=True)
                parts.append(p.astype(BF16))
            first = first if isinstance(first, int) else pl.multiple_of(first, WIDE)
            out = out + jnp.dot(
                values_t[:, pl.ds(first, WIDE)], jnp.concatenate(parts, 0), preferred_element_type=F32
            )
            return norm, out

        def own_part(i):
            chunk = 2 * i + core
            query, opening = two_heads(r.q[i]), r.opening[i]
            start, stop = key_range(group, chunk, WIDE)
            zero = (jnp.zeros((1, 2 * CHUNK), F32), jnp.zeros((HD, 2 * CHUNK), F32))
            norm, out = lax.fori_loop(
                start, stop, lambda t, c: step(r.own, r.own_vt, t, chunk, query, opening, c, True), zero
            )
            r.lse[i] = norm
            r.total[i] = out

        paced(own_part, SLOTS, lambda: steps(bulk, 1))
        next(heads)

        @pl.when(group > 0)
        def _():
            to_group(0).wait_recv()
            across(r.prompt, 1).start()

        if n > 2:

            @pl.when(group > 1)
            def _():
                forward().wait_recv()
                across(r.before, 2).start()

        steps(dy, 3)
        steps(bulk, 1)

        @pl.when(group > 0)
        def _():
            across(r.prompt, 1).wait()
            turn_values(r.prompt, r.prompt_vt)

        def prompt_part(i):
            query = two_heads(r.q[i])
            state = (r.lse[i], r.total[i])
            for t in range(PROMPT // WIDE):
                state = step(r.prompt, r.prompt_vt, t, 0, query, None, state, False)
            r.lse[i], r.total[i] = state

        paced(prompt_part, SLOTS, lambda: steps(bulk, 1), group > 0)

        if n > 2:

            @pl.when(group > 1)
            def _():
                across(r.before, 2).wait()
                turn_values(r.before, r.before_vt)

                def before_part(i, carry):
                    query, opening = two_heads(r.q[i]), r.opening[i]
                    state = (r.lse[i], r.total[i])
                    for t in range(LONGEST // WIDE):
                        state = step(r.before, r.before_vt, t, 2 * i + core, query, opening, state, True, -LONGEST)
                    r.lse[i], r.total[i] = state
                    return carry

                lax.fori_loop(0, SLOTS // 2, before_part, 0)

        steps(dy, 3)
        steps(bulk, 1)
        drive(heads)

        def project_out(i, carry):
            norm = r.lse[i]
            out = r.total[i] / norm
            r.total[i] = out
            r.lse[i] = jnp.log(norm)
            row = two_columns(out.T.astype(BF16))
            r.mixed[i] = row
            r.part[i] = jnp.dot(row, r.w_out[...], preferred_element_type=F32).astype(BF16)
            return carry

        lax.fori_loop(0, SLOTS, project_out, 0)
        beside(scatter_tokens(at, r.part, r.land, r.hidden, r.s4, r.r4), bulk)

        def norm_rows(i, carry):
            rows = pl.ds(pl.multiple_of(i * 32, 32), 32)
            value = r.hidden[rows, :] + r.tokens[rows, :].astype(F32)
            r.hidden[rows, :] = value
            inverse = lax.rsqrt(jnp.mean(value * value, 1, keepdims=True) + EPSILON)
            r.mine[rows, :] = (value * inverse).astype(BF16)
            return carry

        lax.fori_loop(0, CHUNK // 32, norm_rows, 0)
        beside(gather_tokens(at, r.mine, r.xhat2_b, r.local.at[5], r.s2, r.r2), bulk)
        drive(dy, bulk)
        drive(lower, columns)

        @pl.when(group == 0)
        def _():
            for i in range(1, n):
                to_group(i).wait_send()

        if n > 2:

            @pl.when((group >= 1) & (group < n - 1))
            def _():
                forward().wait_send()

    chunks = (SLOTS, CHUNK, 2 * HD)
    block, end = (SLOTS, 2, CHUNK, 2 * HD), (SLOTS // 2, 2, CHUNK, 2 * HD)
    tok = DMA((len(PARTS), 7))
    return kernel(
        1,
        body,
        {name: (a, HBM if name in ("down_mine", "out_mine") else VMEM) for name, a in ins.items()},
        {
            "xhat_b": (like((SLOTS, CHUNK, D)), VMEM),
            "qkv": (like((D, QKV_SLOT)), VMEM),
            "raw": (like((SLOTS, CHUNK, 3 * HD), F32), VMEM),
            "q": (like(chunks), VMEM),
            "mixed": (like(chunks), VMEM),
            "total": (like((SLOTS, HD, 2 * CHUNK), F32), VMEM),
            "lse": (like((SLOTS, 1, 2 * CHUNK), F32), VMEM),
            "own": (like(block), VMEM),
            "prompt": (like(block), VMEM),
            "before": (like(end), VMEM),
            "w_out": (like((D // SLOTS, D)), VMEM),
            "hidden": (like((CHUNK, D), F32), VMEM),
            "xhat2_b": (like((SLOTS, CHUNK, D)), HBM),
            "gu": (like((D, GU_SLOT)), HBM),
            "down": (like((n, 2, hidden_rows, D)), HBM),
            "dy_b": (like((SLOTS, CHUNK, D)), HBM),
        },
        {
            "kv": pltpu.VMEM(chunks, BF16),
            "xhat": pltpu.VMEM((CHUNK, D), BF16),
            "dy": pltpu.VMEM((CHUNK, D), BF16),
            "qkv_mine": pltpu.VMEM((rows, (HQ + 2 * HK) * HD), BF16),
            "gu_mine": pltpu.VMEM((rows, 2 * FF), BF16),
            "own_vt": pltpu.VMEM((HD, 2 * SLOTS * CHUNK), BF16),
            "prompt_vt": pltpu.VMEM((HD, PROMPT), BF16),
            "before_vt": pltpu.VMEM((HD, LONGEST), BF16),
            "part": pltpu.VMEM((SLOTS, CHUNK, D), BF16),
            "land": pltpu.VMEM((7, CHUNK, D), BF16),
            "mine": pltpu.VMEM((CHUNK, D), BF16),
            "out_all": pltpu.VMEM((n, rows, D), BF16),
            "local": DMA((6,)),
            **{name: tok for name in ("s1", "r1", "s2", "r2", "s3", "r3", "s4", "r4")},
            **{name: DMA((7, 3)) for name in ("qs", "qr")},
            **{name: DMA((7, count)) for name in ("cs", "cr")},
            "qkv_local": DMA((3,)),
            "gu_local": DMA((count,)),
            **{name: DMA((n, 2, 1)) for name in ("qms", "qmr", "qss", "qsr")},
            **{name: DMA((n, 2, gu_pieces)) for name in ("cms", "cmr", "css", "csr")},
            **{name: DMA((n, pieces)) for name in ("hms", "hmr")},
            **{name: DMA((n,)) for name in ("hss", "hsr", "fs", "fr", "hl", "hs", "ps")},
            **{name: DMA(()) for name in ("hts", "htr", "os", "orr", "pr", "bs", "br")},
            "hr": DMA((n, 4)),
            **{name: DMA((3,)) for name in ("ks", "kr")},
        },
    )


def attention_back(at, r, part, between, when=None):
    kv, keys_t, acc = getattr(r, part), getattr(r, part + "_kt"), getattr(r, "acc_" + part)

    def begin():
        keys_t[...] = kv[:, :HD].T
        acc[...] = jnp.zeros_like(acc)

    shift = -LONGEST if part == "before" else 0

    def step(t, dq, q, do, dot_rows, logs, chunk, opening):
        first = t * WIDE
        rows = pl.ds(first if isinstance(first, int) else pl.multiple_of(first, WIDE), WIDE)
        keys, values = kv[rows, :HD], kv[rows, HD:]
        p = jnp.exp2(lax.dot_general(keys, q, NT, preferred_element_type=F32) * SCALE_2 - logs)
        if part != "prompt":
            p = jnp.where(visible(first + shift, chunk, opening, WIDE), p, 0.0)
        dp = lax.dot_general(values, do, NT, preferred_element_type=F32)
        ds = (p * (dp - dot_rows)).astype(BF16)
        acc[rows, :HD] += jnp.dot(ds, q, preferred_element_type=F32)
        acc[rows, HD:] += jnp.dot(p.astype(BF16), do, preferred_element_type=F32)
        return dq + jnp.dot(keys_t[:, rows], ds, preferred_element_type=F32)

    def one(i):
        chunk = 2 * i + at.c
        q, do = two_heads(r.q[i]), two_heads(r.do[i])
        args = (q, do, r.dots[i], r.lse[i] * (1.0 / math.log(2.0)), chunk, r.opening[i])
        if part == "own":
            start, stop = key_range(at.g, chunk, WIDE)
            r.dq_sum[i] = lax.fori_loop(start, stop, lambda t, dq: step(t, dq, *args), r.dq_sum[i])
        else:
            dq = r.dq_sum[i]
            for t in range(kv.shape[0] // WIDE):
                dq = step(t, dq, *args)
            r.dq_sum[i] = dq

    def end():
        out = getattr(r, "d_" + part)
        for t in range(out.shape[0] * 2):
            out[t // 2, t % 2, :, :HD] = (acc[t * CHUNK : (t + 1) * CHUNK, :HD] * SCALE).astype(BF16)
            out[t // 2, t % 2, :, HD:] = acc[t * CHUNK : (t + 1) * CHUNK, HD:].astype(BF16)

    count = SLOTS if part != "before" else SLOTS // 2
    if when is None:
        begin()
        paced(one, count, between)
        end()
    else:
        pl.when(when)(begin)
        paced(one, count, between, when)
        pl.when(when)(end)


def add_chunks(dst, first, other, skip=0):
    def one(i, carry):
        dst[i + skip] = (first(i).astype(F32) + other[i].astype(F32)).astype(BF16)
        return carry

    lax.fori_loop(0, other.shape[0], one, 0)


LATE = "late"


def kernel(collective_id, body, ins, outs, scratch):
    late = [name for name, (_, spec) in ins.items() if spec is LATE]
    scratch = {
        **scratch,
        **{name + "_late": pltpu.VMEM(ins[name][0].shape, ins[name][0].dtype) for name in late},
        **({"late": DMA((len(late),))} if late else {}),
    }
    ins = {name: (a, HBM if spec is LATE else spec) for name, (a, spec) in ins.items()}
    names = [*ins, *outs, *scratch]
    return dict(
        zip(
            outs,
            communicate(
                lambda *refs: body(types.SimpleNamespace(**dict(zip(names, refs)))),
                collective_id,
                tuple(a for a, _ in ins.values()),
                tuple(a for a, _ in outs.values()),
                list(scratch.values()),
                [spec for _, spec in ins.values()],
                [spec for _, spec in outs.values()],
            ),
        )
    )


def bring_late(r):
    copies = {}
    for k, name in enumerate([name for name in vars(r) if name.endswith("_late")]):
        name = name[: -len("_late")]
        here = getattr(r, name + "_late")
        copies[name] = pltpu.make_async_copy(getattr(r, name), here, r.late.at[k])
        copies[name].start()
        setattr(r, name, here)

    def wait(*some):
        for name in some or list(copies):
            copies.pop(name).wait()

    return wait


def back_block(groups, rows, ins):
    n = groups

    def body(r):
        at = Place(n)
        group = at.g
        bring_dx = pltpu.make_async_copy(r.part_dx, r.part, r.local.at[3])
        bring_dx.start()
        loaded = bring_late(r)
        meet(everyone(at))
        columns = columns_sum(at, r.g_gu, r.sib_gu, r.mid_gu, r.gu_sum, (r.cms, r.cmr, r.css, r.csr))
        next(columns)
        bring_dx.wait()
        bulk = in_turn((columns, r.cms.shape[1] * r.cms.shape[2] * (n - 1)))
        beside(scatter_tokens(at, r.part, r.land, r.dx, r.s1, r.r1), bulk)
        bring_out = pltpu.make_async_copy(r.part_out, r.part, r.local.at[3])
        bring_out.start()

        def norm(i, carry):
            rows = pl.ds(pl.multiple_of(i * 32, 32), 32)
            value = r.hidden[rows, :]
            inverse = lax.rsqrt(jnp.mean(value * value, 1, keepdims=True) + EPSILON)
            unit = value * inverse
            grad = r.dx[rows, :]
            total = r.cotangent[rows, :] + inverse * (grad - unit * jnp.mean(grad * unit, 1, keepdims=True))
            r.dhidden[rows, :] = total
            r.mine[rows, :] = total.astype(BF16)
            return carry

        lax.fori_loop(0, CHUNK // 32, norm, 0)
        beside(gather_tokens(at, r.mine, r.dbranch, r.local.at[0], r.s2, r.r2), bulk)
        bring_out.wait()
        result = scatter_tokens(at, r.part, r.land2, r.dx, r.s3, r.r3)
        next(result)

        loaded()

        def heads(i, carry):
            do = lax.dot_general(r.dbranch[i], r.w_out[...], NT, preferred_element_type=F32).astype(BF16)
            r.do[i] = do
            r.dots[i] = jnp.sum(two_heads(do).astype(F32).T * r.total[i], 0, keepdims=True)
            r.dq_sum[i] = jnp.zeros((HD, 2 * CHUNK), F32)
            return carry

        lax.fori_loop(0, SLOTS, heads, 0)

        def swap(array, place, i):
            return remote(array.at[:, 1 - at.c], place, r.ks.at[i], r.kr.at[i], at.sibling())

        def home(i):
            return remote(r.land_p, r.far_p.at[i - 1], r.ps, r.pr.at[i - 1], at.mid_at(jnp.int32(0)))

        def back():
            return remote(r.land_b, r.far_b, r.bs, r.br, at.mid_at(group - 1))

        def between():
            steps(bulk, 1)
            steps(result, 1)

        attention_back(at, r, "prompt", between, group > 0)

        @pl.when(group > 0)
        def _():
            swap(r.d_prompt, r.land_p, 1).start()

        if n > 2:
            attention_back(at, r, "before", between, group > 1)

            @pl.when(group > 1)
            def _():
                swap(r.d_before, r.land_b, 2).start()

        @pl.when(group > 0)
        def _():
            swap(r.d_prompt, r.land_p, 1).wait()
            add_chunks(r.land_p, lambda i: r.d_prompt[i, at.c], r.land_p)
            for i in range(1, n):

                @pl.when(group == i)
                def _():
                    home(i).start()

        if n > 2:

            @pl.when(group > 1)
            def _():
                swap(r.d_before, r.land_b, 2).wait()
                add_chunks(r.land_b, lambda i: r.d_before[i, at.c], r.land_b)
                back().start()

        attention_back(at, r, "own", between)
        first = swap(r.d_own, r.land_k, 0)
        first.start()
        drive(bulk)

        def queries(i, carry):
            r.dq[i] = two_columns((r.dq_sum[i].T * SCALE).astype(BF16))
            return carry

        lax.fori_loop(0, SLOTS, queries, 0)
        first.wait()
        add_chunks(r.dkv, lambda i: r.d_own[i, at.c], r.land_k)
        drive(result)

        def add(i, carry):
            rows = pl.ds(pl.multiple_of(i * 32, 32), 32)
            r.output[rows, :] = (r.hidden[rows, :] + r.dx[rows, :]).astype(BF16)
            return carry

        lax.fori_loop(0, CHUNK // 32, add, 0)

        @pl.when(group == 0)
        def _():
            for i in range(1, n):
                home(i).wait_recv()
                add_chunks(r.dkv, lambda j: r.dkv[j], r.far_p.at[i - 1])

        if n > 2:

            @pl.when((group >= 1) & (group < n - 1))
            def _():
                back().wait_recv()
                add_chunks(r.dkv, lambda j: r.dkv[j + SLOTS // 2], r.far_b, SLOTS // 2)

            @pl.when(group > 1)
            def _():
                back().wait_send()

        @pl.when(group > 0)
        def _():
            home(1).wait_send()

        drive(columns)

    chunks = (SLOTS, CHUNK, 2 * HD)
    block, end = (SLOTS, 2, CHUNK, 2 * HD), (SLOTS // 2, 2, CHUNK, 2 * HD)
    tok = DMA((len(PARTS), 7))
    near, half = pltpu.VMEM(chunks, BF16), pltpu.VMEM((SLOTS // 2, CHUNK, 2 * HD), BF16)
    own, prompt, before = 2 * SLOTS * CHUNK, PROMPT, LONGEST
    far = max(n - 1, 1)
    gu_pieces = 4 * (rows // piece_rows(rows))
    late = ("w_out", "q", "own", "prompt", "before", "total")
    return kernel(
        2,
        body,
        {
            name: (a, HBM if name in ("part_dx", "part_out") else LATE if name in late else VMEM)
            for name, a in ins.items()
        },
        {
            "dhidden": (like((CHUNK, D), F32), VMEM),
            "output": (like((CHUNK, D)), VMEM),
            "dbranch": (like((SLOTS, CHUNK, D)), VMEM),
            "dq": (like(chunks), VMEM),
            "dkv": (like(chunks), VMEM),
            "gu_sum": (like((2, 4, rows, GU_SLOT)), VMEM),
        },
        {
            "part": pltpu.VMEM((SLOTS, CHUNK, D), BF16),
            "land": pltpu.VMEM((7, CHUNK, D), BF16),
            "land2": pltpu.VMEM((7, CHUNK, D), BF16),
            "mine": pltpu.VMEM((CHUNK, D), BF16),
            "dx": pltpu.VMEM((CHUNK, D), F32),
            "sib_gu": pltpu.VMEM((2, 4 * n * rows, GU_SLOT), BF16),
            "mid_gu": pltpu.VMEM((far, 2, 4, rows, GU_SLOT), BF16),
            "do": near,
            "dots": pltpu.VMEM((SLOTS, 1, 2 * CHUNK), F32),
            "dq_sum": pltpu.VMEM((SLOTS, HD, 2 * CHUNK), F32),
            "own_kt": pltpu.VMEM((HD, own), BF16),
            "prompt_kt": pltpu.VMEM((HD, prompt), BF16),
            "before_kt": pltpu.VMEM((HD, before), BF16),
            "acc_own": pltpu.VMEM((own, 2 * HD), F32),
            "acc_prompt": pltpu.VMEM((prompt, 2 * HD), F32),
            "acc_before": pltpu.VMEM((before, 2 * HD), F32),
            "d_own": pltpu.VMEM(block, BF16),
            "d_prompt": pltpu.VMEM(block, BF16),
            "d_before": pltpu.VMEM(end, BF16),
            "land_k": near,
            "land_p": near,
            "land_b": half,
            "far_p": pltpu.VMEM((far, *chunks), BF16),
            "far_b": half,
            "local": DMA((4,)),
            **{name: tok for name in ("s1", "r1", "s2", "r2", "s3", "r3")},
            **{name: DMA((n, 2, gu_pieces)) for name in ("cms", "cmr")},
            **{name: DMA((2,)) for name in ("css", "csr")},
            **{name: DMA((3,)) for name in ("ks", "kr")},
            "ps": DMA(()),
            "pr": DMA((n,)),
            "bs": DMA(()),
            "br": DMA(()),
        },
    )


def last_block(groups, rows, hidden_rows, ins):
    n = groups
    gate_up = Columns.gate_up(groups, hidden_rows)
    count = len(gate_up(0, 0, 0))
    late = ("dbranch", "xhat_b", "qkv", "w_gu", "w_qkv")

    def unscale(dst, grad, weight, gain, d_gain):
        total = jnp.zeros((rows, 1), F32)
        for k in range(dst.shape[1] // 2048):
            cols = pl.ds(2048 * k, 2048)
            value = grad[:, cols].astype(F32)
            dst[:, cols] = value * gain[...]
            total = total + jnp.sum(value * weight[:, cols].astype(F32), 1, keepdims=True)
        d_gain[...] = total

    def body(r):
        at = Place(n)
        loaded = bring_late(r)
        meet(everyone(at) + [at.diagonal()])
        bring = columns_home(at, r.gu_sum, r.gu, gate_up, r.ds, r.dr, r.gu_local)
        next(bring)
        lower = turn_hidden(at, r.down_sum, r.down, r.hts, r.htr, r.local.at[0])
        next(lower)
        loaded("dbranch")
        turned = r.mixed[...].reshape(SLOTS * CHUNK, 2 * HD).T

        for k in range(D // 512):
            cols = pl.ds(512 * k, 512)
            r.g_out[:, cols] = jnp.dot(
                turned, r.dbranch[:, :, cols].reshape(SLOTS * CHUNK, 512), preferred_element_type=F32
            ).astype(BF16)
        heads = scatter_heads(at, r.g_out, r.out, r.sib_o, r.mid_o, (r.os, r.orr, r.oms, r.omr, r.oss, r.osr, r.local.at[1]))
        next(heads)
        r.gain_sum[...] = jnp.zeros_like(r.gain_sum)

        def through_heads(i, carry):
            two = pl.ds(pl.multiple_of(2 * i, 2), 2)
            cosine, sine = r.cosine[two].reshape(2 * CHUNK, HD), r.sine[two].reshape(2 * CHUNK, HD)
            raw = r.raw[two].reshape(2 * CHUNK, 3 * HD)
            dq, dkv = r.dq[two].reshape(2 * CHUNK, 2 * HD), r.dkv[two].reshape(2 * CHUNK, 2 * HD)
            parts = []
            for h in range(3):
                grad = (dq[:, h * HD : (h + 1) * HD] if h < 2 else dkv[:, :HD]).astype(F32)
                head = raw[:, h * HD : (h + 1) * HD]
                inverse = lax.rsqrt(jnp.mean(head * head, 1, keepdims=True) + EPSILON)
                unit = head * inverse
                back = grad * cosine + pltpu.roll(grad * sine, HD // 2, 1)
                at_row = 0 if h < 2 else 1
                r.gain_sum[at_row : at_row + 1, :] += jnp.sum(back * unit, 0, keepdims=True)
                back = back * r.head_gain[h : h + 1, :]
                parts.append((inverse * (back - unit * jnp.mean(back * unit, 1, keepdims=True))).astype(BF16))
            draw = jnp.concatenate(parts + [dkv[:, HD:]], 1)
            r.draw[two] = draw.reshape(2, CHUNK, QKV_SLOT)
            return carry

        lax.fori_loop(0, SLOTS // 2, through_heads, 0)
        next(heads)
        sums = sum_everywhere(at, r.gain_sum, r.gain_land, r.gs, r.gr)
        loaded()
        for h in range(QKV_SLOT // HD):
            steps(sums, 1)
            cols = pl.ds(h * HD, HD)
            turned = r.draw[:, :, cols].reshape(SLOTS * CHUNK, HD).T
            grad = jnp.dot(turned, r.xhat_b[...].reshape(SLOTS * CHUNK, D), preferred_element_type=F32)
            r.g_qkv[:, cols] = grad.astype(BF16).T
        wide = columns_sum(at, r.g_qkv, r.sib_q, r.mid_q, r.fin_q, (r.cms, r.cmr, r.css, r.csr), 4)
        next(wide)

        def part_dx(i, carry):
            two = pl.ds(pl.multiple_of(2 * i, 2), 2)
            grad = lax.dot_general(
                r.draw[two].reshape(2 * CHUNK, QKV_SLOT), r.qkv[...], NT, preferred_element_type=F32
            )
            r.part[two] = grad.astype(BF16).reshape(2, CHUNK, D)
            return carry

        lax.fori_loop(0, SLOTS // 2, part_dx, 0)
        steps(wide, 1)
        bulk = in_turn((wide, 2 * (rows // piece_rows(rows)) * (n - 1) - 1))
        main = scatter_tokens(at, r.part, r.land, r.dx, r.s1, r.r1)
        for _ in range(4):
            next(main)
            steps(bulk, 1)
        drive(bring)
        unscale(r.d_gu, r.gu, r.w_gu, r.gain_two, r.d_gain_two)
        next(heads)
        beside(main, bulk)

        def norm(i, carry):
            rows = pl.ds(pl.multiple_of(i * 32, 32), 32)
            value = r.tokens[rows, :].astype(F32)
            inverse = lax.rsqrt(jnp.mean(value * value, 1, keepdims=True) + EPSILON)
            unit = value * inverse
            grad = r.dx[rows, :]
            r.d_tokens[rows, :] = r.dhidden[rows, :] + inverse * (grad - unit * jnp.mean(grad * unit, 1, keepdims=True))
            return carry

        lax.fori_loop(0, CHUNK // 32, norm, 0)
        drive(wide)
        home = columns_home(at, r.fin_q, r.qkv_rows, Columns.qkv, r.cs, r.cr, r.qkv_local)
        next(home)
        drive(lower)

        def lower_out(i, carry):
            rows_i = pl.ds(pl.multiple_of(i * 16, 16), 16)
            r.d_down[rows_i, :] = r.down[rows_i, :].astype(F32)
            return carry

        lax.fori_loop(0, hidden_rows // 16, lower_out, 0)
        drive(bulk, sums, heads)
        r.d_out[...] = r.out[...].astype(F32)
        drive(home)
        unscale(r.d_qkv, r.qkv_rows, r.w_qkv, r.gain_one, r.d_gain_one)

    deep = 4 * n * rows
    far = max(n - 1, 1)
    return kernel(
        3,
        body,
        {name: (a, HBM if name in ("gu_sum", "down_sum") else LATE if name in late else VMEM) for name, a in ins.items()},
        {
            "d_gu": (like((rows, 2 * FF), F32), VMEM),
            "d_tokens": (like((CHUNK, D), F32), VMEM),
            "d_qkv": (like((rows, (HQ + 2 * HK) * HD), F32), VMEM),
            "d_out": (like((rows, D), F32), VMEM),
            "d_down": (like((hidden_rows, D), F32), VMEM),
            "d_gain_one": (like((rows, 1), F32), VMEM),
            "d_gain_two": (like((rows, 1), F32), VMEM),
            "gain_sum": (like((8, HD), F32), VMEM),
        },
        {
            "gu": pltpu.VMEM((rows, 2 * FF), BF16),
            "qkv_rows": pltpu.VMEM((rows, (HQ + 2 * HK) * HD), BF16),
            "out": pltpu.VMEM((rows, D), BF16),
            "down": pltpu.VMEM((hidden_rows, D), BF16),
            **{name: DMA(()) for name in ("hts", "htr")},
            "part": pltpu.VMEM((SLOTS, CHUNK, D), BF16),
            "land": pltpu.VMEM((7, CHUNK, D), BF16),
            "dx": pltpu.VMEM((CHUNK, D), F32),
            "draw": pltpu.VMEM((SLOTS, CHUNK, QKV_SLOT), BF16),
            "g_qkv": pltpu.VMEM((D, QKV_SLOT), BF16),
            "sib_q": pltpu.VMEM((2, deep, QKV_SLOT), BF16),
            "mid_q": pltpu.VMEM((far, 2, 4, rows, QKV_SLOT), BF16),
            "fin_q": pltpu.VMEM((2, 4, rows, QKV_SLOT), BF16),
            "g_out": pltpu.VMEM((D // SLOTS, D), BF16),
            "sib_o": pltpu.VMEM((D // SLOTS, D), BF16),
            "mid_o": pltpu.VMEM((far, 4 * rows, D), BF16),
            "gain_land": pltpu.VMEM((4 + n, 8, HD), F32),
            "local": DMA((2,)),
            **{name: DMA((len(PARTS), 7)) for name in ("s1", "r1")},
            **{name: DMA((7, 3)) for name in ("cs", "cr")},
            "qkv_local": DMA((3,)),
            **{name: DMA((7, count)) for name in ("ds", "dr")},
            "gu_local": DMA((count,)),
            **{name: DMA((n, 2, 4 * (rows // piece_rows(rows)))) for name in ("cms", "cmr")},
            **{name: DMA((2,)) for name in ("css", "csr")},
            "os": DMA((4,)),
            **{name: DMA(()) for name in ("orr", "oss", "osr")},
            **{name: DMA((n,)) for name in ("oms", "omr")},
            **{name: DMA((4 + n,)) for name in ("gs", "gr")},
        },
    )


def dot(a, b, dims=((1,), (0,))):
    return lax.dot_general(a, b, (dims, ((), ())), preferred_element_type=F32)


def body(tokens, lengths, attn_gain, w_qkv, q_gain, k_gain, w_out, mlp_gain, w_gate_up, w_down, cotangent):
    blocks = lax.axis_size("blk")
    groups = blocks // 4
    rows = w_qkv.shape[0]
    hidden_rows = w_down.shape[0]
    group = lax.axis_index("blk") // 4
    core = lax.axis_index("uly") % 2
    gain_one = attn_gain.astype(F32)[:, None]
    gain_two = mlp_gain.astype(F32)[:, None]

    direct = (2 * hidden_rows) % 128 == 0
    w_gu = w_gate_up
    if not direct:
        w_gu = (
            w_gate_up.reshape(rows, 2, 2, 2, groups, 2, 2 * hidden_rows)
            .transpose(0, 2, 5, 3, 1, 4, 6)
            .reshape(rows, 2 * FF)
        )

    starts = PROMPT + jnp.sum(
        jnp.where(jnp.arange(lengths.shape[0])[:, None] > jnp.arange(lengths.shape[0])[None, :], lengths[None, :], 0), 1
    )
    index = (
        group * (2 * SLOTS * CHUNK)
        + (2 * jnp.arange(SLOTS, dtype=jnp.int32)[:, None] + core) * CHUNK
        + jnp.arange(CHUNK, dtype=jnp.int32)[None, :]
    )
    opening = jnp.max(jnp.where(index[..., None] >= starts, starts, 0), -1)
    position = jnp.where(index < PROMPT, index, index - opening + PROMPT)
    opening = opening - group * (2 * SLOTS * CHUNK)
    opening = jnp.concatenate([opening, opening], 1)[:, None, :]
    lane = np.arange(HD)
    angles = position.astype(F32)[:, :, None] * (ROPE_BASE ** (-2.0 * jnp.asarray(lane % (HD // 2), F32) / HD))
    cosine, sine = jnp.cos(angles), jnp.sin(angles) * np.where(lane < HD // 2, -1.0, 1.0).astype(np.float32)
    head_gain = jnp.stack([q_gain, q_gain, k_gain]).astype(F32)

    front = front_block(
        groups,
        rows,
        hidden_rows,
        {
            "tokens": tokens,
            "cotangent": cotangent,
            "w_qkv": w_qkv,
            "w_gu": w_gu,
            "gain_one": gain_one,
            "gain_two": gain_two,
            "opening": opening,
            "cosine": cosine,
            "sine": sine,
            "head_gain": head_gain,
            "down_mine": w_down,
            "out_mine": w_out,
        },
    )
    xhat2_b, dy_b = (front[name].reshape(SLOTS * CHUNK, D) for name in ("xhat2_b", "dy_b"))
    own, prompt, before = (front[name].reshape(-1, 2 * HD) for name in ("own", "prompt", "before"))
    gu_w, down_w = front["gu"], front["down"].reshape(FF_SLOT, D)

    both = dot(xhat2_b, gu_w)
    gate, up = both[:, :FF_SLOT], both[:, FF_SLOT:]
    sigmoid = jax.nn.sigmoid(gate)
    act = (gate * sigmoid * up).astype(BF16)
    part_out = dot(act, down_w).astype(BF16)
    g_down = dot(act, dy_b, ((0,), (0,))).astype(BF16)
    g_down = g_down.reshape(groups, 2, hidden_rows, D)
    theirs = lax.ppermute(
        lax.dynamic_index_in_dim(g_down, 1 - core, 1, keepdims=False), "uly", [(u, u + 1 - 2 * (u % 2)) for u in range(4)]
    )
    down_core = lax.dynamic_index_in_dim(g_down, core, 1, keepdims=False).astype(F32) + theirs.astype(F32)
    down_core, dy_b = lax.optimization_barrier((down_core.astype(BF16), dy_b))
    down_sum = lax.dynamic_index_in_dim(down_core, group, 0, keepdims=False).astype(F32)
    for i in range(1, groups):
        there = lax.dynamic_index_in_dim(down_core, (group + i) % groups, 0, keepdims=False)
        there = lax.ppermute(there, "blk", [(b, (b + 4 * i) % blocks) for b in range(blocks)])
        down_sum = down_sum + there.astype(F32)
    down_sum = down_sum.astype(BF16)
    dact = dot(dy_b, down_w, ((1,), (1,)))
    dboth = jnp.concatenate(
        [dact * up * sigmoid * (1.0 + gate * (1.0 - sigmoid)), dact * gate * sigmoid], 1
    ).astype(BF16)
    g_gu = dot(xhat2_b, dboth, ((0,), (0,))).astype(BF16)
    part_dx2 = dot(dboth, gu_w, ((1,), (1,))).astype(BF16)
    back = back_block(
        groups,
        rows,
        {
            "part_dx": part_dx2.reshape(SLOTS, CHUNK, D),
            "part_out": part_out.reshape(SLOTS, CHUNK, D),
            "hidden": front["hidden"],
            "cotangent": cotangent,
            "g_gu": g_gu,
            "w_out": front["w_out"],
            "q": front["q"],
            "own": own,
            "prompt": prompt,
            "before": before,
            "opening": opening,
            "total": front["total"],
            "lse": front["lse"],
        },
    )
    last = last_block(
        groups,
        rows,
        hidden_rows,
        {
            "gu_sum": back["gu_sum"],
            "down_sum": down_sum,
            "w_qkv": w_qkv,
            "w_gu": w_gu,
            "gain_one": gain_one,
            "gain_two": gain_two,
            "dq": back["dq"],
            "dkv": back["dkv"],
            "raw": front["raw"],
            "cosine": cosine,
            "sine": sine,
            "head_gain": head_gain,
            "xhat_b": front["xhat_b"],
            "qkv": front["qkv"],
            "mixed": front["mixed"],
            "dbranch": back["dbranch"],
            "tokens": tokens,
            "dhidden": back["dhidden"],
        },
    )
    d_gu = last["d_gu"]
    if not direct:
        d_gu = (
            d_gu.reshape(rows, 2, 2, 2, 2, groups, 2 * hidden_rows)
            .transpose(0, 4, 1, 3, 5, 2, 6)
            .reshape(rows, 2 * FF)
        )
    return (
        back["output"],
        last["d_tokens"],
        last["d_gain_one"][:, 0],
        last["d_qkv"],
        last["gain_sum"][0],
        last["gain_sum"][1],
        last["d_out"],
        last["d_gain_two"][:, 0],
        d_gu,
        last["d_down"],
    )


def solution(mesh):
    tokens = P(("blk", "uly"), None)
    weight = P(("uly", "blk"), None)
    gain = P(("uly", "blk"))
    return jax.shard_map(
        body,
        mesh=mesh,
        in_specs=(tokens, P(), gain, weight, P(), P(), weight, gain, weight, weight, tokens),
        out_specs=(tokens, tokens, gain, weight, P(), P(), weight, gain, weight, weight),
        check_vma=False,
    )
```

```python
import math
import types

import jax
import jax.numpy as jnp
import numpy as np
from jax import lax
from jax.experimental import pallas as pl
from jax.experimental.pallas import tpu as pltpu
from jax.sharding import PartitionSpec as P

D = 2048
HQ = 16
HK = 8
HD = 128
FF = 6144
PROMPT = 2048
LONGEST = 1024

SLOTS = 8
CHUNK = 128
QKV_SLOT = 512
GU_SLOT = 2 * FF // SLOTS
FF_SLOT = FF // SLOTS
EPSILON = 1e-06
ROPE_BASE = 1000000.0
SCALE = 1.0 / math.sqrt(HD)
WINDOW = 10

F32 = jnp.float32
BF16 = jnp.bfloat16
MESH = pl.DeviceIdType.MESH
HBM = pl.BlockSpec(memory_space=pl.ANY)
VMEM = pl.BlockSpec(memory_space=pltpu.VMEM)
DMA = pltpu.SemaphoreType.DMA
PARTS = ((0, 1, 2), 384), ((1, 2, 0), 768), ((2, 0, 1), 896)
FRONT = ((0, 1, 2), 256), ((1, 2, 0), 768), ((2, 0, 1), 1024)


def rem(a, n):
    return lax.rem(a, jnp.int32(n))


class Place:
    def __init__(self, groups):
        self.groups = groups
        self.u = lax.axis_index("uly")
        self.b = lax.axis_index("blk")
        self.x = self.u // 2
        self.c = rem(self.u, 2)
        self.g = self.b // 4
        self.bl = rem(self.b, 4)
        self.bits = (self.x, rem(self.bl, 2), self.bl // 2)

    def flip(self, *dims):
        x, y, z = (rem(v + 1, 2) if d in dims else v for d, v in enumerate(self.bits))
        return x, 2 * z + y

    def coords(self, *dims):
        return [rem(v + 1, 2) if d in dims else v for d, v in enumerate(self.bits)]

    def chunk(self, *dims):
        x, bl = self.flip(*dims)
        return 2 * bl + x

    def slot(self, *dims):
        x, bl = self.flip(*dims)
        return 4 * x + bl

    def cube(self, *dims):
        x, bl = self.flip(*dims)
        return (2 * x + self.c, 4 * self.g + bl)

    def sibling(self):
        return (2 * self.x + 1 - self.c, self.b)

    def ahead(self, i):
        return rem(self.g + i, self.groups)

    def behind(self, i):
        return rem(self.g + self.groups - i, self.groups)

    def mid(self, i):
        return (self.u, 4 * self.ahead(i) + self.bl)

    def diagonal(self):
        x, y, z = self.bits
        return (2 * x + 1 - self.c, 4 * self.g + 2 * z + 1 - y)

    def mid_at(self, group):
        return (self.u, 4 * group + self.bl)


PEERS = ((0,), (1,), (2,), (0, 1), (0, 2), (1, 2), (0, 1, 2))


def meet(devices):
    barrier = pltpu.get_barrier_semaphore()
    for device in devices:
        pl.semaphore_signal(barrier, inc=1, device_id=device, device_id_type=MESH)
    pl.semaphore_wait(barrier, len(devices))


def remote(src, dst, send, recv, device):
    return pltpu.make_async_remote_copy(
        src_ref=src, dst_ref=dst, send_sem=send, recv_sem=recv, device_id=device, device_id_type=MESH
    )


def rows_at(start, count):
    return pl.ds(pl.multiple_of(start, 16), count)


def drive(*tasks):
    tasks = list(tasks)
    while tasks:
        tasks = [task for task in tasks if next(task, None) is not None]


def steps(task, count):
    for _ in range(count):
        next(task, None)


def paced(loop, count, between, when=None):
    def one(i, carry):
        loop(i)
        return carry

    for k in range(4):
        run = (k * count // 4, (k + 1) * count // 4)
        if when is None:
            lax.fori_loop(*run, one, 0)
        else:

            @pl.when(when)
            def _():
                lax.fori_loop(*run, one, 0)

        between()


def piece_rows(rows):
    return 32 if rows % 32 == 0 else 16


def beside(main, *bulk):
    for _ in main:
        for task in bulk:
            next(task, None)


def in_turn(*tasks):
    for task, count in tasks:
        for _ in range(count):
            next(task, None)
            yield True


def part_columns(split):
    start = 0
    for p, (order, width) in enumerate(split):
        yield p, order, pl.ds(start, width)
        start += width


def gather_tokens(at, mine, block, local, send, recv, split=None):
    own = pltpu.make_async_copy(mine, block.at[at.chunk()], local)
    own.start()
    sent = []

    def push(p, i, dims, along, cols):
        src = block.at[at.chunk(*dims), :, cols] if dims else mine.at[:, cols]
        copy = remote(src, block.at[at.chunk(*dims), :, cols], send.at[p, i], recv.at[p, i], at.cube(along))
        copy.start()
        sent.append(copy)

    def arrive(p, i, dims, cols):
        there = block.at[at.chunk(*dims), :, cols]
        remote(there, there, send.at[p, i], recv.at[p, i], at.cube(dims[0])).wait_recv()

    parts = list(part_columns(split or PARTS))
    over = [sorted(parts, key=lambda part: part[1][k] == 2) for k in range(3)]
    for p, (a, b, c), cols in parts:
        push(p, 0, (), a, cols)
        push(p, 1, (), b, cols)
        push(p, 2, (), c, cols)
    yield True
    for p, (a, b, c), cols in over[0]:
        arrive(p, 0, (a,), cols)
        push(p, 3, (a,), b, cols)
        push(p, 4, (a,), c, cols)
        yield True
    for p, (a, b, c), cols in over[1]:
        arrive(p, 1, (b,), cols)
        push(p, 5, (b,), c, cols)
        arrive(p, 3, (a, b), cols)
        push(p, 6, (a, b), c, cols)
        yield True
    for p, (a, b, c), cols in parts:
        arrive(p, 2, (c,), cols)
        arrive(p, 4, (a, c), cols)
        arrive(p, 5, (b, c), cols)
        arrive(p, 6, (a, b, c), cols)
    for copy in sent:
        copy.wait_send()
    own.wait()


def add_rows(dst, terms, count, step=32):
    def body(i, carry):
        rows = pl.ds(pl.multiple_of(i * step, step), step)
        total = terms[0][rows, :].astype(F32)
        for term in terms[1:]:
            total = total + term[rows, :].astype(F32)
        dst[rows, :] = total.astype(dst.dtype)
        return carry

    lax.fori_loop(0, count // step, body, 0)


def scatter_tokens(at, part, land, out, send, recv, split=None):
    sent = []

    def push(p, i, dims, along, cols):
        copy = remote(part.at[at.chunk(*dims), :, cols], land.at[i, :, cols], send.at[p, i], recv.at[p, i], at.cube(along))
        copy.start()
        sent.append(copy)

    def arrive(p, i, along, cols):
        remote(land.at[i, :, cols], land.at[i, :, cols], send.at[p, i], recv.at[p, i], at.cube(along)).wait_recv()

    def add(i, dims, cols):
        here = part.at[at.chunk(*dims), :, cols]
        add_rows(here, [here, land.at[i, :, cols]], CHUNK)

    parts = list(part_columns(split or PARTS))
    over = [sorted(parts, key=lambda part: part[1][k] == 2) for k in range(3)]
    for p, (a, b, c), cols in parts:
        push(p, 3, (a, b, c), c, cols)
        push(p, 2, (b, c), c, cols)
    for p, (a, b, c), cols in parts:
        push(p, 1, (a, c), c, cols)
        push(p, 0, (c,), c, cols)
    yield True
    for p, (a, b, c), cols in over[2]:
        arrive(p, 3, c, cols)
        add(3, (a, b), cols)
        push(p, 5, (a, b), b, cols)
        arrive(p, 2, c, cols)
        add(2, (b,), cols)
        push(p, 4, (b,), b, cols)
        yield True
    for p, (a, b, c), cols in over[1]:
        arrive(p, 1, c, cols)
        add(1, (a,), cols)
        arrive(p, 5, b, cols)
        add(5, (a,), cols)
        push(p, 6, (a,), a, cols)
        yield True
    for p, (a, b, c), cols in over[0]:
        arrive(p, 0, c, cols)
        arrive(p, 4, b, cols)
        arrive(p, 6, a, cols)
        add_rows(
            out.at[:, cols],
            [part.at[at.chunk(), :, cols], land.at[0, :, cols], land.at[4, :, cols], land.at[6, :, cols]],
            CHUNK,
        )
    for copy in sent:
        copy.wait_send()


def column_row(at, rows, u, b):
    return (u * (4 * at.groups) + b) * rows


class Columns:
    def qkv(x, y, z):
        pair = 4 * x + 2 * y + z
        return [(pair * (2 * HD), 2 * HD), (HQ * HD + pair * HD, HD), ((HQ + HK) * HD + pair * HD, HD)]

    def gate_up(groups, hidden_rows):
        wide = 2 * hidden_rows
        if wide % 128:
            return lambda x, y, z: [((4 * x + 2 * z + y) * GU_SLOT, GU_SLOT)]

        def runs(x, y, z):
            return [
                (half * FF + (((2 * x + y) * groups + group) * 2 + z) * wide, wide)
                for half in range(2)
                for group in range(groups)
            ]

        return runs


def column_runs(ref, whole, runs):
    at = 0
    for first, width in runs:
        yield ref.at[:, pl.ds(pl.multiple_of(first, 128), width)], whole.at[:, pl.ds(at, width)]
        at += width


def columns_in_cube(at, mine, whole, runs, local, send, recv, rows):
    own = rows_at(column_row(at, rows, at.u, at.b), rows)
    here = []
    for k, (src, dst) in enumerate(column_runs(mine, whole.at[own], runs(*at.coords()))):
        here.append(pltpu.make_async_copy(src, dst, local.at[k]))
        here[-1].start()
    sent = []
    for i, dims in enumerate(PEERS):
        for k, (src, dst) in enumerate(column_runs(mine, whole.at[own], runs(*at.coords(*dims)))):
            copy = remote(src, dst, send.at[i, k], recv.at[i, k], at.cube(*dims))
            copy.start()
            sent.append(copy)
    yield True
    for i, dims in enumerate(PEERS):
        u, b = at.cube(*dims)
        there = whole.at[rows_at(column_row(at, rows, u, b), rows)]
        for k, (_, dst) in enumerate(column_runs(mine, there, runs(*at.coords()))):
            remote(dst, dst, send.at[i, k], recv.at[i, k], (u, b)).wait_recv()
    for copy in sent:
        copy.wait_send()
    for copy in here:
        copy.wait()


def columns_across(at, whole, rows, mid_send, mid_recv, sib_send, sib_recv):
    n, pieces = at.groups, mid_send.shape[2]
    step = 4 * rows // pieces
    sent = []

    def piece(core, group, x, k):
        return whole.at[rows_at(column_row(at, rows, 2 * x + core, 4 * group) + k * step, step)]

    def pass_on(i, x, k):
        there = piece(at.c, at.behind(i), x, k)
        copy = remote(there, there, sib_send.at[i, x, k], sib_recv.at[i, x, k], at.sibling())
        copy.start()
        sent.append(copy)

    order = [(x, k) for x in range(2) for k in range(pieces)]
    every = [(i, x, k) for i in range(1, n) for x, k in order]

    def arrived(i, x, k):
        there = piece(at.c, at.behind(i), x, k)
        remote(there, there, mid_send.at[i, x, k], mid_recv.at[i, x, k], at.mid(i)).wait_recv()
        pass_on(i, x, k)

    for m, (i, x, k) in enumerate(every):
        there = piece(at.c, at.g, x, k)
        copy = remote(there, there, mid_send.at[i, x, k], mid_recv.at[i, x, k], at.mid(i))
        copy.start()
        sent.append(copy)
        if i == 1:
            pass_on(0, x, k)
        if m >= WINDOW:
            arrived(*every[m - WINDOW])
        yield True
    for one in every[max(len(every) - WINDOW, 0) :]:
        arrived(*one)
    for i in range(n):
        for x, k in order:
            there = piece(1 - at.c, at.behind(i), x, k)
            remote(there, there, sib_send.at[i, x, k], sib_recv.at[i, x, k], at.sibling()).wait_recv()
    for copy in sent:
        copy.wait_send()


def gather_hidden(at, mine, whole, local, turn_send, turn_recv, mid_send, mid_recv, sib_send, sib_recv):
    n, rows, pieces = at.groups, mine.shape[0], mid_send.shape[1]
    step = rows // pieces
    own = whole.at[at.g, at.c]
    stays = at.bits[1] == at.c
    here = pltpu.make_async_copy(mine, own, local)
    there = remote(mine, whole.at[at.g, 1 - at.c], turn_send, turn_recv, at.diagonal())

    @pl.when(stays)
    def _():
        here.start()

    @pl.when(jnp.logical_not(stays))
    def _():
        there.start()

    yield True

    @pl.when(stays)
    def _():
        here.wait()

    @pl.when(jnp.logical_not(stays))
    def _():
        there.wait()

    sent = []
    for i in range(1, n):
        for k in range(pieces):
            piece = own.at[pl.ds(k * step, step)]
            copy = remote(piece, piece, mid_send.at[i, k], mid_recv.at[i, k], at.mid(i))
            copy.start()
            sent.append(copy)
            yield True

    def pass_on(i):
        group = whole.at[at.behind(i), at.c]
        copy = remote(group, group, sib_send.at[i], sib_recv.at[i], at.sibling())
        copy.start()
        sent.append(copy)

    pass_on(0)
    for i in range(1, n):
        for k in range(pieces):
            piece = whole.at[at.behind(i), at.c, pl.ds(k * step, step)]
            remote(piece, piece, mid_send.at[i, k], mid_recv.at[i, k], at.mid(i)).wait_recv()
        pass_on(i)
    for i in range(n):
        group = whole.at[at.behind(i), 1 - at.c]
        remote(group, group, sib_send.at[i], sib_recv.at[i], at.sibling()).wait_recv()
    for copy in sent:
        copy.wait_send()


class OutRows:
    def __init__(self, at, rows):
        self.at, self.rows = at, rows
        self.per_half = max(at.groups // 2, 1)
        self.my_half = at.g // self.per_half
        self.to = 2 * self.my_half + at.c
        self.collects = at.bl == self.to
        self.slot_core = rem(at.bl, 2) == at.c
        self.slot_half = at.bl // 2

    def group_rows(self, group, half):
        return rows_at((group - half * self.per_half) * (4 * self.rows), 4 * self.rows)

    def in_half(self, group, half):
        return group // self.per_half == half

    def device(self, bl):
        return (self.at.u, 4 * self.at.g + bl)


def gather_heads(at, mine, whole, local, send, recv, sib_send, sib_recv):
    n, rows = mine.shape[0], mine.shape[1]
    lay = OutRows(at, rows)

    def place(group, bl):
        half = group // lay.per_half
        return whole.at[rows_at(((group - half * lay.per_half) * 4 + bl) * rows, rows)]

    def push(i):
        group = at.behind(i)
        to = 2 * (group // lay.per_half) + at.c
        here = pltpu.make_async_copy(mine.at[i], place(group, at.bl), local.at[i])
        there = remote(mine.at[i], place(group, at.bl), send.at[i], recv.at[i, at.bl], lay.device(to))
        return at.bl == to, here, there

    for i in range(n):
        stays, here, there = push(i)

        @pl.when(stays)
        def _():
            here.start()

        @pl.when(jnp.logical_not(stays))
        def _():
            there.start()

    yield True

    @pl.when(lay.slot_core)
    def _():
        for i in range(n):
            group = at.behind(i)

            @pl.when(lay.in_half(group, lay.slot_half))
            def _():
                pltpu.make_async_copy(mine.at[i], place(group, at.bl), local.at[i]).wait()
                for bl in range(4):

                    @pl.when(at.bl != bl)
                    def _():
                        there = place(group, bl)
                        remote(there, there, send.at[i], recv.at[i, bl], lay.device(bl)).wait_recv()

        remote(whole, whole, sib_send, sib_recv, at.sibling()).start()

    yield True

    @pl.when(lay.slot_core)
    def _():
        remote(whole, whole, sib_send, sib_recv, at.sibling()).wait_send()

    @pl.when(jnp.logical_not(lay.slot_core))
    def _():
        remote(whole, whole, sib_send, sib_recv, at.sibling()).wait_recv()

    for i in range(n):
        stays, here, there = push(i)

        @pl.when(jnp.logical_not(stays))
        def _():
            there.wait_send()


def columns_home(at, final, out, runs, send, recv, local):
    sent = []
    for i, dims in enumerate(PEERS):
        x, bl = at.flip(*dims)
        for k, (dst, src) in enumerate(column_runs(out, final.at[x, bl], runs(*at.coords()))):
            copy = remote(src, dst, send.at[i, k], recv.at[i, k], at.cube(*dims))
            copy.start()
            sent.append(copy)
    here = []
    for k, (dst, src) in enumerate(column_runs(out, final.at[at.x, at.bl], runs(*at.coords()))):
        here.append(pltpu.make_async_copy(src, dst, local.at[k]))
        here[-1].start()
    yield True
    for i, dims in enumerate(PEERS):
        for k, (there, _) in enumerate(column_runs(out, final.at[at.x, at.bl], runs(*at.coords(*dims)))):
            remote(there, there, send.at[i, k], recv.at[i, k], at.cube(*dims)).wait_recv()
    for copy in sent:
        copy.wait_send()
    for copy in here:
        copy.wait()


def columns_sum(at, part, sib_land, mid_land, final, sems, at_once=1):
    n, rows = at.groups, final.shape[2]
    mid_send, mid_recv, sib_send, sib_recv = sems
    run, deep = 4 * rows, 4 * n * rows
    step = piece_rows(rows)
    pieces = [(k, j) for k in range(4) for j in range(rows // step)]
    sent = []

    def of_core(x, core):
        return part.at[rows_at((2 * x + core) * deep, deep)]

    for x in range(2):
        copy = remote(of_core(x, 1 - at.c), sib_land.at[x], sib_send.at[x], sib_recv.at[x], at.sibling())
        copy.start()
        sent.append(copy)
    yield True
    for x in range(2):
        remote(sib_land.at[x], sib_land.at[x], sib_send.at[x], sib_recv.at[x], at.sibling()).wait_recv()
        for i in range(1, n):
            for m, (k, j) in enumerate(pieces):
                offset = at.ahead(i) * run + k * rows + j * step
                there = part.at[rows_at((2 * x + at.c) * deep + offset, step)]
                add_rows(there, [there, sib_land.at[x, rows_at(offset, step)]], step, 16)
                land = mid_land.at[i - 1, x, k, pl.ds(j * step, step)]
                copy = remote(there, land, mid_send.at[i, x, m], mid_recv.at[i, x, m], at.mid(i))
                copy.start()
                sent.append(copy)
                if m % at_once == at_once - 1:
                    yield True
    for x in range(2):
        for m, (k, j) in enumerate(pieces):
            for i in range(1, n):
                there = mid_land.at[i - 1, x, k, pl.ds(j * step, step)]
                remote(there, there, mid_send.at[i, x, m], mid_recv.at[i, x, m], at.mid(i)).wait_recv()
            offset = at.g * run + k * rows + j * step
            rows_here = pl.ds(j * step, step)
            add_rows(
                final.at[x, k, rows_here],
                [part.at[rows_at((2 * x + at.c) * deep + offset, step)], sib_land.at[x, rows_at(offset, step)]]
                + [mid_land.at[i - 1, x, k, rows_here] for i in range(1, n)],
                step,
                16,
            )
    for copy in sent:
        copy.wait_send()


def turn_hidden(at, final, out, turn_send, turn_recv, local):
    stays = at.bits[1] == at.c
    here = pltpu.make_async_copy(final, out, local)
    there = remote(final, out, turn_send, turn_recv, at.diagonal())

    @pl.when(stays)
    def _():
        here.start()

    @pl.when(jnp.logical_not(stays))
    def _():
        there.start()

    yield True

    @pl.when(stays)
    def _():
        here.wait()

    @pl.when(jnp.logical_not(stays))
    def _():
        there.wait()


def scatter_heads(at, part, out, sib_land, mid_land, sems):
    n, rows = at.groups, out.shape[0]
    send, recv, mid_send, mid_recv, sib_send, sib_recv, local = sems
    lay = OutRows(at, rows)

    @pl.when(jnp.logical_not(lay.slot_core))
    def _():
        remote(part, sib_land, sib_send, sib_recv, at.sibling()).start()

    yield True

    @pl.when(lay.slot_core)
    def _():
        remote(part, sib_land, sib_send, sib_recv, at.sibling()).wait_recv()
        add_rows(part, [part, sib_land], 256, 16)
        for i in range(1, n):
            group = at.ahead(i)

            @pl.when(lay.in_half(group, lay.slot_half))
            def _():
                there = part.at[lay.group_rows(group, lay.slot_half)]
                remote(there, mid_land.at[i - 1], mid_send.at[i], mid_recv.at[i], at.mid(i)).start()

    yield True
    mine = part.at[lay.group_rows(at.g, lay.my_half)]
    base = (at.g - lay.my_half * lay.per_half) * (4 * rows)

    @pl.when(lay.collects)
    def _():
        for i in range(1, n):
            remote(mine, mid_land.at[i - 1], mid_send.at[i], mid_recv.at[i], at.mid(i)).wait_recv()
        add_rows(mine, [mine] + [mid_land.at[i - 1] for i in range(1, n)], 4 * rows, 16)
        for bl in range(4):
            there = part.at[rows_at(base + bl * rows, rows)]

            @pl.when(at.bl != bl)
            def _():
                remote(there, out, send.at[bl], recv, lay.device(bl)).start()

            @pl.when(at.bl == bl)
            def _():
                pltpu.make_async_copy(there, out, local).start()

    yield True

    @pl.when(jnp.logical_not(lay.collects))
    def _():
        remote(out, out, send.at[0], recv, lay.device(lay.to)).wait_recv()

    @pl.when(lay.collects)
    def _():
        for bl in range(4):
            there = part.at[rows_at(base + bl * rows, rows)]

            @pl.when(at.bl != bl)
            def _():
                remote(there, out, send.at[bl], recv, lay.device(bl)).wait_send()

            @pl.when(at.bl == bl)
            def _():
                pltpu.make_async_copy(there, out, local).wait()

    @pl.when(jnp.logical_not(lay.slot_core))
    def _():
        remote(part, sib_land, sib_send, sib_recv, at.sibling()).wait_send()

    @pl.when(lay.slot_core)
    def _():
        for i in range(1, n):
            group = at.ahead(i)

            @pl.when(lay.in_half(group, lay.slot_half))
            def _():
                there = part.at[lay.group_rows(group, lay.slot_half)]
                remote(there, mid_land.at[i - 1], mid_send.at[i], mid_recv.at[i], at.mid(i)).wait_send()


def sum_everywhere(at, mine, land, send, recv):
    for i, device in enumerate([at.sibling(), at.cube(0), at.cube(1), at.cube(2)]):
        copy = remote(mine, land.at[i], send.at[i], recv.at[i], device)
        copy.start()
        yield True
        copy.wait()
        mine[...] = mine[...] + land[i]
    sent = []
    for i in range(1, at.groups):
        copy = remote(mine, land.at[3 + i], send.at[3 + i], recv.at[3 + i], at.mid(i))
        copy.start()
        sent.append(copy)
    yield True
    for copy in sent:
        copy.wait()
    for i in range(1, at.groups):
        mine[...] = mine[...] + land[3 + i]


def everyone(at):
    return [at.cube(*dims) for dims in PEERS] + [at.sibling()] + [at.mid(i) for i in range(1, at.groups)]


def cube_only(at):
    return [at.cube(*dims) for dims in ((0,), (1,), (2,))]


def communicate(body, collective_id, ins, outs, scratch, in_specs, out_specs, limit=60):
    return pl.pallas_call(
        body,
        out_shape=outs,
        in_specs=in_specs,
        out_specs=out_specs,
        scratch_shapes=scratch,
        compiler_params=pltpu.CompilerParams(
            collective_id=collective_id, has_side_effects=True, vmem_limit_bytes=limit << 20
        ),
    )(*ins)


def like(shape, dtype=BF16):
    return jax.ShapeDtypeStruct(shape, dtype)


NT = (((1,), (1,)), ((), ()))
WIDE = 512
SCALE_2 = SCALE / math.log(2.0)


def visible(first_key, chunk_of_block, opening, tile):
    key = first_key + lax.broadcasted_iota(jnp.int32, (tile, 2 * CHUNK), 0)
    lane = lax.broadcasted_iota(jnp.int32, (1, 2 * CHUNK), 1)
    row = chunk_of_block * CHUNK + jnp.where(lane >= CHUNK, lane - CHUNK, lane)
    return (key <= row) & (key >= opening)


def key_range(group, chunk_of_block, tile):
    stop = (chunk_of_block * CHUNK + CHUNK + tile - 1) // tile
    start = jnp.where(group > 0, jnp.maximum(chunk_of_block * CHUNK - LONGEST, 0) // tile, 0)
    return start, stop


def two_heads(block):
    return jnp.concatenate([block[:, :HD], block[:, HD:]], 0)


def two_columns(block):
    return jnp.concatenate([block[:CHUNK], block[CHUNK:]], 1)


def turn_values(kv, turned):
    for t in range(kv.shape[0]):
        turned[:, pl.ds(2 * CHUNK * t, 2 * CHUNK)] = kv[t].reshape(2 * CHUNK, 2 * HD)[:, HD:].T


def front_block(groups, rows, hidden_rows, ins):
    n = groups
    gate_up = Columns.gate_up(groups, hidden_rows)
    count = len(gate_up(0, 0, 0))
    pieces = hidden_rows // piece_rows(hidden_rows)
    gu_pieces = 4 * rows // piece_rows(4 * rows)

    def body(r):
        at = Place(n)
        group, core = at.g, at.c

        def first_norm(i, carry):
            rows_i = pl.ds(pl.multiple_of(i * 32, 32), 32)
            value = r.tokens[rows_i, :].astype(F32)
            r.xhat[rows_i, :] = (value * lax.rsqrt(jnp.mean(value * value, 1, keepdims=True) + EPSILON)).astype(BF16)
            return carry

        lax.fori_loop(0, CHUNK // 32, first_norm, 0)
        r.qkv_mine[...] = (r.w_qkv[...].astype(F32) * r.gain_one[...]).astype(BF16)
        meet(everyone(at) + [at.diagonal()])
        far = [remote(r.out_mine, r.out_all.at[i], r.fs.at[i], r.fr.at[i], at.mid(i)) for i in range(1, n)]
        for copy in far:
            copy.start()
        wide = columns_in_cube(at, r.qkv_mine, r.qkv, Columns.qkv, r.qkv_local, r.qs, r.qr, rows)
        next(wide)
        tokens = gather_tokens(at, r.xhat, r.xhat_b, r.local.at[1], r.s1, r.r1, FRONT)
        next(tokens)
        lower = gather_hidden(at, r.down_mine, r.down, r.local.at[2], r.hts, r.htr, r.hms, r.hmr, r.hss, r.hsr)
        next(lower)
        out_here = pltpu.make_async_copy(r.out_mine, r.out_all.at[0], r.local.at[3])
        out_here.start()

        def scale(i, carry):
            cols = pl.ds(pl.multiple_of(i * 1024, 1024), 1024)
            r.gu_mine[:, cols] = (r.w_gu[:, cols].astype(F32) * r.gain_two[...]).astype(BF16)
            return carry

        lax.fori_loop(0, 2 * FF // 1024, scale, 0)

        def round_dy(i, carry):
            rows_i = pl.ds(pl.multiple_of(i * 32, 32), 32)
            r.dy[rows_i, :] = r.cotangent[rows_i, :].astype(BF16)
            return carry

        lax.fori_loop(0, CHUNK // 32, round_dy, 0)
        steps(tokens, 3)
        drive(wide)
        wide = columns_across(at, r.qkv, rows, r.qms, r.qmr, r.qss, r.qsr)
        steps(wide, 2 * (n - 1))
        steps(tokens, 3)
        columns = columns_in_cube(at, r.gu_mine, r.gu, gate_up, r.gu_local, r.cs, r.cr, rows)
        next(columns)
        out_here.wait()
        for copy in far:
            copy.wait()
        heads = gather_heads(at, r.out_all, r.w_out, r.hl, r.hs, r.hr, r.os, r.orr)
        next(heads)
        steps(lower, 1)
        drive(tokens)
        drive(wide)

        def project_in(i):
            four = pl.ds(pl.multiple_of(4 * i, 4), 4)
            raw = jnp.dot(r.xhat_b[four].reshape(4 * CHUNK, D), r.qkv[...], preferred_element_type=F32)
            cosine, sine = r.cosine[four].reshape(4 * CHUNK, HD), r.sine[four].reshape(4 * CHUNK, HD)
            heads = []
            for h in range(3):
                head = raw[:, h * HD : (h + 1) * HD]
                gain = r.head_gain[h : h + 1, :]
                normed = head * lax.rsqrt(jnp.mean(head * head, 1, keepdims=True) + EPSILON) * gain
                heads.append((normed * cosine + pltpu.roll(normed, HD // 2, 1) * sine).astype(BF16))
            r.raw[four] = raw[:, : 3 * HD].reshape(4, CHUNK, 3 * HD)
            r.q[four] = jnp.concatenate(heads[:2], 1).reshape(4, CHUNK, 2 * HD)
            r.kv[four] = jnp.concatenate([heads[2], raw[:, 3 * HD :].astype(BF16)], 1).reshape(4, CHUNK, 2 * HD)

        for i in range(2):
            lax.fori_loop(i, i + 1, lambda i, carry: (project_in(i), carry)[1], 0)

        here = pltpu.make_async_copy(r.kv, r.own.at[:, core], r.local.at[1])
        here.start()
        sib = remote(r.kv, r.own.at[:, core], r.ks.at[0], r.kr.at[0], at.sibling())
        sib.start()

        def to_group(i):
            return remote(r.kv, r.prompt.at[:, core], r.ps.at[i], r.pr, at.mid_at(jnp.int32(i)))

        def forward():
            half = r.kv.at[pl.ds(SLOTS // 2, SLOTS // 2)]
            return remote(half, r.before.at[:, core], r.bs, r.br, at.mid_at(group + 1))

        def across(ref, i):
            return remote(ref.at[:, core], ref.at[:, core], r.ks.at[i], r.kr.at[i], at.sibling())

        @pl.when(group == 0)
        def _():
            for i in range(1, n):
                to_group(i).start()

        if n > 2:

            @pl.when((group >= 1) & (group < n - 1))
            def _():
                forward().start()

        here.wait()
        sib.wait()
        turn_values(r.own, r.own_vt)
        drive(columns)
        columns = columns_across(at, r.gu, rows, r.cms, r.cmr, r.css, r.csr)
        bulk = in_turn((lower, pieces * (n - 1) - 1), (columns, 2 * gu_pieces * (n - 1)))
        steps(bulk, 1)
        dy = gather_tokens(at, r.dy, r.dy_b, r.local.at[4], r.s3, r.r3)
        next(dy)

        def step(kv, values_t, tile, chunk, q, opening, carry, masked, shift=0):
            norm, out = carry
            first = tile * WIDE
            parts = []
            for k in range(WIDE // CHUNK):
                keys = kv[tile * (WIDE // (2 * CHUNK)) + k // 2, k % 2][:, :HD]
                p = jnp.exp2(lax.dot_general(keys, q, NT, preferred_element_type=F32) * SCALE_2)
                if masked:
                    p = jnp.where(visible(first + shift + k * CHUNK, chunk, opening, CHUNK), p, 0.0)
                norm = norm + jnp.sum(p, 0, keepdims=True)
                parts.append(p.astype(BF16))
            first = first if isinstance(first, int) else pl.multiple_of(first, WIDE)
            out = out + jnp.dot(
                values_t[:, pl.ds(first, WIDE)], jnp.concatenate(parts, 0), preferred_element_type=F32
            )
            return norm, out

        def own_part(i):
            chunk = 2 * i + core
            query, opening = two_heads(r.q[i]), r.opening[i]
            start, stop = key_range(group, chunk, WIDE)
            zero = (jnp.zeros((1, 2 * CHUNK), F32), jnp.zeros((HD, 2 * CHUNK), F32))
            norm, out = lax.fori_loop(
                start, stop, lambda t, c: step(r.own, r.own_vt, t, chunk, query, opening, c, True), zero
            )
            r.lse[i] = norm
            r.total[i] = out

        paced(own_part, SLOTS, lambda: steps(bulk, 1))
        next(heads)

        @pl.when(group > 0)
        def _():
            to_group(0).wait_recv()
            across(r.prompt, 1).start()

        if n > 2:

            @pl.when(group > 1)
            def _():
                forward().wait_recv()
                across(r.before, 2).start()

        steps(dy, 3)
        steps(bulk, 1)

        @pl.when(group > 0)
        def _():
            across(r.prompt, 1).wait()
            turn_values(r.prompt, r.prompt_vt)

        def prompt_part(i):
            query = two_heads(r.q[i])
            state = (r.lse[i], r.total[i])
            for t in range(PROMPT // WIDE):
                state = step(r.prompt, r.prompt_vt, t, 0, query, None, state, False)
            r.lse[i], r.total[i] = state

        paced(prompt_part, SLOTS, lambda: steps(bulk, 1), group > 0)

        if n > 2:

            @pl.when(group > 1)
            def _():
                across(r.before, 2).wait()
                turn_values(r.before, r.before_vt)

                def before_part(i, carry):
                    query, opening = two_heads(r.q[i]), r.opening[i]
                    state = (r.lse[i], r.total[i])
                    for t in range(LONGEST // WIDE):
                        state = step(r.before, r.before_vt, t, 2 * i + core, query, opening, state, True, -LONGEST)
                    r.lse[i], r.total[i] = state
                    return carry

                lax.fori_loop(0, SLOTS // 2, before_part, 0)

        steps(dy, 3)
        steps(bulk, 1)
        drive(heads)

        def project_out(i, carry):
            norm = r.lse[i]
            out = r.total[i] / norm
            r.total[i] = out
            r.lse[i] = jnp.log(norm)
            row = two_columns(out.T.astype(BF16))
            r.mixed[i] = row
            r.part[i] = jnp.dot(row, r.w_out[...], preferred_element_type=F32).astype(BF16)
            return carry

        lax.fori_loop(0, SLOTS, project_out, 0)
        beside(scatter_tokens(at, r.part, r.land, r.hidden, r.s4, r.r4, FRONT), bulk)

        def norm_rows(i, carry):
            rows = pl.ds(pl.multiple_of(i * 32, 32), 32)
            value = r.hidden[rows, :] + r.tokens[rows, :].astype(F32)
            r.hidden[rows, :] = value
            inverse = lax.rsqrt(jnp.mean(value * value, 1, keepdims=True) + EPSILON)
            r.mine[rows, :] = (value * inverse).astype(BF16)
            return carry

        lax.fori_loop(0, CHUNK // 32, norm_rows, 0)
        beside(gather_tokens(at, r.mine, r.xhat2_b, r.local.at[5], r.s2, r.r2, FRONT), bulk)
        drive(dy, bulk)
        drive(lower, columns)

        @pl.when(group == 0)
        def _():
            for i in range(1, n):
                to_group(i).wait_send()

        if n > 2:

            @pl.when((group >= 1) & (group < n - 1))
            def _():
                forward().wait_send()

    chunks = (SLOTS, CHUNK, 2 * HD)
    block, end = (SLOTS, 2, CHUNK, 2 * HD), (SLOTS // 2, 2, CHUNK, 2 * HD)
    tok = DMA((len(PARTS), 7))
    return kernel(
        1,
        body,
        {name: (a, HBM if name in ("down_mine", "out_mine") else VMEM) for name, a in ins.items()},
        {
            "xhat_b": (like((SLOTS, CHUNK, D)), VMEM),
            "qkv": (like((D, QKV_SLOT)), VMEM),
            "raw": (like((SLOTS, CHUNK, 3 * HD), F32), VMEM),
            "q": (like(chunks), VMEM),
            "mixed": (like(chunks), VMEM),
            "total": (like((SLOTS, HD, 2 * CHUNK), F32), VMEM),
            "lse": (like((SLOTS, 1, 2 * CHUNK), F32), VMEM),
            "own": (like(block), VMEM),
            "prompt": (like(block), VMEM),
            "before": (like(end), VMEM),
            "w_out": (like((D // SLOTS, D)), VMEM),
            "hidden": (like((CHUNK, D), F32), VMEM),
            "xhat2_b": (like((SLOTS, CHUNK, D)), HBM),
            "gu": (like((D, GU_SLOT)), HBM),
            "down": (like((n, 2, hidden_rows, D)), HBM),
            "dy_b": (like((SLOTS, CHUNK, D)), HBM),
        },
        {
            "kv": pltpu.VMEM(chunks, BF16),
            "xhat": pltpu.VMEM((CHUNK, D), BF16),
            "dy": pltpu.VMEM((CHUNK, D), BF16),
            "qkv_mine": pltpu.VMEM((rows, (HQ + 2 * HK) * HD), BF16),
            "gu_mine": pltpu.VMEM((rows, 2 * FF), BF16),
            "own_vt": pltpu.VMEM((HD, 2 * SLOTS * CHUNK), BF16),
            "prompt_vt": pltpu.VMEM((HD, PROMPT), BF16),
            "before_vt": pltpu.VMEM((HD, LONGEST), BF16),
            "part": pltpu.VMEM((SLOTS, CHUNK, D), BF16),
            "land": pltpu.VMEM((7, CHUNK, D), BF16),
            "mine": pltpu.VMEM((CHUNK, D), BF16),
            "out_all": pltpu.VMEM((n, rows, D), BF16),
            "local": DMA((6,)),
            **{name: tok for name in ("s1", "r1", "s2", "r2", "s3", "r3", "s4", "r4")},
            **{name: DMA((7, 3)) for name in ("qs", "qr")},
            **{name: DMA((7, count)) for name in ("cs", "cr")},
            "qkv_local": DMA((3,)),
            "gu_local": DMA((count,)),
            **{name: DMA((n, 2, 1)) for name in ("qms", "qmr", "qss", "qsr")},
            **{name: DMA((n, 2, gu_pieces)) for name in ("cms", "cmr", "css", "csr")},
            **{name: DMA((n, pieces)) for name in ("hms", "hmr")},
            **{name: DMA((n,)) for name in ("hss", "hsr", "fs", "fr", "hl", "hs", "ps")},
            **{name: DMA(()) for name in ("hts", "htr", "os", "orr", "pr", "bs", "br")},
            "hr": DMA((n, 4)),
            **{name: DMA((3,)) for name in ("ks", "kr")},
        },
    )


def attention_back(at, r, part, between, when=None):
    kv, keys_t, acc = getattr(r, part), getattr(r, part + "_kt"), getattr(r, "acc_" + part)

    def begin():
        keys_t[...] = kv[:, :HD].T
        acc[...] = jnp.zeros_like(acc)

    shift = -LONGEST if part == "before" else 0

    def step(t, dq, q, do, dot_rows, logs, chunk, opening):
        first = t * WIDE
        rows = pl.ds(first if isinstance(first, int) else pl.multiple_of(first, WIDE), WIDE)
        keys, values = kv[rows, :HD], kv[rows, HD:]
        p = jnp.exp2(lax.dot_general(keys, q, NT, preferred_element_type=F32) * SCALE_2 - logs)
        if part != "prompt":
            p = jnp.where(visible(first + shift, chunk, opening, WIDE), p, 0.0)
        dp = lax.dot_general(values, do, NT, preferred_element_type=F32)
        ds = (p * (dp - dot_rows)).astype(BF16)
        acc[rows, :HD] += jnp.dot(ds, q, preferred_element_type=F32)
        acc[rows, HD:] += jnp.dot(p.astype(BF16), do, preferred_element_type=F32)
        return dq + jnp.dot(keys_t[:, rows], ds, preferred_element_type=F32)

    def one(i):
        chunk = 2 * i + at.c
        q, do = two_heads(r.q[i]), two_heads(r.do[i])
        args = (q, do, r.dots[i], r.lse[i] * (1.0 / math.log(2.0)), chunk, r.opening[i])
        if part == "own":
            start, stop = key_range(at.g, chunk, WIDE)
            r.dq_sum[i] = lax.fori_loop(start, stop, lambda t, dq: step(t, dq, *args), r.dq_sum[i])
        else:
            dq = r.dq_sum[i]
            for t in range(kv.shape[0] // WIDE):
                dq = step(t, dq, *args)
            r.dq_sum[i] = dq

    def end():
        out = getattr(r, "d_" + part)
        for t in range(out.shape[0] * 2):
            out[t // 2, t % 2, :, :HD] = (acc[t * CHUNK : (t + 1) * CHUNK, :HD] * SCALE).astype(BF16)
            out[t // 2, t % 2, :, HD:] = acc[t * CHUNK : (t + 1) * CHUNK, HD:].astype(BF16)

    count = SLOTS if part != "before" else SLOTS // 2
    if when is None:
        begin()
        paced(one, count, between)
        end()
    else:
        pl.when(when)(begin)
        paced(one, count, between, when)
        pl.when(when)(end)


def add_chunks(dst, first, other, skip=0):
    def one(i, carry):
        dst[i + skip] = (first(i).astype(F32) + other[i].astype(F32)).astype(BF16)
        return carry

    lax.fori_loop(0, other.shape[0], one, 0)


LATE = "late"


def kernel(collective_id, body, ins, outs, scratch):
    late = [name for name, (_, spec) in ins.items() if spec is LATE]
    scratch = {
        **scratch,
        **{name + "_late": pltpu.VMEM(ins[name][0].shape, ins[name][0].dtype) for name in late},
        **({"late": DMA((len(late),))} if late else {}),
    }
    ins = {name: (a, HBM if spec is LATE else spec) for name, (a, spec) in ins.items()}
    names = [*ins, *outs, *scratch]
    return dict(
        zip(
            outs,
            communicate(
                lambda *refs: body(types.SimpleNamespace(**dict(zip(names, refs)))),
                collective_id,
                tuple(a for a, _ in ins.values()),
                tuple(a for a, _ in outs.values()),
                list(scratch.values()),
                [spec for _, spec in ins.values()],
                [spec for _, spec in outs.values()],
            ),
        )
    )


def bring_late(r):
    copies = {}
    for k, name in enumerate([name for name in vars(r) if name.endswith("_late")]):
        name = name[: -len("_late")]
        here = getattr(r, name + "_late")
        copies[name] = pltpu.make_async_copy(getattr(r, name), here, r.late.at[k])
        copies[name].start()
        setattr(r, name, here)

    def wait(*some):
        for name in some or list(copies):
            copies.pop(name).wait()

    return wait


def back_block(groups, rows, ins):
    n = groups

    def body(r):
        at = Place(n)
        group = at.g
        bring_dx = pltpu.make_async_copy(r.part_dx, r.part, r.local.at[3])
        bring_dx.start()
        loaded = bring_late(r)
        meet(everyone(at))
        columns = columns_sum(at, r.g_gu, r.sib_gu, r.mid_gu, r.gu_sum, (r.cms, r.cmr, r.css, r.csr))
        next(columns)
        bring_dx.wait()
        bulk = in_turn((columns, r.cms.shape[1] * r.cms.shape[2] * (n - 1)))
        beside(scatter_tokens(at, r.part, r.land, r.dx, r.s1, r.r1), bulk)

        def norm(i, carry):
            rows = pl.ds(pl.multiple_of(i * 32, 32), 32)
            value = r.hidden[rows, :]
            inverse = lax.rsqrt(jnp.mean(value * value, 1, keepdims=True) + EPSILON)
            unit = value * inverse
            grad = r.dx[rows, :]
            total = r.cotangent[rows, :] + inverse * (grad - unit * jnp.mean(grad * unit, 1, keepdims=True))
            r.dhidden[rows, :] = total
            r.mine[rows, :] = total.astype(BF16)
            return carry

        lax.fori_loop(0, CHUNK // 32, norm, 0)
        loaded("act", "down")
        for k, _ in enumerate(gather_tokens(at, r.mine, r.dbranch, r.local.at[0], r.s2, r.r2)):
            steps(bulk, 1)
            if k < SLOTS // 2:
                two = pl.ds(2 * k, 2)
                r.part[two] = (
                    jnp.dot(r.act[two].reshape(2 * CHUNK, FF_SLOT), r.down[...], preferred_element_type=F32)
                    .astype(BF16)
                    .reshape(2, CHUNK, D)
                )
        result = scatter_tokens(at, r.part, r.land2, r.dx, r.s3, r.r3)
        next(result)

        loaded()

        def heads(i, carry):
            do = lax.dot_general(r.dbranch[i], r.w_out[...], NT, preferred_element_type=F32).astype(BF16)
            r.do[i] = do
            r.dots[i] = jnp.sum(two_heads(do).astype(F32).T * r.total[i], 0, keepdims=True)
            r.dq_sum[i] = jnp.zeros((HD, 2 * CHUNK), F32)
            return carry

        lax.fori_loop(0, SLOTS, heads, 0)

        def swap(array, place, i):
            return remote(array.at[:, 1 - at.c], place, r.ks.at[i], r.kr.at[i], at.sibling())

        def home(i):
            return remote(r.land_p, r.far_p.at[i - 1], r.ps, r.pr.at[i - 1], at.mid_at(jnp.int32(0)))

        def back():
            return remote(r.land_b, r.far_b, r.bs, r.br, at.mid_at(group - 1))

        def between():
            steps(bulk, 1)
            steps(result, 1)

        attention_back(at, r, "prompt", between, group > 0)

        @pl.when(group > 0)
        def _():
            swap(r.d_prompt, r.land_p, 1).start()

        if n > 2:
            attention_back(at, r, "before", between, group > 1)

            @pl.when(group > 1)
            def _():
                swap(r.d_before, r.land_b, 2).start()

        @pl.when(group > 0)
        def _():
            swap(r.d_prompt, r.land_p, 1).wait()
            add_chunks(r.land_p, lambda i: r.d_prompt[i, at.c], r.land_p)
            for i in range(1, n):

                @pl.when(group == i)
                def _():
                    home(i).start()

        if n > 2:

            @pl.when(group > 1)
            def _():
                swap(r.d_before, r.land_b, 2).wait()
                add_chunks(r.land_b, lambda i: r.d_before[i, at.c], r.land_b)
                back().start()

        attention_back(at, r, "own", between)
        first = swap(r.d_own, r.land_k, 0)
        first.start()
        drive(bulk)

        def queries(i, carry):
            r.dq[i] = two_columns((r.dq_sum[i].T * SCALE).astype(BF16))
            return carry

        lax.fori_loop(0, SLOTS, queries, 0)
        first.wait()
        add_chunks(r.dkv, lambda i: r.d_own[i, at.c], r.land_k)
        drive(result)

        def add(i, carry):
            rows = pl.ds(pl.multiple_of(i * 32, 32), 32)
            r.output[rows, :] = (r.hidden[rows, :] + r.dx[rows, :]).astype(BF16)
            return carry

        lax.fori_loop(0, CHUNK // 32, add, 0)

        @pl.when(group == 0)
        def _():
            for i in range(1, n):
                home(i).wait_recv()
                add_chunks(r.dkv, lambda j: r.dkv[j], r.far_p.at[i - 1])

        if n > 2:

            @pl.when((group >= 1) & (group < n - 1))
            def _():
                back().wait_recv()
                add_chunks(r.dkv, lambda j: r.dkv[j + SLOTS // 2], r.far_b, SLOTS // 2)

            @pl.when(group > 1)
            def _():
                back().wait_send()

        @pl.when(group > 0)
        def _():
            home(1).wait_send()

        drive(columns)

    chunks = (SLOTS, CHUNK, 2 * HD)
    block, end = (SLOTS, 2, CHUNK, 2 * HD), (SLOTS // 2, 2, CHUNK, 2 * HD)
    tok = DMA((len(PARTS), 7))
    near, half = pltpu.VMEM(chunks, BF16), pltpu.VMEM((SLOTS // 2, CHUNK, 2 * HD), BF16)
    own, prompt, before = 2 * SLOTS * CHUNK, PROMPT, LONGEST
    far = max(n - 1, 1)
    gu_pieces = 4 * (rows // piece_rows(rows))
    late = ("act", "down", "w_out", "q", "own", "prompt", "before", "total")
    return kernel(
        2,
        body,
        {
            name: (a, HBM if name == "part_dx" else LATE if name in late else VMEM)
            for name, a in ins.items()
        },
        {
            "dhidden": (like((CHUNK, D), F32), VMEM),
            "output": (like((CHUNK, D)), VMEM),
            "dbranch": (like((SLOTS, CHUNK, D)), VMEM),
            "dq": (like(chunks), VMEM),
            "dkv": (like(chunks), VMEM),
            "gu_sum": (like((2, 4, rows, GU_SLOT)), VMEM),
        },
        {
            "part": pltpu.VMEM((SLOTS, CHUNK, D), BF16),
            "land": pltpu.VMEM((7, CHUNK, D), BF16),
            "land2": pltpu.VMEM((7, CHUNK, D), BF16),
            "mine": pltpu.VMEM((CHUNK, D), BF16),
            "dx": pltpu.VMEM((CHUNK, D), F32),
            "sib_gu": pltpu.VMEM((2, 4 * n * rows, GU_SLOT), BF16),
            "mid_gu": pltpu.VMEM((far, 2, 4, rows, GU_SLOT), BF16),
            "do": near,
            "dots": pltpu.VMEM((SLOTS, 1, 2 * CHUNK), F32),
            "dq_sum": pltpu.VMEM((SLOTS, HD, 2 * CHUNK), F32),
            "own_kt": pltpu.VMEM((HD, own), BF16),
            "prompt_kt": pltpu.VMEM((HD, prompt), BF16),
            "before_kt": pltpu.VMEM((HD, before), BF16),
            "acc_own": pltpu.VMEM((own, 2 * HD), F32),
            "acc_prompt": pltpu.VMEM((prompt, 2 * HD), F32),
            "acc_before": pltpu.VMEM((before, 2 * HD), F32),
            "d_own": pltpu.VMEM(block, BF16),
            "d_prompt": pltpu.VMEM(block, BF16),
            "d_before": pltpu.VMEM(end, BF16),
            "land_k": near,
            "land_p": near,
            "land_b": half,
            "far_p": pltpu.VMEM((far, *chunks), BF16),
            "far_b": half,
            "local": DMA((4,)),
            **{name: tok for name in ("s1", "r1", "s2", "r2", "s3", "r3")},
            **{name: DMA((n, 2, gu_pieces)) for name in ("cms", "cmr")},
            **{name: DMA((2,)) for name in ("css", "csr")},
            **{name: DMA((3,)) for name in ("ks", "kr")},
            "ps": DMA(()),
            "pr": DMA((n,)),
            "bs": DMA(()),
            "br": DMA(()),
        },
    )


def last_block(groups, rows, hidden_rows, ins):
    n = groups
    gate_up = Columns.gate_up(groups, hidden_rows)
    count = len(gate_up(0, 0, 0))
    late = ("dbranch", "xhat_b", "qkv", "w_gu", "w_qkv")

    def unscale(dst, grad, weight, gain, d_gain):
        total = jnp.zeros((rows, 1), F32)
        for k in range(dst.shape[1] // 2048):
            cols = pl.ds(2048 * k, 2048)
            value = grad[:, cols].astype(F32)
            dst[:, cols] = value * gain[...]
            total = total + jnp.sum(value * weight[:, cols].astype(F32), 1, keepdims=True)
        d_gain[...] = total

    def body(r):
        at = Place(n)
        loaded = bring_late(r)
        meet(everyone(at) + [at.diagonal()])
        bring = columns_home(at, r.gu_sum, r.gu, gate_up, r.ds, r.dr, r.gu_local)
        next(bring)
        lower = turn_hidden(at, r.down_sum, r.down, r.hts, r.htr, r.local.at[0])
        next(lower)
        loaded("dbranch")
        turned = r.mixed[...].reshape(SLOTS * CHUNK, 2 * HD).T

        for k in range(D // 512):
            cols = pl.ds(512 * k, 512)
            r.g_out[:, cols] = jnp.dot(
                turned, r.dbranch[:, :, cols].reshape(SLOTS * CHUNK, 512), preferred_element_type=F32
            ).astype(BF16)
        heads = scatter_heads(at, r.g_out, r.out, r.sib_o, r.mid_o, (r.os, r.orr, r.oms, r.omr, r.oss, r.osr, r.local.at[1]))
        next(heads)
        r.gain_sum[...] = jnp.zeros_like(r.gain_sum)

        def through_heads(i, carry):
            two = pl.ds(pl.multiple_of(2 * i, 2), 2)
            cosine, sine = r.cosine[two].reshape(2 * CHUNK, HD), r.sine[two].reshape(2 * CHUNK, HD)
            raw = r.raw[two].reshape(2 * CHUNK, 3 * HD)
            dq, dkv = r.dq[two].reshape(2 * CHUNK, 2 * HD), r.dkv[two].reshape(2 * CHUNK, 2 * HD)
            parts = []
            for h in range(3):
                grad = (dq[:, h * HD : (h + 1) * HD] if h < 2 else dkv[:, :HD]).astype(F32)
                head = raw[:, h * HD : (h + 1) * HD]
                inverse = lax.rsqrt(jnp.mean(head * head, 1, keepdims=True) + EPSILON)
                unit = head * inverse
                back = grad * cosine + pltpu.roll(grad * sine, HD // 2, 1)
                at_row = 0 if h < 2 else 1
                r.gain_sum[at_row : at_row + 1, :] += jnp.sum(back * unit, 0, keepdims=True)
                back = back * r.head_gain[h : h + 1, :]
                parts.append((inverse * (back - unit * jnp.mean(back * unit, 1, keepdims=True))).astype(BF16))
            draw = jnp.concatenate(parts + [dkv[:, HD:]], 1)
            r.draw[two] = draw.reshape(2, CHUNK, QKV_SLOT)
            return carry

        lax.fori_loop(0, SLOTS // 2, through_heads, 0)
        next(heads)
        sums = sum_everywhere(at, r.gain_sum, r.gain_land, r.gs, r.gr)
        loaded()
        for h in range(QKV_SLOT // HD):
            steps(sums, 1)
            cols = pl.ds(h * HD, HD)
            turned = r.draw[:, :, cols].reshape(SLOTS * CHUNK, HD).T
            grad = jnp.dot(turned, r.xhat_b[...].reshape(SLOTS * CHUNK, D), preferred_element_type=F32)
            r.g_qkv[:, cols] = grad.astype(BF16).T
        wide = columns_sum(at, r.g_qkv, r.sib_q, r.mid_q, r.fin_q, (r.cms, r.cmr, r.css, r.csr), 4)
        next(wide)

        def part_dx(i, carry):
            two = pl.ds(pl.multiple_of(2 * i, 2), 2)
            grad = lax.dot_general(
                r.draw[two].reshape(2 * CHUNK, QKV_SLOT), r.qkv[...], NT, preferred_element_type=F32
            )
            r.part[two] = grad.astype(BF16).reshape(2, CHUNK, D)
            return carry

        lax.fori_loop(0, SLOTS // 2, part_dx, 0)
        steps(wide, 1)
        bulk = in_turn((wide, 2 * (rows // piece_rows(rows)) * (n - 1) - 1))
        main = scatter_tokens(at, r.part, r.land, r.dx, r.s1, r.r1)
        for _ in range(4):
            next(main)
            steps(bulk, 1)
        drive(bring)
        unscale(r.d_gu, r.gu, r.w_gu, r.gain_two, r.d_gain_two)
        next(heads)
        beside(main, bulk)

        def norm(i, carry):
            rows = pl.ds(pl.multiple_of(i * 32, 32), 32)
            value = r.tokens[rows, :].astype(F32)
            inverse = lax.rsqrt(jnp.mean(value * value, 1, keepdims=True) + EPSILON)
            unit = value * inverse
            grad = r.dx[rows, :]
            r.d_tokens[rows, :] = r.dhidden[rows, :] + inverse * (grad - unit * jnp.mean(grad * unit, 1, keepdims=True))
            return carry

        lax.fori_loop(0, CHUNK // 32, norm, 0)
        drive(wide)
        home = columns_home(at, r.fin_q, r.qkv_rows, Columns.qkv, r.cs, r.cr, r.qkv_local)
        next(home)
        drive(lower)

        def lower_out(i, carry):
            rows_i = pl.ds(pl.multiple_of(i * 16, 16), 16)
            r.d_down[rows_i, :] = r.down[rows_i, :].astype(F32)
            return carry

        lax.fori_loop(0, hidden_rows // 16, lower_out, 0)
        drive(bulk, sums, heads)
        r.d_out[...] = r.out[...].astype(F32)
        drive(home)
        unscale(r.d_qkv, r.qkv_rows, r.w_qkv, r.gain_one, r.d_gain_one)

    deep = 4 * n * rows
    far = max(n - 1, 1)
    return kernel(
        3,
        body,
        {name: (a, HBM if name in ("gu_sum", "down_sum") else LATE if name in late else VMEM) for name, a in ins.items()},
        {
            "d_gu": (like((rows, 2 * FF), F32), VMEM),
            "d_tokens": (like((CHUNK, D), F32), VMEM),
            "d_qkv": (like((rows, (HQ + 2 * HK) * HD), F32), VMEM),
            "d_out": (like((rows, D), F32), VMEM),
            "d_down": (like((hidden_rows, D), F32), VMEM),
            "d_gain_one": (like((rows, 1), F32), VMEM),
            "d_gain_two": (like((rows, 1), F32), VMEM),
            "gain_sum": (like((8, HD), F32), VMEM),
        },
        {
            "gu": pltpu.VMEM((rows, 2 * FF), BF16),
            "qkv_rows": pltpu.VMEM((rows, (HQ + 2 * HK) * HD), BF16),
            "out": pltpu.VMEM((rows, D), BF16),
            "down": pltpu.VMEM((hidden_rows, D), BF16),
            **{name: DMA(()) for name in ("hts", "htr")},
            "part": pltpu.VMEM((SLOTS, CHUNK, D), BF16),
            "land": pltpu.VMEM((7, CHUNK, D), BF16),
            "dx": pltpu.VMEM((CHUNK, D), F32),
            "draw": pltpu.VMEM((SLOTS, CHUNK, QKV_SLOT), BF16),
            "g_qkv": pltpu.VMEM((D, QKV_SLOT), BF16),
            "sib_q": pltpu.VMEM((2, deep, QKV_SLOT), BF16),
            "mid_q": pltpu.VMEM((far, 2, 4, rows, QKV_SLOT), BF16),
            "fin_q": pltpu.VMEM((2, 4, rows, QKV_SLOT), BF16),
            "g_out": pltpu.VMEM((D // SLOTS, D), BF16),
            "sib_o": pltpu.VMEM((D // SLOTS, D), BF16),
            "mid_o": pltpu.VMEM((far, 4 * rows, D), BF16),
            "gain_land": pltpu.VMEM((4 + n, 8, HD), F32),
            "local": DMA((2,)),
            **{name: DMA((len(PARTS), 7)) for name in ("s1", "r1")},
            **{name: DMA((7, 3)) for name in ("cs", "cr")},
            "qkv_local": DMA((3,)),
            **{name: DMA((7, count)) for name in ("ds", "dr")},
            "gu_local": DMA((count,)),
            **{name: DMA((n, 2, 4 * (rows // piece_rows(rows)))) for name in ("cms", "cmr")},
            **{name: DMA((2,)) for name in ("css", "csr")},
            "os": DMA((4,)),
            **{name: DMA(()) for name in ("orr", "oss", "osr")},
            **{name: DMA((n,)) for name in ("oms", "omr")},
            **{name: DMA((4 + n,)) for name in ("gs", "gr")},
        },
    )


def dot(a, b, dims=((1,), (0,))):
    return lax.dot_general(a, b, (dims, ((), ())), preferred_element_type=F32)


def body(tokens, lengths, attn_gain, w_qkv, q_gain, k_gain, w_out, mlp_gain, w_gate_up, w_down, cotangent):
    blocks = lax.axis_size("blk")
    groups = blocks // 4
    rows = w_qkv.shape[0]
    hidden_rows = w_down.shape[0]
    group = lax.axis_index("blk") // 4
    core = lax.axis_index("uly") % 2
    gain_one = attn_gain.astype(F32)[:, None]
    gain_two = mlp_gain.astype(F32)[:, None]

    direct = (2 * hidden_rows) % 128 == 0
    w_gu = w_gate_up
    if not direct:
        w_gu = (
            w_gate_up.reshape(rows, 2, 2, 2, groups, 2, 2 * hidden_rows)
            .transpose(0, 2, 5, 3, 1, 4, 6)
            .reshape(rows, 2 * FF)
        )

    starts = PROMPT + jnp.sum(
        jnp.where(jnp.arange(lengths.shape[0])[:, None] > jnp.arange(lengths.shape[0])[None, :], lengths[None, :], 0), 1
    )
    index = (
        group * (2 * SLOTS * CHUNK)
        + (2 * jnp.arange(SLOTS, dtype=jnp.int32)[:, None] + core) * CHUNK
        + jnp.arange(CHUNK, dtype=jnp.int32)[None, :]
    )
    opening = jnp.max(jnp.where(index[..., None] >= starts, starts, 0), -1)
    position = jnp.where(index < PROMPT, index, index - opening + PROMPT)
    opening = opening - group * (2 * SLOTS * CHUNK)
    opening = jnp.concatenate([opening, opening], 1)[:, None, :]
    lane = np.arange(HD)
    angles = position.astype(F32)[:, :, None] * (ROPE_BASE ** (-2.0 * jnp.asarray(lane % (HD // 2), F32) / HD))
    cosine, sine = jnp.cos(angles), jnp.sin(angles) * np.where(lane < HD // 2, -1.0, 1.0).astype(np.float32)
    head_gain = jnp.stack([q_gain, q_gain, k_gain]).astype(F32)

    front = front_block(
        groups,
        rows,
        hidden_rows,
        {
            "tokens": tokens,
            "cotangent": cotangent,
            "w_qkv": w_qkv,
            "w_gu": w_gu,
            "gain_one": gain_one,
            "gain_two": gain_two,
            "opening": opening,
            "cosine": cosine,
            "sine": sine,
            "head_gain": head_gain,
            "down_mine": w_down,
            "out_mine": w_out,
        },
    )
    xhat2_b, dy_b = (front[name].reshape(SLOTS * CHUNK, D) for name in ("xhat2_b", "dy_b"))
    own, prompt, before = (front[name].reshape(-1, 2 * HD) for name in ("own", "prompt", "before"))
    gu_w, down_w = front["gu"], front["down"].reshape(FF_SLOT, D)

    both = dot(xhat2_b, gu_w)
    gate, up = both[:, :FF_SLOT], both[:, FF_SLOT:]
    sigmoid = jax.nn.sigmoid(gate)
    act = (gate * sigmoid * up).astype(BF16)
    g_down = dot(act, dy_b, ((0,), (0,))).astype(BF16)
    g_down = g_down.reshape(groups, 2, hidden_rows, D)
    theirs = lax.ppermute(
        lax.dynamic_index_in_dim(g_down, 1 - core, 1, keepdims=False), "uly", [(u, u + 1 - 2 * (u % 2)) for u in range(4)]
    )
    down_core = lax.dynamic_index_in_dim(g_down, core, 1, keepdims=False).astype(F32) + theirs.astype(F32)
    down_core = down_core.astype(BF16)
    dact = dot(dy_b, down_w, ((1,), (1,)))
    dboth = jnp.concatenate(
        [dact * up * sigmoid * (1.0 + gate * (1.0 - sigmoid)), dact * gate * sigmoid], 1
    ).astype(BF16)
    down_core, dboth = lax.optimization_barrier((down_core, dboth))
    down_sum = lax.dynamic_index_in_dim(down_core, group, 0, keepdims=False).astype(F32)
    for i in range(1, groups):
        there = lax.dynamic_index_in_dim(down_core, (group + i) % groups, 0, keepdims=False)
        there = lax.ppermute(there, "blk", [(b, (b + 4 * i) % blocks) for b in range(blocks)])
        down_sum = down_sum + there.astype(F32)
    down_sum = down_sum.astype(BF16)
    g_gu = dot(xhat2_b, dboth, ((0,), (0,))).astype(BF16)
    part_dx2 = dot(dboth, gu_w, ((1,), (1,))).astype(BF16)
    back = back_block(
        groups,
        rows,
        {
            "part_dx": part_dx2.reshape(SLOTS, CHUNK, D),
            "act": act.reshape(SLOTS, CHUNK, FF_SLOT),
            "down": down_w,
            "hidden": front["hidden"],
            "cotangent": cotangent,
            "g_gu": g_gu,
            "w_out": front["w_out"],
            "q": front["q"],
            "own": own,
            "prompt": prompt,
            "before": before,
            "opening": opening,
            "total": front["total"],
            "lse": front["lse"],
        },
    )
    last = last_block(
        groups,
        rows,
        hidden_rows,
        {
            "gu_sum": back["gu_sum"],
            "down_sum": down_sum,
            "w_qkv": w_qkv,
            "w_gu": w_gu,
            "gain_one": gain_one,
            "gain_two": gain_two,
            "dq": back["dq"],
            "dkv": back["dkv"],
            "raw": front["raw"],
            "cosine": cosine,
            "sine": sine,
            "head_gain": head_gain,
            "xhat_b": front["xhat_b"],
            "qkv": front["qkv"],
            "mixed": front["mixed"],
            "dbranch": back["dbranch"],
            "tokens": tokens,
            "dhidden": back["dhidden"],
        },
    )
    d_gu = last["d_gu"]
    if not direct:
        d_gu = (
            d_gu.reshape(rows, 2, 2, 2, 2, groups, 2 * hidden_rows)
            .transpose(0, 4, 1, 3, 5, 2, 6)
            .reshape(rows, 2 * FF)
        )
    return (
        back["output"],
        last["d_tokens"],
        last["d_gain_one"][:, 0],
        last["d_qkv"],
        last["gain_sum"][0],
        last["gain_sum"][1],
        last["d_out"],
        last["d_gain_two"][:, 0],
        d_gu,
        last["d_down"],
    )


def solution(mesh):
    tokens = P(("blk", "uly"), None)
    weight = P(("uly", "blk"), None)
    gain = P(("uly", "blk"))
    return jax.shard_map(
        body,
        mesh=mesh,
        in_specs=(tokens, P(), gain, weight, P(), P(), weight, gain, weight, weight, tokens),
        out_specs=(tokens, tokens, gain, weight, P(), P(), weight, gain, weight, weight),
        check_vma=False,
    )
```

```python
import math
import types

import jax
import jax.numpy as jnp
import numpy as np
from jax import lax
from jax.experimental import pallas as pl
from jax.experimental.pallas import tpu as pltpu
from jax.sharding import PartitionSpec as P

D = 2048
HQ = 16
HK = 8
HD = 128
FF = 6144
PROMPT = 2048
LONGEST = 1024

SLOTS = 8
CHUNK = 128
QKV_SLOT = 512
GU_SLOT = 2 * FF // SLOTS
FF_SLOT = FF // SLOTS
EPSILON = 1e-06
ROPE_BASE = 1000000.0
SCALE = 1.0 / math.sqrt(HD)
WINDOW = 10

F32 = jnp.float32
BF16 = jnp.bfloat16
MESH = pl.DeviceIdType.MESH
HBM = pl.BlockSpec(memory_space=pl.ANY)
VMEM = pl.BlockSpec(memory_space=pltpu.VMEM)
DMA = pltpu.SemaphoreType.DMA
PARTS = ((0, 1, 2), 384), ((1, 2, 0), 768), ((2, 0, 1), 896)
FRONT = ((0, 1, 2), 256), ((1, 2, 0), 768), ((2, 0, 1), 1024)


def rem(a, n):
    return lax.rem(a, jnp.int32(n))


class Place:
    def __init__(self, groups):
        self.groups = groups
        self.u = lax.axis_index("uly")
        self.b = lax.axis_index("blk")
        self.x = self.u // 2
        self.c = rem(self.u, 2)
        self.g = self.b // 4
        self.bl = rem(self.b, 4)
        self.bits = (self.x, rem(self.bl, 2), self.bl // 2)

    def flip(self, *dims):
        x, y, z = (rem(v + 1, 2) if d in dims else v for d, v in enumerate(self.bits))
        return x, 2 * z + y

    def coords(self, *dims):
        return [rem(v + 1, 2) if d in dims else v for d, v in enumerate(self.bits)]

    def chunk(self, *dims):
        x, bl = self.flip(*dims)
        return 2 * bl + x

    def slot(self, *dims):
        x, bl = self.flip(*dims)
        return 4 * x + bl

    def cube(self, *dims):
        x, bl = self.flip(*dims)
        return (2 * x + self.c, 4 * self.g + bl)

    def sibling(self):
        return (2 * self.x + 1 - self.c, self.b)

    def ahead(self, i):
        return rem(self.g + i, self.groups)

    def behind(self, i):
        return rem(self.g + self.groups - i, self.groups)

    def mid(self, i):
        return (self.u, 4 * self.ahead(i) + self.bl)

    def diagonal(self):
        x, y, z = self.bits
        return (2 * x + 1 - self.c, 4 * self.g + 2 * z + 1 - y)

    def mid_at(self, group):
        return (self.u, 4 * group + self.bl)


PEERS = ((0,), (1,), (2,), (0, 1), (0, 2), (1, 2), (0, 1, 2))


def meet(devices):
    barrier = pltpu.get_barrier_semaphore()
    for device in devices:
        pl.semaphore_signal(barrier, inc=1, device_id=device, device_id_type=MESH)
    pl.semaphore_wait(barrier, len(devices))


def remote(src, dst, send, recv, device):
    return pltpu.make_async_remote_copy(
        src_ref=src, dst_ref=dst, send_sem=send, recv_sem=recv, device_id=device, device_id_type=MESH
    )


def rows_at(start, count):
    return pl.ds(pl.multiple_of(start, 16), count)


def drive(*tasks):
    tasks = list(tasks)
    while tasks:
        tasks = [task for task in tasks if next(task, None) is not None]


def steps(task, count):
    for _ in range(count):
        next(task, None)


def paced(loop, count, between, when=None):
    def one(i, carry):
        loop(i)
        return carry

    for k in range(4):
        run = (k * count // 4, (k + 1) * count // 4)
        if when is None:
            lax.fori_loop(*run, one, 0)
        else:

            @pl.when(when)
            def _():
                lax.fori_loop(*run, one, 0)

        between()


def piece_rows(rows):
    return 32 if rows % 32 == 0 else 16


def beside(main, *bulk):
    for _ in main:
        for task in bulk:
            next(task, None)


def in_turn(*tasks):
    for task, count in tasks:
        for _ in range(count):
            next(task, None)
            yield True


def part_columns(split):
    start = 0
    for p, (order, width) in enumerate(split):
        yield p, order, pl.ds(start, width)
        start += width


def gather_tokens(at, mine, block, local, send, recv, split=None):
    own = pltpu.make_async_copy(mine, block.at[at.chunk()], local)
    own.start()
    sent = []

    def push(p, i, dims, along, cols):
        src = block.at[at.chunk(*dims), :, cols] if dims else mine.at[:, cols]
        copy = remote(src, block.at[at.chunk(*dims), :, cols], send.at[p, i], recv.at[p, i], at.cube(along))
        copy.start()
        sent.append(copy)

    def arrive(p, i, dims, cols):
        there = block.at[at.chunk(*dims), :, cols]
        remote(there, there, send.at[p, i], recv.at[p, i], at.cube(dims[0])).wait_recv()

    parts = list(part_columns(split or PARTS))
    over = [sorted(parts, key=lambda part: part[1][k] == 2) for k in range(3)]
    for p, (a, b, c), cols in parts:
        push(p, 0, (), a, cols)
        push(p, 1, (), b, cols)
        push(p, 2, (), c, cols)
    yield True
    for p, (a, b, c), cols in over[0]:
        arrive(p, 0, (a,), cols)
        push(p, 3, (a,), b, cols)
        push(p, 4, (a,), c, cols)
        yield True
    for p, (a, b, c), cols in over[1]:
        arrive(p, 1, (b,), cols)
        push(p, 5, (b,), c, cols)
        arrive(p, 3, (a, b), cols)
        push(p, 6, (a, b), c, cols)
        yield True
    for p, (a, b, c), cols in parts:
        arrive(p, 2, (c,), cols)
        arrive(p, 4, (a, c), cols)
        arrive(p, 5, (b, c), cols)
        arrive(p, 6, (a, b, c), cols)
    for copy in sent:
        copy.wait_send()
    own.wait()


def add_rows(dst, terms, count, step=32):
    def body(i, carry):
        rows = pl.ds(pl.multiple_of(i * step, step), step)
        total = terms[0][rows, :].astype(F32)
        for term in terms[1:]:
            total = total + term[rows, :].astype(F32)
        dst[rows, :] = total.astype(dst.dtype)
        return carry

    lax.fori_loop(0, count // step, body, 0)


def scatter_tokens(at, part, land, out, send, recv, split=None):
    sent = []

    def push(p, i, dims, along, cols):
        copy = remote(part.at[at.chunk(*dims), :, cols], land.at[i, :, cols], send.at[p, i], recv.at[p, i], at.cube(along))
        copy.start()
        sent.append(copy)

    def arrive(p, i, along, cols):
        remote(land.at[i, :, cols], land.at[i, :, cols], send.at[p, i], recv.at[p, i], at.cube(along)).wait_recv()

    def add(i, dims, cols):
        here = part.at[at.chunk(*dims), :, cols]
        add_rows(here, [here, land.at[i, :, cols]], CHUNK)

    parts = list(part_columns(split or PARTS))
    over = [sorted(parts, key=lambda part: part[1][k] == 2) for k in range(3)]
    for p, (a, b, c), cols in parts:
        push(p, 3, (a, b, c), c, cols)
        push(p, 2, (b, c), c, cols)
    for p, (a, b, c), cols in parts:
        push(p, 1, (a, c), c, cols)
        push(p, 0, (c,), c, cols)
    yield True
    for p, (a, b, c), cols in over[2]:
        arrive(p, 3, c, cols)
        add(3, (a, b), cols)
        push(p, 5, (a, b), b, cols)
        arrive(p, 2, c, cols)
        add(2, (b,), cols)
        push(p, 4, (b,), b, cols)
        yield True
    for p, (a, b, c), cols in over[1]:
        arrive(p, 1, c, cols)
        add(1, (a,), cols)
        arrive(p, 5, b, cols)
        add(5, (a,), cols)
        push(p, 6, (a,), a, cols)
        yield True
    for p, (a, b, c), cols in over[0]:
        arrive(p, 0, c, cols)
        arrive(p, 4, b, cols)
        arrive(p, 6, a, cols)
        add_rows(
            out.at[:, cols],
            [part.at[at.chunk(), :, cols], land.at[0, :, cols], land.at[4, :, cols], land.at[6, :, cols]],
            CHUNK,
        )
    for copy in sent:
        copy.wait_send()


def column_row(at, rows, u, b):
    return (u * (4 * at.groups) + b) * rows


class Columns:
    def qkv(x, y, z):
        pair = 4 * x + 2 * y + z
        return [(pair * (2 * HD), 2 * HD), (HQ * HD + pair * HD, HD), ((HQ + HK) * HD + pair * HD, HD)]

    def gate_up(groups, hidden_rows):
        wide = 2 * hidden_rows
        if wide % 128:
            return lambda x, y, z: [((4 * x + 2 * z + y) * GU_SLOT, GU_SLOT)]

        def runs(x, y, z):
            return [
                (half * FF + (((2 * x + y) * groups + group) * 2 + z) * wide, wide)
                for half in range(2)
                for group in range(groups)
            ]

        return runs


def column_runs(ref, whole, runs):
    at = 0
    for first, width in runs:
        yield ref.at[:, pl.ds(pl.multiple_of(first, 128), width)], whole.at[:, pl.ds(at, width)]
        at += width


def columns_in_cube(at, mine, whole, runs, local, send, recv, rows):
    own = rows_at(column_row(at, rows, at.u, at.b), rows)
    here = []
    for k, (src, dst) in enumerate(column_runs(mine, whole.at[own], runs(*at.coords()))):
        here.append(pltpu.make_async_copy(src, dst, local.at[k]))
        here[-1].start()
    sent = []
    for i, dims in enumerate(PEERS):
        for k, (src, dst) in enumerate(column_runs(mine, whole.at[own], runs(*at.coords(*dims)))):
            copy = remote(src, dst, send.at[i, k], recv.at[i, k], at.cube(*dims))
            copy.start()
            sent.append(copy)
    yield True
    for i, dims in enumerate(PEERS):
        u, b = at.cube(*dims)
        there = whole.at[rows_at(column_row(at, rows, u, b), rows)]
        for k, (_, dst) in enumerate(column_runs(mine, there, runs(*at.coords()))):
            remote(dst, dst, send.at[i, k], recv.at[i, k], (u, b)).wait_recv()
    for copy in sent:
        copy.wait_send()
    for copy in here:
        copy.wait()


def columns_across(at, whole, rows, mid_send, mid_recv, sib_send, sib_recv):
    n, pieces = at.groups, mid_send.shape[2]
    step = 4 * rows // pieces
    sent = []

    def piece(core, group, x, k):
        return whole.at[rows_at(column_row(at, rows, 2 * x + core, 4 * group) + k * step, step)]

    def pass_on(i, x, k):
        there = piece(at.c, at.behind(i), x, k)
        copy = remote(there, there, sib_send.at[i, x, k], sib_recv.at[i, x, k], at.sibling())
        copy.start()
        sent.append(copy)

    order = [(x, k) for x in range(2) for k in range(pieces)]
    every = [(i, x, k) for i in range(1, n) for x, k in order]

    def arrived(i, x, k):
        there = piece(at.c, at.behind(i), x, k)
        remote(there, there, mid_send.at[i, x, k], mid_recv.at[i, x, k], at.mid(i)).wait_recv()
        pass_on(i, x, k)

    for m, (i, x, k) in enumerate(every):
        there = piece(at.c, at.g, x, k)
        copy = remote(there, there, mid_send.at[i, x, k], mid_recv.at[i, x, k], at.mid(i))
        copy.start()
        sent.append(copy)
        if i == 1:
            pass_on(0, x, k)
        if m >= WINDOW:
            arrived(*every[m - WINDOW])
        yield True
    for one in every[max(len(every) - WINDOW, 0) :]:
        arrived(*one)
    for i in range(n):
        for x, k in order:
            there = piece(1 - at.c, at.behind(i), x, k)
            remote(there, there, sib_send.at[i, x, k], sib_recv.at[i, x, k], at.sibling()).wait_recv()
    for copy in sent:
        copy.wait_send()


def gather_hidden(at, mine, whole, local, turn_send, turn_recv, mid_send, mid_recv, sib_send, sib_recv):
    n, rows, pieces = at.groups, mine.shape[0], mid_send.shape[1]
    step = rows // pieces
    own = whole.at[at.g, at.c]
    stays = at.bits[1] == at.c
    here = pltpu.make_async_copy(mine, own, local)
    there = remote(mine, whole.at[at.g, 1 - at.c], turn_send, turn_recv, at.diagonal())

    @pl.when(stays)
    def _():
        here.start()

    @pl.when(jnp.logical_not(stays))
    def _():
        there.start()

    yield True

    @pl.when(stays)
    def _():
        here.wait()

    @pl.when(jnp.logical_not(stays))
    def _():
        there.wait()

    sent = []
    for i in range(1, n):
        for k in range(pieces):
            piece = own.at[pl.ds(k * step, step)]
            copy = remote(piece, piece, mid_send.at[i, k], mid_recv.at[i, k], at.mid(i))
            copy.start()
            sent.append(copy)
            yield True

    def pass_on(i):
        group = whole.at[at.behind(i), at.c]
        copy = remote(group, group, sib_send.at[i], sib_recv.at[i], at.sibling())
        copy.start()
        sent.append(copy)

    pass_on(0)
    for i in range(1, n):
        for k in range(pieces):
            piece = whole.at[at.behind(i), at.c, pl.ds(k * step, step)]
            remote(piece, piece, mid_send.at[i, k], mid_recv.at[i, k], at.mid(i)).wait_recv()
        pass_on(i)
    for i in range(n):
        group = whole.at[at.behind(i), 1 - at.c]
        remote(group, group, sib_send.at[i], sib_recv.at[i], at.sibling()).wait_recv()
    for copy in sent:
        copy.wait_send()


class OutRows:
    def __init__(self, at, rows):
        self.at, self.rows = at, rows
        self.per_half = max(at.groups // 2, 1)
        self.my_half = at.g // self.per_half
        self.to = 2 * self.my_half + at.c
        self.collects = at.bl == self.to
        self.slot_core = rem(at.bl, 2) == at.c
        self.slot_half = at.bl // 2

    def group_rows(self, group, half):
        return rows_at((group - half * self.per_half) * (4 * self.rows), 4 * self.rows)

    def in_half(self, group, half):
        return group // self.per_half == half

    def device(self, bl):
        return (self.at.u, 4 * self.at.g + bl)


def gather_heads(at, mine, whole, local, send, recv, sib_send, sib_recv):
    n, rows = mine.shape[0], mine.shape[1]
    lay = OutRows(at, rows)

    def place(group, bl):
        half = group // lay.per_half
        return whole.at[rows_at(((group - half * lay.per_half) * 4 + bl) * rows, rows)]

    def push(i):
        group = at.behind(i)
        to = 2 * (group // lay.per_half) + at.c
        here = pltpu.make_async_copy(mine.at[i], place(group, at.bl), local.at[i])
        there = remote(mine.at[i], place(group, at.bl), send.at[i], recv.at[i, at.bl], lay.device(to))
        return at.bl == to, here, there

    for i in range(n):
        stays, here, there = push(i)

        @pl.when(stays)
        def _():
            here.start()

        @pl.when(jnp.logical_not(stays))
        def _():
            there.start()

    yield True

    @pl.when(lay.slot_core)
    def _():
        for i in range(n):
            group = at.behind(i)

            @pl.when(lay.in_half(group, lay.slot_half))
            def _():
                pltpu.make_async_copy(mine.at[i], place(group, at.bl), local.at[i]).wait()
                for bl in range(4):

                    @pl.when(at.bl != bl)
                    def _():
                        there = place(group, bl)
                        remote(there, there, send.at[i], recv.at[i, bl], lay.device(bl)).wait_recv()

        remote(whole, whole, sib_send, sib_recv, at.sibling()).start()

    yield True

    @pl.when(lay.slot_core)
    def _():
        remote(whole, whole, sib_send, sib_recv, at.sibling()).wait_send()

    @pl.when(jnp.logical_not(lay.slot_core))
    def _():
        remote(whole, whole, sib_send, sib_recv, at.sibling()).wait_recv()

    for i in range(n):
        stays, here, there = push(i)

        @pl.when(jnp.logical_not(stays))
        def _():
            there.wait_send()


def columns_home(at, final, out, runs, send, recv, local):
    sent = []
    for i, dims in enumerate(PEERS):
        x, bl = at.flip(*dims)
        for k, (dst, src) in enumerate(column_runs(out, final.at[x, bl], runs(*at.coords()))):
            copy = remote(src, dst, send.at[i, k], recv.at[i, k], at.cube(*dims))
            copy.start()
            sent.append(copy)
    here = []
    for k, (dst, src) in enumerate(column_runs(out, final.at[at.x, at.bl], runs(*at.coords()))):
        here.append(pltpu.make_async_copy(src, dst, local.at[k]))
        here[-1].start()
    yield True
    for i, dims in enumerate(PEERS):
        for k, (there, _) in enumerate(column_runs(out, final.at[at.x, at.bl], runs(*at.coords(*dims)))):
            remote(there, there, send.at[i, k], recv.at[i, k], at.cube(*dims)).wait_recv()
    for copy in sent:
        copy.wait_send()
    for copy in here:
        copy.wait()


def columns_sum(at, part, sib_land, mid_land, final, sems, at_once=1):
    n, rows = at.groups, final.shape[2]
    mid_send, mid_recv, sib_send, sib_recv = sems
    run, deep = 4 * rows, 4 * n * rows
    step = piece_rows(rows)
    pieces = [(k, j) for k in range(4) for j in range(rows // step)]
    sent = []

    def of_core(x, core):
        return part.at[rows_at((2 * x + core) * deep, deep)]

    for x in range(2):
        copy = remote(of_core(x, 1 - at.c), sib_land.at[x], sib_send.at[x], sib_recv.at[x], at.sibling())
        copy.start()
        sent.append(copy)
    yield True
    for x in range(2):
        remote(sib_land.at[x], sib_land.at[x], sib_send.at[x], sib_recv.at[x], at.sibling()).wait_recv()
        for i in range(1, n):
            for m, (k, j) in enumerate(pieces):
                offset = at.ahead(i) * run + k * rows + j * step
                there = part.at[rows_at((2 * x + at.c) * deep + offset, step)]
                add_rows(there, [there, sib_land.at[x, rows_at(offset, step)]], step, 16)
                land = mid_land.at[i - 1, x, k, pl.ds(j * step, step)]
                copy = remote(there, land, mid_send.at[i, x, m], mid_recv.at[i, x, m], at.mid(i))
                copy.start()
                sent.append(copy)
                if m % at_once == at_once - 1:
                    yield True
    for x in range(2):
        for m, (k, j) in enumerate(pieces):
            for i in range(1, n):
                there = mid_land.at[i - 1, x, k, pl.ds(j * step, step)]
                remote(there, there, mid_send.at[i, x, m], mid_recv.at[i, x, m], at.mid(i)).wait_recv()
            offset = at.g * run + k * rows + j * step
            rows_here = pl.ds(j * step, step)
            add_rows(
                final.at[x, k, rows_here],
                [part.at[rows_at((2 * x + at.c) * deep + offset, step)], sib_land.at[x, rows_at(offset, step)]]
                + [mid_land.at[i - 1, x, k, rows_here] for i in range(1, n)],
                step,
                16,
            )
    for copy in sent:
        copy.wait_send()


def turn_hidden(at, final, out, turn_send, turn_recv, local):
    stays = at.bits[1] == at.c
    here = pltpu.make_async_copy(final, out, local)
    there = remote(final, out, turn_send, turn_recv, at.diagonal())

    @pl.when(stays)
    def _():
        here.start()

    @pl.when(jnp.logical_not(stays))
    def _():
        there.start()

    yield True

    @pl.when(stays)
    def _():
        here.wait()

    @pl.when(jnp.logical_not(stays))
    def _():
        there.wait()


def scatter_heads(at, part, out, sib_land, mid_land, sems):
    n, rows = at.groups, out.shape[0]
    send, recv, mid_send, mid_recv, sib_send, sib_recv, local = sems
    lay = OutRows(at, rows)

    @pl.when(jnp.logical_not(lay.slot_core))
    def _():
        remote(part, sib_land, sib_send, sib_recv, at.sibling()).start()

    yield True

    @pl.when(lay.slot_core)
    def _():
        remote(part, sib_land, sib_send, sib_recv, at.sibling()).wait_recv()
        add_rows(part, [part, sib_land], 256, 16)
        for i in range(1, n):
            group = at.ahead(i)

            @pl.when(lay.in_half(group, lay.slot_half))
            def _():
                there = part.at[lay.group_rows(group, lay.slot_half)]
                remote(there, mid_land.at[i - 1], mid_send.at[i], mid_recv.at[i], at.mid(i)).start()

    yield True
    mine = part.at[lay.group_rows(at.g, lay.my_half)]
    base = (at.g - lay.my_half * lay.per_half) * (4 * rows)

    @pl.when(lay.collects)
    def _():
        for i in range(1, n):
            remote(mine, mid_land.at[i - 1], mid_send.at[i], mid_recv.at[i], at.mid(i)).wait_recv()
        add_rows(mine, [mine] + [mid_land.at[i - 1] for i in range(1, n)], 4 * rows, 16)
        for bl in range(4):
            there = part.at[rows_at(base + bl * rows, rows)]

            @pl.when(at.bl != bl)
            def _():
                remote(there, out, send.at[bl], recv, lay.device(bl)).start()

            @pl.when(at.bl == bl)
            def _():
                pltpu.make_async_copy(there, out, local).start()

    yield True

    @pl.when(jnp.logical_not(lay.collects))
    def _():
        remote(out, out, send.at[0], recv, lay.device(lay.to)).wait_recv()

    @pl.when(lay.collects)
    def _():
        for bl in range(4):
            there = part.at[rows_at(base + bl * rows, rows)]

            @pl.when(at.bl != bl)
            def _():
                remote(there, out, send.at[bl], recv, lay.device(bl)).wait_send()

            @pl.when(at.bl == bl)
            def _():
                pltpu.make_async_copy(there, out, local).wait()

    @pl.when(jnp.logical_not(lay.slot_core))
    def _():
        remote(part, sib_land, sib_send, sib_recv, at.sibling()).wait_send()

    @pl.when(lay.slot_core)
    def _():
        for i in range(1, n):
            group = at.ahead(i)

            @pl.when(lay.in_half(group, lay.slot_half))
            def _():
                there = part.at[lay.group_rows(group, lay.slot_half)]
                remote(there, mid_land.at[i - 1], mid_send.at[i], mid_recv.at[i], at.mid(i)).wait_send()


def sum_everywhere(at, mine, land, send, recv):
    for i, device in enumerate([at.sibling(), at.cube(0), at.cube(1), at.cube(2)]):
        copy = remote(mine, land.at[i], send.at[i], recv.at[i], device)
        copy.start()
        yield True
        copy.wait()
        mine[...] = mine[...] + land[i]
    sent = []
    for i in range(1, at.groups):
        copy = remote(mine, land.at[3 + i], send.at[3 + i], recv.at[3 + i], at.mid(i))
        copy.start()
        sent.append(copy)
    yield True
    for copy in sent:
        copy.wait()
    for i in range(1, at.groups):
        mine[...] = mine[...] + land[3 + i]


def everyone(at):
    return [at.cube(*dims) for dims in PEERS] + [at.sibling()] + [at.mid(i) for i in range(1, at.groups)]


def cube_only(at):
    return [at.cube(*dims) for dims in ((0,), (1,), (2,))]


def communicate(body, collective_id, ins, outs, scratch, in_specs, out_specs, limit=60):
    return pl.pallas_call(
        body,
        out_shape=outs,
        in_specs=in_specs,
        out_specs=out_specs,
        scratch_shapes=scratch,
        compiler_params=pltpu.CompilerParams(
            collective_id=collective_id, has_side_effects=True, vmem_limit_bytes=limit << 20
        ),
    )(*ins)


def like(shape, dtype=BF16):
    return jax.ShapeDtypeStruct(shape, dtype)


NT = (((1,), (1,)), ((), ()))
WIDE = 512
SCALE_2 = SCALE / math.log(2.0)


def visible(first_key, chunk_of_block, opening, tile):
    key = first_key + lax.broadcasted_iota(jnp.int32, (tile, 2 * CHUNK), 0)
    lane = lax.broadcasted_iota(jnp.int32, (1, 2 * CHUNK), 1)
    row = chunk_of_block * CHUNK + jnp.where(lane >= CHUNK, lane - CHUNK, lane)
    return (key <= row) & (key >= opening)


def key_range(group, chunk_of_block, tile):
    stop = (chunk_of_block * CHUNK + CHUNK + tile - 1) // tile
    start = jnp.where(group > 0, jnp.maximum(chunk_of_block * CHUNK - LONGEST, 0) // tile, 0)
    return start, stop


def two_heads(block):
    return jnp.concatenate([block[:, :HD], block[:, HD:]], 0)


def two_columns(block):
    return jnp.concatenate([block[:CHUNK], block[CHUNK:]], 1)


def turn_values(kv, turned):
    for t in range(kv.shape[0]):
        turned[:, pl.ds(2 * CHUNK * t, 2 * CHUNK)] = kv[t].reshape(2 * CHUNK, 2 * HD)[:, HD:].T


def front_block(groups, rows, hidden_rows, ins):
    n = groups
    gate_up = Columns.gate_up(groups, hidden_rows)
    count = len(gate_up(0, 0, 0))
    pieces = hidden_rows // piece_rows(hidden_rows)
    gu_pieces = 4 * rows // piece_rows(4 * rows)

    def body(r):
        at = Place(n)
        group, core = at.g, at.c

        def first_norm(i, carry):
            rows_i = pl.ds(pl.multiple_of(i * 32, 32), 32)
            value = r.tokens[rows_i, :].astype(F32)
            r.xhat[rows_i, :] = (value * lax.rsqrt(jnp.mean(value * value, 1, keepdims=True) + EPSILON)).astype(BF16)
            return carry

        lax.fori_loop(0, CHUNK // 32, first_norm, 0)
        r.qkv_mine[...] = (r.w_qkv[...].astype(F32) * r.gain_one[...]).astype(BF16)
        meet(everyone(at) + [at.diagonal()])
        far = [remote(r.out_mine, r.out_all.at[i], r.fs.at[i], r.fr.at[i], at.mid(i)) for i in range(1, n)]
        for copy in far:
            copy.start()
        wide = columns_in_cube(at, r.qkv_mine, r.qkv, Columns.qkv, r.qkv_local, r.qs, r.qr, rows)
        next(wide)
        tokens = gather_tokens(at, r.xhat, r.xhat_b, r.local.at[1], r.s1, r.r1, FRONT)
        next(tokens)
        lower = gather_hidden(at, r.down_mine, r.down, r.local.at[2], r.hts, r.htr, r.hms, r.hmr, r.hss, r.hsr)
        next(lower)
        out_here = pltpu.make_async_copy(r.out_mine, r.out_all.at[0], r.local.at[3])
        out_here.start()

        def scale(i, carry):
            cols = pl.ds(pl.multiple_of(i * 1024, 1024), 1024)
            r.gu_mine[:, cols] = (r.w_gu[:, cols].astype(F32) * r.gain_two[...]).astype(BF16)
            return carry

        lax.fori_loop(0, 2 * FF // 1024, scale, 0)

        def round_dy(i, carry):
            rows_i = pl.ds(pl.multiple_of(i * 32, 32), 32)
            r.dy[rows_i, :] = r.cotangent[rows_i, :].astype(BF16)
            return carry

        lax.fori_loop(0, CHUNK // 32, round_dy, 0)
        steps(tokens, 3)
        drive(wide)
        wide = columns_across(at, r.qkv, rows, r.qms, r.qmr, r.qss, r.qsr)
        steps(wide, 2 * (n - 1))
        steps(tokens, 3)
        columns = columns_in_cube(at, r.gu_mine, r.gu, gate_up, r.gu_local, r.cs, r.cr, rows)
        next(columns)
        out_here.wait()
        for copy in far:
            copy.wait()
        heads = gather_heads(at, r.out_all, r.w_out, r.hl, r.hs, r.hr, r.os, r.orr)
        next(heads)
        steps(lower, 1)
        drive(tokens)
        drive(wide)

        def project_in(i):
            four = pl.ds(pl.multiple_of(4 * i, 4), 4)
            raw = jnp.dot(r.xhat_b[four].reshape(4 * CHUNK, D), r.qkv[...], preferred_element_type=F32)
            cosine, sine = r.cosine[four].reshape(4 * CHUNK, HD), r.sine[four].reshape(4 * CHUNK, HD)
            heads = []
            for h in range(3):
                head = raw[:, h * HD : (h + 1) * HD]
                gain = r.head_gain[h : h + 1, :]
                normed = head * lax.rsqrt(jnp.mean(head * head, 1, keepdims=True) + EPSILON) * gain
                heads.append((normed * cosine + pltpu.roll(normed, HD // 2, 1) * sine).astype(BF16))
            r.raw[four] = raw[:, : 3 * HD].reshape(4, CHUNK, 3 * HD)
            r.q[four] = jnp.concatenate(heads[:2], 1).reshape(4, CHUNK, 2 * HD)
            r.kv[four] = jnp.concatenate([heads[2], raw[:, 3 * HD :].astype(BF16)], 1).reshape(4, CHUNK, 2 * HD)

        for i in range(2):
            lax.fori_loop(i, i + 1, lambda i, carry: (project_in(i), carry)[1], 0)
        leaving = send_early(r, "xhat_b", "qkv", "raw")

        here = pltpu.make_async_copy(r.kv, r.own.at[:, core], r.local.at[1])
        here.start()
        sib = remote(r.kv, r.own.at[:, core], r.ks.at[0], r.kr.at[0], at.sibling())
        sib.start()

        def to_group(i):
            return remote(r.kv, r.prompt.at[:, core], r.ps.at[i], r.pr, at.mid_at(jnp.int32(i)))

        def forward():
            half = r.kv.at[pl.ds(SLOTS // 2, SLOTS // 2)]
            return remote(half, r.before.at[:, core], r.bs, r.br, at.mid_at(group + 1))

        def across(ref, i):
            return remote(ref.at[:, core], ref.at[:, core], r.ks.at[i], r.kr.at[i], at.sibling())

        @pl.when(group == 0)
        def _():
            for i in range(1, n):
                to_group(i).start()

        if n > 2:

            @pl.when((group >= 1) & (group < n - 1))
            def _():
                forward().start()

        here.wait()
        sib.wait()
        turn_values(r.own, r.own_vt)
        drive(columns)
        columns = columns_across(at, r.gu, rows, r.cms, r.cmr, r.css, r.csr)
        bulk = in_turn((lower, pieces * (n - 1) - 1), (columns, 2 * gu_pieces * (n - 1)))
        steps(bulk, 1)
        dy = gather_tokens(at, r.dy, r.dy_b, r.local.at[4], r.s3, r.r3)
        next(dy)

        def step(kv, values_t, tile, chunk, q, opening, carry, masked, shift=0):
            norm, out = carry
            first = tile * WIDE
            parts = []
            for k in range(WIDE // CHUNK):
                keys = kv[tile * (WIDE // (2 * CHUNK)) + k // 2, k % 2][:, :HD]
                p = jnp.exp2(lax.dot_general(keys, q, NT, preferred_element_type=F32) * SCALE_2)
                if masked:
                    p = jnp.where(visible(first + shift + k * CHUNK, chunk, opening, CHUNK), p, 0.0)
                norm = norm + jnp.sum(p, 0, keepdims=True)
                parts.append(p.astype(BF16))
            first = first if isinstance(first, int) else pl.multiple_of(first, WIDE)
            out = out + jnp.dot(
                values_t[:, pl.ds(first, WIDE)], jnp.concatenate(parts, 0), preferred_element_type=F32
            )
            return norm, out

        def own_part(i):
            chunk = 2 * i + core
            query, opening = two_heads(r.q[i]), r.opening[i]
            start, stop = key_range(group, chunk, WIDE)
            zero = (jnp.zeros((1, 2 * CHUNK), F32), jnp.zeros((HD, 2 * CHUNK), F32))
            norm, out = lax.fori_loop(
                start, stop, lambda t, c: step(r.own, r.own_vt, t, chunk, query, opening, c, True), zero
            )
            r.lse[i] = norm
            r.total[i] = out

        paced(own_part, SLOTS, lambda: steps(bulk, 1))
        next(heads)

        @pl.when(group > 0)
        def _():
            to_group(0).wait_recv()
            across(r.prompt, 1).start()

        if n > 2:

            @pl.when(group > 1)
            def _():
                forward().wait_recv()
                across(r.before, 2).start()

        steps(dy, 3)
        steps(bulk, 1)

        @pl.when(group > 0)
        def _():
            across(r.prompt, 1).wait()
            turn_values(r.prompt, r.prompt_vt)

        def prompt_part(i):
            query = two_heads(r.q[i])
            state = (r.lse[i], r.total[i])
            for t in range(PROMPT // WIDE):
                state = step(r.prompt, r.prompt_vt, t, 0, query, None, state, False)
            r.lse[i], r.total[i] = state

        paced(prompt_part, SLOTS, lambda: steps(bulk, 1), group > 0)

        if n > 2:

            @pl.when(group > 1)
            def _():
                across(r.before, 2).wait()
                turn_values(r.before, r.before_vt)

                def before_part(i, carry):
                    query, opening = two_heads(r.q[i]), r.opening[i]
                    state = (r.lse[i], r.total[i])
                    for t in range(LONGEST // WIDE):
                        state = step(r.before, r.before_vt, t, 2 * i + core, query, opening, state, True, -LONGEST)
                    r.lse[i], r.total[i] = state
                    return carry

                lax.fori_loop(0, SLOTS // 2, before_part, 0)

        steps(dy, 3)
        steps(bulk, 1)
        drive(heads)

        def project_out(i, carry):
            norm = r.lse[i]
            out = r.total[i] / norm
            r.total[i] = out
            r.lse[i] = jnp.log(norm)
            row = two_columns(out.T.astype(BF16))
            r.mixed[i] = row
            r.part[i] = jnp.dot(row, r.w_out[...], preferred_element_type=F32).astype(BF16)
            return carry

        lax.fori_loop(0, SLOTS, project_out, 0)
        beside(scatter_tokens(at, r.part, r.land, r.hidden, r.s4, r.r4, FRONT), bulk)

        def norm_rows(i, carry):
            rows = pl.ds(pl.multiple_of(i * 32, 32), 32)
            value = r.hidden[rows, :] + r.tokens[rows, :].astype(F32)
            r.hidden[rows, :] = value
            inverse = lax.rsqrt(jnp.mean(value * value, 1, keepdims=True) + EPSILON)
            r.mine[rows, :] = (value * inverse).astype(BF16)
            return carry

        lax.fori_loop(0, CHUNK // 32, norm_rows, 0)
        beside(gather_tokens(at, r.mine, r.xhat2_b, r.local.at[5], r.s2, r.r2, FRONT), bulk)
        drive(dy, bulk)
        drive(lower, columns)
        for copy in leaving:
            copy.wait()

        @pl.when(group == 0)
        def _():
            for i in range(1, n):
                to_group(i).wait_send()

        if n > 2:

            @pl.when((group >= 1) & (group < n - 1))
            def _():
                forward().wait_send()

    chunks = (SLOTS, CHUNK, 2 * HD)
    block, end = (SLOTS, 2, CHUNK, 2 * HD), (SLOTS // 2, 2, CHUNK, 2 * HD)
    tok = DMA((len(PARTS), 7))
    return kernel(
        1,
        body,
        {name: (a, HBM if name in ("down_mine", "out_mine") else VMEM) for name, a in ins.items()},
        {
            "xhat_b": (like((SLOTS, CHUNK, D)), EARLY),
            "qkv": (like((D, QKV_SLOT)), EARLY),
            "raw": (like((SLOTS, CHUNK, 3 * HD), F32), EARLY),
            "q": (like(chunks), VMEM),
            "mixed": (like(chunks), VMEM),
            "total": (like((SLOTS, HD, 2 * CHUNK), F32), VMEM),
            "lse": (like((SLOTS, 1, 2 * CHUNK), F32), VMEM),
            "own": (like(block), VMEM),
            "prompt": (like(block), VMEM),
            "before": (like(end), VMEM),
            "w_out": (like((D // SLOTS, D)), VMEM),
            "hidden": (like((CHUNK, D), F32), VMEM),
            "xhat2_b": (like((SLOTS, CHUNK, D)), HBM),
            "gu": (like((D, GU_SLOT)), HBM),
            "down": (like((n, 2, hidden_rows, D)), HBM),
            "dy_b": (like((SLOTS, CHUNK, D)), HBM),
        },
        {
            "kv": pltpu.VMEM(chunks, BF16),
            "xhat": pltpu.VMEM((CHUNK, D), BF16),
            "dy": pltpu.VMEM((CHUNK, D), BF16),
            "qkv_mine": pltpu.VMEM((rows, (HQ + 2 * HK) * HD), BF16),
            "gu_mine": pltpu.VMEM((rows, 2 * FF), BF16),
            "own_vt": pltpu.VMEM((HD, 2 * SLOTS * CHUNK), BF16),
            "prompt_vt": pltpu.VMEM((HD, PROMPT), BF16),
            "before_vt": pltpu.VMEM((HD, LONGEST), BF16),
            "part": pltpu.VMEM((SLOTS, CHUNK, D), BF16),
            "land": pltpu.VMEM((7, CHUNK, D), BF16),
            "mine": pltpu.VMEM((CHUNK, D), BF16),
            "out_all": pltpu.VMEM((n, rows, D), BF16),
            "local": DMA((6,)),
            **{name: tok for name in ("s1", "r1", "s2", "r2", "s3", "r3", "s4", "r4")},
            **{name: DMA((7, 3)) for name in ("qs", "qr")},
            **{name: DMA((7, count)) for name in ("cs", "cr")},
            "qkv_local": DMA((3,)),
            "gu_local": DMA((count,)),
            **{name: DMA((n, 2, 1)) for name in ("qms", "qmr", "qss", "qsr")},
            **{name: DMA((n, 2, gu_pieces)) for name in ("cms", "cmr", "css", "csr")},
            **{name: DMA((n, pieces)) for name in ("hms", "hmr")},
            **{name: DMA((n,)) for name in ("hss", "hsr", "fs", "fr", "hl", "hs", "ps")},
            **{name: DMA(()) for name in ("hts", "htr", "os", "orr", "pr", "bs", "br")},
            "hr": DMA((n, 4)),
            **{name: DMA((3,)) for name in ("ks", "kr")},
        },
    )


def attention_back(at, r, part, between, when=None):
    kv, keys_t, acc = getattr(r, part), getattr(r, part + "_kt"), getattr(r, "acc_" + part)

    def begin():
        keys_t[...] = kv[:, :HD].T
        acc[...] = jnp.zeros_like(acc)

    shift = -LONGEST if part == "before" else 0

    def step(t, dq, q, do, dot_rows, logs, chunk, opening):
        first = t * WIDE
        rows = pl.ds(first if isinstance(first, int) else pl.multiple_of(first, WIDE), WIDE)
        keys, values = kv[rows, :HD], kv[rows, HD:]
        p = jnp.exp2(lax.dot_general(keys, q, NT, preferred_element_type=F32) * SCALE_2 - logs)
        if part != "prompt":
            p = jnp.where(visible(first + shift, chunk, opening, WIDE), p, 0.0)
        dp = lax.dot_general(values, do, NT, preferred_element_type=F32)
        ds = (p * (dp - dot_rows)).astype(BF16)
        acc[rows, :HD] += jnp.dot(ds, q, preferred_element_type=F32)
        acc[rows, HD:] += jnp.dot(p.astype(BF16), do, preferred_element_type=F32)
        return dq + jnp.dot(keys_t[:, rows], ds, preferred_element_type=F32)

    def one(i):
        chunk = 2 * i + at.c
        q, do = two_heads(r.q[i]), two_heads(r.do[i])
        args = (q, do, r.dots[i], r.lse[i] * (1.0 / math.log(2.0)), chunk, r.opening[i])
        if part == "own":
            start, stop = key_range(at.g, chunk, WIDE)
            r.dq_sum[i] = lax.fori_loop(start, stop, lambda t, dq: step(t, dq, *args), r.dq_sum[i])
        else:
            dq = r.dq_sum[i]
            for t in range(kv.shape[0] // WIDE):
                dq = step(t, dq, *args)
            r.dq_sum[i] = dq

    def end():
        out = getattr(r, "d_" + part)
        for t in range(out.shape[0] * 2):
            out[t // 2, t % 2, :, :HD] = (acc[t * CHUNK : (t + 1) * CHUNK, :HD] * SCALE).astype(BF16)
            out[t // 2, t % 2, :, HD:] = acc[t * CHUNK : (t + 1) * CHUNK, HD:].astype(BF16)

    count = SLOTS if part != "before" else SLOTS // 2
    if when is None:
        begin()
        paced(one, count, between)
        end()
    else:
        pl.when(when)(begin)
        paced(one, count, between, when)
        pl.when(when)(end)


def add_chunks(dst, first, other, skip=0):
    def one(i, carry):
        dst[i + skip] = (first(i).astype(F32) + other[i].astype(F32)).astype(BF16)
        return carry

    lax.fori_loop(0, other.shape[0], one, 0)


LATE, EARLY = "late", "early"


def kernel(collective_id, body, ins, outs, scratch):
    results = list(outs)
    early = [name for name, (_, spec) in outs.items() if spec is EARLY]
    scratch = {
        **scratch,
        **{name: pltpu.VMEM(outs[name][0].shape, outs[name][0].dtype) for name in early},
        **({"early": DMA((len(early),))} if early else {}),
    }
    outs = {name + "_out" if name in early else name: (a, HBM if name in early else spec) for name, (a, spec) in outs.items()}
    late = [name for name, (_, spec) in ins.items() if spec is LATE]
    scratch = {
        **scratch,
        **{name + "_late": pltpu.VMEM(ins[name][0].shape, ins[name][0].dtype) for name in late},
        **({"late": DMA((len(late),))} if late else {}),
    }
    ins = {name: (a, HBM if spec is LATE else spec) for name, (a, spec) in ins.items()}
    names = [*ins, *outs, *scratch]
    return dict(
        zip(
            results,
            communicate(
                lambda *refs: body(types.SimpleNamespace(**dict(zip(names, refs)), early_names=early)),
                collective_id,
                tuple(a for a, _ in ins.values()),
                tuple(a for a, _ in outs.values()),
                list(scratch.values()),
                [spec for _, spec in ins.values()],
                [spec for _, spec in outs.values()],
            ),
        )
    )


def bring_late(r):
    copies = {}
    for k, name in enumerate([name for name in vars(r) if name.endswith("_late")]):
        name = name[: -len("_late")]
        here = getattr(r, name + "_late")
        copies[name] = pltpu.make_async_copy(getattr(r, name), here, r.late.at[k])
        copies[name].start()
        setattr(r, name, here)

    def wait(*some):
        for name in some or list(copies):
            copies.pop(name).wait()

    return wait


def send_early(r, *names):
    copies = []
    for name in names:
        k = r.early_names.index(name)
        copies.append(pltpu.make_async_copy(getattr(r, name), getattr(r, name + "_out"), r.early.at[k]))
        copies[-1].start()
    return copies


def back_block(groups, rows, ins):
    n = groups

    def body(r):
        at = Place(n)
        group = at.g
        bring_dx = pltpu.make_async_copy(r.part_dx, r.part, r.local.at[3])
        bring_dx.start()
        loaded = bring_late(r)
        meet(everyone(at))
        columns = columns_sum(at, r.g_gu, r.sib_gu, r.mid_gu, r.gu_sum, (r.cms, r.cmr, r.css, r.csr))
        next(columns)
        bring_dx.wait()
        bulk = in_turn((columns, r.cms.shape[1] * r.cms.shape[2] * (n - 1)))
        beside(scatter_tokens(at, r.part, r.land, r.dx, r.s1, r.r1), bulk)

        def norm(i, carry):
            rows = pl.ds(pl.multiple_of(i * 32, 32), 32)
            value = r.hidden[rows, :]
            inverse = lax.rsqrt(jnp.mean(value * value, 1, keepdims=True) + EPSILON)
            unit = value * inverse
            grad = r.dx[rows, :]
            total = r.cotangent[rows, :] + inverse * (grad - unit * jnp.mean(grad * unit, 1, keepdims=True))
            r.dhidden[rows, :] = total
            r.mine[rows, :] = total.astype(BF16)
            return carry

        lax.fori_loop(0, CHUNK // 32, norm, 0)
        loaded("act", "down")
        for k, _ in enumerate(gather_tokens(at, r.mine, r.dbranch, r.local.at[0], r.s2, r.r2)):
            steps(bulk, 1)
            if k < SLOTS // 2:
                two = pl.ds(2 * k, 2)
                r.part[two] = (
                    jnp.dot(r.act[two].reshape(2 * CHUNK, FF_SLOT), r.down[...], preferred_element_type=F32)
                    .astype(BF16)
                    .reshape(2, CHUNK, D)
                )
        result = scatter_tokens(at, r.part, r.land2, r.dx, r.s3, r.r3)
        next(result)

        loaded()
        leaving = send_early(r, "dhidden", "dbranch")

        def heads(i, carry):
            do = lax.dot_general(r.dbranch[i], r.w_out[...], NT, preferred_element_type=F32).astype(BF16)
            r.do[i] = do
            r.dots[i] = jnp.sum(two_heads(do).astype(F32).T * r.total[i], 0, keepdims=True)
            r.dq_sum[i] = jnp.zeros((HD, 2 * CHUNK), F32)
            return carry

        lax.fori_loop(0, SLOTS, heads, 0)

        def swap(array, place, i):
            return remote(array.at[:, 1 - at.c], place, r.ks.at[i], r.kr.at[i], at.sibling())

        def home(i):
            return remote(r.land_p, r.far_p.at[i - 1], r.ps, r.pr.at[i - 1], at.mid_at(jnp.int32(0)))

        def back():
            return remote(r.land_b, r.far_b, r.bs, r.br, at.mid_at(group - 1))

        def between():
            steps(bulk, 1)
            steps(result, 1)

        attention_back(at, r, "prompt", between, group > 0)

        @pl.when(group > 0)
        def _():
            swap(r.d_prompt, r.land_p, 1).start()

        if n > 2:
            attention_back(at, r, "before", between, group > 1)

            @pl.when(group > 1)
            def _():
                swap(r.d_before, r.land_b, 2).start()

        @pl.when(group > 0)
        def _():
            swap(r.d_prompt, r.land_p, 1).wait()
            add_chunks(r.land_p, lambda i: r.d_prompt[i, at.c], r.land_p)
            for i in range(1, n):

                @pl.when(group == i)
                def _():
                    home(i).start()

        if n > 2:

            @pl.when(group > 1)
            def _():
                swap(r.d_before, r.land_b, 2).wait()
                add_chunks(r.land_b, lambda i: r.d_before[i, at.c], r.land_b)
                back().start()

        attention_back(at, r, "own", between)
        first = swap(r.d_own, r.land_k, 0)
        first.start()
        drive(bulk)

        def queries(i, carry):
            r.dq[i] = two_columns((r.dq_sum[i].T * SCALE).astype(BF16))
            return carry

        lax.fori_loop(0, SLOTS, queries, 0)
        first.wait()
        add_chunks(r.dkv, lambda i: r.d_own[i, at.c], r.land_k)
        drive(result)

        def add(i, carry):
            rows = pl.ds(pl.multiple_of(i * 32, 32), 32)
            r.output[rows, :] = (r.hidden[rows, :] + r.dx[rows, :]).astype(BF16)
            return carry

        lax.fori_loop(0, CHUNK // 32, add, 0)

        @pl.when(group == 0)
        def _():
            for i in range(1, n):
                home(i).wait_recv()
                add_chunks(r.dkv, lambda j: r.dkv[j], r.far_p.at[i - 1])

        if n > 2:

            @pl.when((group >= 1) & (group < n - 1))
            def _():
                back().wait_recv()
                add_chunks(r.dkv, lambda j: r.dkv[j + SLOTS // 2], r.far_b, SLOTS // 2)

            @pl.when(group > 1)
            def _():
                back().wait_send()

        @pl.when(group > 0)
        def _():
            home(1).wait_send()

        drive(columns)
        for copy in leaving:
            copy.wait()

    chunks = (SLOTS, CHUNK, 2 * HD)
    block, end = (SLOTS, 2, CHUNK, 2 * HD), (SLOTS // 2, 2, CHUNK, 2 * HD)
    tok = DMA((len(PARTS), 7))
    near, half = pltpu.VMEM(chunks, BF16), pltpu.VMEM((SLOTS // 2, CHUNK, 2 * HD), BF16)
    own, prompt, before = 2 * SLOTS * CHUNK, PROMPT, LONGEST
    far = max(n - 1, 1)
    gu_pieces = 4 * (rows // piece_rows(rows))
    late = ("act", "down", "w_out", "q", "own", "prompt", "before", "total")
    return kernel(
        2,
        body,
        {
            name: (a, HBM if name == "part_dx" else LATE if name in late else VMEM)
            for name, a in ins.items()
        },
        {
            "dhidden": (like((CHUNK, D), F32), EARLY),
            "output": (like((CHUNK, D)), VMEM),
            "dbranch": (like((SLOTS, CHUNK, D)), EARLY),
            "dq": (like(chunks), VMEM),
            "dkv": (like(chunks), VMEM),
            "gu_sum": (like((2, 4, rows, GU_SLOT)), VMEM),
        },
        {
            "part": pltpu.VMEM((SLOTS, CHUNK, D), BF16),
            "land": pltpu.VMEM((7, CHUNK, D), BF16),
            "land2": pltpu.VMEM((7, CHUNK, D), BF16),
            "mine": pltpu.VMEM((CHUNK, D), BF16),
            "dx": pltpu.VMEM((CHUNK, D), F32),
            "sib_gu": pltpu.VMEM((2, 4 * n * rows, GU_SLOT), BF16),
            "mid_gu": pltpu.VMEM((far, 2, 4, rows, GU_SLOT), BF16),
            "do": near,
            "dots": pltpu.VMEM((SLOTS, 1, 2 * CHUNK), F32),
            "dq_sum": pltpu.VMEM((SLOTS, HD, 2 * CHUNK), F32),
            "own_kt": pltpu.VMEM((HD, own), BF16),
            "prompt_kt": pltpu.VMEM((HD, prompt), BF16),
            "before_kt": pltpu.VMEM((HD, before), BF16),
            "acc_own": pltpu.VMEM((own, 2 * HD), F32),
            "acc_prompt": pltpu.VMEM((prompt, 2 * HD), F32),
            "acc_before": pltpu.VMEM((before, 2 * HD), F32),
            "d_own": pltpu.VMEM(block, BF16),
            "d_prompt": pltpu.VMEM(block, BF16),
            "d_before": pltpu.VMEM(end, BF16),
            "land_k": near,
            "land_p": near,
            "land_b": half,
            "far_p": pltpu.VMEM((far, *chunks), BF16),
            "far_b": half,
            "local": DMA((4,)),
            **{name: tok for name in ("s1", "r1", "s2", "r2", "s3", "r3")},
            **{name: DMA((n, 2, gu_pieces)) for name in ("cms", "cmr")},
            **{name: DMA((2,)) for name in ("css", "csr")},
            **{name: DMA((3,)) for name in ("ks", "kr")},
            "ps": DMA(()),
            "pr": DMA((n,)),
            "bs": DMA(()),
            "br": DMA(()),
        },
    )


def last_block(groups, rows, hidden_rows, ins):
    n = groups
    gate_up = Columns.gate_up(groups, hidden_rows)
    count = len(gate_up(0, 0, 0))
    late = ("dbranch", "xhat_b", "qkv", "w_gu", "w_qkv")

    def unscale(dst, grad, weight, gain, d_gain):
        total = jnp.zeros((rows, 1), F32)
        for k in range(dst.shape[1] // 2048):
            cols = pl.ds(2048 * k, 2048)
            value = grad[:, cols].astype(F32)
            dst[:, cols] = value * gain[...]
            total = total + jnp.sum(value * weight[:, cols].astype(F32), 1, keepdims=True)
        d_gain[...] = total

    def body(r):
        at = Place(n)
        loaded = bring_late(r)
        meet(everyone(at) + [at.diagonal()])
        bring = columns_home(at, r.gu_sum, r.gu, gate_up, r.ds, r.dr, r.gu_local)
        next(bring)
        lower = turn_hidden(at, r.down_sum, r.down, r.hts, r.htr, r.local.at[0])
        next(lower)
        loaded("dbranch")
        turned = r.mixed[...].reshape(SLOTS * CHUNK, 2 * HD).T

        for k in range(D // 512):
            cols = pl.ds(512 * k, 512)
            r.g_out[:, cols] = jnp.dot(
                turned, r.dbranch[:, :, cols].reshape(SLOTS * CHUNK, 512), preferred_element_type=F32
            ).astype(BF16)
        heads = scatter_heads(at, r.g_out, r.out, r.sib_o, r.mid_o, (r.os, r.orr, r.oms, r.omr, r.oss, r.osr, r.local.at[1]))
        next(heads)
        r.gain_sum[...] = jnp.zeros_like(r.gain_sum)

        def through_heads(i, carry):
            two = pl.ds(pl.multiple_of(2 * i, 2), 2)
            cosine, sine = r.cosine[two].reshape(2 * CHUNK, HD), r.sine[two].reshape(2 * CHUNK, HD)
            raw = r.raw[two].reshape(2 * CHUNK, 3 * HD)
            dq, dkv = r.dq[two].reshape(2 * CHUNK, 2 * HD), r.dkv[two].reshape(2 * CHUNK, 2 * HD)
            parts = []
            for h in range(3):
                grad = (dq[:, h * HD : (h + 1) * HD] if h < 2 else dkv[:, :HD]).astype(F32)
                head = raw[:, h * HD : (h + 1) * HD]
                inverse = lax.rsqrt(jnp.mean(head * head, 1, keepdims=True) + EPSILON)
                unit = head * inverse
                back = grad * cosine + pltpu.roll(grad * sine, HD // 2, 1)
                at_row = 0 if h < 2 else 1
                r.gain_sum[at_row : at_row + 1, :] += jnp.sum(back * unit, 0, keepdims=True)
                back = back * r.head_gain[h : h + 1, :]
                parts.append((inverse * (back - unit * jnp.mean(back * unit, 1, keepdims=True))).astype(BF16))
            draw = jnp.concatenate(parts + [dkv[:, HD:]], 1)
            r.draw[two] = draw.reshape(2, CHUNK, QKV_SLOT)
            return carry

        lax.fori_loop(0, SLOTS // 2, through_heads, 0)
        next(heads)
        sums = sum_everywhere(at, r.gain_sum, r.gain_land, r.gs, r.gr)
        loaded()
        for h in range(QKV_SLOT // HD):
            steps(sums, 1)
            cols = pl.ds(h * HD, HD)
            turned = r.draw[:, :, cols].reshape(SLOTS * CHUNK, HD).T
            grad = jnp.dot(turned, r.xhat_b[...].reshape(SLOTS * CHUNK, D), preferred_element_type=F32)
            r.g_qkv[:, cols] = grad.astype(BF16).T
        wide = columns_sum(at, r.g_qkv, r.sib_q, r.mid_q, r.fin_q, (r.cms, r.cmr, r.css, r.csr), 4)
        next(wide)

        def part_dx(i, carry):
            two = pl.ds(pl.multiple_of(2 * i, 2), 2)
            grad = lax.dot_general(
                r.draw[two].reshape(2 * CHUNK, QKV_SLOT), r.qkv[...], NT, preferred_element_type=F32
            )
            r.part[two] = grad.astype(BF16).reshape(2, CHUNK, D)
            return carry

        lax.fori_loop(0, SLOTS // 2, part_dx, 0)
        steps(wide, 1)
        bulk = in_turn((wide, 2 * (rows // piece_rows(rows)) * (n - 1) - 1))
        main = scatter_tokens(at, r.part, r.land, r.dx, r.s1, r.r1)
        for _ in range(4):
            next(main)
            steps(bulk, 1)
        drive(bring)
        unscale(r.d_gu, r.gu, r.w_gu, r.gain_two, r.d_gain_two)
        leaving = send_early(r, "d_gu")
        next(heads)
        beside(main, bulk)

        def norm(i, carry):
            rows = pl.ds(pl.multiple_of(i * 32, 32), 32)
            value = r.tokens[rows, :].astype(F32)
            inverse = lax.rsqrt(jnp.mean(value * value, 1, keepdims=True) + EPSILON)
            unit = value * inverse
            grad = r.dx[rows, :]
            r.d_tokens[rows, :] = r.dhidden[rows, :] + inverse * (grad - unit * jnp.mean(grad * unit, 1, keepdims=True))
            return carry

        lax.fori_loop(0, CHUNK // 32, norm, 0)
        leaving += send_early(r, "d_tokens")
        drive(wide)
        home = columns_home(at, r.fin_q, r.qkv_rows, Columns.qkv, r.cs, r.cr, r.qkv_local)
        next(home)
        drive(lower)

        def lower_out(i, carry):
            rows_i = pl.ds(pl.multiple_of(i * 16, 16), 16)
            r.d_down[rows_i, :] = r.down[rows_i, :].astype(F32)
            return carry

        lax.fori_loop(0, hidden_rows // 16, lower_out, 0)
        leaving += send_early(r, "d_down")
        drive(bulk, sums, heads)
        r.d_out[...] = r.out[...].astype(F32)
        drive(home)
        unscale(r.d_qkv, r.qkv_rows, r.w_qkv, r.gain_one, r.d_gain_one)
        for copy in leaving:
            copy.wait()

    deep = 4 * n * rows
    far = max(n - 1, 1)
    return kernel(
        3,
        body,
        {name: (a, HBM if name in ("gu_sum", "down_sum") else LATE if name in late else VMEM) for name, a in ins.items()},
        {
            "d_gu": (like((rows, 2 * FF), F32), EARLY),
            "d_tokens": (like((CHUNK, D), F32), EARLY),
            "d_qkv": (like((rows, (HQ + 2 * HK) * HD), F32), VMEM),
            "d_out": (like((rows, D), F32), VMEM),
            "d_down": (like((hidden_rows, D), F32), EARLY),
            "d_gain_one": (like((rows, 1), F32), VMEM),
            "d_gain_two": (like((rows, 1), F32), VMEM),
            "gain_sum": (like((8, HD), F32), VMEM),
        },
        {
            "gu": pltpu.VMEM((rows, 2 * FF), BF16),
            "qkv_rows": pltpu.VMEM((rows, (HQ + 2 * HK) * HD), BF16),
            "out": pltpu.VMEM((rows, D), BF16),
            "down": pltpu.VMEM((hidden_rows, D), BF16),
            **{name: DMA(()) for name in ("hts", "htr")},
            "part": pltpu.VMEM((SLOTS, CHUNK, D), BF16),
            "land": pltpu.VMEM((7, CHUNK, D), BF16),
            "dx": pltpu.VMEM((CHUNK, D), F32),
            "draw": pltpu.VMEM((SLOTS, CHUNK, QKV_SLOT), BF16),
            "g_qkv": pltpu.VMEM((D, QKV_SLOT), BF16),
            "sib_q": pltpu.VMEM((2, deep, QKV_SLOT), BF16),
            "mid_q": pltpu.VMEM((far, 2, 4, rows, QKV_SLOT), BF16),
            "fin_q": pltpu.VMEM((2, 4, rows, QKV_SLOT), BF16),
            "g_out": pltpu.VMEM((D // SLOTS, D), BF16),
            "sib_o": pltpu.VMEM((D // SLOTS, D), BF16),
            "mid_o": pltpu.VMEM((far, 4 * rows, D), BF16),
            "gain_land": pltpu.VMEM((4 + n, 8, HD), F32),
            "local": DMA((2,)),
            **{name: DMA((len(PARTS), 7)) for name in ("s1", "r1")},
            **{name: DMA((7, 3)) for name in ("cs", "cr")},
            "qkv_local": DMA((3,)),
            **{name: DMA((7, count)) for name in ("ds", "dr")},
            "gu_local": DMA((count,)),
            **{name: DMA((n, 2, 4 * (rows // piece_rows(rows)))) for name in ("cms", "cmr")},
            **{name: DMA((2,)) for name in ("css", "csr")},
            "os": DMA((4,)),
            **{name: DMA(()) for name in ("orr", "oss", "osr")},
            **{name: DMA((n,)) for name in ("oms", "omr")},
            **{name: DMA((4 + n,)) for name in ("gs", "gr")},
        },
    )


def dot(a, b, dims=((1,), (0,))):
    return lax.dot_general(a, b, (dims, ((), ())), preferred_element_type=F32)


def body(tokens, lengths, attn_gain, w_qkv, q_gain, k_gain, w_out, mlp_gain, w_gate_up, w_down, cotangent):
    blocks = lax.axis_size("blk")
    groups = blocks // 4
    rows = w_qkv.shape[0]
    hidden_rows = w_down.shape[0]
    group = lax.axis_index("blk") // 4
    core = lax.axis_index("uly") % 2
    gain_one = attn_gain.astype(F32)[:, None]
    gain_two = mlp_gain.astype(F32)[:, None]

    direct = (2 * hidden_rows) % 128 == 0
    w_gu = w_gate_up
    if not direct:
        w_gu = (
            w_gate_up.reshape(rows, 2, 2, 2, groups, 2, 2 * hidden_rows)
            .transpose(0, 2, 5, 3, 1, 4, 6)
            .reshape(rows, 2 * FF)
        )

    starts = PROMPT + jnp.sum(
        jnp.where(jnp.arange(lengths.shape[0])[:, None] > jnp.arange(lengths.shape[0])[None, :], lengths[None, :], 0), 1
    )
    index = (
        group * (2 * SLOTS * CHUNK)
        + (2 * jnp.arange(SLOTS, dtype=jnp.int32)[:, None] + core) * CHUNK
        + jnp.arange(CHUNK, dtype=jnp.int32)[None, :]
    )
    opening = jnp.max(jnp.where(index[..., None] >= starts, starts, 0), -1)
    position = jnp.where(index < PROMPT, index, index - opening + PROMPT)
    opening = opening - group * (2 * SLOTS * CHUNK)
    opening = jnp.concatenate([opening, opening], 1)[:, None, :]
    lane = np.arange(HD)
    angles = position.astype(F32)[:, :, None] * (ROPE_BASE ** (-2.0 * jnp.asarray(lane % (HD // 2), F32) / HD))
    cosine, sine = jnp.cos(angles), jnp.sin(angles) * np.where(lane < HD // 2, -1.0, 1.0).astype(np.float32)
    head_gain = jnp.stack([q_gain, q_gain, k_gain]).astype(F32)

    front = front_block(
        groups,
        rows,
        hidden_rows,
        {
            "tokens": tokens,
            "cotangent": cotangent,
            "w_qkv": w_qkv,
            "w_gu": w_gu,
            "gain_one": gain_one,
            "gain_two": gain_two,
            "opening": opening,
            "cosine": cosine,
            "sine": sine,
            "head_gain": head_gain,
            "down_mine": w_down,
            "out_mine": w_out,
        },
    )
    xhat2_b, dy_b = (front[name].reshape(SLOTS * CHUNK, D) for name in ("xhat2_b", "dy_b"))
    own, prompt, before = (front[name].reshape(-1, 2 * HD) for name in ("own", "prompt", "before"))
    gu_w, down_w = front["gu"], front["down"].reshape(FF_SLOT, D)

    both = dot(xhat2_b, gu_w)
    gate, up = both[:, :FF_SLOT], both[:, FF_SLOT:]
    sigmoid = jax.nn.sigmoid(gate)
    act = (gate * sigmoid * up).astype(BF16)
    g_down = dot(act, dy_b, ((0,), (0,))).astype(BF16)
    g_down = g_down.reshape(groups, 2, hidden_rows, D)
    theirs = lax.ppermute(
        lax.dynamic_index_in_dim(g_down, 1 - core, 1, keepdims=False), "uly", [(u, u + 1 - 2 * (u % 2)) for u in range(4)]
    )
    down_core = lax.dynamic_index_in_dim(g_down, core, 1, keepdims=False).astype(F32) + theirs.astype(F32)
    down_core = down_core.astype(BF16)
    dact = dot(dy_b, down_w, ((1,), (1,)))
    dboth = jnp.concatenate(
        [dact * up * sigmoid * (1.0 + gate * (1.0 - sigmoid)), dact * gate * sigmoid], 1
    ).astype(BF16)
    down_core, dboth = lax.optimization_barrier((down_core, dboth))
    down_sum = lax.dynamic_index_in_dim(down_core, group, 0, keepdims=False).astype(F32)
    for i in range(1, groups):
        there = lax.dynamic_index_in_dim(down_core, (group + i) % groups, 0, keepdims=False)
        there = lax.ppermute(there, "blk", [(b, (b + 4 * i) % blocks) for b in range(blocks)])
        down_sum = down_sum + there.astype(F32)
    down_sum = down_sum.astype(BF16)
    g_gu = dot(xhat2_b, dboth, ((0,), (0,))).astype(BF16)
    part_dx2 = dot(dboth, gu_w, ((1,), (1,))).astype(BF16)
    back = back_block(
        groups,
        rows,
        {
            "part_dx": part_dx2.reshape(SLOTS, CHUNK, D),
            "act": act.reshape(SLOTS, CHUNK, FF_SLOT),
            "down": down_w,
            "hidden": front["hidden"],
            "cotangent": cotangent,
            "g_gu": g_gu,
            "w_out": front["w_out"],
            "q": front["q"],
            "own": own,
            "prompt": prompt,
            "before": before,
            "opening": opening,
            "total": front["total"],
            "lse": front["lse"],
        },
    )
    last = last_block(
        groups,
        rows,
        hidden_rows,
        {
            "gu_sum": back["gu_sum"],
            "down_sum": down_sum,
            "w_qkv": w_qkv,
            "w_gu": w_gu,
            "gain_one": gain_one,
            "gain_two": gain_two,
            "dq": back["dq"],
            "dkv": back["dkv"],
            "raw": front["raw"],
            "cosine": cosine,
            "sine": sine,
            "head_gain": head_gain,
            "xhat_b": front["xhat_b"],
            "qkv": front["qkv"],
            "mixed": front["mixed"],
            "dbranch": back["dbranch"],
            "tokens": tokens,
            "dhidden": back["dhidden"],
        },
    )
    d_gu = last["d_gu"]
    if not direct:
        d_gu = (
            d_gu.reshape(rows, 2, 2, 2, 2, groups, 2 * hidden_rows)
            .transpose(0, 4, 1, 3, 5, 2, 6)
            .reshape(rows, 2 * FF)
        )
    return (
        back["output"],
        last["d_tokens"],
        last["d_gain_one"][:, 0],
        last["d_qkv"],
        last["gain_sum"][0],
        last["gain_sum"][1],
        last["d_out"],
        last["d_gain_two"][:, 0],
        d_gu,
        last["d_down"],
    )


def solution(mesh):
    tokens = P(("blk", "uly"), None)
    weight = P(("uly", "blk"), None)
    gain = P(("uly", "blk"))
    return jax.shard_map(
        body,
        mesh=mesh,
        in_specs=(tokens, P(), gain, weight, P(), P(), weight, gain, weight, weight, tokens),
        out_specs=(tokens, tokens, gain, weight, P(), P(), weight, gain, weight, weight),
        check_vma=False,
    )
```

```python
import math
import types

import jax
import jax.numpy as jnp
import numpy as np
from jax import lax
from jax.experimental import pallas as pl
from jax.experimental.pallas import tpu as pltpu
from jax.sharding import PartitionSpec as P

D = 2048
HQ = 16
HK = 8
HD = 128
FF = 6144
PROMPT = 2048
LONGEST = 1024

SLOTS = 8
CHUNK = 128
QKV_SLOT = 512
GU_SLOT = 2 * FF // SLOTS
FF_SLOT = FF // SLOTS
EPSILON = 1e-06
ROPE_BASE = 1000000.0
SCALE = 1.0 / math.sqrt(HD)
WINDOW = 10

F32 = jnp.float32
BF16 = jnp.bfloat16
MESH = pl.DeviceIdType.MESH
HBM = pl.BlockSpec(memory_space=pl.ANY)
VMEM = pl.BlockSpec(memory_space=pltpu.VMEM)
DMA = pltpu.SemaphoreType.DMA
PARTS = ((0, 1, 2), 384), ((1, 2, 0), 768), ((2, 0, 1), 896)
FRONT = ((0, 1, 2), 256), ((1, 2, 0), 768), ((2, 0, 1), 1024)


def rem(a, n):
    return lax.rem(a, jnp.int32(n))


class Place:
    def __init__(self, groups):
        self.groups = groups
        self.u = lax.axis_index("uly")
        self.b = lax.axis_index("blk")
        self.x = self.u // 2
        self.c = rem(self.u, 2)
        self.g = self.b // 4
        self.bl = rem(self.b, 4)
        self.bits = (self.x, rem(self.bl, 2), self.bl // 2)

    def flip(self, *dims):
        x, y, z = (rem(v + 1, 2) if d in dims else v for d, v in enumerate(self.bits))
        return x, 2 * z + y

    def coords(self, *dims):
        return [rem(v + 1, 2) if d in dims else v for d, v in enumerate(self.bits)]

    def chunk(self, *dims):
        x, bl = self.flip(*dims)
        return 2 * bl + x

    def slot(self, *dims):
        x, bl = self.flip(*dims)
        return 4 * x + bl

    def cube(self, *dims):
        x, bl = self.flip(*dims)
        return (2 * x + self.c, 4 * self.g + bl)

    def sibling(self):
        return (2 * self.x + 1 - self.c, self.b)

    def ahead(self, i):
        return rem(self.g + i, self.groups)

    def behind(self, i):
        return rem(self.g + self.groups - i, self.groups)

    def mid(self, i):
        return (self.u, 4 * self.ahead(i) + self.bl)

    def diagonal(self):
        x, y, z = self.bits
        return (2 * x + 1 - self.c, 4 * self.g + 2 * z + 1 - y)

    def mid_at(self, group):
        return (self.u, 4 * group + self.bl)


PEERS = ((0,), (1,), (2,), (0, 1), (0, 2), (1, 2), (0, 1, 2))


def meet(devices):
    barrier = pltpu.get_barrier_semaphore()
    for device in devices:
        pl.semaphore_signal(barrier, inc=1, device_id=device, device_id_type=MESH)
    pl.semaphore_wait(barrier, len(devices))


def remote(src, dst, send, recv, device):
    return pltpu.make_async_remote_copy(
        src_ref=src, dst_ref=dst, send_sem=send, recv_sem=recv, device_id=device, device_id_type=MESH
    )


def rows_at(start, count):
    return pl.ds(pl.multiple_of(start, 16), count)


def drive(*tasks):
    tasks = list(tasks)
    while tasks:
        tasks = [task for task in tasks if next(task, None) is not None]


def steps(task, count):
    for _ in range(count):
        next(task, None)


def paced(loop, count, between, when=None):
    def one(i, carry):
        loop(i)
        return carry

    for k in range(4):
        run = (k * count // 4, (k + 1) * count // 4)
        if when is None:
            lax.fori_loop(*run, one, 0)
        else:

            @pl.when(when)
            def _():
                lax.fori_loop(*run, one, 0)

        between()


def piece_rows(rows):
    return 32 if rows % 32 == 0 else 16


def beside(main, *bulk):
    for _ in main:
        for task in bulk:
            next(task, None)


def in_turn(*tasks):
    for task, count in tasks:
        for _ in range(count):
            next(task, None)
            yield True


def part_columns(split):
    start = 0
    for p, (order, width) in enumerate(split):
        yield p, order, pl.ds(start, width)
        start += width


def gather_tokens(at, mine, block, local, send, recv, split=None):
    own = pltpu.make_async_copy(mine, block.at[at.chunk()], local)
    own.start()
    sent = []

    def push(p, i, dims, along, cols):
        src = block.at[at.chunk(*dims), :, cols] if dims else mine.at[:, cols]
        copy = remote(src, block.at[at.chunk(*dims), :, cols], send.at[p, i], recv.at[p, i], at.cube(along))
        copy.start()
        sent.append(copy)

    def arrive(p, i, dims, cols):
        there = block.at[at.chunk(*dims), :, cols]
        remote(there, there, send.at[p, i], recv.at[p, i], at.cube(dims[0])).wait_recv()

    parts = list(part_columns(split or PARTS))
    over = [sorted(parts, key=lambda part: part[1][k] == 2) for k in range(3)]
    for p, (a, b, c), cols in parts:
        push(p, 0, (), a, cols)
        push(p, 1, (), b, cols)
        push(p, 2, (), c, cols)
    yield True
    for p, (a, b, c), cols in over[0]:
        arrive(p, 0, (a,), cols)
        push(p, 3, (a,), b, cols)
        push(p, 4, (a,), c, cols)
        yield True
    for p, (a, b, c), cols in over[1]:
        arrive(p, 1, (b,), cols)
        push(p, 5, (b,), c, cols)
        arrive(p, 3, (a, b), cols)
        push(p, 6, (a, b), c, cols)
        yield True
    for p, (a, b, c), cols in parts:
        arrive(p, 2, (c,), cols)
        arrive(p, 4, (a, c), cols)
        arrive(p, 5, (b, c), cols)
        arrive(p, 6, (a, b, c), cols)
    for copy in sent:
        copy.wait_send()
    own.wait()


def add_rows(dst, terms, count, step=32):
    def body(i, carry):
        rows = pl.ds(pl.multiple_of(i * step, step), step)
        total = terms[0][rows, :].astype(F32)
        for term in terms[1:]:
            total = total + term[rows, :].astype(F32)
        dst[rows, :] = total.astype(dst.dtype)
        return carry

    lax.fori_loop(0, count // step, body, 0)


def scatter_tokens(at, part, land, out, send, recv, split=None):
    sent = []

    def push(p, i, dims, along, cols):
        copy = remote(part.at[at.chunk(*dims), :, cols], land.at[i, :, cols], send.at[p, i], recv.at[p, i], at.cube(along))
        copy.start()
        sent.append(copy)

    def arrive(p, i, along, cols):
        remote(land.at[i, :, cols], land.at[i, :, cols], send.at[p, i], recv.at[p, i], at.cube(along)).wait_recv()

    def add(i, dims, cols):
        here = part.at[at.chunk(*dims), :, cols]
        add_rows(here, [here, land.at[i, :, cols]], CHUNK)

    parts = list(part_columns(split or PARTS))
    over = [sorted(parts, key=lambda part: part[1][k] == 2) for k in range(3)]
    for p, (a, b, c), cols in parts:
        push(p, 3, (a, b, c), c, cols)
        push(p, 2, (b, c), c, cols)
    for p, (a, b, c), cols in parts:
        push(p, 1, (a, c), c, cols)
        push(p, 0, (c,), c, cols)
    yield True
    for p, (a, b, c), cols in over[2]:
        arrive(p, 3, c, cols)
        add(3, (a, b), cols)
        push(p, 5, (a, b), b, cols)
        arrive(p, 2, c, cols)
        add(2, (b,), cols)
        push(p, 4, (b,), b, cols)
        yield True
    for p, (a, b, c), cols in over[1]:
        arrive(p, 1, c, cols)
        add(1, (a,), cols)
        arrive(p, 5, b, cols)
        add(5, (a,), cols)
        push(p, 6, (a,), a, cols)
        yield True
    for p, (a, b, c), cols in over[0]:
        arrive(p, 0, c, cols)
        arrive(p, 4, b, cols)
        arrive(p, 6, a, cols)
        add_rows(
            out.at[:, cols],
            [part.at[at.chunk(), :, cols], land.at[0, :, cols], land.at[4, :, cols], land.at[6, :, cols]],
            CHUNK,
        )
    for copy in sent:
        copy.wait_send()


def column_row(at, rows, u, b):
    return (u * (4 * at.groups) + b) * rows


class Columns:
    def qkv(x, y, z):
        pair = 4 * x + 2 * y + z
        return [(pair * (2 * HD), 2 * HD), (HQ * HD + pair * HD, HD), ((HQ + HK) * HD + pair * HD, HD)]

    def gate_up(groups, hidden_rows):
        wide = 2 * hidden_rows
        if wide % 128:
            return lambda x, y, z: [((4 * x + 2 * z + y) * GU_SLOT, GU_SLOT)]

        def runs(x, y, z):
            return [
                (half * FF + (((2 * x + y) * groups + group) * 2 + z) * wide, wide)
                for half in range(2)
                for group in range(groups)
            ]

        return runs


def column_runs(ref, whole, runs):
    at = 0
    for first, width in runs:
        yield ref.at[:, pl.ds(pl.multiple_of(first, 128), width)], whole.at[:, pl.ds(at, width)]
        at += width


def columns_in_cube(at, mine, whole, runs, local, send, recv, rows):
    own = rows_at(column_row(at, rows, at.u, at.b), rows)
    here = []
    for k, (src, dst) in enumerate(column_runs(mine, whole.at[own], runs(*at.coords()))):
        here.append(pltpu.make_async_copy(src, dst, local.at[k]))
        here[-1].start()
    sent = []
    for i, dims in enumerate(PEERS):
        for k, (src, dst) in enumerate(column_runs(mine, whole.at[own], runs(*at.coords(*dims)))):
            copy = remote(src, dst, send.at[i, k], recv.at[i, k], at.cube(*dims))
            copy.start()
            sent.append(copy)
    yield True
    for i, dims in enumerate(PEERS):
        u, b = at.cube(*dims)
        there = whole.at[rows_at(column_row(at, rows, u, b), rows)]
        for k, (_, dst) in enumerate(column_runs(mine, there, runs(*at.coords()))):
            remote(dst, dst, send.at[i, k], recv.at[i, k], (u, b)).wait_recv()
    for copy in sent:
        copy.wait_send()
    for copy in here:
        copy.wait()


def columns_across(at, whole, rows, mid_send, mid_recv, sib_send, sib_recv):
    n, pieces = at.groups, mid_send.shape[2]
    step = 4 * rows // pieces
    sent = []

    def piece(core, group, x, k):
        return whole.at[rows_at(column_row(at, rows, 2 * x + core, 4 * group) + k * step, step)]

    def pass_on(i, x, k):
        there = piece(at.c, at.behind(i), x, k)
        copy = remote(there, there, sib_send.at[i, x, k], sib_recv.at[i, x, k], at.sibling())
        copy.start()
        sent.append(copy)

    order = [(x, k) for x in range(2) for k in range(pieces)]
    every = [(i, x, k) for i in range(1, n) for x, k in order]

    def arrived(i, x, k):
        there = piece(at.c, at.behind(i), x, k)
        remote(there, there, mid_send.at[i, x, k], mid_recv.at[i, x, k], at.mid(i)).wait_recv()
        pass_on(i, x, k)

    for m, (i, x, k) in enumerate(every):
        there = piece(at.c, at.g, x, k)
        copy = remote(there, there, mid_send.at[i, x, k], mid_recv.at[i, x, k], at.mid(i))
        copy.start()
        sent.append(copy)
        if i == 1:
            pass_on(0, x, k)
        if m >= WINDOW:
            arrived(*every[m - WINDOW])
        yield True
    for one in every[max(len(every) - WINDOW, 0) :]:
        arrived(*one)
    for i in range(n):
        for x, k in order:
            there = piece(1 - at.c, at.behind(i), x, k)
            remote(there, there, sib_send.at[i, x, k], sib_recv.at[i, x, k], at.sibling()).wait_recv()
    for copy in sent:
        copy.wait_send()


def gather_hidden(at, mine, whole, local, turn_send, turn_recv, mid_send, mid_recv, sib_send, sib_recv):
    n, rows, pieces = at.groups, mine.shape[0], mid_send.shape[1]
    step = rows // pieces
    own = whole.at[at.g, at.c]
    stays = at.bits[1] == at.c
    here = pltpu.make_async_copy(mine, own, local)
    there = remote(mine, whole.at[at.g, 1 - at.c], turn_send, turn_recv, at.diagonal())

    @pl.when(stays)
    def _():
        here.start()

    @pl.when(jnp.logical_not(stays))
    def _():
        there.start()

    yield True

    @pl.when(stays)
    def _():
        here.wait()

    @pl.when(jnp.logical_not(stays))
    def _():
        there.wait()

    sent = []
    for i in range(1, n):
        for k in range(pieces):
            piece = own.at[pl.ds(k * step, step)]
            copy = remote(piece, piece, mid_send.at[i, k], mid_recv.at[i, k], at.mid(i))
            copy.start()
            sent.append(copy)
            yield True

    def pass_on(i):
        group = whole.at[at.behind(i), at.c]
        copy = remote(group, group, sib_send.at[i], sib_recv.at[i], at.sibling())
        copy.start()
        sent.append(copy)

    pass_on(0)
    for i in range(1, n):
        for k in range(pieces):
            piece = whole.at[at.behind(i), at.c, pl.ds(k * step, step)]
            remote(piece, piece, mid_send.at[i, k], mid_recv.at[i, k], at.mid(i)).wait_recv()
        pass_on(i)
    for i in range(n):
        group = whole.at[at.behind(i), 1 - at.c]
        remote(group, group, sib_send.at[i], sib_recv.at[i], at.sibling()).wait_recv()
    for copy in sent:
        copy.wait_send()


class OutRows:
    def __init__(self, at, rows):
        self.at, self.rows = at, rows
        self.per_half = max(at.groups // 2, 1)
        self.my_half = at.g // self.per_half
        self.to = 2 * self.my_half + at.c
        self.collects = at.bl == self.to
        self.slot_core = rem(at.bl, 2) == at.c
        self.slot_half = at.bl // 2

    def group_rows(self, group, half):
        return rows_at((group - half * self.per_half) * (4 * self.rows), 4 * self.rows)

    def in_half(self, group, half):
        return group // self.per_half == half

    def device(self, bl):
        return (self.at.u, 4 * self.at.g + bl)


def gather_heads(at, mine, whole, local, send, recv, sib_send, sib_recv):
    n, rows = mine.shape[0], mine.shape[1]
    lay = OutRows(at, rows)

    def place(group, bl):
        half = group // lay.per_half
        return whole.at[rows_at(((group - half * lay.per_half) * 4 + bl) * rows, rows)]

    def push(i):
        group = at.behind(i)
        to = 2 * (group // lay.per_half) + at.c
        here = pltpu.make_async_copy(mine.at[i], place(group, at.bl), local.at[i])
        there = remote(mine.at[i], place(group, at.bl), send.at[i], recv.at[i, at.bl], lay.device(to))
        return at.bl == to, here, there

    for i in range(n):
        stays, here, there = push(i)

        @pl.when(stays)
        def _():
            here.start()

        @pl.when(jnp.logical_not(stays))
        def _():
            there.start()

    yield True

    @pl.when(lay.slot_core)
    def _():
        for i in range(n):
            group = at.behind(i)

            @pl.when(lay.in_half(group, lay.slot_half))
            def _():
                pltpu.make_async_copy(mine.at[i], place(group, at.bl), local.at[i]).wait()
                for bl in range(4):

                    @pl.when(at.bl != bl)
                    def _():
                        there = place(group, bl)
                        remote(there, there, send.at[i], recv.at[i, bl], lay.device(bl)).wait_recv()

        remote(whole, whole, sib_send, sib_recv, at.sibling()).start()

    yield True

    @pl.when(lay.slot_core)
    def _():
        remote(whole, whole, sib_send, sib_recv, at.sibling()).wait_send()

    @pl.when(jnp.logical_not(lay.slot_core))
    def _():
        remote(whole, whole, sib_send, sib_recv, at.sibling()).wait_recv()

    for i in range(n):
        stays, here, there = push(i)

        @pl.when(jnp.logical_not(stays))
        def _():
            there.wait_send()


def columns_home(at, final, out, runs, send, recv, local):
    sent = []
    for i, dims in enumerate(PEERS):
        x, bl = at.flip(*dims)
        for k, (dst, src) in enumerate(column_runs(out, final.at[x, bl], runs(*at.coords()))):
            copy = remote(src, dst, send.at[i, k], recv.at[i, k], at.cube(*dims))
            copy.start()
            sent.append(copy)
    here = []
    for k, (dst, src) in enumerate(column_runs(out, final.at[at.x, at.bl], runs(*at.coords()))):
        here.append(pltpu.make_async_copy(src, dst, local.at[k]))
        here[-1].start()
    yield True
    for i, dims in enumerate(PEERS):
        for k, (there, _) in enumerate(column_runs(out, final.at[at.x, at.bl], runs(*at.coords(*dims)))):
            remote(there, there, send.at[i, k], recv.at[i, k], at.cube(*dims)).wait_recv()
    for copy in sent:
        copy.wait_send()
    for copy in here:
        copy.wait()


def columns_sum(at, part, sib_land, mid_land, final, sems, at_once=1):
    n, rows = at.groups, final.shape[2]
    mid_send, mid_recv, sib_send, sib_recv = sems
    run, deep = 4 * rows, 4 * n * rows
    step = piece_rows(rows)
    pieces = [(k, j) for k in range(4) for j in range(rows // step)]
    sent = []

    def of_core(x, core):
        return part.at[rows_at((2 * x + core) * deep, deep)]

    for x in range(2):
        copy = remote(of_core(x, 1 - at.c), sib_land.at[x], sib_send.at[x], sib_recv.at[x], at.sibling())
        copy.start()
        sent.append(copy)
    yield True
    for x in range(2):
        remote(sib_land.at[x], sib_land.at[x], sib_send.at[x], sib_recv.at[x], at.sibling()).wait_recv()
        for i in range(1, n):
            for m, (k, j) in enumerate(pieces):
                offset = at.ahead(i) * run + k * rows + j * step
                there = part.at[rows_at((2 * x + at.c) * deep + offset, step)]
                add_rows(there, [there, sib_land.at[x, rows_at(offset, step)]], step, 16)
                land = mid_land.at[i - 1, x, k, pl.ds(j * step, step)]
                copy = remote(there, land, mid_send.at[i, x, m], mid_recv.at[i, x, m], at.mid(i))
                copy.start()
                sent.append(copy)
                if m % at_once == at_once - 1:
                    yield True
    for x in range(2):
        for m, (k, j) in enumerate(pieces):
            for i in range(1, n):
                there = mid_land.at[i - 1, x, k, pl.ds(j * step, step)]
                remote(there, there, mid_send.at[i, x, m], mid_recv.at[i, x, m], at.mid(i)).wait_recv()
            offset = at.g * run + k * rows + j * step
            rows_here = pl.ds(j * step, step)
            add_rows(
                final.at[x, k, rows_here],
                [part.at[rows_at((2 * x + at.c) * deep + offset, step)], sib_land.at[x, rows_at(offset, step)]]
                + [mid_land.at[i - 1, x, k, rows_here] for i in range(1, n)],
                step,
                16,
            )
    for copy in sent:
        copy.wait_send()


def turn_hidden(at, final, out, turn_send, turn_recv, local):
    stays = at.bits[1] == at.c
    here = pltpu.make_async_copy(final, out, local)
    there = remote(final, out, turn_send, turn_recv, at.diagonal())

    @pl.when(stays)
    def _():
        here.start()

    @pl.when(jnp.logical_not(stays))
    def _():
        there.start()

    yield True

    @pl.when(stays)
    def _():
        here.wait()

    @pl.when(jnp.logical_not(stays))
    def _():
        there.wait()


def scatter_heads(at, part, out, sib_land, mid_land, sems):
    n, rows = at.groups, out.shape[0]
    send, recv, mid_send, mid_recv, sib_send, sib_recv, local = sems
    lay = OutRows(at, rows)

    @pl.when(jnp.logical_not(lay.slot_core))
    def _():
        remote(part, sib_land, sib_send, sib_recv, at.sibling()).start()

    yield True

    @pl.when(lay.slot_core)
    def _():
        remote(part, sib_land, sib_send, sib_recv, at.sibling()).wait_recv()
        add_rows(part, [part, sib_land], 256, 16)
        for i in range(1, n):
            group = at.ahead(i)

            @pl.when(lay.in_half(group, lay.slot_half))
            def _():
                there = part.at[lay.group_rows(group, lay.slot_half)]
                remote(there, mid_land.at[i - 1], mid_send.at[i], mid_recv.at[i], at.mid(i)).start()

    yield True
    mine = part.at[lay.group_rows(at.g, lay.my_half)]
    base = (at.g - lay.my_half * lay.per_half) * (4 * rows)

    @pl.when(lay.collects)
    def _():
        for i in range(1, n):
            remote(mine, mid_land.at[i - 1], mid_send.at[i], mid_recv.at[i], at.mid(i)).wait_recv()
        add_rows(mine, [mine] + [mid_land.at[i - 1] for i in range(1, n)], 4 * rows, 16)
        for bl in range(4):
            there = part.at[rows_at(base + bl * rows, rows)]

            @pl.when(at.bl != bl)
            def _():
                remote(there, out, send.at[bl], recv, lay.device(bl)).start()

            @pl.when(at.bl == bl)
            def _():
                pltpu.make_async_copy(there, out, local).start()

    yield True

    @pl.when(jnp.logical_not(lay.collects))
    def _():
        remote(out, out, send.at[0], recv, lay.device(lay.to)).wait_recv()

    @pl.when(lay.collects)
    def _():
        for bl in range(4):
            there = part.at[rows_at(base + bl * rows, rows)]

            @pl.when(at.bl != bl)
            def _():
                remote(there, out, send.at[bl], recv, lay.device(bl)).wait_send()

            @pl.when(at.bl == bl)
            def _():
                pltpu.make_async_copy(there, out, local).wait()

    @pl.when(jnp.logical_not(lay.slot_core))
    def _():
        remote(part, sib_land, sib_send, sib_recv, at.sibling()).wait_send()

    @pl.when(lay.slot_core)
    def _():
        for i in range(1, n):
            group = at.ahead(i)

            @pl.when(lay.in_half(group, lay.slot_half))
            def _():
                there = part.at[lay.group_rows(group, lay.slot_half)]
                remote(there, mid_land.at[i - 1], mid_send.at[i], mid_recv.at[i], at.mid(i)).wait_send()


def sum_everywhere(at, mine, land, send, recv):
    for i, device in enumerate([at.sibling(), at.cube(0), at.cube(1), at.cube(2)]):
        copy = remote(mine, land.at[i], send.at[i], recv.at[i], device)
        copy.start()
        yield True
        copy.wait()
        mine[...] = mine[...] + land[i]
    sent = []
    for i in range(1, at.groups):
        copy = remote(mine, land.at[3 + i], send.at[3 + i], recv.at[3 + i], at.mid(i))
        copy.start()
        sent.append(copy)
    yield True
    for copy in sent:
        copy.wait()
    for i in range(1, at.groups):
        mine[...] = mine[...] + land[3 + i]


def everyone(at):
    return [at.cube(*dims) for dims in PEERS] + [at.sibling()] + [at.mid(i) for i in range(1, at.groups)]


def cube_only(at):
    return [at.cube(*dims) for dims in ((0,), (1,), (2,))]


def communicate(body, collective_id, ins, outs, scratch, in_specs, out_specs, limit=60):
    return pl.pallas_call(
        body,
        out_shape=outs,
        in_specs=in_specs,
        out_specs=out_specs,
        scratch_shapes=scratch,
        compiler_params=pltpu.CompilerParams(
            collective_id=collective_id, has_side_effects=True, vmem_limit_bytes=limit << 20
        ),
    )(*ins)


def like(shape, dtype=BF16):
    return jax.ShapeDtypeStruct(shape, dtype)


NT = (((1,), (1,)), ((), ()))
WIDE = 512
SCALE_2 = SCALE / math.log(2.0)


def visible(first_key, chunk_of_block, opening, tile):
    key = first_key + lax.broadcasted_iota(jnp.int32, (tile, 2 * CHUNK), 0)
    lane = lax.broadcasted_iota(jnp.int32, (1, 2 * CHUNK), 1)
    row = chunk_of_block * CHUNK + jnp.where(lane >= CHUNK, lane - CHUNK, lane)
    return (key <= row) & (key >= opening)


def key_range(group, chunk_of_block, tile):
    stop = (chunk_of_block * CHUNK + CHUNK + tile - 1) // tile
    start = jnp.where(group > 0, jnp.maximum(chunk_of_block * CHUNK - LONGEST, 0) // tile, 0)
    return start, stop


def two_heads(block):
    return jnp.concatenate([block[:, :HD], block[:, HD:]], 0)


def two_columns(block):
    return jnp.concatenate([block[:CHUNK], block[CHUNK:]], 1)


def turn_values(kv, turned):
    for t in range(kv.shape[0]):
        turned[:, pl.ds(2 * CHUNK * t, 2 * CHUNK)] = kv[t].reshape(2 * CHUNK, 2 * HD)[:, HD:].T


def front_block(groups, rows, hidden_rows, ins):
    n = groups
    gate_up = Columns.gate_up(groups, hidden_rows)
    count = len(gate_up(0, 0, 0))
    pieces = hidden_rows // piece_rows(hidden_rows)
    gu_pieces = 4 * rows // piece_rows(4 * rows)

    def body(r):
        at = Place(n)
        group, core = at.g, at.c

        def first_norm(i, carry):
            rows_i = pl.ds(pl.multiple_of(i * 32, 32), 32)
            value = r.tokens[rows_i, :].astype(F32)
            r.xhat[rows_i, :] = (value * lax.rsqrt(jnp.mean(value * value, 1, keepdims=True) + EPSILON)).astype(BF16)
            return carry

        lax.fori_loop(0, CHUNK // 32, first_norm, 0)
        r.qkv_mine[...] = (r.w_qkv[...].astype(F32) * r.gains[:, 0:1]).astype(BF16)
        meet(everyone(at) + [at.diagonal()])
        far = [remote(r.out_mine, r.out_all.at[i], r.fs.at[i], r.fr.at[i], at.mid(i)) for i in range(1, n)]
        for copy in far:
            copy.start()
        wide = columns_in_cube(at, r.qkv_mine, r.qkv, Columns.qkv, r.qkv_local, r.qs, r.qr, rows)
        next(wide)
        tokens = gather_tokens(at, r.xhat, r.xhat_b, r.local.at[1], r.s1, r.r1, FRONT)
        next(tokens)
        lower = gather_hidden(at, r.down_mine, r.down, r.local.at[2], r.hts, r.htr, r.hms, r.hmr, r.hss, r.hsr)
        next(lower)
        out_here = pltpu.make_async_copy(r.out_mine, r.out_all.at[0], r.local.at[3])
        out_here.start()

        def scale(i, carry):
            cols = pl.ds(pl.multiple_of(i * 1024, 1024), 1024)
            r.gu_mine[:, cols] = (r.w_gu[:, cols].astype(F32) * r.gains[:, 1:2]).astype(BF16)
            return carry

        lax.fori_loop(0, 2 * FF // 1024, scale, 0)

        def round_dy(i, carry):
            rows_i = pl.ds(pl.multiple_of(i * 32, 32), 32)
            r.dy[rows_i, :] = r.cotangent[rows_i, :].astype(BF16)
            return carry

        lax.fori_loop(0, CHUNK // 32, round_dy, 0)
        steps(tokens, 3)
        drive(wide)
        wide = columns_across(at, r.qkv, rows, r.qms, r.qmr, r.qss, r.qsr)
        steps(wide, 2 * (n - 1))
        steps(tokens, 3)
        columns = columns_in_cube(at, r.gu_mine, r.gu, gate_up, r.gu_local, r.cs, r.cr, rows)
        next(columns)
        out_here.wait()
        for copy in far:
            copy.wait()
        heads = gather_heads(at, r.out_all, r.w_out, r.hl, r.hs, r.hr, r.os, r.orr)
        next(heads)
        steps(lower, 1)
        drive(tokens)
        drive(wide)

        def project_in(i):
            four = pl.ds(pl.multiple_of(4 * i, 4), 4)
            raw = jnp.dot(r.xhat_b[four].reshape(4 * CHUNK, D), r.qkv[...], preferred_element_type=F32)
            cosine, sine = r.cosine[four].reshape(4 * CHUNK, HD), r.sine[four].reshape(4 * CHUNK, HD)
            heads = []
            for h in range(3):
                head = raw[:, h * HD : (h + 1) * HD]
                gain = r.head_gain[h : h + 1, :]
                normed = head * lax.rsqrt(jnp.mean(head * head, 1, keepdims=True) + EPSILON) * gain
                heads.append((normed * cosine + pltpu.roll(normed, HD // 2, 1) * sine).astype(BF16))
            r.raw[four] = raw[:, : 3 * HD].reshape(4, CHUNK, 3 * HD)
            r.q[four] = jnp.concatenate(heads[:2], 1).reshape(4, CHUNK, 2 * HD)
            r.kv[four] = jnp.concatenate([heads[2], raw[:, 3 * HD :].astype(BF16)], 1).reshape(4, CHUNK, 2 * HD)

        for i in range(2):
            lax.fori_loop(i, i + 1, lambda i, carry: (project_in(i), carry)[1], 0)
        leaving = send_early(r, "xhat_b", "qkv", "raw")

        here = pltpu.make_async_copy(r.kv, r.own.at[:, core], r.local.at[1])
        here.start()
        sib = remote(r.kv, r.own.at[:, core], r.ks.at[0], r.kr.at[0], at.sibling())
        sib.start()

        def to_group(i):
            return remote(r.kv, r.prompt.at[:, core], r.ps.at[i], r.pr, at.mid_at(jnp.int32(i)))

        def forward():
            half = r.kv.at[pl.ds(SLOTS // 2, SLOTS // 2)]
            return remote(half, r.before.at[:, core], r.bs, r.br, at.mid_at(group + 1))

        def across(ref, i):
            return remote(ref.at[:, core], ref.at[:, core], r.ks.at[i], r.kr.at[i], at.sibling())

        @pl.when(group == 0)
        def _():
            for i in range(1, n):
                to_group(i).start()

        if n > 2:

            @pl.when((group >= 1) & (group < n - 1))
            def _():
                forward().start()

        here.wait()
        sib.wait()
        turn_values(r.own, r.own_vt)
        drive(columns)
        columns = columns_across(at, r.gu, rows, r.cms, r.cmr, r.css, r.csr)
        bulk = in_turn((lower, pieces * (n - 1) - 1), (columns, 2 * gu_pieces * (n - 1)))
        steps(bulk, 1)
        dy = gather_tokens(at, r.dy, r.dy_b, r.local.at[4], r.s3, r.r3)
        next(dy)

        def step(kv, values_t, tile, chunk, q, opening, carry, masked, shift=0):
            norm, out = carry
            first = tile * WIDE
            parts = []
            for k in range(WIDE // CHUNK):
                keys = kv[tile * (WIDE // (2 * CHUNK)) + k // 2, k % 2][:, :HD]
                p = jnp.exp2(lax.dot_general(keys, q, NT, preferred_element_type=F32) * SCALE_2)
                if masked:
                    p = jnp.where(visible(first + shift + k * CHUNK, chunk, opening, CHUNK), p, 0.0)
                norm = norm + jnp.sum(p, 0, keepdims=True)
                parts.append(p.astype(BF16))
            first = first if isinstance(first, int) else pl.multiple_of(first, WIDE)
            out = out + jnp.dot(
                values_t[:, pl.ds(first, WIDE)], jnp.concatenate(parts, 0), preferred_element_type=F32
            )
            return norm, out

        def own_part(i):
            chunk = 2 * i + core
            query, opening = two_heads(r.q[i]), r.opening[i]
            start, stop = key_range(group, chunk, WIDE)
            zero = (jnp.zeros((1, 2 * CHUNK), F32), jnp.zeros((HD, 2 * CHUNK), F32))
            norm, out = lax.fori_loop(
                start, stop, lambda t, c: step(r.own, r.own_vt, t, chunk, query, opening, c, True), zero
            )
            r.lse[i] = norm
            r.total[i] = out

        paced(own_part, SLOTS, lambda: None)
        next(heads)

        @pl.when(group > 0)
        def _():
            to_group(0).wait_recv()
            across(r.prompt, 1).start()

        if n > 2:

            @pl.when(group > 1)
            def _():
                forward().wait_recv()
                across(r.before, 2).start()

        steps(dy, 3)
        steps(bulk, 1)

        @pl.when(group > 0)
        def _():
            across(r.prompt, 1).wait()
            turn_values(r.prompt, r.prompt_vt)

        def prompt_part(i):
            query = two_heads(r.q[i])
            state = (r.lse[i], r.total[i])
            for t in range(PROMPT // WIDE):
                state = step(r.prompt, r.prompt_vt, t, 0, query, None, state, False)
            r.lse[i], r.total[i] = state

        paced(prompt_part, SLOTS, lambda: steps(bulk, 1), group > 0)

        if n > 2:

            @pl.when(group > 1)
            def _():
                across(r.before, 2).wait()
                turn_values(r.before, r.before_vt)

                def before_part(i, carry):
                    query, opening = two_heads(r.q[i]), r.opening[i]
                    state = (r.lse[i], r.total[i])
                    for t in range(LONGEST // WIDE):
                        state = step(r.before, r.before_vt, t, 2 * i + core, query, opening, state, True, -LONGEST)
                    r.lse[i], r.total[i] = state
                    return carry

                lax.fori_loop(0, SLOTS // 2, before_part, 0)

        steps(dy, 3)
        steps(bulk, 1)
        drive(heads)

        def project_out(i, carry):
            norm = r.lse[i]
            out = r.total[i] / norm
            r.total[i] = out
            r.lse[i] = jnp.log(norm)
            row = two_columns(out.T.astype(BF16))
            r.mixed[i] = row
            r.part[i] = jnp.dot(row, r.w_out[...], preferred_element_type=F32).astype(BF16)
            return carry

        lax.fori_loop(0, SLOTS, project_out, 0)
        beside(scatter_tokens(at, r.part, r.land, r.hidden, r.s4, r.r4, FRONT), bulk)

        def norm_rows(i, carry):
            rows = pl.ds(pl.multiple_of(i * 32, 32), 32)
            value = r.hidden[rows, :] + r.tokens[rows, :].astype(F32)
            r.hidden[rows, :] = value
            inverse = lax.rsqrt(jnp.mean(value * value, 1, keepdims=True) + EPSILON)
            r.mine[rows, :] = (value * inverse).astype(BF16)
            return carry

        lax.fori_loop(0, CHUNK // 32, norm_rows, 0)
        beside(gather_tokens(at, r.mine, r.xhat2_b, r.local.at[5], r.s2, r.r2, FRONT), bulk)
        drive(dy, bulk)
        drive(lower, columns)
        for copy in leaving:
            copy.wait()

        @pl.when(group == 0)
        def _():
            for i in range(1, n):
                to_group(i).wait_send()

        if n > 2:

            @pl.when((group >= 1) & (group < n - 1))
            def _():
                forward().wait_send()

    chunks = (SLOTS, CHUNK, 2 * HD)
    block, end = (SLOTS, 2, CHUNK, 2 * HD), (SLOTS // 2, 2, CHUNK, 2 * HD)
    tok = DMA((len(PARTS), 7))
    return kernel(
        1,
        body,
        {name: (a, HBM if name in ("down_mine", "out_mine") else VMEM) for name, a in ins.items()},
        {
            "xhat_b": (like((SLOTS, CHUNK, D)), EARLY),
            "qkv": (like((D, QKV_SLOT)), EARLY),
            "raw": (like((SLOTS, CHUNK, 3 * HD), F32), EARLY),
            "q": (like(chunks), VMEM),
            "mixed": (like(chunks), VMEM),
            "total": (like((SLOTS, HD, 2 * CHUNK), F32), VMEM),
            "lse": (like((SLOTS, 1, 2 * CHUNK), F32), VMEM),
            "own": (like(block), VMEM),
            "prompt": (like(block), VMEM),
            "before": (like(end), VMEM),
            "w_out": (like((D // SLOTS, D)), VMEM),
            "hidden": (like((CHUNK, D), F32), VMEM),
            "xhat2_b": (like((SLOTS, CHUNK, D)), HBM),
            "gu": (like((D, GU_SLOT)), HBM),
            "down": (like((n, 2, hidden_rows, D)), HBM),
            "dy_b": (like((SLOTS, CHUNK, D)), HBM),
        },
        {
            "kv": pltpu.VMEM(chunks, BF16),
            "xhat": pltpu.VMEM((CHUNK, D), BF16),
            "dy": pltpu.VMEM((CHUNK, D), BF16),
            "qkv_mine": pltpu.VMEM((rows, (HQ + 2 * HK) * HD), BF16),
            "gu_mine": pltpu.VMEM((rows, 2 * FF), BF16),
            "own_vt": pltpu.VMEM((HD, 2 * SLOTS * CHUNK), BF16),
            "prompt_vt": pltpu.VMEM((HD, PROMPT), BF16),
            "before_vt": pltpu.VMEM((HD, LONGEST), BF16),
            "part": pltpu.VMEM((SLOTS, CHUNK, D), BF16),
            "land": pltpu.VMEM((7, CHUNK, D), BF16),
            "mine": pltpu.VMEM((CHUNK, D), BF16),
            "out_all": pltpu.VMEM((n, rows, D), BF16),
            "local": DMA((6,)),
            **{name: tok for name in ("s1", "r1", "s2", "r2", "s3", "r3", "s4", "r4")},
            **{name: DMA((7, 3)) for name in ("qs", "qr")},
            **{name: DMA((7, count)) for name in ("cs", "cr")},
            "qkv_local": DMA((3,)),
            "gu_local": DMA((count,)),
            **{name: DMA((n, 2, 1)) for name in ("qms", "qmr", "qss", "qsr")},
            **{name: DMA((n, 2, gu_pieces)) for name in ("cms", "cmr", "css", "csr")},
            **{name: DMA((n, pieces)) for name in ("hms", "hmr")},
            **{name: DMA((n,)) for name in ("hss", "hsr", "fs", "fr", "hl", "hs", "ps")},
            **{name: DMA(()) for name in ("hts", "htr", "os", "orr", "pr", "bs", "br")},
            "hr": DMA((n, 4)),
            **{name: DMA((3,)) for name in ("ks", "kr")},
        },
    )


def attention_back(at, r, part, between, when=None):
    kv, keys_t, acc = getattr(r, part), getattr(r, part + "_kt"), getattr(r, "acc_" + part)

    def begin():
        keys_t[...] = kv[:, :HD].T
        acc[...] = jnp.zeros_like(acc)

    shift = -LONGEST if part == "before" else 0

    def step(t, dq, q, do, dot_rows, logs, chunk, opening):
        first = t * WIDE
        rows = pl.ds(first if isinstance(first, int) else pl.multiple_of(first, WIDE), WIDE)
        keys, values = kv[rows, :HD], kv[rows, HD:]
        p = jnp.exp2(lax.dot_general(keys, q, NT, preferred_element_type=F32) * SCALE_2 - logs)
        if part != "prompt":
            p = jnp.where(visible(first + shift, chunk, opening, WIDE), p, 0.0)
        dp = lax.dot_general(values, do, NT, preferred_element_type=F32)
        ds = (p * (dp - dot_rows)).astype(BF16)
        acc[rows, :HD] += jnp.dot(ds, q, preferred_element_type=F32)
        acc[rows, HD:] += jnp.dot(p.astype(BF16), do, preferred_element_type=F32)
        return dq + jnp.dot(keys_t[:, rows], ds, preferred_element_type=F32)

    def one(i):
        chunk = 2 * i + at.c
        q, do = two_heads(r.q[i]), two_heads(r.do[i])
        args = (q, do, r.dots[i], r.lse[i] * (1.0 / math.log(2.0)), chunk, r.opening[i])
        if part == "own":
            start, stop = key_range(at.g, chunk, WIDE)
            r.dq_sum[i] = lax.fori_loop(start, stop, lambda t, dq: step(t, dq, *args), r.dq_sum[i])
        else:
            dq = r.dq_sum[i]
            for t in range(kv.shape[0] // WIDE):
                dq = step(t, dq, *args)
            r.dq_sum[i] = dq

    def end():
        out = getattr(r, "d_" + part)
        for t in range(out.shape[0] * 2):
            out[t // 2, t % 2, :, :HD] = (acc[t * CHUNK : (t + 1) * CHUNK, :HD] * SCALE).astype(BF16)
            out[t // 2, t % 2, :, HD:] = acc[t * CHUNK : (t + 1) * CHUNK, HD:].astype(BF16)

    count = SLOTS if part != "before" else SLOTS // 2
    if when is None:
        begin()
        paced(one, count, between)
        end()
    else:
        pl.when(when)(begin)
        paced(one, count, between, when)
        pl.when(when)(end)


def add_chunks(dst, first, other, skip=0):
    def one(i, carry):
        dst[i + skip] = (first(i).astype(F32) + other[i].astype(F32)).astype(BF16)
        return carry

    lax.fori_loop(0, other.shape[0], one, 0)


LATE, EARLY = "late", "early"


def kernel(collective_id, body, ins, outs, scratch):
    results = list(outs)
    early = [name for name, (_, spec) in outs.items() if spec is EARLY]
    scratch = {
        **scratch,
        **{name: pltpu.VMEM(outs[name][0].shape, outs[name][0].dtype) for name in early},
        **({"early": DMA((len(early),))} if early else {}),
    }
    outs = {name + "_out" if name in early else name: (a, HBM if name in early else spec) for name, (a, spec) in outs.items()}
    late = [name for name, (_, spec) in ins.items() if spec is LATE]
    scratch = {
        **scratch,
        **{name + "_late": pltpu.VMEM(ins[name][0].shape, ins[name][0].dtype) for name in late},
        **({"late": DMA((len(late),))} if late else {}),
    }
    ins = {name: (a, HBM if spec is LATE else spec) for name, (a, spec) in ins.items()}
    names = [*ins, *outs, *scratch]
    return dict(
        zip(
            results,
            communicate(
                lambda *refs: body(types.SimpleNamespace(**dict(zip(names, refs)), early_names=early)),
                collective_id,
                tuple(a for a, _ in ins.values()),
                tuple(a for a, _ in outs.values()),
                list(scratch.values()),
                [spec for _, spec in ins.values()],
                [spec for _, spec in outs.values()],
            ),
        )
    )


def bring_late(r):
    copies = {}
    for k, name in enumerate([name for name in vars(r) if name.endswith("_late")]):
        name = name[: -len("_late")]
        here = getattr(r, name + "_late")
        copies[name] = pltpu.make_async_copy(getattr(r, name), here, r.late.at[k])
        copies[name].start()
        setattr(r, name, here)

    def wait(*some):
        for name in some or list(copies):
            copies.pop(name).wait()

    return wait


def send_early(r, *names):
    copies = []
    for name in names:
        k = r.early_names.index(name)
        copies.append(pltpu.make_async_copy(getattr(r, name), getattr(r, name + "_out"), r.early.at[k]))
        copies[-1].start()
    return copies


def back_block(groups, rows, ins):
    n = groups

    def body(r):
        at = Place(n)
        group = at.g
        bring_dx = pltpu.make_async_copy(r.part_dx, r.part, r.local.at[3])
        bring_dx.start()
        loaded = bring_late(r)
        meet(everyone(at))
        columns = columns_sum(at, r.g_gu, r.sib_gu, r.mid_gu, r.gu_sum, (r.cms, r.cmr, r.css, r.csr))
        next(columns)
        bring_dx.wait()
        bulk = in_turn((columns, r.cms.shape[1] * r.cms.shape[2] * (n - 1)))
        beside(scatter_tokens(at, r.part, r.land, r.dx, r.s1, r.r1), bulk)

        def norm(i, carry):
            rows = pl.ds(pl.multiple_of(i * 32, 32), 32)
            value = r.hidden[rows, :]
            inverse = lax.rsqrt(jnp.mean(value * value, 1, keepdims=True) + EPSILON)
            unit = value * inverse
            grad = r.dx[rows, :]
            total = r.cotangent[rows, :] + inverse * (grad - unit * jnp.mean(grad * unit, 1, keepdims=True))
            r.dhidden[rows, :] = total
            r.mine[rows, :] = total.astype(BF16)
            return carry

        lax.fori_loop(0, CHUNK // 32, norm, 0)
        loaded("act", "down")
        for k, _ in enumerate(gather_tokens(at, r.mine, r.dbranch, r.local.at[0], r.s2, r.r2)):
            steps(bulk, 1)
            if k < SLOTS // 2:
                two = pl.ds(2 * k, 2)
                r.part[two] = (
                    jnp.dot(r.act[two].reshape(2 * CHUNK, FF_SLOT), r.down[...], preferred_element_type=F32)
                    .astype(BF16)
                    .reshape(2, CHUNK, D)
                )
        result = scatter_tokens(at, r.part, r.land2, r.dx, r.s3, r.r3)
        next(result)

        loaded()
        leaving = send_early(r, "dhidden", "dbranch")

        def heads(i, carry):
            do = lax.dot_general(r.dbranch[i], r.w_out[...], NT, preferred_element_type=F32).astype(BF16)
            r.do[i] = do
            r.dots[i] = jnp.sum(two_heads(do).astype(F32).T * r.total[i], 0, keepdims=True)
            r.dq_sum[i] = jnp.zeros((HD, 2 * CHUNK), F32)
            return carry

        lax.fori_loop(0, SLOTS, heads, 0)

        def swap(array, place, i):
            return remote(array.at[:, 1 - at.c], place, r.ks.at[i], r.kr.at[i], at.sibling())

        def home(i):
            return remote(r.land_p, r.far_p.at[i - 1], r.ps, r.pr.at[i - 1], at.mid_at(jnp.int32(0)))

        def back():
            return remote(r.land_b, r.far_b, r.bs, r.br, at.mid_at(group - 1))

        def between():
            steps(bulk, 1)
            steps(result, 1)

        attention_back(at, r, "prompt", between, group > 0)

        @pl.when(group > 0)
        def _():
            swap(r.d_prompt, r.land_p, 1).start()

        if n > 2:
            attention_back(at, r, "before", between, group > 1)

            @pl.when(group > 1)
            def _():
                swap(r.d_before, r.land_b, 2).start()

        @pl.when(group > 0)
        def _():
            swap(r.d_prompt, r.land_p, 1).wait()
            add_chunks(r.land_p, lambda i: r.d_prompt[i, at.c], r.land_p)
            for i in range(1, n):

                @pl.when(group == i)
                def _():
                    home(i).start()

        if n > 2:

            @pl.when(group > 1)
            def _():
                swap(r.d_before, r.land_b, 2).wait()
                add_chunks(r.land_b, lambda i: r.d_before[i, at.c], r.land_b)
                back().start()

        attention_back(at, r, "own", between)
        first = swap(r.d_own, r.land_k, 0)
        first.start()
        drive(bulk)

        def queries(i, carry):
            r.dq[i] = two_columns((r.dq_sum[i].T * SCALE).astype(BF16))
            return carry

        lax.fori_loop(0, SLOTS, queries, 0)
        first.wait()
        add_chunks(r.dkv, lambda i: r.d_own[i, at.c], r.land_k)
        drive(result)

        def add(i, carry):
            rows = pl.ds(pl.multiple_of(i * 32, 32), 32)
            r.output[rows, :] = (r.hidden[rows, :] + r.dx[rows, :]).astype(BF16)
            return carry

        lax.fori_loop(0, CHUNK // 32, add, 0)

        @pl.when(group == 0)
        def _():
            for i in range(1, n):
                home(i).wait_recv()
                add_chunks(r.dkv, lambda j: r.dkv[j], r.far_p.at[i - 1])

        if n > 2:

            @pl.when((group >= 1) & (group < n - 1))
            def _():
                back().wait_recv()
                add_chunks(r.dkv, lambda j: r.dkv[j + SLOTS // 2], r.far_b, SLOTS // 2)

            @pl.when(group > 1)
            def _():
                back().wait_send()

        @pl.when(group > 0)
        def _():
            home(1).wait_send()

        drive(columns)
        for copy in leaving:
            copy.wait()

    chunks = (SLOTS, CHUNK, 2 * HD)
    block, end = (SLOTS, 2, CHUNK, 2 * HD), (SLOTS // 2, 2, CHUNK, 2 * HD)
    tok = DMA((len(PARTS), 7))
    near, half = pltpu.VMEM(chunks, BF16), pltpu.VMEM((SLOTS // 2, CHUNK, 2 * HD), BF16)
    own, prompt, before = 2 * SLOTS * CHUNK, PROMPT, LONGEST
    far = max(n - 1, 1)
    gu_pieces = 4 * (rows // piece_rows(rows))
    late = ("act", "down", "w_out", "q", "own", "prompt", "before", "total")
    return kernel(
        2,
        body,
        {
            name: (a, HBM if name == "part_dx" else LATE if name in late else VMEM)
            for name, a in ins.items()
        },
        {
            "dhidden": (like((CHUNK, D), F32), EARLY),
            "output": (like((CHUNK, D)), VMEM),
            "dbranch": (like((SLOTS, CHUNK, D)), EARLY),
            "dq": (like(chunks), VMEM),
            "dkv": (like(chunks), VMEM),
            "gu_sum": (like((2, 4, rows, GU_SLOT)), VMEM),
        },
        {
            "part": pltpu.VMEM((SLOTS, CHUNK, D), BF16),
            "land": pltpu.VMEM((7, CHUNK, D), BF16),
            "land2": pltpu.VMEM((7, CHUNK, D), BF16),
            "mine": pltpu.VMEM((CHUNK, D), BF16),
            "dx": pltpu.VMEM((CHUNK, D), F32),
            "sib_gu": pltpu.VMEM((2, 4 * n * rows, GU_SLOT), BF16),
            "mid_gu": pltpu.VMEM((far, 2, 4, rows, GU_SLOT), BF16),
            "do": near,
            "dots": pltpu.VMEM((SLOTS, 1, 2 * CHUNK), F32),
            "dq_sum": pltpu.VMEM((SLOTS, HD, 2 * CHUNK), F32),
            "own_kt": pltpu.VMEM((HD, own), BF16),
            "prompt_kt": pltpu.VMEM((HD, prompt), BF16),
            "before_kt": pltpu.VMEM((HD, before), BF16),
            "acc_own": pltpu.VMEM((own, 2 * HD), F32),
            "acc_prompt": pltpu.VMEM((prompt, 2 * HD), F32),
            "acc_before": pltpu.VMEM((before, 2 * HD), F32),
            "d_own": pltpu.VMEM(block, BF16),
            "d_prompt": pltpu.VMEM(block, BF16),
            "d_before": pltpu.VMEM(end, BF16),
            "land_k": near,
            "land_p": near,
            "land_b": half,
            "far_p": pltpu.VMEM((far, *chunks), BF16),
            "far_b": half,
            "local": DMA((4,)),
            **{name: tok for name in ("s1", "r1", "s2", "r2", "s3", "r3")},
            **{name: DMA((n, 2, gu_pieces)) for name in ("cms", "cmr")},
            **{name: DMA((2,)) for name in ("css", "csr")},
            **{name: DMA((3,)) for name in ("ks", "kr")},
            "ps": DMA(()),
            "pr": DMA((n,)),
            "bs": DMA(()),
            "br": DMA(()),
        },
    )


def last_block(groups, rows, hidden_rows, ins):
    n = groups
    gate_up = Columns.gate_up(groups, hidden_rows)
    count = len(gate_up(0, 0, 0))
    late = ("dbranch", "xhat_b", "qkv", "w_gu", "w_qkv")

    def unscale(dst, grad, weight, gain, d_gain):
        total = jnp.zeros((rows, 1), F32)
        for k in range(dst.shape[1] // 2048):
            cols = pl.ds(2048 * k, 2048)
            value = grad[:, cols].astype(F32)
            dst[:, cols] = value * gain
            total = total + jnp.sum(value * weight[:, cols].astype(F32), 1, keepdims=True)
        d_gain[...] = total

    def body(r):
        at = Place(n)
        loaded = bring_late(r)
        meet(everyone(at) + [at.diagonal()])
        bring = columns_home(at, r.gu_sum, r.gu, gate_up, r.ds, r.dr, r.gu_local)
        next(bring)
        lower = turn_hidden(at, r.down_sum, r.down, r.hts, r.htr, r.local.at[0])
        next(lower)
        loaded("dbranch")
        turned = r.mixed[...].reshape(SLOTS * CHUNK, 2 * HD).T

        for k in range(D // 512):
            cols = pl.ds(512 * k, 512)
            r.g_out[:, cols] = jnp.dot(
                turned, r.dbranch[:, :, cols].reshape(SLOTS * CHUNK, 512), preferred_element_type=F32
            ).astype(BF16)
        heads = scatter_heads(at, r.g_out, r.out, r.sib_o, r.mid_o, (r.os, r.orr, r.oms, r.omr, r.oss, r.osr, r.local.at[1]))
        next(heads)
        r.gain_sum[...] = jnp.zeros_like(r.gain_sum)

        def through_heads(i, carry):
            two = pl.ds(pl.multiple_of(2 * i, 2), 2)
            cosine, sine = r.cosine[two].reshape(2 * CHUNK, HD), r.sine[two].reshape(2 * CHUNK, HD)
            raw = r.raw[two].reshape(2 * CHUNK, 3 * HD)
            dq, dkv = r.dq[two].reshape(2 * CHUNK, 2 * HD), r.dkv[two].reshape(2 * CHUNK, 2 * HD)
            parts = []
            for h in range(3):
                grad = (dq[:, h * HD : (h + 1) * HD] if h < 2 else dkv[:, :HD]).astype(F32)
                head = raw[:, h * HD : (h + 1) * HD]
                inverse = lax.rsqrt(jnp.mean(head * head, 1, keepdims=True) + EPSILON)
                unit = head * inverse
                back = grad * cosine + pltpu.roll(grad * sine, HD // 2, 1)
                at_row = 0 if h < 2 else 1
                r.gain_sum[at_row : at_row + 1, :] += jnp.sum(back * unit, 0, keepdims=True)
                back = back * r.head_gain[h : h + 1, :]
                parts.append((inverse * (back - unit * jnp.mean(back * unit, 1, keepdims=True))).astype(BF16))
            draw = jnp.concatenate(parts + [dkv[:, HD:]], 1)
            r.draw[two] = draw.reshape(2, CHUNK, QKV_SLOT)
            return carry

        lax.fori_loop(0, SLOTS // 2, through_heads, 0)
        next(heads)
        sums = sum_everywhere(at, r.gain_sum, r.gain_land, r.gs, r.gr)
        loaded()
        for h in range(QKV_SLOT // HD):
            steps(sums, 1)
            cols = pl.ds(h * HD, HD)
            turned = r.draw[:, :, cols].reshape(SLOTS * CHUNK, HD).T
            grad = jnp.dot(turned, r.xhat_b[...].reshape(SLOTS * CHUNK, D), preferred_element_type=F32)
            r.g_qkv[:, cols] = grad.astype(BF16).T
        wide = columns_sum(at, r.g_qkv, r.sib_q, r.mid_q, r.fin_q, (r.cms, r.cmr, r.css, r.csr), 4)
        next(wide)

        def part_dx(i, carry):
            two = pl.ds(pl.multiple_of(2 * i, 2), 2)
            grad = lax.dot_general(
                r.draw[two].reshape(2 * CHUNK, QKV_SLOT), r.qkv[...], NT, preferred_element_type=F32
            )
            r.part[two] = grad.astype(BF16).reshape(2, CHUNK, D)
            return carry

        lax.fori_loop(0, SLOTS // 2, part_dx, 0)
        steps(wide, 1)
        bulk = in_turn((wide, 2 * (rows // piece_rows(rows)) * (n - 1) - 1))
        main = scatter_tokens(at, r.part, r.land, r.dx, r.s1, r.r1)
        for _ in range(4):
            next(main)
            steps(bulk, 1)
        drive(bring)
        unscale(r.d_gu, r.gu, r.w_gu, r.gains[:, 1:2], r.d_gain_two)
        leaving = send_early(r, "d_gu")
        next(heads)
        beside(main, bulk)

        def norm(i, carry):
            rows = pl.ds(pl.multiple_of(i * 32, 32), 32)
            value = r.tokens[rows, :].astype(F32)
            inverse = lax.rsqrt(jnp.mean(value * value, 1, keepdims=True) + EPSILON)
            unit = value * inverse
            grad = r.dx[rows, :]
            r.d_tokens[rows, :] = r.dhidden[rows, :] + inverse * (grad - unit * jnp.mean(grad * unit, 1, keepdims=True))
            return carry

        lax.fori_loop(0, CHUNK // 32, norm, 0)
        leaving += send_early(r, "d_tokens")
        drive(wide)
        home = columns_home(at, r.fin_q, r.qkv_rows, Columns.qkv, r.cs, r.cr, r.qkv_local)
        next(home)
        drive(lower)

        def lower_out(i, carry):
            rows_i = pl.ds(pl.multiple_of(i * 16, 16), 16)
            r.d_down[rows_i, :] = r.down[rows_i, :].astype(F32)
            return carry

        lax.fori_loop(0, hidden_rows // 16, lower_out, 0)
        leaving += send_early(r, "d_down")
        drive(bulk, sums, heads)
        r.d_out[...] = r.out[...].astype(F32)
        drive(home)
        unscale(r.d_qkv, r.qkv_rows, r.w_qkv, r.gains[:, 0:1], r.d_gain_one)
        for copy in leaving:
            copy.wait()

    deep = 4 * n * rows
    far = max(n - 1, 1)
    return kernel(
        3,
        body,
        {name: (a, HBM if name in ("gu_sum", "down_sum") else LATE if name in late else VMEM) for name, a in ins.items()},
        {
            "d_gu": (like((rows, 2 * FF), F32), EARLY),
            "d_tokens": (like((CHUNK, D), F32), EARLY),
            "d_qkv": (like((rows, (HQ + 2 * HK) * HD), F32), VMEM),
            "d_out": (like((rows, D), F32), VMEM),
            "d_down": (like((hidden_rows, D), F32), EARLY),
            "d_gain_one": (like((rows, 1), F32), VMEM),
            "d_gain_two": (like((rows, 1), F32), VMEM),
            "gain_sum": (like((8, HD), F32), VMEM),
        },
        {
            "gu": pltpu.VMEM((rows, 2 * FF), BF16),
            "qkv_rows": pltpu.VMEM((rows, (HQ + 2 * HK) * HD), BF16),
            "out": pltpu.VMEM((rows, D), BF16),
            "down": pltpu.VMEM((hidden_rows, D), BF16),
            **{name: DMA(()) for name in ("hts", "htr")},
            "part": pltpu.VMEM((SLOTS, CHUNK, D), BF16),
            "land": pltpu.VMEM((7, CHUNK, D), BF16),
            "dx": pltpu.VMEM((CHUNK, D), F32),
            "draw": pltpu.VMEM((SLOTS, CHUNK, QKV_SLOT), BF16),
            "g_qkv": pltpu.VMEM((D, QKV_SLOT), BF16),
            "sib_q": pltpu.VMEM((2, deep, QKV_SLOT), BF16),
            "mid_q": pltpu.VMEM((far, 2, 4, rows, QKV_SLOT), BF16),
            "fin_q": pltpu.VMEM((2, 4, rows, QKV_SLOT), BF16),
            "g_out": pltpu.VMEM((D // SLOTS, D), BF16),
            "sib_o": pltpu.VMEM((D // SLOTS, D), BF16),
            "mid_o": pltpu.VMEM((far, 4 * rows, D), BF16),
            "gain_land": pltpu.VMEM((4 + n, 8, HD), F32),
            "local": DMA((2,)),
            **{name: DMA((len(PARTS), 7)) for name in ("s1", "r1")},
            **{name: DMA((7, 3)) for name in ("cs", "cr")},
            "qkv_local": DMA((3,)),
            **{name: DMA((7, count)) for name in ("ds", "dr")},
            "gu_local": DMA((count,)),
            **{name: DMA((n, 2, 4 * (rows // piece_rows(rows)))) for name in ("cms", "cmr")},
            **{name: DMA((2,)) for name in ("css", "csr")},
            "os": DMA((4,)),
            **{name: DMA(()) for name in ("orr", "oss", "osr")},
            **{name: DMA((n,)) for name in ("oms", "omr")},
            **{name: DMA((4 + n,)) for name in ("gs", "gr")},
        },
    )


def dot(a, b, dims=((1,), (0,))):
    return lax.dot_general(a, b, (dims, ((), ())), preferred_element_type=F32)


def body(tokens, lengths, attn_gain, w_qkv, q_gain, k_gain, w_out, mlp_gain, w_gate_up, w_down, cotangent):
    blocks = lax.axis_size("blk")
    groups = blocks // 4
    rows = w_qkv.shape[0]
    hidden_rows = w_down.shape[0]
    group = lax.axis_index("blk") // 4
    core = lax.axis_index("uly") % 2
    gains = jnp.stack([attn_gain, mlp_gain], 1).astype(F32)

    direct = (2 * hidden_rows) % 128 == 0
    w_gu = w_gate_up
    if not direct:
        w_gu = (
            w_gate_up.reshape(rows, 2, 2, 2, groups, 2, 2 * hidden_rows)
            .transpose(0, 2, 5, 3, 1, 4, 6)
            .reshape(rows, 2 * FF)
        )

    starts = PROMPT + jnp.sum(
        jnp.where(jnp.arange(lengths.shape[0])[:, None] > jnp.arange(lengths.shape[0])[None, :], lengths[None, :], 0), 1
    )
    index = (
        group * (2 * SLOTS * CHUNK)
        + (2 * jnp.arange(SLOTS, dtype=jnp.int32)[:, None] + core) * CHUNK
        + jnp.arange(CHUNK, dtype=jnp.int32)[None, :]
    )
    opening = jnp.max(jnp.where(index[..., None] >= starts, starts, 0), -1)
    position = jnp.where(index < PROMPT, index, index - opening + PROMPT)
    opening = opening - group * (2 * SLOTS * CHUNK)
    opening = jnp.concatenate([opening, opening], 1)[:, None, :]
    lane = np.arange(HD)
    angles = position.astype(F32)[:, :, None] * (ROPE_BASE ** (-2.0 * jnp.asarray(lane % (HD // 2), F32) / HD))
    cosine, sine = jnp.cos(angles), jnp.sin(angles) * np.where(lane < HD // 2, -1.0, 1.0).astype(np.float32)
    head_gain = jnp.stack([q_gain, q_gain, k_gain]).astype(F32)

    front = front_block(
        groups,
        rows,
        hidden_rows,
        {
            "tokens": tokens,
            "cotangent": cotangent,
            "w_qkv": w_qkv,
            "w_gu": w_gu,
            "gains": gains,
            "opening": opening,
            "cosine": cosine,
            "sine": sine,
            "head_gain": head_gain,
            "down_mine": w_down,
            "out_mine": w_out,
        },
    )
    xhat2_b, dy_b = (front[name].reshape(SLOTS * CHUNK, D) for name in ("xhat2_b", "dy_b"))
    own, prompt, before = (front[name].reshape(-1, 2 * HD) for name in ("own", "prompt", "before"))
    gu_w, down_w = front["gu"], front["down"].reshape(FF_SLOT, D)

    both = dot(xhat2_b, gu_w)
    gate, up = both[:, :FF_SLOT], both[:, FF_SLOT:]
    sigmoid = jax.nn.sigmoid(gate)
    act = (gate * sigmoid * up).astype(BF16)
    g_down = dot(act, dy_b, ((0,), (0,))).astype(BF16)
    g_down = g_down.reshape(groups, 2, hidden_rows, D)
    theirs = lax.ppermute(
        lax.dynamic_index_in_dim(g_down, 1 - core, 1, keepdims=False), "uly", [(u, u + 1 - 2 * (u % 2)) for u in range(4)]
    )
    down_core = lax.dynamic_index_in_dim(g_down, core, 1, keepdims=False).astype(F32) + theirs.astype(F32)
    down_core = down_core.astype(BF16)
    dact = dot(dy_b, down_w, ((1,), (1,)))
    dboth = jnp.concatenate(
        [dact * up * sigmoid * (1.0 + gate * (1.0 - sigmoid)), dact * gate * sigmoid], 1
    ).astype(BF16)
    down_core, dboth = lax.optimization_barrier((down_core, dboth))
    down_sum = lax.dynamic_index_in_dim(down_core, group, 0, keepdims=False).astype(F32)
    for i in range(1, groups):
        there = lax.dynamic_index_in_dim(down_core, (group + i) % groups, 0, keepdims=False)
        there = lax.ppermute(there, "blk", [(b, (b + 4 * i) % blocks) for b in range(blocks)])
        down_sum = down_sum + there.astype(F32)
    down_sum = down_sum.astype(BF16)
    g_gu = dot(xhat2_b, dboth, ((0,), (0,))).astype(BF16)
    part_dx2 = dot(dboth, gu_w, ((1,), (1,))).astype(BF16)
    back = back_block(
        groups,
        rows,
        {
            "part_dx": part_dx2.reshape(SLOTS, CHUNK, D),
            "act": act.reshape(SLOTS, CHUNK, FF_SLOT),
            "down": down_w,
            "hidden": front["hidden"],
            "cotangent": cotangent,
            "g_gu": g_gu,
            "w_out": front["w_out"],
            "q": front["q"],
            "own": own,
            "prompt": prompt,
            "before": before,
            "opening": opening,
            "total": front["total"],
            "lse": front["lse"],
        },
    )
    last = last_block(
        groups,
        rows,
        hidden_rows,
        {
            "gu_sum": back["gu_sum"],
            "down_sum": down_sum,
            "w_qkv": w_qkv,
            "w_gu": w_gu,
            "gains": gains,
            "dq": back["dq"],
            "dkv": back["dkv"],
            "raw": front["raw"],
            "cosine": cosine,
            "sine": sine,
            "head_gain": head_gain,
            "xhat_b": front["xhat_b"],
            "qkv": front["qkv"],
            "mixed": front["mixed"],
            "dbranch": back["dbranch"],
            "tokens": tokens,
            "dhidden": back["dhidden"],
        },
    )
    d_gu = last["d_gu"]
    if not direct:
        d_gu = (
            d_gu.reshape(rows, 2, 2, 2, 2, groups, 2 * hidden_rows)
            .transpose(0, 4, 1, 3, 5, 2, 6)
            .reshape(rows, 2 * FF)
        )
    return (
        back["output"],
        last["d_tokens"],
        last["d_gain_one"][:, 0],
        last["d_qkv"],
        last["gain_sum"][0],
        last["gain_sum"][1],
        last["d_out"],
        last["d_gain_two"][:, 0],
        d_gu,
        last["d_down"],
    )


def solution(mesh):
    tokens = P(("blk", "uly"), None)
    weight = P(("uly", "blk"), None)
    gain = P(("uly", "blk"))
    return jax.shard_map(
        body,
        mesh=mesh,
        in_specs=(tokens, P(), gain, weight, P(), P(), weight, gain, weight, weight, tokens),
        out_specs=(tokens, tokens, gain, weight, P(), P(), weight, gain, weight, weight),
        check_vma=False,
    )
```
